32 devices in a mesh: gx: 4 (over z), gy: 4 (over y, core), gz: 2 (over x).
Axes of the slice: x: 2, y: 2, z: 4, core: 2. Of those that a mesh axis runs over, the one named last changes fastest.
Arguments:
- offset_vector_field: float32 [3, 64, 64, 256], P(None, 'gx', 'gy', 'gz'), may hold values from -2 to 2
- earlier_creep_deformation: float32 [6, 64, 64, 256], P(None, 'gx', 'gy', 'gz'), may hold values from -0.6 to 0.6
- thermal_state: float32 [64, 64, 256], P('gx', 'gy', 'gz'), may hold values from 1 to 2
- rock_mass_per_volume: float32 [64, 64, 256], P('gx', 'gy', 'gz'), may hold values from 0.5 to 1.5
- rupture_band_indicator: int32 [64, 64, 256], P('gx', 'gy', 'gz'), may hold values 0 or 1
Outputs:
- strain_next: float32 [6, 64, 64, 256], P(None, 'gx', 'gy', 'gz')
- momentum_residual: float32 [3, 64, 64, 256], P(None, 'gx', 'gy', 'gz')
The draws below stay inside these ranges and needn't reach their ends.
All inputs are finite; a program needn't handle non-finite values. No bound on the sum of `rupture_band_indicator` on one device may be relied on, other than what follows from the above.
Results may differ from the reference program's by a relative error of at most 0.00009.
Values sent between devices are 32-bit elements; how exact they have to be, the bound alone decides.
A program may use at most 64 MiB of HBM per device.

```python
import jax
import jax.numpy as jnp
from jax import lax

TRACE_POINTS = 64
INCLINE_POINTS = 64
VERTICAL_POINTS = 256


def plant(drawn, stream_key, least, high):
    shape = drawn.shape
    index_at = [jax.random.randint(jax.random.fold_in(stream_key, axis), (), 0, shape[axis]) for axis in range(len(shape))]
    drawn = drawn.at[tuple(index_at)].set(least)
    longest = shape.index(max(shape))
    index_at[longest] = (index_at[longest] + 1) % shape[longest]
    return drawn.at[tuple(index_at)].set(high)


def steps_of(own_key, extent, cuts, low, largest):
    def one(axis_at, blocks):
        heights = jax.random.uniform(jax.random.fold_in(jax.random.fold_in(own_key, 6), axis_at), (blocks,), jnp.float32, low / len(cuts), largest / len(cuts))
        return jnp.repeat(jnp.exp(heights), extent[axis_at] // blocks).reshape((-1,) + (1,) * (len(extent) - axis_at - 1))

    loudness = one(*cuts[0])
    for cut in cuts[1:]:
        loudness = loudness * one(*cut)
    return loudness


def noise(rng, extent, spread, reach, split=(), held_as=jnp.bfloat16):
    entries = jax.random.normal(rng, extent, jnp.float32) * spread
    if len(split) > 0:
        entries = steps_of(rng, extent, split, -0.22, 0.18) * entries
    return jnp.clip(entries, min=-reach, max=reach).astype(held_as)


def setup_inputs(seed: int = 0) -> dict:
    arg_keys = jax.random.split(jax.random.key(seed), 6)
    return {
        "offset_vector_field": noise(arg_keys[0], (3, TRACE_POINTS, INCLINE_POINTS, VERTICAL_POINTS), 0.3, 2.0, ((1, 4), (2, 4), (3, 2)), jnp.float32),
        "earlier_creep_deformation": noise(arg_keys[1], (6, TRACE_POINTS, INCLINE_POINTS, VERTICAL_POINTS), 0.1, 0.6, ((1, 4), (2, 4), (3, 2)), jnp.float32),
        "thermal_state": jnp.clip(1.0 + 1.0 * jax.random.uniform(arg_keys[2], (TRACE_POINTS, INCLINE_POINTS, VERTICAL_POINTS), jnp.float32) ** steps_of(arg_keys[2], (TRACE_POINTS, INCLINE_POINTS, VERTICAL_POINTS), ((0, 4), (1, 4), (2, 2)), -0.2, 0.2), 1.0, 2.0),
        "rock_mass_per_volume": jnp.clip(0.5 + 1.0 * jax.random.uniform(arg_keys[3], (TRACE_POINTS, INCLINE_POINTS, VERTICAL_POINTS), jnp.float32) ** steps_of(arg_keys[3], (TRACE_POINTS, INCLINE_POINTS, VERTICAL_POINTS), ((0, 4), (1, 4), (2, 2)), -0.2, 0.2), 0.5, 1.5),
        "rupture_band_indicator": plant((jax.random.randint(arg_keys[4], (TRACE_POINTS, INCLINE_POINTS, VERTICAL_POINTS), 0, 8) < 1).astype(jnp.int32), jax.random.fold_in(arg_keys[4], 1), 0, 1),
    }


def central(field, axis):
    pad_list = [(0, 0), (0, 0), (0, 0)]
    pad_list[axis] = (1, 1)
    padded = jnp.pad(field, pad_list)
    length = padded.shape[axis]
    upper = lax.slice_in_dim(padded, 2, length, axis=axis)
    lower = lax.slice_in_dim(padded, 0, length - 2, axis=axis)
    return (upper - lower) * 0.5


def stress_of(elastic):
    trace = elastic[0] + elastic[1] + elastic[2]
    return [2.0 * elastic[0] + trace, 2.0 * elastic[1] + trace, 2.0 * elastic[2] + trace,
            2.0 * elastic[3], 2.0 * elastic[4], 2.0 * elastic[5]]


def evolve_deformation(deformation_parts, earlier_creep_deformation, lithostatic_load, thermal_state, rupture_band_indicator):
    traction_matrix = stress_of([deformation_parts[index] - earlier_creep_deformation[index] for index in range(6)])
    mean_stress = (traction_matrix[0] + traction_matrix[1] + traction_matrix[2]) / 3.0
    deviator = [traction_matrix[0] - mean_stress, traction_matrix[1] - mean_stress, traction_matrix[2] - mean_stress,
                traction_matrix[3], traction_matrix[4], traction_matrix[5]]
    quadratic_scalar_measure = 0.5 * (deviator[0] * deviator[0] + deviator[1] * deviator[1] + deviator[2] * deviator[2])
    quadratic_scalar_measure = quadratic_scalar_measure + deviator[3] * deviator[3] + deviator[4] * deviator[4] + deviator[5] * deviator[5]
    rupture_weakening = 1.0 + 7.0 * rupture_band_indicator.astype(jnp.float32)
    weakening_multiplier = 0.5 * rupture_weakening * jnp.exp(-(2.0 + 2.0 * lithostatic_load) / thermal_state) * quadratic_scalar_measure
    fresh_deformation = jnp.stack([earlier_creep_deformation[index] + weakening_multiplier * deviator[index] for index in range(6)])
    stress_next = stress_of([deformation_parts[index] - fresh_deformation[index] for index in range(6)])
    return fresh_deformation, stress_next


def reference(offset_vector_field, earlier_creep_deformation, thermal_state, rock_mass_per_volume, rupture_band_indicator):
    gradient = [[central(offset_vector_field[component], direction) for direction in range(3)] for component in range(3)]
    deformation_parts = [gradient[0][0], gradient[1][1], gradient[2][2],
                    0.5 * (gradient[0][1] + gradient[1][0]),
                    0.5 * (gradient[0][2] + gradient[2][0]),
                    0.5 * (gradient[1][2] + gradient[2][1])]
    depth_index = jnp.arange(VERTICAL_POINTS, dtype=jnp.float32)
    weight = rock_mass_per_volume * (1.0 + 2.0 * depth_index / VERTICAL_POINTS) / VERTICAL_POINTS
    lithostatic_load = jnp.cumsum(weight, axis=2) - 0.5 * weight
    fresh_deformation, traction_matrix = evolve_deformation(deformation_parts, earlier_creep_deformation, lithostatic_load, thermal_state, rupture_band_indicator)
    along_x = jnp.stack([central(traction_matrix[0], 0), central(traction_matrix[3], 0), central(traction_matrix[4], 0)])
    along_y = jnp.stack([central(traction_matrix[3], 1), central(traction_matrix[1], 1), central(traction_matrix[5], 1)])
    along_z = jnp.stack([central(traction_matrix[4], 2), central(traction_matrix[5], 2), central(traction_matrix[2], 2)])
    zeros = jnp.zeros_like(rock_mass_per_volume)
    momentum = along_x + along_y + along_z - jnp.stack([zeros, zeros, 0.5 * rock_mass_per_volume])
    return fresh_deformation, momentum
```

```python
import functools

import jax
import jax.numpy as jnp
from jax import lax
from jax.experimental import pallas as pl
from jax.experimental.pallas import tpu as pltpu
from jax.sharding import PartitionSpec as P

MESH = pl.DeviceIdType.MESH
AXES = ("gx", "gy", "gz")
ORDER = (2, 1, 0)
TERMS = (
    ((0, 0.5), (3, 0.25), (4, 0.25)),
    ((3, 0.25), (1, 0.5), (5, 0.25)),
    ((4, 0.25), (5, 0.25), (2, 0.5)),
)
X_SET = (0, 3, 4)
Y_SET = (3, 1, 5)
Z_SET = (4, 5, 2)


def upper(o):
    return tuple(o[a] for a in ORDER) > (0, 0, 0)


def offsets(layers):
    near = [
        (x, y, z)
        for x in (-1, 0, 1)
        for y in (-1, 0, 1)
        for z in (-1, 0, 1)
        if 1 <= abs(x) + abs(y) + abs(z) <= 2
    ]
    far = [
        (x, y, s * d)
        for d in range(2, layers)
        for s in (-1, 1)
        for x, y in ((0, 0), (-1, 0), (1, 0), (0, -1), (0, 1))
    ]
    return near + far


def minus(o):
    return tuple(-v for v in o)


def merge(low, high):
    Z = low.shape[1]
    even = (lax.broadcasted_iota(jnp.int32, low.shape, 1) & 1) == 0
    return jnp.where(even, low, pltpu.roll(high, Z - 2, 1))


def edge_term(tile, q, z_edge):
    Z = tile.shape[1]
    return (pltpu.roll(tile, (Z - 2 * q) % Z, 1) if q else tile) * z_edge


def flow(e, pace):
    trace = e[0] + e[1] + e[2]
    third = trace * (1.0 / 3.0)
    half = [e[0] - third, e[1] - third, e[2] - third, e[3], e[4], e[5]]
    second = half[0] * half[0] + half[1] * half[1] + half[2] * half[2]
    second = second + 2.0 * (half[3] * half[3] + half[4] * half[4] + half[5] * half[5])
    rate = pace * second
    return trace, [rate * h for h in half]


def stress(e, change, trace, part):
    out = 2.0 * (e[part] - change[part])
    return out + trace if part < 3 else out


def kernel(
    dims, sizes,
    u_hbm, e_hbm, t_hbm, r_hbm, b_hbm,
    fv, mv,
    uv, ev, tv, rv, bv, pv, tot, el, av, nt, sp,
    xs, ys, yu, zu, zs, xy, zt, xt, yt,
    rxu, rxs, ryu, rys, rzu, rzs, rxy, rxz, ryz, rt, rtx, rty,
    in_sem, ready,
    xu_send, xu_recv, xs_send, xs_recv, yu_send, yu_recv, ys_send, ys_recv,
    zu_send, zu_recv, zs_send, zs_recv, xy_send, xy_recv, xz_send, xz_recv, yz_send, yz_recv,
    t_send, t_recv, tx_send, tx_recv, ty_send, ty_recv,
):
    X, Y, Z = dims
    N = X * Y
    layers = sizes[2]
    depths = range(1, layers)
    me = [lax.axis_index(a) for a in AXES]
    offs = offsets(layers)
    uppers = [o for o in offs if upper(o)]
    lowers = [o for o in offs if not upper(o)]

    def exists(o):
        ok = None
        for a in range(3):
            if o[a]:
                here = me[a] + o[a]
                test = here < sizes[a] if o[a] > 0 else here >= 0
                ok = test if ok is None else jnp.logical_and(ok, test)
        return ok

    def partner(o):
        return {AXES[a]: me[a] + o[a] for a in range(3) if o[a]}

    has = {o: exists(o) for o in offs}
    faces = {a: [tuple(s if i == a else 0 for i in range(3)) for s in (-1, 1)] for a in range(3)}

    loads = [
        pltpu.make_async_copy(src, dst, in_sem.at[i])
        for i, (src, dst) in enumerate(
            (
                (u_hbm, uv.at[:, pl.ds(Y, N), :]),
                (r_hbm, rv),
                (t_hbm, tv),
                (b_hbm, bv),
                (e_hbm, ev),
            )
        )
    ]
    for copy in loads:
        copy.start()

    barrier = pltpu.get_barrier_semaphore()
    for o in uppers:
        @pl.when(has[o])
        def _(o=o):
            pl.semaphore_signal(barrier, inc=1, device_id=partner(o), device_id_type=MESH)
    expected = jnp.int32(0)
    for o in lowers:
        expected = expected + has[o].astype(jnp.int32)

    plane = jnp.zeros((Y, Z), jnp.float32)
    row_plane = jnp.zeros((X, Z), jnp.float32)
    for c in range(3):
        uv[c, pl.ds(0, Y), :] = plane
        uv[c, pl.ds(Y + N, Y), :] = plane
    for c in range(6):
        sp[c, pl.ds(0, Y), :] = plane
        sp[c, pl.ds(Y + N, Y), :] = plane

    def blank(o, *refs):
        @pl.when(jnp.logical_not(has[o]))
        def _():
            for ref in refs:
                ref[...] = jnp.zeros(ref.shape, jnp.float32)

    for i, sz in enumerate((-1, 1)):
        blank((0, 0, sz), rzu.at[i], rzs.at[i])
        for j, s in enumerate((-1, 1)):
            blank((s, 0, sz), rxz.at[j, i])
            blank((0, s, sz), ryz.at[j, i])
    for i, sx in enumerate((-1, 1)):
        for j, sy in enumerate((-1, 1)):
            blank((sx, sy, 0), rxy.at[i, j])
    for d in depths:
        blank((0, 0, -d), rt.at[d - 1])
        for j, s in enumerate((-1, 1)):
            blank((s, 0, -d), rtx.at[j, d - 1])
            blank((0, s, -d), rty.at[j, d - 1])

    lane = lax.broadcasted_iota(jnp.int32, (Y, Z), 1)
    row = lax.broadcasted_iota(jnp.int32, (Y, Z), 0)
    pair = lane >> 1
    even = (lane & 1) == 0
    not_last = jnp.where(row < Y - 1, 0.5, 0.0).astype(jnp.float32)
    not_first = jnp.where(row > 0, 0.5, 0.0).astype(jnp.float32)
    z_first = jnp.where(lane > 0, 0.5, 0.0).astype(jnp.float32)
    z_last = jnp.where(lane < Z - 1, 0.5, 0.0).astype(jnp.float32)
    z_edge = jnp.where(lane == 0, -0.5, jnp.where(lane == Z - 1, 0.5, 0.0)).astype(jnp.float32)
    if X == Y:
        row_x, z_edge_x = row, z_edge
    else:
        lane_x = lax.broadcasted_iota(jnp.int32, (X, Z), 1)
        row_x = lax.broadcasted_iota(jnp.int32, (X, Z), 0)
        z_edge_x = jnp.where(lane_x == 0, -0.5, jnp.where(lane_x == Z - 1, 0.5, 0.0)).astype(jnp.float32)

    sends = {o: [] for o in offs}
    recvs = {}

    def message(kind, o, src, dst, send, recv):
        copy = pltpu.make_async_remote_copy(
            src_ref=src, dst_ref=dst, send_sem=send, recv_sem=recv,
            device_id=partner(o), device_id_type=MESH,
        )
        sends[o].append((kind, copy))
        recvs[kind, minus(o)] = copy

    for i, s in enumerate((-1, 1)):
        k = 1 - i
        at = (Y, Y * X)[i]
        message("xu", (s, 0, 0), uv.at[:, pl.ds(at, Y), :], rxu.at[k], xu_send.at[i], xu_recv.at[k])
        message("xs", (s, 0, 0), xs.at[i], rxs.at[k], xs_send.at[i], xs_recv.at[k])
        message("yu", (0, s, 0), yu.at[i], ryu.at[k], yu_send.at[i], yu_recv.at[k])
        message("ys", (0, s, 0), ys.at[i], rys.at[k], ys_send.at[i], ys_recv.at[k])
        message("zu", (0, 0, s), zu.at[0, pl.ds(0, Y)], rzu.at[k], zu_send.at[i], zu_recv.at[k])
        message("zs", (0, 0, s), zs, rzs.at[k], zs_send.at[i], zs_recv.at[k])
        for j, s2 in enumerate((-1, 1)):
            m = 1 - j
            message("xy", (s, s2, 0), xy.at[i, j], rxy.at[k, m], xy_send.at[i, j], xy_recv.at[k, m])
            message("xz", (s, 0, s2), zu.at[0, pl.ds(0, Y)], rxz.at[k, m], xz_send.at[i, j], xz_recv.at[k, m])
            message("yz", (0, s, s2), zu, ryz.at[k, m], yz_send.at[i, j], yz_recv.at[k, m])
        for d in depths:
            message("tx", (s, 0, d), xt.at[i], rtx.at[k, d - 1], tx_send.at[i, d - 1], tx_recv.at[k, d - 1])
            message("ty", (0, s, d), yt.at[i], rty.at[k, d - 1], ty_send.at[i, d - 1], ty_recv.at[k, d - 1])
    for d in depths:
        message("t", (0, 0, d), zt, rt.at[d - 1], t_send.at[d - 1], t_recv.at[d - 1])

    def start(offsets_in, kinds):
        for o in offsets_in:
            chosen = [copy for kind, copy in sends[o] if kind in kinds]
            if chosen:
                @pl.when(has[o])
                def _(chosen=chosen):
                    for copy in chosen:
                        copy.start()

    def arrive(*kinds):
        for (kind, o), copy in recvs.items():
            if kind in kinds:
                @pl.when(has[o])
                def _(copy=copy):
                    copy.wait_recv()

    loads[0].wait()
    tile0 = plane
    for x in range(X):
        for c in range(3):
            q = c * X + x
            tile = pltpu.roll(uv[c, pl.ds(Y + x * Y, Y), :], (2 * q + 1) % Z, 1)
            tile0 = jnp.where(pair == q, tile, tile0)
    zu[0, pl.ds(0, Y), :] = tile0
    tile = row_plane
    pair_x = lax.broadcasted_iota(jnp.int32, (X, Z), 1) >> 1
    for i, line in enumerate((0, Y - 1)):
        for c in range(3):
            p = 3 * i + c
            lines = uv[c, pl.ds(Y + line, X, stride=Y), :]
            yu[i, c] = lines
            tile = jnp.where(pair_x == p, pltpu.roll(lines, (2 * p + 1) % Z, 1), tile)
            for j, at in enumerate((0, X - 1)):
                xy[j, i, pl.ds(c, 1), :] = uv[c, pl.ds(Y + at * Y + line, 1), :]
    zu[1, pl.ds(0, X), :] = tile

    loads[1].wait()
    total_depth = Z * layers
    depth = (me[2] * Z + lane).astype(jnp.float32)
    scale = (1.0 + 2.0 * depth / total_depth) / total_depth
    weight = jnp.concatenate([rv[pl.ds(x * Y, Y), :] * scale for x in range(X)], axis=0)
    above_row = lax.broadcasted_iota(jnp.int32, (Z, 2 * Z), 0)
    column = lax.broadcasted_iota(jnp.int32, (Z, 2 * Z), 1)
    triangle = jnp.where(
        (above_row < column) | (column >= Z),
        1.0,
        jnp.where(above_row == column, 0.5, 0.0),
    ).astype(jnp.float32)
    sums = jnp.dot(
        weight, triangle, precision=lax.Precision.HIGHEST, preferred_element_type=jnp.float32
    )
    pv[...] = sums[:, :Z] + 1.0
    tot[...] = sums[:, Z:]
    tile = plane
    for x in range(X):
        tile = jnp.where(pair == x, tot[pl.ds(x * Y, Y), :], tile)
    zt[...] = tile
    for i, (at, line) in enumerate(((0, 0), (X - 1, Y - 1))):
        xt[i] = tot[pl.ds(at * Y, Y), :]
        yt[i] = tot[pl.ds(line, X, stride=Y), :]

    for copy in loads[2:]:
        copy.wait()
    tiles = [plane, plane]

    def local(x, tiles):
        base = Y + x * Y
        own = pl.ds(x * Y, Y)
        grad = []
        for c in range(3):
            here = uv[c, pl.ds(base, Y), :]
            grad.append((
                (uv[c, pl.ds(base + Y, Y), :] - uv[c, pl.ds(base - Y, Y), :]) * 0.5,
                uv[c, pl.ds(base + 1, Y), :] * not_last - uv[c, pl.ds(base - 1, Y), :] * not_first,
                pltpu.roll(here, Z - 1, 1) * z_last - pltpu.roll(here, 1, 1) * z_first,
            ))
        minus_two = -2.0 / tv[own, :]
        parts = [
            grad[0][0] - ev[0, own, :],
            grad[1][1] - ev[1, own, :],
            grad[2][2] - ev[2, own, :],
            0.5 * (grad[0][1] + grad[1][0]) - ev[3, own, :],
            0.5 * (grad[0][2] + grad[2][0]) - ev[4, own, :],
            0.5 * (grad[1][2] + grad[2][1]) - ev[5, own, :],
            (2.0 + 14.0 * bv[own, :].astype(jnp.float32)) * jnp.exp(pv[own, :] * minus_two),
            minus_two,
        ]
        for k in range(6):
            el[k, own, :] = parts[k]
        av[own, :] = parts[6]
        nt[own, :] = parts[7]
        for i, at in enumerate((0, X - 1)):
            if x == at:
                for k in range(8):
                    xs[i, k] = parts[k]
        tiles = list(tiles)
        for k in range(8):
            q = (k % 4) * X + x
            tile = pltpu.roll(parts[k], (2 * q + 1) % Z, 1)
            tiles[k // 4] = jnp.where(pair == q, tile, tiles[k // 4])
        return tiles

    ends = sorted({0, X - 1})
    for x in ends:
        tiles = local(x, tiles)

    @pl.when(expected > 0)
    def _():
        pl.semaphore_wait(barrier, expected)

    for o in lowers:
        @pl.when(has[o])
        def _(o=o):
            pl.semaphore_signal(
                ready.at[uppers.index(minus(o))], inc=1, device_id=partner(o), device_id_type=MESH
            )
    early = ("xu", "xs", "yu", "zu", "xy", "xz", "yz", "t", "tx", "ty")
    start(lowers, early)

    for x in range(X):
        if x not in ends:
            tiles = local(x, tiles)
    for i, line in enumerate((0, Y - 1)):
        for k in range(8):
            src = el.at[k] if k < 6 else (av, nt)[k - 6]
            ys[i, k] = src[pl.ds(line, X, stride=Y), :]
    start(lowers, ("ys",))
    for k in range(2):
        zs[k] = tiles[k]
    start(lowers, ("zs",))

    for o in uppers:
        @pl.when(has[o])
        def _(o=o):
            pl.semaphore_wait(ready.at[uppers.index(o)], 1)
    start(uppers, early + ("ys", "zs"))

    arrive("yu")
    for side, line in enumerate((0, Y - 1)):
        sign = 2.0 * side - 1.0

        @pl.when(has[faces[1][side]])
        def _(side=side, sign=sign, line=line):
            own = pl.ds(line, X, stride=Y)
            for c, (part, factor) in enumerate(TERMS[1]):
                el[part, own, :] = el[part, own, :] + (sign * factor) * ryu[side, c]

    arrive("zu", "t")
    carried = plane
    for d in depths:
        carried = carried + rt[d - 1]
    merged = merge(rzu[0], rzu[1])

    def advance(x):
        own = pl.ds(x * Y, Y)
        e = [el[c, own, :] for c in range(6)]
        for c, (part, factor) in enumerate(TERMS[2]):
            e[part] = e[part] + (2.0 * factor) * edge_term(merged, c * X + x, z_edge)
        load = jnp.broadcast_to(carried[:, 2 * x:2 * x + 1], (Y, Z))
        trace, change = flow(e, av[own, :] * jnp.exp(load * nt[own, :]))
        for c in range(6):
            fv[c, own, :] = ev[c, own, :] + change[c]
            sp[c, pl.ds(Y + x * Y, Y), :] = stress(e, change, trace, c)

    for x in range(X):
        if x not in ends:
            advance(x)
    arrive("xu")
    for side, at in enumerate((0, X - 1)):
        sign = 2.0 * side - 1.0

        @pl.when(has[faces[0][side]])
        def _(side=side, sign=sign, at=at):
            own = pl.ds(at * Y, Y)
            for c, (part, factor) in enumerate(TERMS[0]):
                el[part, own, :] = el[part, own, :] + (sign * factor) * rxu[side, c]

    for x in ends:
        advance(x)

    for x in range(X):
        base = Y + x * Y
        own = pl.ds(x * Y, Y)
        for c in range(3):
            cx, cy, cz = X_SET[c], Y_SET[c], Z_SET[c]
            here = sp[cz, pl.ds(base, Y), :]
            total = (sp[cx, pl.ds(base + Y, Y), :] - sp[cx, pl.ds(base - Y, Y), :]) * 0.5
            total = total + (
                sp[cy, pl.ds(base + 1, Y), :] * not_last - sp[cy, pl.ds(base - 1, Y), :] * not_first
            )
            total = total + (pltpu.roll(here, Z - 1, 1) * z_last - pltpu.roll(here, 1, 1) * z_first)
            if c == 2:
                total = total - 0.5 * rv[own, :]
            mv[c, own, :] = total

    def add(e, axis, factor, values):
        for c, (part, f) in enumerate(TERMS[axis]):
            e[part] = e[part] + (factor * f) * values[c]

    def ends_of(first, last, rows, count):
        return jnp.where(rows == 0, -first, jnp.where(rows == count - 1, last, 0.0))

    arrive("ys", "xy", "yz", "ty")
    for side, line in enumerate((0, Y - 1)):
        @pl.when(has[faces[1][side]])
        def _(side=side, line=line):
            e = [rys[side, k] for k in range(6)]
            add(e, 1, 1.0 - 2.0 * side, [uv[c, pl.ds(Y + line, X, stride=Y), :] for c in range(3)])
            add(e, 0, 1.0, [
                ends_of(rxy[0, side, pl.ds(c, 1), :], rxy[1, side, pl.ds(c, 1), :], row_x, X) for c in range(3)
            ])
            joined = merge(ryz[side, 0, 1, pl.ds(0, X), :], ryz[side, 1, 1, pl.ds(0, X), :])
            add(e, 2, 2.0, [edge_term(joined, 3 * (1 - side) + c, z_edge_x) for c in range(3)])
            load = row_plane
            for d in depths:
                load = load + rty[side, d - 1]
            trace, change = flow(e, rys[side, 6] * jnp.exp(load * rys[side, 7]))
            own = pl.ds(line, X, stride=Y)
            for c in range(3):
                mv[c, own, :] = mv[c, own, :] + (side - 0.5) * stress(e, change, trace, Y_SET[c])

    arrive("zs", "xz")
    block = 2 * X

    def shift(tile, by):
        return pltpu.roll(tile, by % Z, 1) if by % Z else tile

    halo = [jnp.where(even, rzs[0, k], rzs[1, k]) for k in range(2)]
    parts = [shift(halo[k // 4], -(k % 4) * block) for k in range(8)]
    mine = zu[0, pl.ds(0, Y), :]
    from_z = jnp.where(even, shift(mine, -1), -shift(mine, 1))
    left = jnp.where(even, rxz[0, 0], rxz[0, 1])
    right = jnp.where(even, rxz[1, 0], rxz[1, 1])
    spot = pair % X
    from_x = jnp.where(
        spot == 0, -shift(left, -2 * (X - 1)), jnp.where(spot == X - 1, shift(right, 2 * (X - 1)), 0.0)
    )
    even_row = (lax.broadcasted_iota(jnp.int32, (1, Z), 1) & 1) == 0
    from_y = ends_of(
        jnp.where(even_row, ryz[0, 0, 0, pl.ds(Y - 1, 1), :], ryz[0, 1, 0, pl.ds(Y - 1, 1), :]),
        jnp.where(even_row, ryz[1, 0, 0, pl.ds(0, 1), :], ryz[1, 1, 0, pl.ds(0, 1), :]),
        row, Y,
    )
    e = list(parts[:6])
    for axis, tile in enumerate((from_x, from_y, from_z)):
        add(e, axis, 1.0, [shift(tile, -c * block) for c in range(3)])
    deeper = plane
    for d in depths:
        if d >= 2:
            deeper = deeper + rt[d - 1]
    load = jnp.where(even, deeper, carried + zt[...])
    trace, change = flow(e, parts[6] * jnp.exp(load * parts[7]))
    known = jnp.where(
        even,
        has[0, 0, -1].astype(jnp.float32),
        has[0, 0, 1].astype(jnp.float32),
    )
    gathered = plane
    for c in range(3):
        tile = shift(stress(e, change, trace, Z_SET[c]) * known, c * block)
        gathered = jnp.where((pair >= c * X) & (pair < (c + 1) * X), tile, gathered)
    joined = jnp.where(even, gathered, shift(gathered, -2))
    for c in range(3):
        for x in range(X):
            own = pl.ds(x * Y, Y)
            mv[c, own, :] = mv[c, own, :] + edge_term(joined, c * X + x, z_edge)

    arrive("xs", "tx")
    for side, at in enumerate((0, X - 1)):
        @pl.when(has[faces[0][side]])
        def _(side=side, at=at):
            e = [rxs[side, k] for k in range(6)]
            add(e, 0, 1.0 - 2.0 * side, [uv[c, pl.ds(Y + at * Y, Y), :] for c in range(3)])
            add(e, 1, 1.0, [
                ends_of(rxy[side, 0, pl.ds(c, 1), :], rxy[side, 1, pl.ds(c, 1), :], row, Y) for c in range(3)
            ])
            facing = (X - 1) * (1 - side)
            joined = merge(rxz[side, 0], rxz[side, 1])
            add(e, 2, 2.0, [edge_term(joined, c * X + facing, z_edge) for c in range(3)])
            load = plane
            for d in depths:
                load = load + rtx[side, d - 1]
            trace, change = flow(e, rxs[side, 6] * jnp.exp(load * rxs[side, 7]))
            own = pl.ds(at * Y, Y)
            for c in range(3):
                mv[c, own, :] = mv[c, own, :] + (side - 0.5) * stress(e, change, trace, X_SET[c])

    for o in offs:
        if sends[o]:
            @pl.when(has[o])
            def _(o=o):
                for _, copy in sends[o]:
                    copy.wait_send()


def finish(fv, mv, f_hbm, m_hbm, sem):
    copies = [
        pltpu.make_async_copy(mv, m_hbm, sem.at[0]),
        pltpu.make_async_copy(fv, f_hbm, sem.at[1]),
    ]
    for copy in copies:
        copy.start()
    for copy in copies:
        copy.wait()


def shards(sizes, u, e, t, r, b):
    X, Y, Z = t.shape
    N = X * Y
    layers = sizes[2]
    assert 8 * X <= Z and Z % 128 == 0 and Y % 8 == 0 and X % 8 == 0
    W = max(X, Y)
    f32 = jnp.float32
    vmem = pltpu.VMEM
    dma = pltpu.SemaphoreType.DMA
    any_space = pl.BlockSpec(memory_space=pl.ANY)
    in_vmem = pl.BlockSpec(memory_space=vmem)
    D = max(layers - 1, 1)
    n_upper = sum(upper(o) for o in offsets(layers))
    kept = pl.pallas_call(
        functools.partial(kernel, (X, Y, Z), sizes),
        out_shape=(vmem((6, N, Z), f32), vmem((3, N, Z), f32)),
        in_specs=[any_space] * 5,
        out_specs=(in_vmem, in_vmem),
        scratch_shapes=[
            vmem((3, N + 2 * Y, Z), f32),
            vmem((6, N, Z), f32),
            vmem((N, Z), f32),
            vmem((N, Z), f32),
            vmem((N, Z), jnp.int32),
            vmem((N, Z), f32),
            vmem((N, Z), f32),
            vmem((6, N, Z), f32),
            vmem((N, Z), f32),
            vmem((N, Z), f32),
            vmem((6, N + 2 * Y, Z), f32),
            vmem((2, 8, Y, Z), f32),
            vmem((2, 8, X, Z), f32),
            vmem((2, 3, X, Z), f32),
            vmem((2, W, Z), f32),
            vmem((2, Y, Z), f32),
            vmem((2, 2, 8, Z), f32),
            vmem((Y, Z), f32),
            vmem((2, Y, Z), f32),
            vmem((2, X, Z), f32),
            vmem((2, 3, Y, Z), f32),
            vmem((2, 8, Y, Z), f32),
            vmem((2, 3, X, Z), f32),
            vmem((2, 8, X, Z), f32),
            vmem((2, Y, Z), f32),
            vmem((2, 2, Y, Z), f32),
            vmem((2, 2, 8, Z), f32),
            vmem((2, 2, Y, Z), f32),
            vmem((2, 2, 2, W, Z), f32),
            vmem((D, Y, Z), f32),
            vmem((2, D, Y, Z), f32),
            vmem((2, D, X, Z), f32),
            dma((5,)),
            pltpu.SemaphoreType.REGULAR((n_upper,)),
        ] + [dma((2,))] * 12 + [dma((2, 2))] * 6 + [dma((D,))] * 2 + [dma((2, D))] * 4,
        compiler_params=pltpu.CompilerParams(collective_id=0, has_side_effects=True),
        name="strain_step",
    )(u.reshape(3, N, Z), e.reshape(6, N, Z), t.reshape(N, Z), r.reshape(N, Z), b.reshape(N, Z))
    f, m = pl.pallas_call(
        finish,
        out_shape=(jax.ShapeDtypeStruct((6, N, Z), f32), jax.ShapeDtypeStruct((3, N, Z), f32)),
        in_specs=[in_vmem] * 2,
        out_specs=(any_space, any_space),
        scratch_shapes=[dma((2,))],
        name="finish",
    )(*(pltpu.with_memory_space_constraint(k, vmem) for k in kept))
    return f.reshape(6, X, Y, Z), m.reshape(3, X, Y, Z)


def solution(mesh):
    sizes = tuple(mesh.shape[a] for a in AXES)
    field = P("gx", "gy", "gz")
    fields = P(None, "gx", "gy", "gz")
    return jax.shard_map(
        functools.partial(shards, sizes),
        mesh=mesh,
        in_specs=(fields, fields, field, field, field),
        out_specs=(fields, fields),
        check_vma=False,
    )
```

```python
import functools

import jax
import jax.numpy as jnp
from jax import lax
from jax.experimental import pallas as pl
from jax.experimental.pallas import tpu as pltpu
from jax.sharding import PartitionSpec as P

MESH = pl.DeviceIdType.MESH
AXES = ("gx", "gy", "gz")
ORDER = (2, 1, 0)
TERMS = (
    ((0, 0.5), (3, 0.25), (4, 0.25)),
    ((3, 0.25), (1, 0.5), (5, 0.25)),
    ((4, 0.25), (5, 0.25), (2, 0.5)),
)
X_SET = (0, 3, 4)
Y_SET = (3, 1, 5)
Z_SET = (4, 5, 2)


def upper(o):
    return tuple(o[a] for a in ORDER) > (0, 0, 0)


def offsets(layers):
    near = [
        (x, y, z)
        for x in (-1, 0, 1)
        for y in (-1, 0, 1)
        for z in (-1, 0, 1)
        if 1 <= abs(x) + abs(y) + abs(z) <= 2
    ]
    far = [
        (x, y, s * d)
        for d in range(2, layers)
        for s in (-1, 1)
        for x, y in ((0, 0), (-1, 0), (1, 0), (0, -1), (0, 1))
    ]
    return near + far


def minus(o):
    return tuple(-v for v in o)


def merge(low, high):
    Z = low.shape[1]
    even = (lax.broadcasted_iota(jnp.int32, low.shape, 1) & 1) == 0
    return jnp.where(even, low, pltpu.roll(high, Z - 2, 1))


def edge_term(tile, q, z_edge):
    Z = tile.shape[1]
    return (pltpu.roll(tile, (Z - 2 * q) % Z, 1) if q else tile) * z_edge


def flow(e, pace):
    trace = e[0] + e[1] + e[2]
    third = trace * (1.0 / 3.0)
    half = [e[0] - third, e[1] - third, e[2] - third, e[3], e[4], e[5]]
    second = half[0] * half[0] + half[1] * half[1] + half[2] * half[2]
    second = second + 2.0 * (half[3] * half[3] + half[4] * half[4] + half[5] * half[5])
    rate = pace * second
    return trace, [rate * h for h in half]


def stress(e, change, trace, part):
    out = 2.0 * (e[part] - change[part])
    return out + trace if part < 3 else out


def kernel(
    dims, sizes,
    u_hbm, e_hbm, t_hbm, r_hbm, b_hbm,
    fv, mv,
    uv, ev, tv, rv, bv, pv, tot, el, av, nt, sp,
    xs, ys, yu, zu, zs, xy, zt, xt, yt,
    rxu, rxs, ryu, rys, rzu, rzs, rxy, rxz, ryz, rt, rtx, rty,
    in_sem, ready,
    xu_send, xu_recv, xs_send, xs_recv, yu_send, yu_recv, ys_send, ys_recv,
    zu_send, zu_recv, zs_send, zs_recv, xy_send, xy_recv, xz_send, xz_recv, yz_send, yz_recv,
    t_send, t_recv, tx_send, tx_recv, ty_send, ty_recv,
):
    X, Y, Z = dims
    N = X * Y
    layers = sizes[2]
    depths = range(1, layers)
    me = [lax.axis_index(a) for a in AXES]
    offs = offsets(layers)
    uppers = [o for o in offs if upper(o)]
    lowers = [o for o in offs if not upper(o)]

    def exists(o):
        ok = None
        for a in range(3):
            if o[a]:
                here = me[a] + o[a]
                test = here < sizes[a] if o[a] > 0 else here >= 0
                ok = test if ok is None else jnp.logical_and(ok, test)
        return ok

    def partner(o):
        return {AXES[a]: me[a] + o[a] for a in range(3) if o[a]}

    has = {o: exists(o) for o in offs}
    faces = {a: [tuple(s if i == a else 0 for i in range(3)) for s in (-1, 1)] for a in range(3)}

    loads = [
        pltpu.make_async_copy(src, dst, in_sem.at[i])
        for i, (src, dst) in enumerate(
            (
                (u_hbm, uv.at[:, pl.ds(Y, N), :]),
                (r_hbm, rv),
                (e_hbm.at[:, pl.ds(0, Y), :], ev.at[:, pl.ds(0, Y), :]),
                (e_hbm.at[:, pl.ds(N - Y, Y), :], ev.at[:, pl.ds(N - Y, Y), :]),
                (t_hbm, tv),
                (b_hbm, bv),
                (e_hbm.at[:, pl.ds(Y, N - 2 * Y), :], ev.at[:, pl.ds(Y, N - 2 * Y), :]),
            )
        )
    ]
    for copy in loads:
        copy.start()

    barrier = pltpu.get_barrier_semaphore()
    for o in uppers:
        @pl.when(has[o])
        def _(o=o):
            pl.semaphore_signal(barrier, inc=1, device_id=partner(o), device_id_type=MESH)
    expected = jnp.int32(0)
    for o in lowers:
        expected = expected + has[o].astype(jnp.int32)

    plane = jnp.zeros((Y, Z), jnp.float32)
    row_plane = jnp.zeros((X, Z), jnp.float32)
    for c in range(3):
        uv[c, pl.ds(0, Y), :] = plane
        uv[c, pl.ds(Y + N, Y), :] = plane
    for c in range(6):
        sp[c, pl.ds(0, Y), :] = plane
        sp[c, pl.ds(Y + N, Y), :] = plane

    def blank(o, *refs):
        @pl.when(jnp.logical_not(has[o]))
        def _():
            for ref in refs:
                ref[...] = jnp.zeros(ref.shape, jnp.float32)

    for i, sz in enumerate((-1, 1)):
        blank((0, 0, sz), rzu.at[i], rzs.at[i])
        for j, s in enumerate((-1, 1)):
            blank((s, 0, sz), rxz.at[j, i])
            blank((0, s, sz), ryz.at[j, i])
    for i, sx in enumerate((-1, 1)):
        for j, sy in enumerate((-1, 1)):
            blank((sx, sy, 0), rxy.at[i, j])
    for d in depths:
        blank((0, 0, -d), rt.at[d - 1])
        for j, s in enumerate((-1, 1)):
            blank((s, 0, -d), rtx.at[j, d - 1])
            blank((0, s, -d), rty.at[j, d - 1])

    lane = lax.broadcasted_iota(jnp.int32, (Y, Z), 1)
    row = lax.broadcasted_iota(jnp.int32, (Y, Z), 0)
    pair = lane >> 1
    even = (lane & 1) == 0
    not_last = jnp.where(row < Y - 1, 0.5, 0.0).astype(jnp.float32)
    not_first = jnp.where(row > 0, 0.5, 0.0).astype(jnp.float32)
    z_first = jnp.where(lane > 0, 0.5, 0.0).astype(jnp.float32)
    z_last = jnp.where(lane < Z - 1, 0.5, 0.0).astype(jnp.float32)
    z_edge = jnp.where(lane == 0, -0.5, jnp.where(lane == Z - 1, 0.5, 0.0)).astype(jnp.float32)
    if X == Y:
        row_x, z_edge_x = row, z_edge
    else:
        lane_x = lax.broadcasted_iota(jnp.int32, (X, Z), 1)
        row_x = lax.broadcasted_iota(jnp.int32, (X, Z), 0)
        z_edge_x = jnp.where(lane_x == 0, -0.5, jnp.where(lane_x == Z - 1, 0.5, 0.0)).astype(jnp.float32)

    sends = {o: [] for o in offs}
    recvs = {}

    def message(kind, o, src, dst, send, recv):
        copy = pltpu.make_async_remote_copy(
            src_ref=src, dst_ref=dst, send_sem=send, recv_sem=recv,
            device_id=partner(o), device_id_type=MESH,
        )
        sends[o].append((kind, copy))
        recvs[kind, minus(o)] = copy

    for i, s in enumerate((-1, 1)):
        k = 1 - i
        at = (Y, Y * X)[i]
        message("xu", (s, 0, 0), uv.at[:, pl.ds(at, Y), :], rxu.at[k], xu_send.at[i], xu_recv.at[k])
        message("xs", (s, 0, 0), xs.at[i], rxs.at[k], xs_send.at[i], xs_recv.at[k])
        message("yu", (0, s, 0), yu.at[i], ryu.at[k], yu_send.at[i], yu_recv.at[k])
        message("ys", (0, s, 0), ys.at[i], rys.at[k], ys_send.at[i], ys_recv.at[k])
        message("zu", (0, 0, s), zu.at[0, pl.ds(0, Y)], rzu.at[k], zu_send.at[i], zu_recv.at[k])
        message("zs", (0, 0, s), zs, rzs.at[k], zs_send.at[i], zs_recv.at[k])
        for j, s2 in enumerate((-1, 1)):
            m = 1 - j
            message("xy", (s, s2, 0), xy.at[i, j], rxy.at[k, m], xy_send.at[i, j], xy_recv.at[k, m])
            message("xz", (s, 0, s2), zu.at[0, pl.ds(0, Y)], rxz.at[k, m], xz_send.at[i, j], xz_recv.at[k, m])
            message("yz", (0, s, s2), zu, ryz.at[k, m], yz_send.at[i, j], yz_recv.at[k, m])
        for d in depths:
            message("tx", (s, 0, d), xt.at[i], rtx.at[k, d - 1], tx_send.at[i, d - 1], tx_recv.at[k, d - 1])
            message("ty", (0, s, d), yt.at[i], rty.at[k, d - 1], ty_send.at[i, d - 1], ty_recv.at[k, d - 1])
    for d in depths:
        message("t", (0, 0, d), zt, rt.at[d - 1], t_send.at[d - 1], t_recv.at[d - 1])

    def start(offsets_in, kinds):
        for o in offsets_in:
            chosen = [copy for kind, copy in sends[o] if kind in kinds]
            if chosen:
                @pl.when(has[o])
                def _(chosen=chosen):
                    for copy in chosen:
                        copy.start()

    def arrive(*kinds):
        for (kind, o), copy in recvs.items():
            if kind in kinds:
                @pl.when(has[o])
                def _(copy=copy):
                    copy.wait_recv()

    loads[0].wait()
    tile0 = plane
    for x in range(X):
        for c in range(3):
            q = c * X + x
            tile = pltpu.roll(uv[c, pl.ds(Y + x * Y, Y), :], (2 * q + 1) % Z, 1)
            tile0 = jnp.where(pair == q, tile, tile0)
    zu[0, pl.ds(0, Y), :] = tile0
    tile = row_plane
    pair_x = lax.broadcasted_iota(jnp.int32, (X, Z), 1) >> 1
    for i, line in enumerate((0, Y - 1)):
        for c in range(3):
            p = 3 * i + c
            lines = uv[c, pl.ds(Y + line, X, stride=Y), :]
            yu[i, c] = lines
            tile = jnp.where(pair_x == p, pltpu.roll(lines, (2 * p + 1) % Z, 1), tile)
            for j, at in enumerate((0, X - 1)):
                xy[j, i, pl.ds(c, 1), :] = uv[c, pl.ds(Y + at * Y + line, 1), :]
    zu[1, pl.ds(0, X), :] = tile

    @pl.when(expected > 0)
    def _():
        pl.semaphore_wait(barrier, expected)

    for o in lowers:
        @pl.when(has[o])
        def _(o=o):
            pl.semaphore_signal(
                ready.at[uppers.index(minus(o))], inc=1, device_id=partner(o), device_id_type=MESH
            )
    first = ("xu", "yu", "zu", "xy", "xz", "yz")
    start(lowers, first)

    loads[1].wait()
    total_depth = Z * layers
    depth = (me[2] * Z + lane).astype(jnp.float32)
    scale = (1.0 + 2.0 * depth / total_depth) / total_depth
    thirds = [[], [], []]
    for x in range(X):
        rest = rv[pl.ds(x * Y, Y), :] * scale
        for k in range(3):
            piece = rest.astype(jnp.bfloat16)
            thirds[k].append(piece)
            rest = rest - piece.astype(jnp.float32)
    weight = jnp.concatenate([jnp.concatenate(k, axis=0) for k in thirds], axis=1)
    above_row = lax.broadcasted_iota(jnp.int32, (Z, 2 * Z), 0)
    column = lax.broadcasted_iota(jnp.int32, (Z, 2 * Z), 1)
    triangle = jnp.where(
        (above_row < column) | (column >= Z),
        1.0,
        jnp.where(above_row == column, 0.5, 0.0),
    ).astype(jnp.bfloat16)
    triangle = jnp.concatenate([triangle] * 3, axis=0)
    sums = jnp.dot(weight, triangle, preferred_element_type=jnp.float32)
    pv[...] = sums[:, :Z] + 1.0
    tot[...] = sums[:, Z:]
    tile = plane
    for x in range(X):
        tile = jnp.where(pair == x, tot[pl.ds(x * Y, Y), :], tile)
    zt[...] = tile
    for i, (at, line) in enumerate(((0, 0), (X - 1, Y - 1))):
        xt[i] = tot[pl.ds(at * Y, Y), :]
        yt[i] = tot[pl.ds(line, X, stride=Y), :]

    tiles = [plane, plane]

    def strain(x):
        base = Y + x * Y
        own = pl.ds(x * Y, Y)
        grad = []
        for c in range(3):
            here = uv[c, pl.ds(base, Y), :]
            grad.append((
                (uv[c, pl.ds(base + Y, Y), :] - uv[c, pl.ds(base - Y, Y), :]) * 0.5,
                uv[c, pl.ds(base + 1, Y), :] * not_last - uv[c, pl.ds(base - 1, Y), :] * not_first,
                pltpu.roll(here, Z - 1, 1) * z_last - pltpu.roll(here, 1, 1) * z_first,
            ))
        el[0, own, :] = grad[0][0]
        el[1, own, :] = grad[1][1]
        el[2, own, :] = grad[2][2]
        el[3, own, :] = 0.5 * (grad[0][1] + grad[1][0])
        el[4, own, :] = 0.5 * (grad[0][2] + grad[2][0])
        el[5, own, :] = 0.5 * (grad[1][2] + grad[2][1])

    def pack(k, x, part, tiles):
        q = (k % 4) * X + x
        tile = pltpu.roll(part, (2 * q + 1) % Z, 1)
        tiles[k // 4] = jnp.where(pair == q, tile, tiles[k // 4])

    def factors(x, tiles):
        own = pl.ds(x * Y, Y)
        minus_two = -2.0 / tv[own, :]
        factor = (2.0 + 14.0 * bv[own, :].astype(jnp.float32)) * jnp.exp(pv[own, :] * minus_two)
        av[own, :] = factor
        nt[own, :] = minus_two
        for i, at in enumerate((0, X - 1)):
            if x == at:
                xs[i, 6] = factor
                xs[i, 7] = minus_two
        pack(6, x, factor, tiles)
        pack(7, x, minus_two, tiles)

    def elastic(x, tiles):
        own = pl.ds(x * Y, Y)
        for k in range(6):
            part = el[k, own, :] - ev[k, own, :]
            el[k, own, :] = part
            for i, at in enumerate((0, X - 1)):
                if x == at:
                    xs[i, k] = part
            pack(k, x, part, tiles)

    ends = sorted({0, X - 1})
    for x in ends:
        strain(x)
    for copy in loads[2:6]:
        copy.wait()
    for x in ends:
        elastic(x, tiles)
        factors(x, tiles)
    start(lowers, ("xs", "t", "tx", "ty"))

    inner = [x for x in range(X) if x not in ends]
    for x in inner:
        strain(x)
        factors(x, tiles)
    loads[6].wait()
    for x in inner:
        elastic(x, tiles)
    for i, line in enumerate((0, Y - 1)):
        for k in range(8):
            src = el.at[k] if k < 6 else (av, nt)[k - 6]
            ys[i, k] = src[pl.ds(line, X, stride=Y), :]
    start(lowers, ("ys",))
    for k in range(2):
        zs[k] = tiles[k]
    start(lowers, ("zs",))

    for o in uppers:
        @pl.when(has[o])
        def _(o=o):
            pl.semaphore_wait(ready.at[uppers.index(o)], 1)
    start(uppers, first + ("xs", "ys", "zs", "t", "tx", "ty"))

    arrive("yu")
    for side, line in enumerate((0, Y - 1)):
        sign = 2.0 * side - 1.0

        @pl.when(has[faces[1][side]])
        def _(side=side, sign=sign, line=line):
            own = pl.ds(line, X, stride=Y)
            for c, (part, factor) in enumerate(TERMS[1]):
                el[part, own, :] = el[part, own, :] + (sign * factor) * ryu[side, c]

    arrive("zu", "t")
    carried = plane
    for d in depths:
        carried = carried + rt[d - 1]
    merged = merge(rzu[0], rzu[1])

    def advance(x):
        own = pl.ds(x * Y, Y)
        e = [el[c, own, :] for c in range(6)]
        for c, (part, factor) in enumerate(TERMS[2]):
            e[part] = e[part] + (2.0 * factor) * edge_term(merged, c * X + x, z_edge)
        load = jnp.broadcast_to(carried[:, 2 * x:2 * x + 1], (Y, Z))
        trace, change = flow(e, av[own, :] * jnp.exp(load * nt[own, :]))
        for c in range(6):
            fv[c, own, :] = ev[c, own, :] + change[c]
            sp[c, pl.ds(Y + x * Y, Y), :] = stress(e, change, trace, c)

    for x in range(X):
        if x not in ends:
            advance(x)
    arrive("xu")
    for side, at in enumerate((0, X - 1)):
        sign = 2.0 * side - 1.0

        @pl.when(has[faces[0][side]])
        def _(side=side, sign=sign, at=at):
            own = pl.ds(at * Y, Y)
            for c, (part, factor) in enumerate(TERMS[0]):
                el[part, own, :] = el[part, own, :] + (sign * factor) * rxu[side, c]

    for x in ends:
        advance(x)

    for x in range(X):
        base = Y + x * Y
        own = pl.ds(x * Y, Y)
        for c in range(3):
            cx, cy, cz = X_SET[c], Y_SET[c], Z_SET[c]
            here = sp[cz, pl.ds(base, Y), :]
            total = (sp[cx, pl.ds(base + Y, Y), :] - sp[cx, pl.ds(base - Y, Y), :]) * 0.5
            total = total + (
                sp[cy, pl.ds(base + 1, Y), :] * not_last - sp[cy, pl.ds(base - 1, Y), :] * not_first
            )
            total = total + (pltpu.roll(here, Z - 1, 1) * z_last - pltpu.roll(here, 1, 1) * z_first)
            if c == 2:
                total = total - 0.5 * rv[own, :]
            mv[c, own, :] = total

    def add(e, axis, factor, values):
        for c, (part, f) in enumerate(TERMS[axis]):
            e[part] = e[part] + (factor * f) * values[c]

    def ends_of(first, last, rows, count):
        return jnp.where(rows == 0, -first, jnp.where(rows == count - 1, last, 0.0))

    arrive("ys", "xy", "yz", "ty")
    for side, line in enumerate((0, Y - 1)):
        @pl.when(has[faces[1][side]])
        def _(side=side, line=line):
            e = [rys[side, k] for k in range(6)]
            add(e, 1, 1.0 - 2.0 * side, [uv[c, pl.ds(Y + line, X, stride=Y), :] for c in range(3)])
            add(e, 0, 1.0, [
                ends_of(rxy[0, side, pl.ds(c, 1), :], rxy[1, side, pl.ds(c, 1), :], row_x, X) for c in range(3)
            ])
            joined = merge(ryz[side, 0, 1, pl.ds(0, X), :], ryz[side, 1, 1, pl.ds(0, X), :])
            add(e, 2, 2.0, [edge_term(joined, 3 * (1 - side) + c, z_edge_x) for c in range(3)])
            load = row_plane
            for d in depths:
                load = load + rty[side, d - 1]
            trace, change = flow(e, rys[side, 6] * jnp.exp(load * rys[side, 7]))
            own = pl.ds(line, X, stride=Y)
            for c in range(3):
                mv[c, own, :] = mv[c, own, :] + (side - 0.5) * stress(e, change, trace, Y_SET[c])

    arrive("zs", "xz")
    block = 2 * X

    def shift(tile, by):
        return pltpu.roll(tile, by % Z, 1) if by % Z else tile

    halo = [jnp.where(even, rzs[0, k], rzs[1, k]) for k in range(2)]
    parts = [shift(halo[k // 4], -(k % 4) * block) for k in range(8)]
    mine = zu[0, pl.ds(0, Y), :]
    from_z = jnp.where(even, shift(mine, -1), -shift(mine, 1))
    left = jnp.where(even, rxz[0, 0], rxz[0, 1])
    right = jnp.where(even, rxz[1, 0], rxz[1, 1])
    spot = pair % X
    from_x = jnp.where(
        spot == 0, -shift(left, -2 * (X - 1)), jnp.where(spot == X - 1, shift(right, 2 * (X - 1)), 0.0)
    )
    even_row = (lax.broadcasted_iota(jnp.int32, (1, Z), 1) & 1) == 0
    from_y = ends_of(
        jnp.where(even_row, ryz[0, 0, 0, pl.ds(Y - 1, 1), :], ryz[0, 1, 0, pl.ds(Y - 1, 1), :]),
        jnp.where(even_row, ryz[1, 0, 0, pl.ds(0, 1), :], ryz[1, 1, 0, pl.ds(0, 1), :]),
        row, Y,
    )
    e = list(parts[:6])
    for axis, tile in enumerate((from_x, from_y, from_z)):
        add(e, axis, 1.0, [shift(tile, -c * block) for c in range(3)])
    deeper = plane
    for d in depths:
        if d >= 2:
            deeper = deeper + rt[d - 1]
    load = jnp.where(even, deeper, carried + zt[...])
    trace, change = flow(e, parts[6] * jnp.exp(load * parts[7]))
    known = jnp.where(
        even,
        has[0, 0, -1].astype(jnp.float32),
        has[0, 0, 1].astype(jnp.float32),
    )
    gathered = plane
    for c in range(3):
        tile = shift(stress(e, change, trace, Z_SET[c]) * known, c * block)
        gathered = jnp.where((pair >= c * X) & (pair < (c + 1) * X), tile, gathered)
    joined = jnp.where(even, gathered, shift(gathered, -2))
    for c in range(3):
        for x in range(X):
            own = pl.ds(x * Y, Y)
            mv[c, own, :] = mv[c, own, :] + edge_term(joined, c * X + x, z_edge)

    arrive("xs", "tx")
    for side, at in enumerate((0, X - 1)):
        @pl.when(has[faces[0][side]])
        def _(side=side, at=at):
            e = [rxs[side, k] for k in range(6)]
            add(e, 0, 1.0 - 2.0 * side, [uv[c, pl.ds(Y + at * Y, Y), :] for c in range(3)])
            add(e, 1, 1.0, [
                ends_of(rxy[side, 0, pl.ds(c, 1), :], rxy[side, 1, pl.ds(c, 1), :], row, Y) for c in range(3)
            ])
            facing = (X - 1) * (1 - side)
            joined = merge(rxz[side, 0], rxz[side, 1])
            add(e, 2, 2.0, [edge_term(joined, c * X + facing, z_edge) for c in range(3)])
            load = plane
            for d in depths:
                load = load + rtx[side, d - 1]
            trace, change = flow(e, rxs[side, 6] * jnp.exp(load * rxs[side, 7]))
            own = pl.ds(at * Y, Y)
            for c in range(3):
                mv[c, own, :] = mv[c, own, :] + (side - 0.5) * stress(e, change, trace, X_SET[c])

    for o in offs:
        if sends[o]:
            @pl.when(has[o])
            def _(o=o):
                for _, copy in sends[o]:
                    copy.wait_send()


def finish(fv, mv, f_hbm, m_hbm, sem):
    copies = [
        pltpu.make_async_copy(mv, m_hbm, sem.at[0]),
        pltpu.make_async_copy(fv, f_hbm, sem.at[1]),
    ]
    for copy in copies:
        copy.start()
    for copy in copies:
        copy.wait()


def shards(sizes, u, e, t, r, b):
    X, Y, Z = t.shape
    N = X * Y
    layers = sizes[2]
    assert 8 * X <= Z and Z % 128 == 0 and Y % 8 == 0 and X % 8 == 0
    W = max(X, Y)
    f32 = jnp.float32
    vmem = pltpu.VMEM
    dma = pltpu.SemaphoreType.DMA
    any_space = pl.BlockSpec(memory_space=pl.ANY)
    in_vmem = pl.BlockSpec(memory_space=vmem)
    D = max(layers - 1, 1)
    n_upper = sum(upper(o) for o in offsets(layers))
    kept = pl.pallas_call(
        functools.partial(kernel, (X, Y, Z), sizes),
        out_shape=(vmem((6, N, Z), f32), vmem((3, N, Z), f32)),
        in_specs=[any_space] * 5,
        out_specs=(in_vmem, in_vmem),
        scratch_shapes=[
            vmem((3, N + 2 * Y, Z), f32),
            vmem((6, N, Z), f32),
            vmem((N, Z), f32),
            vmem((N, Z), f32),
            vmem((N, Z), jnp.int32),
            vmem((N, Z), f32),
            vmem((N, Z), f32),
            vmem((6, N, Z), f32),
            vmem((N, Z), f32),
            vmem((N, Z), f32),
            vmem((6, N + 2 * Y, Z), f32),
            vmem((2, 8, Y, Z), f32),
            vmem((2, 8, X, Z), f32),
            vmem((2, 3, X, Z), f32),
            vmem((2, W, Z), f32),
            vmem((2, Y, Z), f32),
            vmem((2, 2, 8, Z), f32),
            vmem((Y, Z), f32),
            vmem((2, Y, Z), f32),
            vmem((2, X, Z), f32),
            vmem((2, 3, Y, Z), f32),
            vmem((2, 8, Y, Z), f32),
            vmem((2, 3, X, Z), f32),
            vmem((2, 8, X, Z), f32),
            vmem((2, Y, Z), f32),
            vmem((2, 2, Y, Z), f32),
            vmem((2, 2, 8, Z), f32),
            vmem((2, 2, Y, Z), f32),
            vmem((2, 2, 2, W, Z), f32),
            vmem((D, Y, Z), f32),
            vmem((2, D, Y, Z), f32),
            vmem((2, D, X, Z), f32),
            dma((7,)),
            pltpu.SemaphoreType.REGULAR((n_upper,)),
        ] + [dma((2,))] * 12 + [dma((2, 2))] * 6 + [dma((D,))] * 2 + [dma((2, D))] * 4,
        compiler_params=pltpu.CompilerParams(collective_id=0, has_side_effects=True),
        name="strain_step",
    )(u.reshape(3, N, Z), e.reshape(6, N, Z), t.reshape(N, Z), r.reshape(N, Z), b.reshape(N, Z))
    f, m = pl.pallas_call(
        finish,
        out_shape=(jax.ShapeDtypeStruct((6, N, Z), f32), jax.ShapeDtypeStruct((3, N, Z), f32)),
        in_specs=[in_vmem] * 2,
        out_specs=(any_space, any_space),
        scratch_shapes=[dma((2,))],
        name="finish",
    )(*(pltpu.with_memory_space_constraint(k, vmem) for k in kept))
    return f.reshape(6, X, Y, Z), m.reshape(3, X, Y, Z)


def solution(mesh):
    sizes = tuple(mesh.shape[a] for a in AXES)
    field = P("gx", "gy", "gz")
    fields = P(None, "gx", "gy", "gz")
    return jax.shard_map(
        functools.partial(shards, sizes),
        mesh=mesh,
        in_specs=(fields, fields, field, field, field),
        out_specs=(fields, fields),
        check_vma=False,
    )
```

```python
import functools

import jax
import jax.numpy as jnp
from jax import lax
from jax.experimental import pallas as pl
from jax.experimental.pallas import tpu as pltpu
from jax.sharding import PartitionSpec as P

MESH = pl.DeviceIdType.MESH
AXES = ("gx", "gy", "gz")
TERMS = (
    ((0, 0.5), (3, 0.25), (4, 0.25)),
    ((3, 0.25), (1, 0.5), (5, 0.25)),
    ((4, 0.25), (5, 0.25), (2, 0.5)),
)
X_SET = (0, 3, 4)
Y_SET = (3, 1, 5)
Z_SET = (4, 5, 2)


def offsets(layers):
    near = [
        (x, y, z)
        for x in (-1, 0, 1)
        for y in (-1, 0, 1)
        for z in (-1, 0, 1)
        if 1 <= abs(x) + abs(y) + abs(z) <= 2
    ]
    far = [
        (x, y, s * d)
        for d in range(2, layers)
        for s in (-1, 1)
        for x, y in ((0, 0), (-1, 0), (1, 0), (0, -1), (0, 1))
    ]
    return near + far


def minus(o):
    return tuple(-v for v in o)


def plus(o, p):
    return tuple(v + w for v, w in zip(o, p))


def split(o):
    return tuple(min(v, 0) for v in o), tuple(max(v, 0) for v in o)


def kinds_of(layers):
    offs = offsets(layers)
    uppers = [o for o in offs if min(o) >= 0]
    lowers = [o for o in offs if max(o) <= 0]
    mixed = [o for o in offs if min(o) < 0 < max(o)]
    return uppers, lowers, mixed


def merge(low, high):
    Z = low.shape[1]
    even = (lax.broadcasted_iota(jnp.int32, low.shape, 1) & 1) == 0
    return jnp.where(even, low, pltpu.roll(high, Z - 2, 1))


def edge_term(tile, q, z_edge):
    Z = tile.shape[1]
    return (pltpu.roll(tile, (Z - 2 * q) % Z, 1) if q else tile) * z_edge


def flow(e, pace):
    trace = e[0] + e[1] + e[2]
    third = trace * (1.0 / 3.0)
    half = [e[0] - third, e[1] - third, e[2] - third, e[3], e[4], e[5]]
    second = half[0] * half[0] + half[1] * half[1] + half[2] * half[2]
    second = second + 2.0 * (half[3] * half[3] + half[4] * half[4] + half[5] * half[5])
    rate = pace * second
    return trace, [rate * h for h in half]


def stress(e, change, trace, part):
    out = 2.0 * (e[part] - change[part])
    return out + trace if part < 3 else out


def kernel(
    dims, sizes,
    u_hbm, e_hbm, t_hbm, r_hbm, b_hbm,
    fv, mv,
    uv, ev, tv, rv, bv, pv, tot, el, av, nt, sp,
    xs, ys, yu, zu, zs, xy, zt, xt, yt,
    rxu, rxs, ryu, rys, rzu, rzs, rxy, rxz, ryz, rt, rtx, rty,
    in_sem, ready, told,
    xu_send, xu_recv, xs_send, xs_recv, yu_send, yu_recv, ys_send, ys_recv,
    zu_send, zu_recv, zs_send, zs_recv, xy_send, xy_recv, xz_send, xz_recv, yz_send, yz_recv,
    t_send, t_recv, tx_send, tx_recv, ty_send, ty_recv,
):
    X, Y, Z = dims
    N = X * Y
    layers = sizes[2]
    depths = range(1, layers)
    me = [lax.axis_index(a) for a in AXES]
    offs = offsets(layers)
    uppers, lowers, mixed = kinds_of(layers)

    def exists(o):
        ok = None
        for a in range(3):
            if o[a]:
                here = me[a] + o[a]
                test = here < sizes[a] if o[a] > 0 else here >= 0
                ok = test if ok is None else jnp.logical_and(ok, test)
        return ok

    def partner(o):
        return {AXES[a]: me[a] + o[a] for a in range(3) if o[a]}

    has = {o: exists(o) for o in offs}
    faces = {a: [tuple(s if i == a else 0 for i in range(3)) for s in (-1, 1)] for a in range(3)}

    loads = [
        pltpu.make_async_copy(src, dst, in_sem.at[i])
        for i, (src, dst) in enumerate(
            (
                (u_hbm, uv.at[:, pl.ds(Y, N), :]),
                (r_hbm, rv),
                (e_hbm.at[:, pl.ds(0, Y), :], ev.at[:, pl.ds(0, Y), :]),
                (e_hbm.at[:, pl.ds(N - Y, Y), :], ev.at[:, pl.ds(N - Y, Y), :]),
                (t_hbm, tv),
                (b_hbm, bv),
                (e_hbm.at[:, pl.ds(Y, N - 2 * Y), :], ev.at[:, pl.ds(Y, N - 2 * Y), :]),
            )
        )
    ]
    for copy in loads:
        copy.start()

    barrier = pltpu.get_barrier_semaphore()
    for o in uppers:
        @pl.when(has[o])
        def _(o=o):
            pl.semaphore_signal(barrier, inc=1, device_id=partner(o), device_id_type=MESH)
    expected = jnp.int32(0)
    for o in lowers:
        expected = expected + has[o].astype(jnp.int32)

    plane = jnp.zeros((Y, Z), jnp.float32)
    row_plane = jnp.zeros((X, Z), jnp.float32)
    for c in range(3):
        uv[c, pl.ds(0, Y), :] = plane
        uv[c, pl.ds(Y + N, Y), :] = plane
    for c in range(6):
        sp[c, pl.ds(0, Y), :] = plane
        sp[c, pl.ds(Y + N, Y), :] = plane

    def blank(o, *refs):
        @pl.when(jnp.logical_not(has[o]))
        def _():
            for ref in refs:
                ref[...] = jnp.zeros(ref.shape, jnp.float32)

    for i, sz in enumerate((-1, 1)):
        blank((0, 0, sz), rzu.at[i], rzs.at[i])
        for j, s in enumerate((-1, 1)):
            blank((s, 0, sz), rxz.at[j, i])
            blank((0, s, sz), ryz.at[j, i])
    for i, sx in enumerate((-1, 1)):
        for j, sy in enumerate((-1, 1)):
            blank((sx, sy, 0), rxy.at[i, j])
    for d in depths:
        blank((0, 0, -d), rt.at[d - 1])
        for j, s in enumerate((-1, 1)):
            blank((s, 0, -d), rtx.at[j, d - 1])
            blank((0, s, -d), rty.at[j, d - 1])

    lane = lax.broadcasted_iota(jnp.int32, (Y, Z), 1)
    row = lax.broadcasted_iota(jnp.int32, (Y, Z), 0)
    pair = lane >> 1
    even = (lane & 1) == 0
    not_last = jnp.where(row < Y - 1, 0.5, 0.0).astype(jnp.float32)
    not_first = jnp.where(row > 0, 0.5, 0.0).astype(jnp.float32)
    z_first = jnp.where(lane > 0, 0.5, 0.0).astype(jnp.float32)
    z_last = jnp.where(lane < Z - 1, 0.5, 0.0).astype(jnp.float32)
    z_edge = jnp.where(lane == 0, -0.5, jnp.where(lane == Z - 1, 0.5, 0.0)).astype(jnp.float32)
    if X == Y:
        row_x, z_edge_x = row, z_edge
    else:
        lane_x = lax.broadcasted_iota(jnp.int32, (X, Z), 1)
        row_x = lax.broadcasted_iota(jnp.int32, (X, Z), 0)
        z_edge_x = jnp.where(lane_x == 0, -0.5, jnp.where(lane_x == Z - 1, 0.5, 0.0)).astype(jnp.float32)

    sends = {o: [] for o in offs}
    recvs = {}

    def message(kind, o, src, dst, send, recv):
        copy = pltpu.make_async_remote_copy(
            src_ref=src, dst_ref=dst, send_sem=send, recv_sem=recv,
            device_id=partner(o), device_id_type=MESH,
        )
        sends[o].append((kind, copy))
        recvs[kind, minus(o)] = copy

    for i, s in enumerate((-1, 1)):
        k = 1 - i
        at = (Y, Y * X)[i]
        message("xu", (s, 0, 0), uv.at[:, pl.ds(at, Y), :], rxu.at[k], xu_send.at[i], xu_recv.at[k])
        message("xs", (s, 0, 0), xs.at[i], rxs.at[k], xs_send.at[i], xs_recv.at[k])
        message("yu", (0, s, 0), yu.at[i], ryu.at[k], yu_send.at[i], yu_recv.at[k])
        message("ys", (0, s, 0), ys.at[i], rys.at[k], ys_send.at[i], ys_recv.at[k])
        message("zu", (0, 0, s), zu.at[0, pl.ds(0, Y)], rzu.at[k], zu_send.at[i], zu_recv.at[k])
        message("zs", (0, 0, s), zs, rzs.at[k], zs_send.at[i], zs_recv.at[k])
        for j, s2 in enumerate((-1, 1)):
            m = 1 - j
            message("xy", (s, s2, 0), xy.at[i, j], rxy.at[k, m], xy_send.at[i, j], xy_recv.at[k, m])
            message("xz", (s, 0, s2), zu.at[0, pl.ds(0, Y)], rxz.at[k, m], xz_send.at[i, j], xz_recv.at[k, m])
            message("yz", (0, s, s2), zu, ryz.at[k, m], yz_send.at[i, j], yz_recv.at[k, m])
        for d in depths:
            message("tx", (s, 0, d), xt.at[i], rtx.at[k, d - 1], tx_send.at[i, d - 1], tx_recv.at[k, d - 1])
            message("ty", (0, s, d), yt.at[i], rty.at[k, d - 1], ty_send.at[i, d - 1], ty_recv.at[k, d - 1])
    for d in depths:
        message("t", (0, 0, d), zt, rt.at[d - 1], t_send.at[d - 1], t_recv.at[d - 1])

    def start(offsets_in, kinds):
        for o in offsets_in:
            chosen = [copy for kind, copy in sends[o] if kind in kinds]
            if chosen:
                @pl.when(has[o])
                def _(chosen=chosen):
                    for copy in chosen:
                        copy.start()

    def arrive(*kinds):
        for (kind, o), copy in recvs.items():
            if kind in kinds:
                @pl.when(has[o])
                def _(copy=copy):
                    copy.wait_recv()

    @pl.when(expected > 0)
    def _():
        pl.semaphore_wait(barrier, expected)

    for o in lowers:
        @pl.when(has[o])
        def _(o=o):
            pl.semaphore_signal(
                ready.at[uppers.index(minus(o))], inc=1, device_id=partner(o), device_id_type=MESH
            )

    loads[0].wait()
    tile0 = plane
    for x in range(X):
        for c in range(3):
            q = c * X + x
            tile = pltpu.roll(uv[c, pl.ds(Y + x * Y, Y), :], (2 * q + 1) % Z, 1)
            tile0 = jnp.where(pair == q, tile, tile0)
    zu[0, pl.ds(0, Y), :] = tile0
    tile = row_plane
    pair_x = lax.broadcasted_iota(jnp.int32, (X, Z), 1) >> 1
    for i, line in enumerate((0, Y - 1)):
        for c in range(3):
            p = 3 * i + c
            lines = uv[c, pl.ds(Y + line, X, stride=Y), :]
            yu[i, c] = lines
            tile = jnp.where(pair_x == p, pltpu.roll(lines, (2 * p + 1) % Z, 1), tile)
            for j, at in enumerate((0, X - 1)):
                xy[j, i, pl.ds(c, 1), :] = uv[c, pl.ds(Y + at * Y + line, 1), :]
    zu[1, pl.ds(0, X), :] = tile

    first = ("xu", "yu", "zu", "xy", "xz", "yz")
    start(lowers, first)

    loads[1].wait()
    total_depth = Z * layers
    depth = (me[2] * Z + lane).astype(jnp.float32)
    scale = (1.0 + 2.0 * depth / total_depth) / total_depth
    thirds = [[], [], []]
    for x in range(X):
        rest = rv[pl.ds(x * Y, Y), :] * scale
        for k in range(3):
            piece = rest.astype(jnp.bfloat16)
            thirds[k].append(piece)
            rest = rest - piece.astype(jnp.float32)
    weight = jnp.concatenate([jnp.concatenate(k, axis=0) for k in thirds], axis=1)
    above_row = lax.broadcasted_iota(jnp.int32, (Z, 2 * Z), 0)
    column = lax.broadcasted_iota(jnp.int32, (Z, 2 * Z), 1)
    triangle = jnp.where(
        (above_row < column) | (column >= Z),
        1.0,
        jnp.where(above_row == column, 0.5, 0.0),
    ).astype(jnp.bfloat16)
    triangle = jnp.concatenate([triangle] * 3, axis=0)
    sums = jnp.dot(weight, triangle, preferred_element_type=jnp.float32)
    pv[...] = sums[:, :Z] + 1.0
    tot[...] = sums[:, Z:]
    tile = plane
    for x in range(X):
        tile = jnp.where(pair == x, tot[pl.ds(x * Y, Y), :], tile)
    zt[...] = tile
    for i, (at, line) in enumerate(((0, 0), (X - 1, Y - 1))):
        xt[i] = tot[pl.ds(at * Y, Y), :]
        yt[i] = tot[pl.ds(line, X, stride=Y), :]

    tiles = [plane, plane]

    def strain(x):
        base = Y + x * Y
        own = pl.ds(x * Y, Y)
        grad = []
        for c in range(3):
            here = uv[c, pl.ds(base, Y), :]
            grad.append((
                (uv[c, pl.ds(base + Y, Y), :] - uv[c, pl.ds(base - Y, Y), :]) * 0.5,
                uv[c, pl.ds(base + 1, Y), :] * not_last - uv[c, pl.ds(base - 1, Y), :] * not_first,
                pltpu.roll(here, Z - 1, 1) * z_last - pltpu.roll(here, 1, 1) * z_first,
            ))
        el[0, own, :] = grad[0][0]
        el[1, own, :] = grad[1][1]
        el[2, own, :] = grad[2][2]
        el[3, own, :] = 0.5 * (grad[0][1] + grad[1][0])
        el[4, own, :] = 0.5 * (grad[0][2] + grad[2][0])
        el[5, own, :] = 0.5 * (grad[1][2] + grad[2][1])

    def pack(k, x, part, tiles):
        q = (k % 4) * X + x
        tile = pltpu.roll(part, (2 * q + 1) % Z, 1)
        tiles[k // 4] = jnp.where(pair == q, tile, tiles[k // 4])

    def factors(x, tiles):
        own = pl.ds(x * Y, Y)
        minus_two = -2.0 / tv[own, :]
        factor = (2.0 + 14.0 * bv[own, :].astype(jnp.float32)) * jnp.exp(pv[own, :] * minus_two)
        av[own, :] = factor
        nt[own, :] = minus_two
        for i, at in enumerate((0, X - 1)):
            if x == at:
                xs[i, 6] = factor
                xs[i, 7] = minus_two
        pack(6, x, factor, tiles)
        pack(7, x, minus_two, tiles)

    def elastic(x, tiles):
        own = pl.ds(x * Y, Y)
        for k in range(6):
            part = el[k, own, :] - ev[k, own, :]
            el[k, own, :] = part
            for i, at in enumerate((0, X - 1)):
                if x == at:
                    xs[i, k] = part
            pack(k, x, part, tiles)

    ends = sorted({0, X - 1})
    for x in ends:
        strain(x)
    for copy in loads[2:6]:
        copy.wait()
    for x in ends:
        elastic(x, tiles)
        factors(x, tiles)
    start(lowers, ("xs", "t", "tx", "ty"))

    inner = [x for x in range(X) if x not in ends]
    for x in inner:
        strain(x)
        factors(x, tiles)
    loads[6].wait()
    for x in inner:
        elastic(x, tiles)
    for i, line in enumerate((0, Y - 1)):
        for k in range(8):
            src = el.at[k] if k < 6 else (av, nt)[k - 6]
            ys[i, k] = src[pl.ds(line, X, stride=Y), :]
    start(lowers, ("ys",))
    for k in range(2):
        zs[k] = tiles[k]
    start(lowers, ("zs",))

    everything = first + ("xs", "ys", "zs", "t", "tx", "ty")
    for o in sorted(uppers, key=lambda o: sum(map(abs, o))):
        @pl.when(has[o])
        def _(o=o):
            pl.semaphore_wait(ready.at[uppers.index(o)], 1)

        start([o], everything)
    for o in mixed:
        low, high = split(o)

        @pl.when(jnp.logical_and(has[minus(low)], has[high]))
        def _(o=o, low=low):
            pl.semaphore_signal(
                told.at[mixed.index(o)], inc=1, device_id=partner(minus(low)), device_id_type=MESH
            )
    for o in mixed:
        @pl.when(has[o])
        def _(o=o):
            pl.semaphore_wait(told.at[mixed.index(o)], 1)

        start([o], everything)

    arrive("yu")
    for side, line in enumerate((0, Y - 1)):
        sign = 2.0 * side - 1.0

        @pl.when(has[faces[1][side]])
        def _(side=side, sign=sign, line=line):
            own = pl.ds(line, X, stride=Y)
            for c, (part, factor) in enumerate(TERMS[1]):
                el[part, own, :] = el[part, own, :] + (sign * factor) * ryu[side, c]

    arrive("zu", "t")
    carried = plane
    for d in depths:
        carried = carried + rt[d - 1]
    merged = merge(rzu[0], rzu[1])

    def advance(x):
        own = pl.ds(x * Y, Y)
        e = [el[c, own, :] for c in range(6)]
        for c, (part, factor) in enumerate(TERMS[2]):
            e[part] = e[part] + (2.0 * factor) * edge_term(merged, c * X + x, z_edge)
        load = jnp.broadcast_to(carried[:, 2 * x:2 * x + 1], (Y, Z))
        trace, change = flow(e, av[own, :] * jnp.exp(load * nt[own, :]))
        for c in range(6):
            fv[c, own, :] = ev[c, own, :] + change[c]
            sp[c, pl.ds(Y + x * Y, Y), :] = stress(e, change, trace, c)

    for x in range(X):
        if x not in ends:
            advance(x)
    arrive("xu")
    for side, at in enumerate((0, X - 1)):
        sign = 2.0 * side - 1.0

        @pl.when(has[faces[0][side]])
        def _(side=side, sign=sign, at=at):
            own = pl.ds(at * Y, Y)
            for c, (part, factor) in enumerate(TERMS[0]):
                el[part, own, :] = el[part, own, :] + (sign * factor) * rxu[side, c]

    for x in ends:
        advance(x)

    for x in range(X):
        base = Y + x * Y
        own = pl.ds(x * Y, Y)
        for c in range(3):
            cx, cy, cz = X_SET[c], Y_SET[c], Z_SET[c]
            here = sp[cz, pl.ds(base, Y), :]
            total = (sp[cx, pl.ds(base + Y, Y), :] - sp[cx, pl.ds(base - Y, Y), :]) * 0.5
            total = total + (
                sp[cy, pl.ds(base + 1, Y), :] * not_last - sp[cy, pl.ds(base - 1, Y), :] * not_first
            )
            total = total + (pltpu.roll(here, Z - 1, 1) * z_last - pltpu.roll(here, 1, 1) * z_first)
            if c == 2:
                total = total - 0.5 * rv[own, :]
            mv[c, own, :] = total

    def add(e, axis, factor, values):
        for c, (part, f) in enumerate(TERMS[axis]):
            e[part] = e[part] + (factor * f) * values[c]

    def ends_of(first, last, rows, count):
        return jnp.where(rows == 0, -first, jnp.where(rows == count - 1, last, 0.0))

    arrive("ys", "xy", "yz", "ty")
    for side, line in enumerate((0, Y - 1)):
        @pl.when(has[faces[1][side]])
        def _(side=side, line=line):
            e = [rys[side, k] for k in range(6)]
            add(e, 1, 1.0 - 2.0 * side, [uv[c, pl.ds(Y + line, X, stride=Y), :] for c in range(3)])
            add(e, 0, 1.0, [
                ends_of(rxy[0, side, pl.ds(c, 1), :], rxy[1, side, pl.ds(c, 1), :], row_x, X) for c in range(3)
            ])
            joined = merge(ryz[side, 0, 1, pl.ds(0, X), :], ryz[side, 1, 1, pl.ds(0, X), :])
            add(e, 2, 2.0, [edge_term(joined, 3 * (1 - side) + c, z_edge_x) for c in range(3)])
            load = row_plane
            for d in depths:
                load = load + rty[side, d - 1]
            trace, change = flow(e, rys[side, 6] * jnp.exp(load * rys[side, 7]))
            own = pl.ds(line, X, stride=Y)
            for c in range(3):
                mv[c, own, :] = mv[c, own, :] + (side - 0.5) * stress(e, change, trace, Y_SET[c])

    arrive("zs", "xz")
    block = 2 * X

    def shift(tile, by):
        return pltpu.roll(tile, by % Z, 1) if by % Z else tile

    halo = [jnp.where(even, rzs[0, k], rzs[1, k]) for k in range(2)]
    parts = [shift(halo[k // 4], -(k % 4) * block) for k in range(8)]
    mine = zu[0, pl.ds(0, Y), :]
    from_z = jnp.where(even, shift(mine, -1), -shift(mine, 1))
    left = jnp.where(even, rxz[0, 0], rxz[0, 1])
    right = jnp.where(even, rxz[1, 0], rxz[1, 1])
    spot = pair % X
    from_x = jnp.where(
        spot == 0, -shift(left, -2 * (X - 1)), jnp.where(spot == X - 1, shift(right, 2 * (X - 1)), 0.0)
    )
    even_row = (lax.broadcasted_iota(jnp.int32, (1, Z), 1) & 1) == 0
    from_y = ends_of(
        jnp.where(even_row, ryz[0, 0, 0, pl.ds(Y - 1, 1), :], ryz[0, 1, 0, pl.ds(Y - 1, 1), :]),
        jnp.where(even_row, ryz[1, 0, 0, pl.ds(0, 1), :], ryz[1, 1, 0, pl.ds(0, 1), :]),
        row, Y,
    )
    e = list(parts[:6])
    for axis, tile in enumerate((from_x, from_y, from_z)):
        add(e, axis, 1.0, [shift(tile, -c * block) for c in range(3)])
    deeper = plane
    for d in depths:
        if d >= 2:
            deeper = deeper + rt[d - 1]
    load = jnp.where(even, deeper, carried + zt[...])
    trace, change = flow(e, parts[6] * jnp.exp(load * parts[7]))
    known = jnp.where(
        even,
        has[0, 0, -1].astype(jnp.float32),
        has[0, 0, 1].astype(jnp.float32),
    )
    gathered = plane
    for c in range(3):
        tile = shift(stress(e, change, trace, Z_SET[c]) * known, c * block)
        gathered = jnp.where((pair >= c * X) & (pair < (c + 1) * X), tile, gathered)
    joined = jnp.where(even, gathered, shift(gathered, -2))
    for c in range(3):
        for x in range(X):
            own = pl.ds(x * Y, Y)
            mv[c, own, :] = mv[c, own, :] + edge_term(joined, c * X + x, z_edge)

    arrive("xs", "tx")
    for side, at in enumerate((0, X - 1)):
        @pl.when(has[faces[0][side]])
        def _(side=side, at=at):
            e = [rxs[side, k] for k in range(6)]
            add(e, 0, 1.0 - 2.0 * side, [uv[c, pl.ds(Y + at * Y, Y), :] for c in range(3)])
            add(e, 1, 1.0, [
                ends_of(rxy[side, 0, pl.ds(c, 1), :], rxy[side, 1, pl.ds(c, 1), :], row, Y) for c in range(3)
            ])
            facing = (X - 1) * (1 - side)
            joined = merge(rxz[side, 0], rxz[side, 1])
            add(e, 2, 2.0, [edge_term(joined, c * X + facing, z_edge) for c in range(3)])
            load = plane
            for d in depths:
                load = load + rtx[side, d - 1]
            trace, change = flow(e, rxs[side, 6] * jnp.exp(load * rxs[side, 7]))
            own = pl.ds(at * Y, Y)
            for c in range(3):
                mv[c, own, :] = mv[c, own, :] + (side - 0.5) * stress(e, change, trace, X_SET[c])

    for o in offs:
        if sends[o]:
            @pl.when(has[o])
            def _(o=o):
                for _, copy in sends[o]:
                    copy.wait_send()


def finish(fv, mv, f_hbm, m_hbm, sem):
    copies = [
        pltpu.make_async_copy(mv, m_hbm, sem.at[0]),
        pltpu.make_async_copy(fv, f_hbm, sem.at[1]),
    ]
    for copy in copies:
        copy.start()
    for copy in copies:
        copy.wait()


def shards(sizes, u, e, t, r, b):
    X, Y, Z = t.shape
    N = X * Y
    layers = sizes[2]
    assert 8 * X <= Z and Z % 128 == 0 and Y % 8 == 0 and X % 8 == 0
    W = max(X, Y)
    f32 = jnp.float32
    vmem = pltpu.VMEM
    dma = pltpu.SemaphoreType.DMA
    any_space = pl.BlockSpec(memory_space=pl.ANY)
    in_vmem = pl.BlockSpec(memory_space=vmem)
    D = max(layers - 1, 1)
    uppers, _, mixed = kinds_of(layers)
    kept = pl.pallas_call(
        functools.partial(kernel, (X, Y, Z), sizes),
        out_shape=(vmem((6, N, Z), f32), vmem((3, N, Z), f32)),
        in_specs=[any_space] * 5,
        out_specs=(in_vmem, in_vmem),
        scratch_shapes=[
            vmem((3, N + 2 * Y, Z), f32),
            vmem((6, N, Z), f32),
            vmem((N, Z), f32),
            vmem((N, Z), f32),
            vmem((N, Z), jnp.int32),
            vmem((N, Z), f32),
            vmem((N, Z), f32),
            vmem((6, N, Z), f32),
            vmem((N, Z), f32),
            vmem((N, Z), f32),
            vmem((6, N + 2 * Y, Z), f32),
            vmem((2, 8, Y, Z), f32),
            vmem((2, 8, X, Z), f32),
            vmem((2, 3, X, Z), f32),
            vmem((2, W, Z), f32),
            vmem((2, Y, Z), f32),
            vmem((2, 2, 8, Z), f32),
            vmem((Y, Z), f32),
            vmem((2, Y, Z), f32),
            vmem((2, X, Z), f32),
            vmem((2, 3, Y, Z), f32),
            vmem((2, 8, Y, Z), f32),
            vmem((2, 3, X, Z), f32),
            vmem((2, 8, X, Z), f32),
            vmem((2, Y, Z), f32),
            vmem((2, 2, Y, Z), f32),
            vmem((2, 2, 8, Z), f32),
            vmem((2, 2, Y, Z), f32),
            vmem((2, 2, 2, W, Z), f32),
            vmem((D, Y, Z), f32),
            vmem((2, D, Y, Z), f32),
            vmem((2, D, X, Z), f32),
            dma((7,)),
            pltpu.SemaphoreType.REGULAR((len(uppers),)),
            pltpu.SemaphoreType.REGULAR((len(mixed),)),
        ] + [dma((2,))] * 12 + [dma((2, 2))] * 6 + [dma((D,))] * 2 + [dma((2, D))] * 4,
        compiler_params=pltpu.CompilerParams(collective_id=0, has_side_effects=True),
        name="strain_step",
    )(u.reshape(3, N, Z), e.reshape(6, N, Z), t.reshape(N, Z), r.reshape(N, Z), b.reshape(N, Z))
    f, m = pl.pallas_call(
        finish,
        out_shape=(jax.ShapeDtypeStruct((6, N, Z), f32), jax.ShapeDtypeStruct((3, N, Z), f32)),
        in_specs=[in_vmem] * 2,
        out_specs=(any_space, any_space),
        scratch_shapes=[dma((2,))],
        name="finish",
    )(*(pltpu.with_memory_space_constraint(k, vmem) for k in kept))
    return f.reshape(6, X, Y, Z), m.reshape(3, X, Y, Z)


def solution(mesh):
    sizes = tuple(mesh.shape[a] for a in AXES)
    field = P("gx", "gy", "gz")
    fields = P(None, "gx", "gy", "gz")
    return jax.shard_map(
        functools.partial(shards, sizes),
        mesh=mesh,
        in_specs=(fields, fields, field, field, field),
        out_specs=(fields, fields),
        check_vma=False,
    )
```

```python
import functools

import jax
import jax.numpy as jnp
from jax import lax
from jax.experimental import pallas as pl
from jax.experimental.pallas import tpu as pltpu
from jax.sharding import PartitionSpec as P

MESH = pl.DeviceIdType.MESH
AXES = ("gx", "gy", "gz")
TERMS = (
    ((0, 0.5), (3, 0.25), (4, 0.25)),
    ((3, 0.25), (1, 0.5), (5, 0.25)),
    ((4, 0.25), (5, 0.25), (2, 0.5)),
)
X_SET = (0, 3, 4)
Y_SET = (3, 1, 5)
Z_SET = (4, 5, 2)


def offsets(layers):
    near = [
        (x, y, z)
        for x in (-1, 0, 1)
        for y in (-1, 0, 1)
        for z in (-1, 0, 1)
        if 1 <= abs(x) + abs(y) + abs(z) <= 2
    ]
    far = [
        (x, y, s * d)
        for d in range(2, layers)
        for s in (-1, 1)
        for x, y in ((0, 0), (-1, 0), (1, 0), (0, -1), (0, 1))
    ]
    return near + far


def minus(o):
    return tuple(-v for v in o)


def plus(o, p):
    return tuple(v + w for v, w in zip(o, p))


def split(o):
    return tuple(min(v, 0) for v in o), tuple(max(v, 0) for v in o)


def kinds_of(layers):
    offs = offsets(layers)
    uppers = [o for o in offs if min(o) >= 0]
    lowers = [o for o in offs if max(o) <= 0]
    mixed = [o for o in offs if min(o) < 0 < max(o)]
    return uppers, lowers, mixed


def merge(low, high):
    Z = low.shape[1]
    even = (lax.broadcasted_iota(jnp.int32, low.shape, 1) & 1) == 0
    return jnp.where(even, low, pltpu.roll(high, Z - 2, 1))


def edge_term(tile, q, z_edge):
    Z = tile.shape[1]
    return (pltpu.roll(tile, (Z - 2 * q) % Z, 1) if q else tile) * z_edge


def flow(e, pace):
    trace = e[0] + e[1] + e[2]
    third = trace * (1.0 / 3.0)
    half = [e[0] - third, e[1] - third, e[2] - third, e[3], e[4], e[5]]
    second = half[0] * half[0] + half[1] * half[1] + half[2] * half[2]
    second = second + 2.0 * (half[3] * half[3] + half[4] * half[4] + half[5] * half[5])
    rate = pace * second
    return trace, [rate * h for h in half]


def stress(e, change, trace, part):
    out = 2.0 * (e[part] - change[part])
    return out + trace if part < 3 else out


def kernel(
    dims, sizes,
    u_hbm, e_hbm, t_hbm, r_hbm, b_hbm,
    fv, mv,
    uv, ev, tv, rv, bv, pv, tot, el, av, nt, sp,
    xs, ys, yu, zu, zs, xy, zt, xt, yt,
    rxu, rxs, ryu, rys, rzu, rzs, rxy, rxz, ryz, rt, rtx, rty,
    in_sem, ready, told, send_sem, recv_sem,
):
    X, Y, Z = dims
    N = X * Y
    layers = sizes[2]
    depths = range(1, layers)
    me = [lax.axis_index(a) for a in AXES]
    offs = offsets(layers)
    uppers, lowers, mixed = kinds_of(layers)
    W = max(X, Y)

    def ready_index(o):
        return o.index(1) if sum(o) == 1 else 3

    def exists(o):
        ok = None
        for a in range(3):
            if o[a]:
                here = me[a] + o[a]
                test = here < sizes[a] if o[a] > 0 else here >= 0
                ok = test if ok is None else jnp.logical_and(ok, test)
        return ok

    def partner(o):
        return {AXES[a]: me[a] + o[a] for a in range(3) if o[a]}

    has = {o: exists(o) for o in offs}
    faces = {a: [tuple(s if i == a else 0 for i in range(3)) for s in (-1, 1)] for a in range(3)}

    loads = [
        pltpu.make_async_copy(src, dst, in_sem.at[min(i, 2) if i < 6 else 3])
        for i, (src, dst) in enumerate(
            (
                (u_hbm, uv.at[:, pl.ds(Y, N), :]),
                (r_hbm, rv),
                (e_hbm.at[:, pl.ds(0, Y), :], ev.at[:, pl.ds(0, Y), :]),
                (e_hbm.at[:, pl.ds(N - Y, Y), :], ev.at[:, pl.ds(N - Y, Y), :]),
                (t_hbm, tv),
                (b_hbm, bv),
                (e_hbm.at[:, pl.ds(Y, N - 2 * Y), :], ev.at[:, pl.ds(Y, N - 2 * Y), :]),
            )
        )
    ]
    for copy in loads:
        copy.start()

    def take(sem, rows):
        planes = next(k for k in range(1, 7) if rows % (8 * k) == 0 and rows // k <= N + 2 * Y)
        spot = sp.at[pl.ds(0, planes), pl.ds(0, rows // planes)]
        pltpu.make_async_copy(spot, spot, sem).wait()

    barrier = pltpu.get_barrier_semaphore()
    for o in uppers:
        @pl.when(has[o])
        def _(o=o):
            pl.semaphore_signal(barrier, inc=1, device_id=partner(o), device_id_type=MESH)
    expected = jnp.int32(0)
    for o in lowers:
        expected = expected + has[o].astype(jnp.int32)

    plane = jnp.zeros((Y, Z), jnp.float32)
    row_plane = jnp.zeros((X, Z), jnp.float32)
    for c in range(3):
        uv[c, pl.ds(0, Y), :] = plane
        uv[c, pl.ds(Y + N, Y), :] = plane
    for c in range(6):
        sp[c, pl.ds(0, Y), :] = plane
        sp[c, pl.ds(Y + N, Y), :] = plane

    def blank(o, *refs):
        @pl.when(jnp.logical_not(has[o]))
        def _():
            for ref in refs:
                ref[...] = jnp.zeros(ref.shape, jnp.float32)

    for i, sz in enumerate((-1, 1)):
        blank((0, 0, sz), rzu.at[i], rzs.at[i])
        for j, s in enumerate((-1, 1)):
            blank((s, 0, sz), rxz.at[j, i])
            blank((0, s, sz), ryz.at[j, i])
    for i, sx in enumerate((-1, 1)):
        for j, sy in enumerate((-1, 1)):
            blank((sx, sy, 0), rxy.at[i, j])
    for d in depths:
        blank((0, 0, -d), rt.at[d - 1])
        for j, s in enumerate((-1, 1)):
            blank((s, 0, -d), rtx.at[j, d - 1])
            blank((0, s, -d), rty.at[j, d - 1])

    lane = lax.broadcasted_iota(jnp.int32, (Y, Z), 1)
    row = lax.broadcasted_iota(jnp.int32, (Y, Z), 0)
    pair = lane >> 1
    even = (lane & 1) == 0
    not_last = jnp.where(row < Y - 1, 0.5, 0.0).astype(jnp.float32)
    not_first = jnp.where(row > 0, 0.5, 0.0).astype(jnp.float32)
    z_first = jnp.where(lane > 0, 0.5, 0.0).astype(jnp.float32)
    z_last = jnp.where(lane < Z - 1, 0.5, 0.0).astype(jnp.float32)
    z_edge = jnp.where(lane == 0, -0.5, jnp.where(lane == Z - 1, 0.5, 0.0)).astype(jnp.float32)
    if X == Y:
        row_x, z_edge_x = row, z_edge
    else:
        lane_x = lax.broadcasted_iota(jnp.int32, (X, Z), 1)
        row_x = lax.broadcasted_iota(jnp.int32, (X, Z), 0)
        z_edge_x = jnp.where(lane_x == 0, -0.5, jnp.where(lane_x == Z - 1, 0.5, 0.0)).astype(jnp.float32)

    beside = [sum(has[o].astype(jnp.int32) for o in faces[a]) for a in range(3)]
    some = [1, 2]
    above, below = me[2], layers - 1 - me[2]
    counts = {
        "xu": (3 * Y, beside[0], some), "xs": (8 * Y, beside[0], some),
        "yu": (3 * X, beside[1], some), "ys": (8 * X, beside[1], some),
        "zu": (Y, beside[2], some), "zs": (2 * Y, beside[2], some),
        "xy": (8, beside[0] * beside[1], [1, 2, 4]),
        "xz": (Y, beside[0] * beside[2], [1, 2, 4]),
        "yz": (2 * W, beside[1] * beside[2], [1, 2, 4]),
    }
    totals = {
        "t": (Y, 1, list(depths)),
        "tx": (Y, beside[0], sorted({n * d for n in some for d in depths})),
        "ty": (X, beside[1], sorted({n * d for n in some for d in depths})),
    }
    recv_index = {kind: i for i, kind in enumerate((*counts, *totals))}
    send_index = {
        "xu": 0, "xs": 0, "yu": 1, "ys": 1, "zu": 2, "zs": 2, "xy": 3, "xz": 4, "yz": 5, "t": 6, "tx": 7, "ty": 8,
    }
    sends = {o: [] for o in offs}

    def message(kind, o, src, dst):
        sends[o].append((kind, pltpu.make_async_remote_copy(
            src_ref=src, dst_ref=dst,
            send_sem=send_sem.at[send_index[kind]], recv_sem=recv_sem.at[recv_index[kind]],
            device_id=partner(o), device_id_type=MESH,
        )))

    for i, s in enumerate((-1, 1)):
        k = 1 - i
        at = (Y, Y * X)[i]
        message("xu", (s, 0, 0), uv.at[:, pl.ds(at, Y), :], rxu.at[k])
        message("xs", (s, 0, 0), xs.at[i], rxs.at[k])
        message("yu", (0, s, 0), yu.at[i], ryu.at[k])
        message("ys", (0, s, 0), ys.at[i], rys.at[k])
        message("zu", (0, 0, s), zu.at[0, pl.ds(0, Y)], rzu.at[k])
        message("zs", (0, 0, s), zs, rzs.at[k])
        for j, s2 in enumerate((-1, 1)):
            m = 1 - j
            message("xy", (s, s2, 0), xy.at[i, j], rxy.at[k, m])
            message("xz", (s, 0, s2), zu.at[0, pl.ds(0, Y)], rxz.at[k, m])
            message("yz", (0, s, s2), zu, ryz.at[k, m])
        for d in depths:
            message("tx", (s, 0, d), xt.at[i], rtx.at[k, d - 1])
            message("ty", (0, s, d), yt.at[i], rty.at[k, d - 1])
    for d in depths:
        message("t", (0, 0, d), zt, rt.at[d - 1])

    def settle(sem, rows, count, values):
        for n in values:
            @pl.when(count == n)
            def _(n=n):
                take(sem, n * rows)

    def start(offsets_in, kinds):
        for o in offsets_in:
            chosen = [copy for kind, copy in sends[o] if kind in kinds]
            if chosen:
                @pl.when(has[o])
                def _(chosen=chosen):
                    for copy in chosen:
                        copy.start()

    def arrive(*kinds):
        for kind in kinds:
            if kind in counts:
                rows, count, values = counts[kind]
            else:
                rows, count, values = totals[kind]
                count = count * above
            settle(recv_sem.at[recv_index[kind]], rows, count, values)

    @pl.when(expected > 0)
    def _():
        pl.semaphore_wait(barrier, expected)

    for o in lowers:
        @pl.when(has[o])
        def _(o=o):
            pl.semaphore_signal(
                ready.at[ready_index(minus(o))], inc=1, device_id=partner(o), device_id_type=MESH
            )

    def announce(o):
        low, high = split(o)

        @pl.when(jnp.logical_and(has[minus(low)], has[high]))
        def _():
            pl.semaphore_signal(told.at[0], inc=1, device_id=partner(minus(low)), device_id_type=MESH)

    lowers = sorted(lowers, key=lambda o: (sum(map(abs, o)), o[2], o[1]))

    loads[0].wait()
    tile0 = plane
    for x in range(X):
        for c in range(3):
            q = c * X + x
            tile = pltpu.roll(uv[c, pl.ds(Y + x * Y, Y), :], (2 * q + 1) % Z, 1)
            tile0 = jnp.where(pair == q, tile, tile0)
    zu[0, pl.ds(0, Y), :] = tile0
    tile = row_plane
    pair_x = lax.broadcasted_iota(jnp.int32, (X, Z), 1) >> 1
    for i, line in enumerate((0, Y - 1)):
        for c in range(3):
            p = 3 * i + c
            lines = uv[c, pl.ds(Y + line, X, stride=Y), :]
            yu[i, c] = lines
            tile = jnp.where(pair_x == p, pltpu.roll(lines, (2 * p + 1) % Z, 1), tile)
            for j, at in enumerate((0, X - 1)):
                xy[j, i, pl.ds(c, 1), :] = uv[c, pl.ds(Y + at * Y + line, 1), :]
    zu[1, pl.ds(0, X), :] = tile

    first = ("xu", "yu", "zu", "xy", "xz", "yz")
    start(lowers, first)

    loads[1].wait()
    total_depth = Z * layers
    depth = (me[2] * Z + lane).astype(jnp.float32)
    scale = (1.0 + 2.0 * depth / total_depth) / total_depth
    thirds = [[], [], []]
    for x in range(X):
        rest = rv[pl.ds(x * Y, Y), :] * scale
        for k in range(3):
            piece = rest.astype(jnp.bfloat16)
            thirds[k].append(piece)
            rest = rest - piece.astype(jnp.float32)
    weight = jnp.concatenate([jnp.concatenate(k, axis=0) for k in thirds], axis=1)
    above_row = lax.broadcasted_iota(jnp.int32, (Z, 2 * Z), 0)
    column = lax.broadcasted_iota(jnp.int32, (Z, 2 * Z), 1)
    triangle = jnp.where(
        (above_row < column) | (column >= Z),
        1.0,
        jnp.where(above_row == column, 0.5, 0.0),
    ).astype(jnp.bfloat16)
    triangle = jnp.concatenate([triangle] * 3, axis=0)
    sums = jnp.dot(weight, triangle, preferred_element_type=jnp.float32)
    pv[...] = sums[:, :Z] + 1.0
    tot[...] = sums[:, Z:]
    tile = plane
    for x in range(X):
        tile = jnp.where(pair == x, tot[pl.ds(x * Y, Y), :], tile)
    zt[...] = tile
    for i, (at, line) in enumerate(((0, 0), (X - 1, Y - 1))):
        xt[i] = tot[pl.ds(at * Y, Y), :]
        yt[i] = tot[pl.ds(line, X, stride=Y), :]

    tiles = [plane, plane]

    def strain(x):
        base = Y + x * Y
        own = pl.ds(x * Y, Y)
        grad = []
        for c in range(3):
            here = uv[c, pl.ds(base, Y), :]
            grad.append((
                (uv[c, pl.ds(base + Y, Y), :] - uv[c, pl.ds(base - Y, Y), :]) * 0.5,
                uv[c, pl.ds(base + 1, Y), :] * not_last - uv[c, pl.ds(base - 1, Y), :] * not_first,
                pltpu.roll(here, Z - 1, 1) * z_last - pltpu.roll(here, 1, 1) * z_first,
            ))
        el[0, own, :] = grad[0][0]
        el[1, own, :] = grad[1][1]
        el[2, own, :] = grad[2][2]
        el[3, own, :] = 0.5 * (grad[0][1] + grad[1][0])
        el[4, own, :] = 0.5 * (grad[0][2] + grad[2][0])
        el[5, own, :] = 0.5 * (grad[1][2] + grad[2][1])

    def pack(k, x, part, tiles):
        q = (k % 4) * X + x
        tile = pltpu.roll(part, (2 * q + 1) % Z, 1)
        tiles[k // 4] = jnp.where(pair == q, tile, tiles[k // 4])

    def factors(x, tiles):
        own = pl.ds(x * Y, Y)
        minus_two = -2.0 / tv[own, :]
        factor = (2.0 + 14.0 * bv[own, :].astype(jnp.float32)) * jnp.exp(pv[own, :] * minus_two)
        av[own, :] = factor
        nt[own, :] = minus_two
        for i, at in enumerate((0, X - 1)):
            if x == at:
                xs[i, 6] = factor
                xs[i, 7] = minus_two
        pack(6, x, factor, tiles)
        pack(7, x, minus_two, tiles)

    def elastic(x, tiles):
        own = pl.ds(x * Y, Y)
        for k in range(6):
            part = el[k, own, :] - ev[k, own, :]
            el[k, own, :] = part
            for i, at in enumerate((0, X - 1)):
                if x == at:
                    xs[i, k] = part
            pack(k, x, part, tiles)

    ends = sorted({0, X - 1})
    for x in ends:
        strain(x)
    take(in_sem.at[2], 12 * Y + 2 * N)
    for x in ends:
        elastic(x, tiles)
        factors(x, tiles)
    start(lowers, ("xs", "t", "tx", "ty"))

    inner = [x for x in range(X) if x not in ends]
    for x in inner:
        strain(x)
        factors(x, tiles)
    loads[6].wait()
    for x in inner:
        elastic(x, tiles)
    for i, line in enumerate((0, Y - 1)):
        for k in range(8):
            src = el.at[k] if k < 6 else (av, nt)[k - 6]
            ys[i, k] = src[pl.ds(line, X, stride=Y), :]
    start(lowers, ("ys",))
    for k in range(2):
        zs[k] = tiles[k]
    start(lowers, ("zs",))

    everything = first + ("xs", "ys", "zs", "t", "tx", "ty")
    near = [o for o in uppers if sum(o) == 1]
    for o in sorted(near):
        @pl.when(has[o])
        def _(o=o):
            pl.semaphore_wait(ready.at[ready_index(o)], 1)

    for o in mixed:
        low, high = split(o)
        if high in near and minus(low) in near:
            announce(o)
    start(sorted(near), everything)
    others = [o for o in uppers if o not in near]
    total = sum(has[o].astype(jnp.int32) for o in others)

    @pl.when(total > 0)
    def _():
        pl.semaphore_wait(ready.at[3], total)

    for o in mixed:
        low, high = split(o)
        if not (high in near and minus(low) in near):
            announce(o)
    start(others, everything)
    total_mixed = sum(has[o].astype(jnp.int32) for o in mixed)

    @pl.when(total_mixed > 0)
    def _():
        pl.semaphore_wait(told.at[0], total_mixed)

    start(mixed, everything)

    arrive("yu")
    for side, line in enumerate((0, Y - 1)):
        sign = 2.0 * side - 1.0

        @pl.when(has[faces[1][side]])
        def _(side=side, sign=sign, line=line):
            own = pl.ds(line, X, stride=Y)
            for c, (part, factor) in enumerate(TERMS[1]):
                el[part, own, :] = el[part, own, :] + (sign * factor) * ryu[side, c]

    arrive("zu", "t")
    carried = plane
    for d in depths:
        carried = carried + rt[d - 1]
    merged = merge(rzu[0], rzu[1])

    def advance(x):
        own = pl.ds(x * Y, Y)
        e = [el[c, own, :] for c in range(6)]
        for c, (part, factor) in enumerate(TERMS[2]):
            e[part] = e[part] + (2.0 * factor) * edge_term(merged, c * X + x, z_edge)
        load = jnp.broadcast_to(carried[:, 2 * x:2 * x + 1], (Y, Z))
        trace, change = flow(e, av[own, :] * jnp.exp(load * nt[own, :]))
        for c in range(6):
            fv[c, own, :] = ev[c, own, :] + change[c]
            sp[c, pl.ds(Y + x * Y, Y), :] = stress(e, change, trace, c)

    for x in range(X):
        if x not in ends:
            advance(x)
    arrive("xu")
    for side, at in enumerate((0, X - 1)):
        sign = 2.0 * side - 1.0

        @pl.when(has[faces[0][side]])
        def _(side=side, sign=sign, at=at):
            own = pl.ds(at * Y, Y)
            for c, (part, factor) in enumerate(TERMS[0]):
                el[part, own, :] = el[part, own, :] + (sign * factor) * rxu[side, c]

    for x in ends:
        advance(x)

    for x in range(X):
        base = Y + x * Y
        own = pl.ds(x * Y, Y)
        for c in range(3):
            cx, cy, cz = X_SET[c], Y_SET[c], Z_SET[c]
            here = sp[cz, pl.ds(base, Y), :]
            total = (sp[cx, pl.ds(base + Y, Y), :] - sp[cx, pl.ds(base - Y, Y), :]) * 0.5
            total = total + (
                sp[cy, pl.ds(base + 1, Y), :] * not_last - sp[cy, pl.ds(base - 1, Y), :] * not_first
            )
            total = total + (pltpu.roll(here, Z - 1, 1) * z_last - pltpu.roll(here, 1, 1) * z_first)
            if c == 2:
                total = total - 0.5 * rv[own, :]
            mv[c, own, :] = total

    def add(e, axis, factor, values):
        for c, (part, f) in enumerate(TERMS[axis]):
            e[part] = e[part] + (factor * f) * values[c]

    def ends_of(first, last, rows, count):
        return jnp.where(rows == 0, -first, jnp.where(rows == count - 1, last, 0.0))

    def along_gy():
        arrive("ys", "ty")
        for side, line in enumerate((0, Y - 1)):
            @pl.when(has[faces[1][side]])
            def _(side=side, line=line):
                e = [rys[side, k] for k in range(6)]
                add(e, 1, 1.0 - 2.0 * side, [uv[c, pl.ds(Y + line, X, stride=Y), :] for c in range(3)])
                add(e, 0, 1.0, [
                    ends_of(rxy[0, side, pl.ds(c, 1), :], rxy[1, side, pl.ds(c, 1), :], row_x, X) for c in range(3)
                ])
                joined = merge(ryz[side, 0, 1, pl.ds(0, X), :], ryz[side, 1, 1, pl.ds(0, X), :])
                add(e, 2, 2.0, [edge_term(joined, 3 * (1 - side) + c, z_edge_x) for c in range(3)])
                load = row_plane
                for d in depths:
                    load = load + rty[side, d - 1]
                trace, change = flow(e, rys[side, 6] * jnp.exp(load * rys[side, 7]))
                own = pl.ds(line, X, stride=Y)
                for c in range(3):
                    mv[c, own, :] = mv[c, own, :] + (side - 0.5) * stress(e, change, trace, Y_SET[c])

    first_row = me[1] == 0

    @pl.when(first_row)
    def _():
        arrive("xy", "yz")
        along_gy()

    @pl.when(jnp.logical_not(first_row))
    def _():
        arrive("yz")

    arrive("zs", "xz")
    block = 2 * X

    def shift(tile, by):
        return pltpu.roll(tile, by % Z, 1) if by % Z else tile

    halo = [jnp.where(even, rzs[0, k], rzs[1, k]) for k in range(2)]
    parts = [shift(halo[k // 4], -(k % 4) * block) for k in range(8)]
    mine = zu[0, pl.ds(0, Y), :]
    from_z = jnp.where(even, shift(mine, -1), -shift(mine, 1))
    left = jnp.where(even, rxz[0, 0], rxz[0, 1])
    right = jnp.where(even, rxz[1, 0], rxz[1, 1])
    spot = pair % X
    from_x = jnp.where(
        spot == 0, -shift(left, -2 * (X - 1)), jnp.where(spot == X - 1, shift(right, 2 * (X - 1)), 0.0)
    )
    even_row = (lax.broadcasted_iota(jnp.int32, (1, Z), 1) & 1) == 0
    from_y = ends_of(
        jnp.where(even_row, ryz[0, 0, 0, pl.ds(Y - 1, 1), :], ryz[0, 1, 0, pl.ds(Y - 1, 1), :]),
        jnp.where(even_row, ryz[1, 0, 0, pl.ds(0, 1), :], ryz[1, 1, 0, pl.ds(0, 1), :]),
        row, Y,
    )
    e = list(parts[:6])
    for axis, tile in enumerate((from_x, from_y, from_z)):
        add(e, axis, 1.0, [shift(tile, -c * block) for c in range(3)])
    deeper = plane
    for d in depths:
        if d >= 2:
            deeper = deeper + rt[d - 1]
    load = jnp.where(even, deeper, carried + zt[...])
    trace, change = flow(e, parts[6] * jnp.exp(load * parts[7]))
    known = jnp.where(
        even,
        has[0, 0, -1].astype(jnp.float32),
        has[0, 0, 1].astype(jnp.float32),
    )
    gathered = plane
    for c in range(3):
        tile = shift(stress(e, change, trace, Z_SET[c]) * known, c * block)
        gathered = jnp.where((pair >= c * X) & (pair < (c + 1) * X), tile, gathered)
    joined = jnp.where(even, gathered, shift(gathered, -2))
    for c in range(3):
        for x in range(X):
            own = pl.ds(x * Y, Y)
            mv[c, own, :] = mv[c, own, :] + edge_term(joined, c * X + x, z_edge)

    @pl.when(jnp.logical_not(first_row))
    def _():
        arrive("xy")

    arrive("xs", "tx")
    for side, at in enumerate((0, X - 1)):
        @pl.when(has[faces[0][side]])
        def _(side=side, at=at):
            e = [rxs[side, k] for k in range(6)]
            add(e, 0, 1.0 - 2.0 * side, [uv[c, pl.ds(Y + at * Y, Y), :] for c in range(3)])
            add(e, 1, 1.0, [
                ends_of(rxy[side, 0, pl.ds(c, 1), :], rxy[side, 1, pl.ds(c, 1), :], row, Y) for c in range(3)
            ])
            facing = (X - 1) * (1 - side)
            joined = merge(rxz[side, 0], rxz[side, 1])
            add(e, 2, 2.0, [edge_term(joined, c * X + facing, z_edge) for c in range(3)])
            load = plane
            for d in depths:
                load = load + rtx[side, d - 1]
            trace, change = flow(e, rxs[side, 6] * jnp.exp(load * rxs[side, 7]))
            own = pl.ds(at * Y, Y)
            for c in range(3):
                mv[c, own, :] = mv[c, own, :] + (side - 0.5) * stress(e, change, trace, X_SET[c])

    pl.when(jnp.logical_not(first_row))(along_gy)
    settle(send_sem.at[0], 11 * Y, beside[0], some)
    settle(send_sem.at[1], 11 * X, beside[1], some)
    settle(send_sem.at[2], 3 * Y, beside[2], some)
    for i, kind in enumerate(("xy", "xz", "yz")):
        settle(send_sem.at[3 + i], *counts[kind])
    for i, (rows, count, values) in enumerate(totals.values()):
        settle(send_sem.at[6 + i], rows, count * below, values)


def finish(fv, mv, f_hbm, m_hbm, sem):
    copies = [
        pltpu.make_async_copy(mv, m_hbm, sem.at[0]),
        pltpu.make_async_copy(fv, f_hbm, sem.at[1]),
    ]
    for copy in copies:
        copy.start()
    for copy in copies:
        copy.wait()


def shards(sizes, u, e, t, r, b):
    X, Y, Z = t.shape
    N = X * Y
    layers = sizes[2]
    assert 8 * X <= Z and Z % 128 == 0 and Y % 8 == 0 and X % 8 == 0
    W = max(X, Y)
    f32 = jnp.float32
    vmem = pltpu.VMEM
    dma = pltpu.SemaphoreType.DMA
    any_space = pl.BlockSpec(memory_space=pl.ANY)
    in_vmem = pl.BlockSpec(memory_space=vmem)
    D = max(layers - 1, 1)
    kept = pl.pallas_call(
        functools.partial(kernel, (X, Y, Z), sizes),
        out_shape=(vmem((6, N, Z), f32), vmem((3, N, Z), f32)),
        in_specs=[any_space] * 5,
        out_specs=(in_vmem, in_vmem),
        scratch_shapes=[
            vmem((3, N + 2 * Y, Z), f32),
            vmem((6, N, Z), f32),
            vmem((N, Z), f32),
            vmem((N, Z), f32),
            vmem((N, Z), jnp.int32),
            vmem((N, Z), f32),
            vmem((N, Z), f32),
            vmem((6, N, Z), f32),
            vmem((N, Z), f32),
            vmem((N, Z), f32),
            vmem((6, N + 2 * Y, Z), f32),
            vmem((2, 8, Y, Z), f32),
            vmem((2, 8, X, Z), f32),
            vmem((2, 3, X, Z), f32),
            vmem((2, W, Z), f32),
            vmem((2, Y, Z), f32),
            vmem((2, 2, 8, Z), f32),
            vmem((Y, Z), f32),
            vmem((2, Y, Z), f32),
            vmem((2, X, Z), f32),
            vmem((2, 3, Y, Z), f32),
            vmem((2, 8, Y, Z), f32),
            vmem((2, 3, X, Z), f32),
            vmem((2, 8, X, Z), f32),
            vmem((2, Y, Z), f32),
            vmem((2, 2, Y, Z), f32),
            vmem((2, 2, 8, Z), f32),
            vmem((2, 2, Y, Z), f32),
            vmem((2, 2, 2, W, Z), f32),
            vmem((D, Y, Z), f32),
            vmem((2, D, Y, Z), f32),
            vmem((2, D, X, Z), f32),
            dma((4,)),
            pltpu.SemaphoreType.REGULAR((4,)),
            pltpu.SemaphoreType.REGULAR((1,)),
            dma((9,)),
            dma((12,)),
        ],
        compiler_params=pltpu.CompilerParams(collective_id=0, has_side_effects=True),
        name="strain_step",
    )(u.reshape(3, N, Z), e.reshape(6, N, Z), t.reshape(N, Z), r.reshape(N, Z), b.reshape(N, Z))
    f, m = pl.pallas_call(
        finish,
        out_shape=(jax.ShapeDtypeStruct((6, N, Z), f32), jax.ShapeDtypeStruct((3, N, Z), f32)),
        in_specs=[in_vmem] * 2,
        out_specs=(any_space, any_space),
        scratch_shapes=[dma((2,))],
        name="finish",
    )(*(pltpu.with_memory_space_constraint(k, vmem) for k in kept))
    return f.reshape(6, X, Y, Z), m.reshape(3, X, Y, Z)


def solution(mesh):
    sizes = tuple(mesh.shape[a] for a in AXES)
    field = P("gx", "gy", "gz")
    fields = P(None, "gx", "gy", "gz")
    return jax.shard_map(
        functools.partial(shards, sizes),
        mesh=mesh,
        in_specs=(fields, fields, field, field, field),
        out_specs=(fields, fields),
        check_vma=False,
    )
```

```python
import functools

import jax
import jax.numpy as jnp
from jax import lax
from jax.experimental import pallas as pl
from jax.experimental.pallas import tpu as pltpu
from jax.sharding import PartitionSpec as P

MESH = pl.DeviceIdType.MESH
AXES = ("gx", "gy", "gz")
TERMS = (
    ((0, 0.5), (3, 0.25), (4, 0.25)),
    ((3, 0.25), (1, 0.5), (5, 0.25)),
    ((4, 0.25), (5, 0.25), (2, 0.5)),
)
X_SET = (0, 3, 4)
Y_SET = (3, 1, 5)
Z_SET = (4, 5, 2)


def offsets(layers):
    near = [
        (x, y, z)
        for x in (-1, 0, 1)
        for y in (-1, 0, 1)
        for z in (-1, 0, 1)
        if 1 <= abs(x) + abs(y) + abs(z) <= 2
    ]
    far = [
        (x, y, s * d)
        for d in range(2, layers)
        for s in (-1, 1)
        for x, y in ((0, 0), (-1, 0), (1, 0), (0, -1), (0, 1))
    ]
    return near + far


def minus(o):
    return tuple(-v for v in o)


def plus(o, p):
    return tuple(v + w for v, w in zip(o, p))


def split(o):
    return tuple(min(v, 0) for v in o), tuple(max(v, 0) for v in o)


def kinds_of(layers):
    offs = offsets(layers)
    uppers = [o for o in offs if min(o) >= 0]
    lowers = [o for o in offs if max(o) <= 0]
    mixed = [o for o in offs if min(o) < 0 < max(o)]
    return uppers, lowers, mixed


def merge(low, high):
    Z = low.shape[1]
    even = (lax.broadcasted_iota(jnp.int32, low.shape, 1) & 1) == 0
    return jnp.where(even, low, pltpu.roll(high, Z - 2, 1))


def edge_term(tile, q, z_edge):
    Z = tile.shape[1]
    return (pltpu.roll(tile, (Z - 2 * q) % Z, 1) if q else tile) * z_edge


def flow(e, pace):
    trace = e[0] + e[1] + e[2]
    third = trace * (1.0 / 3.0)
    half = [e[0] - third, e[1] - third, e[2] - third, e[3], e[4], e[5]]
    second = half[0] * half[0] + half[1] * half[1] + half[2] * half[2]
    second = second + 2.0 * (half[3] * half[3] + half[4] * half[4] + half[5] * half[5])
    rate = pace * second
    return trace, [rate * h for h in half]


def stress(e, change, trace, part):
    out = 2.0 * (e[part] - change[part])
    return out + trace if part < 3 else out


def kernel(
    dims, sizes,
    u_hbm, u_rows, e_hbm, t_hbm, r_hbm, b_hbm,
    fv, mv,
    uv, ev, tv, rv, bv, pv, tot, el, av, nt, sp,
    xs, ys, yu, zu, zs, xy, zt, xt, yt,
    rxu, rxs, ryu, rys, rzu, rzs, rxy, rxz, ryz, rt, rtx, rty,
    in_sem, ready, told, send_sem, recv_sem,
):
    X, Y, Z = dims
    N = X * Y
    layers = sizes[2]
    depths = range(1, layers)
    me = [lax.axis_index(a) for a in AXES]
    offs = offsets(layers)
    uppers, lowers, mixed = kinds_of(layers)
    W = max(X, Y)

    def ready_index(o):
        return o.index(1) if sum(o) == 1 else 3

    def exists(o):
        ok = None
        for a in range(3):
            if o[a]:
                here = me[a] + o[a]
                test = here < sizes[a] if o[a] > 0 else here >= 0
                ok = test if ok is None else jnp.logical_and(ok, test)
        return ok

    def partner(o):
        return {AXES[a]: me[a] + o[a] for a in range(3) if o[a]}

    has = {o: exists(o) for o in offs}
    faces = {a: [tuple(s if i == a else 0 for i in range(3)) for s in (-1, 1)] for a in range(3)}

    loads = [
        pltpu.make_async_copy(src, dst, in_sem.at[min(i, 2) if i < 6 else 3])
        for i, (src, dst) in enumerate(
            (
                (u_hbm, uv.at[:, pl.ds(Y, N), :]),
                (r_hbm, rv),
                (e_hbm.at[:, pl.ds(0, Y), :], ev.at[:, pl.ds(0, Y), :]),
                (e_hbm.at[:, pl.ds(N - Y, Y), :], ev.at[:, pl.ds(N - Y, Y), :]),
                (t_hbm, tv),
                (b_hbm, bv),
                (e_hbm.at[:, pl.ds(Y, N - 2 * Y), :], ev.at[:, pl.ds(Y, N - 2 * Y), :]),
            )
        )
    ]
    for copy in loads:
        copy.start()

    def take(sem, rows):
        planes = next(k for k in range(1, 7) if rows % (8 * k) == 0 and rows // k <= N + 2 * Y)
        spot = sp.at[pl.ds(0, planes), pl.ds(0, rows // planes)]
        pltpu.make_async_copy(spot, spot, sem).wait()

    barrier = pltpu.get_barrier_semaphore()
    for o in uppers:
        @pl.when(has[o])
        def _(o=o):
            pl.semaphore_signal(barrier, inc=1, device_id=partner(o), device_id_type=MESH)
    expected = jnp.int32(0)
    for o in lowers:
        expected = expected + has[o].astype(jnp.int32)

    plane = jnp.zeros((Y, Z), jnp.float32)
    row_plane = jnp.zeros((X, Z), jnp.float32)
    for c in range(3):
        uv[c, pl.ds(0, Y), :] = plane
        uv[c, pl.ds(Y + N, Y), :] = plane
    for c in range(6):
        sp[c, pl.ds(0, Y), :] = plane
        sp[c, pl.ds(Y + N, Y), :] = plane

    def blank(o, *refs):
        @pl.when(jnp.logical_not(has[o]))
        def _():
            for ref in refs:
                ref[...] = jnp.zeros(ref.shape, jnp.float32)

    for i, sz in enumerate((-1, 1)):
        blank((0, 0, sz), rzu.at[i], rzs.at[i])
        for j, s in enumerate((-1, 1)):
            blank((s, 0, sz), rxz.at[j, i])
            blank((0, s, sz), ryz.at[j, i])
    for i, sx in enumerate((-1, 1)):
        for j, sy in enumerate((-1, 1)):
            blank((sx, sy, 0), rxy.at[i, j])
    for d in depths:
        blank((0, 0, -d), rt.at[d - 1])
        for j, s in enumerate((-1, 1)):
            blank((s, 0, -d), rtx.at[j, d - 1])
            blank((0, s, -d), rty.at[j, d - 1])

    lane = lax.broadcasted_iota(jnp.int32, (Y, Z), 1)
    row = lax.broadcasted_iota(jnp.int32, (Y, Z), 0)
    pair = lane >> 1
    even = (lane & 1) == 0
    not_last = jnp.where(row < Y - 1, 0.5, 0.0).astype(jnp.float32)
    not_first = jnp.where(row > 0, 0.5, 0.0).astype(jnp.float32)
    z_first = jnp.where(lane > 0, 0.5, 0.0).astype(jnp.float32)
    z_last = jnp.where(lane < Z - 1, 0.5, 0.0).astype(jnp.float32)
    z_edge = jnp.where(lane == 0, -0.5, jnp.where(lane == Z - 1, 0.5, 0.0)).astype(jnp.float32)
    if X == Y:
        row_x, z_edge_x = row, z_edge
    else:
        lane_x = lax.broadcasted_iota(jnp.int32, (X, Z), 1)
        row_x = lax.broadcasted_iota(jnp.int32, (X, Z), 0)
        z_edge_x = jnp.where(lane_x == 0, -0.5, jnp.where(lane_x == Z - 1, 0.5, 0.0)).astype(jnp.float32)

    beside = [sum(has[o].astype(jnp.int32) for o in faces[a]) for a in range(3)]
    above, below = me[2], layers - 1 - me[2]

    def products(*ranges):
        values = {1}
        for r in ranges:
            values = {v * w for v in values for w in r}
        return sorted(values - {0})

    some, any_depth = (1, 2), range(layers)
    four = products(some, some)
    arrivals = {
        "xu": (3 * Y, beside[0], some),
        "xs": (Y, beside[0] * (8 + above), products(some, [8 + d for d in any_depth])),
        "yu": (3 * X, beside[1], some),
        "ys": (X, beside[1] * (8 + above), products(some, [8 + d for d in any_depth])),
        "zu": (Y, beside[2] + above, sorted({n + d for n in some for d in any_depth})),
        "zs": (2 * Y, beside[2], some),
        "xy": (8, beside[0] * beside[1], four),
        "xz": (3 * Y, beside[0] * beside[2], four),
        "yz": (2 * W, beside[1] * beside[2], four),
    }
    departures = (
        (Y, beside[0] * (11 + below), products(some, [11 + d for d in any_depth])),
        (X, beside[1] * (11 + below), products(some, [11 + d for d in any_depth])),
        (Y, 3 * beside[2] + below, sorted({3 * n + d for n in some for d in any_depth})),
        arrivals["xy"], arrivals["xz"], arrivals["yz"],
    )
    recv_index = {kind: i for i, kind in enumerate(arrivals)}
    recv_index |= {"tx": recv_index["xs"], "ty": recv_index["ys"], "t": recv_index["zu"]}
    send_index = {
        "xu": 0, "xs": 0, "tx": 0, "yu": 1, "ys": 1, "ty": 1, "zu": 2, "zs": 2, "t": 2, "xy": 3, "xz": 4, "yz": 5,
    }
    sends = {o: [] for o in offs}

    def message(kind, o, src, dst):
        sends[o].append((kind, pltpu.make_async_remote_copy(
            src_ref=src, dst_ref=dst,
            send_sem=send_sem.at[send_index[kind]], recv_sem=recv_sem.at[recv_index[kind]],
            device_id=partner(o), device_id_type=MESH,
        )))

    for i, s in enumerate((-1, 1)):
        k = 1 - i
        at = (Y, Y * X)[i]
        strike = u_hbm.at[:, pl.ds((0, N - Y)[i], Y), :] if s < 0 else uv.at[:, pl.ds(at, Y), :]
        message("xu", (s, 0, 0), strike, rxu.at[k])
        message("xs", (s, 0, 0), xs.at[i], rxs.at[k])
        message("yu", (0, s, 0), u_rows.at[:, :, 0, :] if s < 0 else yu, ryu.at[k])
        message("ys", (0, s, 0), ys.at[i], rys.at[k])
        message("zu", (0, 0, s), zu.at[0, pl.ds(0, Y)], rzu.at[k])
        message("zs", (0, 0, s), zs, rzs.at[k])
        for j, s2 in enumerate((-1, 1)):
            m = 1 - j
            message("xy", (s, s2, 0), xy.at[i, j], rxy.at[k, m])
            strike = u_hbm.at[:, pl.ds(0, Y), :] if s + s2 < 0 else uv.at[:, pl.ds(at, Y), :]
            message("xz", (s, 0, s2), strike, rxz.at[k, m])
            message("yz", (0, s, s2), zu, ryz.at[k, m])
        for d in depths:
            message("tx", (s, 0, d), xt.at[i], rtx.at[k, d - 1])
            message("ty", (0, s, d), yt.at[i], rty.at[k, d - 1])
    for d in depths:
        message("t", (0, 0, d), zt, rt.at[d - 1])

    def settle(sem, rows, count, values):
        for n in values:
            @pl.when(count == n)
            def _(n=n):
                take(sem, n * rows)

    def start(offsets_in, kinds):
        for o in offsets_in:
            chosen = [copy for kind, copy in sends[o] if kind in kinds]
            if chosen:
                @pl.when(has[o])
                def _(chosen=chosen):
                    for copy in chosen:
                        copy.start()

    def arrive(*kinds):
        for kind in kinds:
            settle(recv_sem.at[recv_index[kind]], *arrivals[kind])

    @pl.when(expected > 0)
    def _():
        pl.semaphore_wait(barrier, expected)

    for o in lowers:
        @pl.when(has[o])
        def _(o=o):
            pl.semaphore_signal(
                ready.at[ready_index(minus(o))], inc=1, device_id=partner(o), device_id_type=MESH
            )

    def announce(o):
        low, high = split(o)

        @pl.when(jnp.logical_and(has[minus(low)], has[high]))
        def _():
            kind = 0 if max(high) == 1 and min(low) == -1 else 1
            pl.semaphore_signal(told.at[kind], inc=1, device_id=partner(minus(low)), device_id_type=MESH)

    lowers = sorted(lowers, key=lambda o: (sum(map(abs, o)), o[2], o[1]))
    for kind in ("xz", "yu", "xu"):
        start(lowers, (kind,))

    loads[0].wait()
    tile0 = plane
    for x in range(X):
        for c in range(3):
            q = c * X + x
            tile = pltpu.roll(uv[c, pl.ds(Y + x * Y, Y), :], (2 * q + 1) % Z, 1)
            tile0 = jnp.where(pair == q, tile, tile0)
    zu[0, pl.ds(0, Y), :] = tile0
    start(lowers, ("zu",))
    tile = row_plane
    pair_x = lax.broadcasted_iota(jnp.int32, (X, Z), 1) >> 1
    for i, line in enumerate((0, Y - 1)):
        for c in range(3):
            p = 3 * i + c
            lines = uv[c, pl.ds(Y + line, X, stride=Y), :]
            if i:
                yu[c] = lines
            tile = jnp.where(pair_x == p, pltpu.roll(lines, (2 * p + 1) % Z, 1), tile)
            for j, at in enumerate((0, X - 1)):
                xy[j, i, pl.ds(c, 1), :] = uv[c, pl.ds(Y + at * Y + line, 1), :]
    zu[1, pl.ds(0, X), :] = tile

    start(lowers, ("xy", "yz"))

    loads[1].wait()
    total_depth = Z * layers
    depth = (me[2] * Z + lane).astype(jnp.float32)
    scale = (1.0 + 2.0 * depth / total_depth) / total_depth
    thirds = [[], [], []]
    for x in range(X):
        rest = rv[pl.ds(x * Y, Y), :] * scale
        for k in range(3):
            piece = rest.astype(jnp.bfloat16)
            thirds[k].append(piece)
            rest = rest - piece.astype(jnp.float32)
    weight = jnp.concatenate([jnp.concatenate(k, axis=0) for k in thirds], axis=1)
    above_row = lax.broadcasted_iota(jnp.int32, (Z, 2 * Z), 0)
    column = lax.broadcasted_iota(jnp.int32, (Z, 2 * Z), 1)
    triangle = jnp.where(
        (above_row < column) | (column >= Z),
        1.0,
        jnp.where(above_row == column, 0.5, 0.0),
    ).astype(jnp.bfloat16)
    triangle = jnp.concatenate([triangle] * 3, axis=0)
    sums = jnp.dot(weight, triangle, preferred_element_type=jnp.float32)
    pv[...] = sums[:, :Z] + 1.0
    tot[...] = sums[:, Z:]
    tile = plane
    for x in range(X):
        tile = jnp.where(pair == x, tot[pl.ds(x * Y, Y), :], tile)
    zt[...] = tile
    for i, (at, line) in enumerate(((0, 0), (X - 1, Y - 1))):
        xt[i] = tot[pl.ds(at * Y, Y), :]
        yt[i] = tot[pl.ds(line, X, stride=Y), :]

    tiles = [plane, plane]

    def strain(x):
        base = Y + x * Y
        own = pl.ds(x * Y, Y)
        grad = []
        for c in range(3):
            here = uv[c, pl.ds(base, Y), :]
            grad.append((
                (uv[c, pl.ds(base + Y, Y), :] - uv[c, pl.ds(base - Y, Y), :]) * 0.5,
                uv[c, pl.ds(base + 1, Y), :] * not_last - uv[c, pl.ds(base - 1, Y), :] * not_first,
                pltpu.roll(here, Z - 1, 1) * z_last - pltpu.roll(here, 1, 1) * z_first,
            ))
        el[0, own, :] = grad[0][0]
        el[1, own, :] = grad[1][1]
        el[2, own, :] = grad[2][2]
        el[3, own, :] = 0.5 * (grad[0][1] + grad[1][0])
        el[4, own, :] = 0.5 * (grad[0][2] + grad[2][0])
        el[5, own, :] = 0.5 * (grad[1][2] + grad[2][1])

    def pack(k, x, part, tiles):
        q = (k % 4) * X + x
        tile = pltpu.roll(part, (2 * q + 1) % Z, 1)
        tiles[k // 4] = jnp.where(pair == q, tile, tiles[k // 4])

    def factors(x, tiles):
        own = pl.ds(x * Y, Y)
        minus_two = -2.0 / tv[own, :]
        factor = (2.0 + 14.0 * bv[own, :].astype(jnp.float32)) * jnp.exp(pv[own, :] * minus_two)
        av[own, :] = factor
        nt[own, :] = minus_two
        for i, at in enumerate((0, X - 1)):
            if x == at:
                xs[i, 6] = factor
                xs[i, 7] = minus_two
        pack(6, x, factor, tiles)
        pack(7, x, minus_two, tiles)

    def elastic(x, tiles):
        own = pl.ds(x * Y, Y)
        for k in range(6):
            part = el[k, own, :] - ev[k, own, :]
            el[k, own, :] = part
            for i, at in enumerate((0, X - 1)):
                if x == at:
                    xs[i, k] = part
            pack(k, x, part, tiles)

    ends = sorted({0, X - 1})
    for x in ends:
        strain(x)
    take(in_sem.at[2], 12 * Y + 2 * N)
    for x in ends:
        elastic(x, tiles)
        factors(x, tiles)
    start(lowers, ("xs", "t", "tx", "ty"))

    inner = [x for x in range(X) if x not in ends]
    for x in inner:
        strain(x)
        factors(x, tiles)
    loads[6].wait()
    for x in inner:
        elastic(x, tiles)
    for i, line in enumerate((0, Y - 1)):
        for k in range(8):
            src = el.at[k] if k < 6 else (av, nt)[k - 6]
            ys[i, k] = src[pl.ds(line, X, stride=Y), :]
    start(lowers, ("ys",))
    for k in range(2):
        zs[k] = tiles[k]
    start(lowers, ("zs",))

    everything = ("zu", "yu", "xu", "t", "zs", "ys", "xs", "tx", "ty", "xy", "xz", "yz")
    near = [o for o in uppers if sum(o) == 1]
    for o in sorted(near):
        @pl.when(has[o])
        def _(o=o):
            pl.semaphore_wait(ready.at[ready_index(o)], 1)

    for o in mixed:
        low, high = split(o)
        if high in near and minus(low) in near:
            announce(o)
    start(sorted(near), everything)
    others = [o for o in uppers if o not in near]
    far = [o for o in mixed if split(o)[1] not in near or minus(split(o)[0]) not in near]
    close = [o for o in mixed if o not in far]

    def hear(offsets_in, sem):
        number = sum(has[o].astype(jnp.int32) for o in offsets_in)

        @pl.when(number > 0)
        def _():
            pl.semaphore_wait(sem, number)

        start(offsets_in, everything)

    hear(close, told.at[0])
    hear(others, ready.at[3])
    for o in far:
        announce(o)
    if far:
        hear(far, told.at[1])

    arrive("yu")
    for side, line in enumerate((0, Y - 1)):
        sign = 2.0 * side - 1.0

        @pl.when(has[faces[1][side]])
        def _(side=side, sign=sign, line=line):
            own = pl.ds(line, X, stride=Y)
            for c, (part, factor) in enumerate(TERMS[1]):
                el[part, own, :] = el[part, own, :] + (sign * factor) * ryu[side, c]

    arrive("zu")
    carried = plane
    for d in depths:
        carried = carried + rt[d - 1]
    merged = merge(rzu[0], rzu[1])

    def advance(x):
        own = pl.ds(x * Y, Y)
        e = [el[c, own, :] for c in range(6)]
        for c, (part, factor) in enumerate(TERMS[2]):
            e[part] = e[part] + (2.0 * factor) * edge_term(merged, c * X + x, z_edge)
        load = jnp.broadcast_to(carried[:, 2 * x:2 * x + 1], (Y, Z))
        trace, change = flow(e, av[own, :] * jnp.exp(load * nt[own, :]))
        for c in range(6):
            fv[c, own, :] = ev[c, own, :] + change[c]
            sp[c, pl.ds(Y + x * Y, Y), :] = stress(e, change, trace, c)

    for x in range(X):
        if x not in ends:
            advance(x)
    arrive("xu")
    for side, at in enumerate((0, X - 1)):
        sign = 2.0 * side - 1.0

        @pl.when(has[faces[0][side]])
        def _(side=side, sign=sign, at=at):
            own = pl.ds(at * Y, Y)
            for c, (part, factor) in enumerate(TERMS[0]):
                el[part, own, :] = el[part, own, :] + (sign * factor) * rxu[side, c]

    for x in ends:
        advance(x)

    for x in range(X):
        base = Y + x * Y
        own = pl.ds(x * Y, Y)
        for c in range(3):
            cx, cy, cz = X_SET[c], Y_SET[c], Z_SET[c]
            here = sp[cz, pl.ds(base, Y), :]
            total = (sp[cx, pl.ds(base + Y, Y), :] - sp[cx, pl.ds(base - Y, Y), :]) * 0.5
            total = total + (
                sp[cy, pl.ds(base + 1, Y), :] * not_last - sp[cy, pl.ds(base - 1, Y), :] * not_first
            )
            total = total + (pltpu.roll(here, Z - 1, 1) * z_last - pltpu.roll(here, 1, 1) * z_first)
            if c == 2:
                total = total - 0.5 * rv[own, :]
            mv[c, own, :] = total

    def add(e, axis, factor, values):
        for c, (part, f) in enumerate(TERMS[axis]):
            e[part] = e[part] + (factor * f) * values[c]

    def ends_of(first, last, rows, count):
        return jnp.where(rows == 0, -first, jnp.where(rows == count - 1, last, 0.0))

    def along_gy():
        arrive("ys")
        for side, line in enumerate((0, Y - 1)):
            @pl.when(has[faces[1][side]])
            def _(side=side, line=line):
                e = [rys[side, k] for k in range(6)]
                add(e, 1, 1.0 - 2.0 * side, [uv[c, pl.ds(Y + line, X, stride=Y), :] for c in range(3)])
                add(e, 0, 1.0, [
                    ends_of(rxy[0, side, pl.ds(c, 1), :], rxy[1, side, pl.ds(c, 1), :], row_x, X) for c in range(3)
                ])
                joined = merge(ryz[side, 0, 1, pl.ds(0, X), :], ryz[side, 1, 1, pl.ds(0, X), :])
                add(e, 2, 2.0, [edge_term(joined, 3 * (1 - side) + c, z_edge_x) for c in range(3)])
                load = row_plane
                for d in depths:
                    load = load + rty[side, d - 1]
                trace, change = flow(e, rys[side, 6] * jnp.exp(load * rys[side, 7]))
                own = pl.ds(line, X, stride=Y)
                for c in range(3):
                    mv[c, own, :] = mv[c, own, :] + (side - 0.5) * stress(e, change, trace, Y_SET[c])

    first_row = me[1] == 0

    @pl.when(first_row)
    def _():
        arrive("xy", "yz")
        along_gy()

    @pl.when(jnp.logical_not(first_row))
    def _():
        arrive("yz")

    arrive("zs", "xz")
    block = 2 * X

    def shift(tile, by):
        return pltpu.roll(tile, by % Z, 1) if by % Z else tile

    halo = [jnp.where(even, rzs[0, k], rzs[1, k]) for k in range(2)]
    parts = [shift(halo[k // 4], -(k % 4) * block) for k in range(8)]
    mine = zu[0, pl.ds(0, Y), :]
    from_z = jnp.where(even, shift(mine, -1), -shift(mine, 1))
    from_x = []
    for c in range(3):
        left, right = (jnp.where(lane == Z - 1, rxz[i, 0, c], rxz[i, 1, c]) for i in range(2))
        from_x.append(jnp.where(
            pair == 0, -shift(left, 1), jnp.where(pair == X - 1, shift(right, 2 * X - 1), 0.0)
        ))
    even_row = (lax.broadcasted_iota(jnp.int32, (1, Z), 1) & 1) == 0
    from_y = ends_of(
        jnp.where(even_row, ryz[0, 0, 0, pl.ds(Y - 1, 1), :], ryz[0, 1, 0, pl.ds(Y - 1, 1), :]),
        jnp.where(even_row, ryz[1, 0, 0, pl.ds(0, 1), :], ryz[1, 1, 0, pl.ds(0, 1), :]),
        row, Y,
    )
    e = list(parts[:6])
    add(e, 0, 1.0, from_x)
    for axis, tile in ((1, from_y), (2, from_z)):
        add(e, axis, 1.0, [shift(tile, -c * block) for c in range(3)])
    deeper = plane
    for d in depths:
        if d >= 2:
            deeper = deeper + rt[d - 1]
    load = jnp.where(even, deeper, carried + zt[...])
    trace, change = flow(e, parts[6] * jnp.exp(load * parts[7]))
    known = jnp.where(
        even,
        has[0, 0, -1].astype(jnp.float32),
        has[0, 0, 1].astype(jnp.float32),
    )
    gathered = plane
    for c in range(3):
        tile = shift(stress(e, change, trace, Z_SET[c]) * known, c * block)
        gathered = jnp.where((pair >= c * X) & (pair < (c + 1) * X), tile, gathered)
    joined = jnp.where(even, gathered, shift(gathered, -2))
    for c in range(3):
        for x in range(X):
            own = pl.ds(x * Y, Y)
            mv[c, own, :] = mv[c, own, :] + edge_term(joined, c * X + x, z_edge)

    @pl.when(jnp.logical_not(first_row))
    def _():
        arrive("xy")

    arrive("xs")
    for side, at in enumerate((0, X - 1)):
        @pl.when(has[faces[0][side]])
        def _(side=side, at=at):
            e = [rxs[side, k] for k in range(6)]
            add(e, 0, 1.0 - 2.0 * side, [uv[c, pl.ds(Y + at * Y, Y), :] for c in range(3)])
            add(e, 1, 1.0, [
                ends_of(rxy[side, 0, pl.ds(c, 1), :], rxy[side, 1, pl.ds(c, 1), :], row, Y) for c in range(3)
            ])
            add(e, 2, 1.0, [
                jnp.where(
                    lane == 0, -pltpu.roll(rxz[side, 0, c], 1, 1),
                    jnp.where(lane == Z - 1, pltpu.roll(rxz[side, 1, c], Z - 1, 1), 0.0),
                )
                for c in range(3)
            ])
            load = plane
            for d in depths:
                load = load + rtx[side, d - 1]
            trace, change = flow(e, rxs[side, 6] * jnp.exp(load * rxs[side, 7]))
            own = pl.ds(at * Y, Y)
            for c in range(3):
                mv[c, own, :] = mv[c, own, :] + (side - 0.5) * stress(e, change, trace, X_SET[c])

    pl.when(jnp.logical_not(first_row))(along_gy)
    for i, departure in enumerate(departures):
        settle(send_sem.at[i], *departure)


def finish(fv, mv, f_hbm, m_hbm, sem):
    copies = [
        pltpu.make_async_copy(mv, m_hbm, sem.at[0]),
        pltpu.make_async_copy(fv, f_hbm, sem.at[1]),
    ]
    for copy in copies:
        copy.start()
    for copy in copies:
        copy.wait()


def shards(sizes, u, e, t, r, b):
    X, Y, Z = t.shape
    N = X * Y
    layers = sizes[2]
    assert 8 * X <= Z and Z % 128 == 0 and Y % 8 == 0 and X % 8 == 0
    W = max(X, Y)
    f32 = jnp.float32
    vmem = pltpu.VMEM
    dma = pltpu.SemaphoreType.DMA
    any_space = pl.BlockSpec(memory_space=pl.ANY)
    in_vmem = pl.BlockSpec(memory_space=vmem)
    D = max(layers - 1, 1)
    kept = pl.pallas_call(
        functools.partial(kernel, (X, Y, Z), sizes),
        out_shape=(vmem((6, N, Z), f32), vmem((3, N, Z), f32)),
        in_specs=[any_space] * 6,
        out_specs=(in_vmem, in_vmem),
        scratch_shapes=[
            vmem((3, N + 2 * Y, Z), f32),
            vmem((6, N, Z), f32),
            vmem((N, Z), f32),
            vmem((N, Z), f32),
            vmem((N, Z), jnp.int32),
            vmem((N, Z), f32),
            vmem((N, Z), f32),
            vmem((6, N, Z), f32),
            vmem((N, Z), f32),
            vmem((N, Z), f32),
            vmem((6, N + 2 * Y, Z), f32),
            vmem((2, 8, Y, Z), f32),
            vmem((2, 8, X, Z), f32),
            vmem((3, X, Z), f32),
            vmem((2, W, Z), f32),
            vmem((2, Y, Z), f32),
            vmem((2, 2, 8, Z), f32),
            vmem((Y, Z), f32),
            vmem((2, Y, Z), f32),
            vmem((2, X, Z), f32),
            vmem((2, 3, Y, Z), f32),
            vmem((2, 8, Y, Z), f32),
            vmem((2, 3, X, Z), f32),
            vmem((2, 8, X, Z), f32),
            vmem((2, Y, Z), f32),
            vmem((2, 2, Y, Z), f32),
            vmem((2, 2, 8, Z), f32),
            vmem((2, 2, 3, Y, Z), f32),
            vmem((2, 2, 2, W, Z), f32),
            vmem((D, Y, Z), f32),
            vmem((2, D, Y, Z), f32),
            vmem((2, D, X, Z), f32),
            dma((4,)),
            pltpu.SemaphoreType.REGULAR((4,)),
            pltpu.SemaphoreType.REGULAR((1 if layers == 2 else 2,)),
            dma((6,)),
            dma((9,)),
        ],
        compiler_params=pltpu.CompilerParams(collective_id=0, has_side_effects=True),
        name="strain_step",
    )(u.reshape(3, N, Z), u, e.reshape(6, N, Z), t.reshape(N, Z), r.reshape(N, Z), b.reshape(N, Z))
    f, m = pl.pallas_call(
        finish,
        out_shape=(jax.ShapeDtypeStruct((6, N, Z), f32), jax.ShapeDtypeStruct((3, N, Z), f32)),
        in_specs=[in_vmem] * 2,
        out_specs=(any_space, any_space),
        scratch_shapes=[dma((2,))],
        name="finish",
    )(*(pltpu.with_memory_space_constraint(k, vmem) for k in kept))
    return f.reshape(6, X, Y, Z), m.reshape(3, X, Y, Z)


def solution(mesh):
    sizes = tuple(mesh.shape[a] for a in AXES)
    field = P("gx", "gy", "gz")
    fields = P(None, "gx", "gy", "gz")
    return jax.shard_map(
        functools.partial(shards, sizes),
        mesh=mesh,
        in_specs=(fields, fields, field, field, field),
        out_specs=(fields, fields),
        check_vma=False,
    )
```

```python
import functools

import jax
import jax.numpy as jnp
from jax import lax
from jax.experimental import pallas as pl
from jax.experimental.pallas import tpu as pltpu
from jax.sharding import PartitionSpec as P

MESH = pl.DeviceIdType.MESH
AXES = ("gx", "gy", "gz")
TERMS = (
    ((0, 0.5), (3, 0.25), (4, 0.25)),
    ((3, 0.25), (1, 0.5), (5, 0.25)),
    ((4, 0.25), (5, 0.25), (2, 0.5)),
)
X_SET = (0, 3, 4)
Y_SET = (3, 1, 5)
Z_SET = (4, 5, 2)


def offsets(layers):
    near = [
        (x, y, z)
        for x in (-1, 0, 1)
        for y in (-1, 0, 1)
        for z in (-1, 0, 1)
        if 1 <= abs(x) + abs(y) + abs(z) <= 2
    ]
    far = [
        (x, y, s * d)
        for d in range(2, layers)
        for s in (-1, 1)
        for x, y in ((0, 0), (-1, 0), (1, 0), (0, -1), (0, 1))
    ]
    return near + far


def minus(o):
    return tuple(-v for v in o)


def plus(o, p):
    return tuple(v + w for v, w in zip(o, p))


def split(o):
    return tuple(min(v, 0) for v in o), tuple(max(v, 0) for v in o)


def kinds_of(layers):
    offs = offsets(layers)
    uppers = [o for o in offs if min(o) >= 0]
    lowers = [o for o in offs if max(o) <= 0]
    mixed = [o for o in offs if min(o) < 0 < max(o)]
    return uppers, lowers, mixed


def merge(low, high):
    Z = low.shape[1]
    even = (lax.broadcasted_iota(jnp.int32, low.shape, 1) & 1) == 0
    return jnp.where(even, low, pltpu.roll(high, Z - 2, 1))


def edge_term(tile, q, z_edge):
    Z = tile.shape[1]
    return (pltpu.roll(tile, (Z - 2 * q) % Z, 1) if q else tile) * z_edge


def flow(e, pace):
    trace = e[0] + e[1] + e[2]
    third = trace * (1.0 / 3.0)
    half = [e[0] - third, e[1] - third, e[2] - third, e[3], e[4], e[5]]
    second = half[0] * half[0] + half[1] * half[1] + half[2] * half[2]
    second = second + 2.0 * (half[3] * half[3] + half[4] * half[4] + half[5] * half[5])
    rate = pace * second
    return trace, [rate * h for h in half]


def stress(e, change, trace, part):
    out = 2.0 * (e[part] - change[part])
    return out + trace if part < 3 else out


def kernel(
    dims, sizes,
    u_hbm, u_rows, e_hbm, t_hbm, r_hbm, b_hbm,
    fv, mv, jv,
    uv, ev, tv, rv, bv, pv, tot, el, av, nt, sp,
    xs, ys, yu, zu, zs, xy, zt, xt, yt,
    rxu, rxs, ryu, rys, rzu, rzs, rxy, rxz, ryz, rt, rtx, rty,
    in_sem, ready, told, send_sem, recv_sem,
):
    X, Y, Z = dims
    N = X * Y
    layers = sizes[2]
    depths = range(1, layers)
    me = [lax.axis_index(a) for a in AXES]
    offs = offsets(layers)
    uppers, lowers, mixed = kinds_of(layers)
    W = max(X, Y)

    def ready_index(o):
        return o.index(1) if sum(o) == 1 else 3

    def exists(o):
        ok = None
        for a in range(3):
            if o[a]:
                here = me[a] + o[a]
                test = here < sizes[a] if o[a] > 0 else here >= 0
                ok = test if ok is None else jnp.logical_and(ok, test)
        return ok

    def partner(o):
        return {AXES[a]: me[a] + o[a] for a in range(3) if o[a]}

    has = {o: exists(o) for o in offs}
    faces = {a: [tuple(s if i == a else 0 for i in range(3)) for s in (-1, 1)] for a in range(3)}

    loads = [
        pltpu.make_async_copy(src, dst, in_sem.at[min(i, 2) if i < 6 else 3])
        for i, (src, dst) in enumerate(
            (
                (u_hbm, uv.at[:, pl.ds(Y, N), :]),
                (r_hbm, rv),
                (e_hbm.at[:, pl.ds(0, Y), :], ev.at[:, pl.ds(0, Y), :]),
                (e_hbm.at[:, pl.ds(N - Y, Y), :], ev.at[:, pl.ds(N - Y, Y), :]),
                (t_hbm, tv),
                (b_hbm, bv),
                (e_hbm.at[:, pl.ds(Y, N - 2 * Y), :], ev.at[:, pl.ds(Y, N - 2 * Y), :]),
            )
        )
    ]
    for copy in loads:
        copy.start()

    def take(sem, rows):
        planes = next(k for k in range(1, 7) if rows % (8 * k) == 0 and rows // k <= N + 2 * Y)
        spot = sp.at[pl.ds(0, planes), pl.ds(0, rows // planes)]
        pltpu.make_async_copy(spot, spot, sem).wait()

    barrier = pltpu.get_barrier_semaphore()
    for o in uppers:
        @pl.when(has[o])
        def _(o=o):
            pl.semaphore_signal(barrier, inc=1, device_id=partner(o), device_id_type=MESH)
    expected = jnp.int32(0)
    for o in lowers:
        expected = expected + has[o].astype(jnp.int32)

    plane = jnp.zeros((Y, Z), jnp.float32)
    row_plane = jnp.zeros((X, Z), jnp.float32)
    for c in range(3):
        uv[c, pl.ds(0, Y), :] = plane
        uv[c, pl.ds(Y + N, Y), :] = plane
    for c in range(6):
        sp[c, pl.ds(0, Y), :] = plane
        sp[c, pl.ds(Y + N, Y), :] = plane

    def blank(o, *refs):
        @pl.when(jnp.logical_not(has[o]))
        def _():
            for ref in refs:
                ref[...] = jnp.zeros(ref.shape, jnp.float32)

    for i, sz in enumerate((-1, 1)):
        blank((0, 0, sz), rzu.at[i], rzs.at[i])
        for j, s in enumerate((-1, 1)):
            blank((s, 0, sz), rxz.at[j, i])
            blank((0, s, sz), ryz.at[j, i])
    for i, sx in enumerate((-1, 1)):
        for j, sy in enumerate((-1, 1)):
            blank((sx, sy, 0), rxy.at[i, j])
    for d in depths:
        blank((0, 0, -d), rt.at[d - 1])
        for j, s in enumerate((-1, 1)):
            blank((s, 0, -d), rtx.at[j, d - 1])
            blank((0, s, -d), rty.at[j, d - 1])

    lane = lax.broadcasted_iota(jnp.int32, (Y, Z), 1)
    row = lax.broadcasted_iota(jnp.int32, (Y, Z), 0)
    pair = lane >> 1
    even = (lane & 1) == 0
    not_last = jnp.where(row < Y - 1, 0.5, 0.0).astype(jnp.float32)
    not_first = jnp.where(row > 0, 0.5, 0.0).astype(jnp.float32)
    z_first = jnp.where(lane > 0, 0.5, 0.0).astype(jnp.float32)
    z_last = jnp.where(lane < Z - 1, 0.5, 0.0).astype(jnp.float32)
    z_edge = jnp.where(lane == 0, -0.5, jnp.where(lane == Z - 1, 0.5, 0.0)).astype(jnp.float32)
    if X == Y:
        row_x, z_edge_x = row, z_edge
    else:
        lane_x = lax.broadcasted_iota(jnp.int32, (X, Z), 1)
        row_x = lax.broadcasted_iota(jnp.int32, (X, Z), 0)
        z_edge_x = jnp.where(lane_x == 0, -0.5, jnp.where(lane_x == Z - 1, 0.5, 0.0)).astype(jnp.float32)

    beside = [sum(has[o].astype(jnp.int32) for o in faces[a]) for a in range(3)]
    above, below = me[2], layers - 1 - me[2]

    def products(*ranges):
        values = {1}
        for r in ranges:
            values = {v * w for v in values for w in r}
        return sorted(values - {0})

    some, any_depth = (1, 2), range(layers)
    four = products(some, some)
    arrivals = {
        "xu": (3 * Y, beside[0], some),
        "xs": (Y, beside[0] * (8 + above), products(some, [8 + d for d in any_depth])),
        "yu": (3 * X, beside[1], some),
        "ys": (X, beside[1] * (8 + above), products(some, [8 + d for d in any_depth])),
        "zu": (Y, beside[2] + above, sorted({n + d for n in some for d in any_depth})),
        "zs": (2 * Y, beside[2], some),
        "xy": (8, beside[0] * beside[1], four),
        "xz": (3 * Y, beside[0] * beside[2], four),
        "yz": (2 * W, beside[1] * beside[2], four),
    }
    departures = (
        (Y, beside[0] * (11 + below), products(some, [11 + d for d in any_depth])),
        (X, beside[1] * (11 + below), products(some, [11 + d for d in any_depth])),
        (Y, 3 * beside[2] + below, sorted({3 * n + d for n in some for d in any_depth})),
        arrivals["xy"], arrivals["xz"], arrivals["yz"],
    )
    recv_index = {kind: i for i, kind in enumerate(arrivals)}
    recv_index |= {"tx": recv_index["xs"], "ty": recv_index["ys"], "t": recv_index["zu"]}
    send_index = {
        "xu": 0, "xs": 0, "tx": 0, "yu": 1, "ys": 1, "ty": 1, "zu": 2, "zs": 2, "t": 2, "xy": 3, "xz": 4, "yz": 5,
    }
    sends = {o: [] for o in offs}

    def message(kind, o, src, dst):
        sends[o].append((kind, pltpu.make_async_remote_copy(
            src_ref=src, dst_ref=dst,
            send_sem=send_sem.at[send_index[kind]], recv_sem=recv_sem.at[recv_index[kind]],
            device_id=partner(o), device_id_type=MESH,
        )))

    for i, s in enumerate((-1, 1)):
        k = 1 - i
        at = (Y, Y * X)[i]
        strike = u_hbm.at[:, pl.ds((0, N - Y)[i], Y), :] if s < 0 else uv.at[:, pl.ds(at, Y), :]
        message("xu", (s, 0, 0), strike, rxu.at[k])
        message("xs", (s, 0, 0), xs.at[i], rxs.at[k])
        message("yu", (0, s, 0), u_rows.at[:, :, 0, :] if s < 0 else yu, ryu.at[k])
        message("ys", (0, s, 0), ys.at[i], rys.at[k])
        message("zu", (0, 0, s), zu.at[0, pl.ds(0, Y)], rzu.at[k])
        message("zs", (0, 0, s), zs, rzs.at[k])
        for j, s2 in enumerate((-1, 1)):
            m = 1 - j
            message("xy", (s, s2, 0), xy.at[i, j], rxy.at[k, m])
            strike = u_hbm.at[:, pl.ds(0, Y), :] if s + s2 < 0 else uv.at[:, pl.ds(at, Y), :]
            message("xz", (s, 0, s2), strike, rxz.at[k, m])
            message("yz", (0, s, s2), zu, ryz.at[k, m])
        for d in depths:
            message("tx", (s, 0, d), xt.at[i], rtx.at[k, d - 1])
            message("ty", (0, s, d), yt.at[i], rty.at[k, d - 1])
    for d in depths:
        message("t", (0, 0, d), zt, rt.at[d - 1])

    def settle(sem, rows, count, values):
        for n in values:
            @pl.when(count == n)
            def _(n=n):
                take(sem, n * rows)

    def start(offsets_in, kinds):
        for o in offsets_in:
            chosen = [copy for kind, copy in sends[o] if kind in kinds]
            if chosen:
                @pl.when(has[o])
                def _(chosen=chosen):
                    for copy in chosen:
                        copy.start()

    def arrive(*kinds):
        for kind in kinds:
            settle(recv_sem.at[recv_index[kind]], *arrivals[kind])

    @pl.when(expected > 0)
    def _():
        pl.semaphore_wait(barrier, expected)

    for o in lowers:
        @pl.when(has[o])
        def _(o=o):
            pl.semaphore_signal(
                ready.at[ready_index(minus(o))], inc=1, device_id=partner(o), device_id_type=MESH
            )

    def announce(o):
        low, high = split(o)

        @pl.when(jnp.logical_and(has[minus(low)], has[high]))
        def _():
            kind = 0 if max(high) == 1 and min(low) == -1 else 1
            pl.semaphore_signal(told.at[kind], inc=1, device_id=partner(minus(low)), device_id_type=MESH)

    lowers = sorted(lowers, key=lambda o: (sum(map(abs, o)), o[2], o[1]))
    for kind in ("xz", "yu", "xu"):
        start(lowers, (kind,))

    loads[0].wait()
    tile0 = plane
    for x in range(X):
        for c in range(3):
            q = c * X + x
            tile = pltpu.roll(uv[c, pl.ds(Y + x * Y, Y), :], (2 * q + 1) % Z, 1)
            tile0 = jnp.where(pair == q, tile, tile0)
    zu[0, pl.ds(0, Y), :] = tile0
    start(lowers, ("zu",))
    tile = row_plane
    pair_x = lax.broadcasted_iota(jnp.int32, (X, Z), 1) >> 1
    for i, line in enumerate((0, Y - 1)):
        for c in range(3):
            p = 3 * i + c
            lines = uv[c, pl.ds(Y + line, X, stride=Y), :]
            if i:
                yu[c] = lines
            tile = jnp.where(pair_x == p, pltpu.roll(lines, (2 * p + 1) % Z, 1), tile)
            for j, at in enumerate((0, X - 1)):
                xy[j, i, pl.ds(c, 1), :] = uv[c, pl.ds(Y + at * Y + line, 1), :]
    zu[1, pl.ds(0, X), :] = tile

    start(lowers, ("xy", "yz"))

    loads[1].wait()
    total_depth = Z * layers
    depth = (me[2] * Z + lane).astype(jnp.float32)
    scale = (1.0 + 2.0 * depth / total_depth) / total_depth
    thirds = [[], [], []]
    for x in range(X):
        rest = rv[pl.ds(x * Y, Y), :] * scale
        for k in range(3):
            piece = rest.astype(jnp.bfloat16)
            thirds[k].append(piece)
            rest = rest - piece.astype(jnp.float32)
    weight = jnp.concatenate([jnp.concatenate(k, axis=0) for k in thirds], axis=1)
    above_row = lax.broadcasted_iota(jnp.int32, (Z, 2 * Z), 0)
    column = lax.broadcasted_iota(jnp.int32, (Z, 2 * Z), 1)
    triangle = jnp.where(
        (above_row < column) | (column >= Z),
        1.0,
        jnp.where(above_row == column, 0.5, 0.0),
    ).astype(jnp.bfloat16)
    triangle = jnp.concatenate([triangle] * 3, axis=0)
    sums = jnp.dot(weight, triangle, preferred_element_type=jnp.float32)
    pv[...] = sums[:, :Z] + 1.0
    tot[...] = sums[:, Z:]
    tile = plane
    for x in range(X):
        tile = jnp.where(pair == x, tot[pl.ds(x * Y, Y), :], tile)
    zt[...] = tile
    for i, (at, line) in enumerate(((0, 0), (X - 1, Y - 1))):
        xt[i] = tot[pl.ds(at * Y, Y), :]
        yt[i] = tot[pl.ds(line, X, stride=Y), :]

    tiles = [plane, plane]

    def strain(x):
        base = Y + x * Y
        own = pl.ds(x * Y, Y)
        grad = []
        for c in range(3):
            here = uv[c, pl.ds(base, Y), :]
            grad.append((
                (uv[c, pl.ds(base + Y, Y), :] - uv[c, pl.ds(base - Y, Y), :]) * 0.5,
                uv[c, pl.ds(base + 1, Y), :] * not_last - uv[c, pl.ds(base - 1, Y), :] * not_first,
                pltpu.roll(here, Z - 1, 1) * z_last - pltpu.roll(here, 1, 1) * z_first,
            ))
        el[0, own, :] = grad[0][0]
        el[1, own, :] = grad[1][1]
        el[2, own, :] = grad[2][2]
        el[3, own, :] = 0.5 * (grad[0][1] + grad[1][0])
        el[4, own, :] = 0.5 * (grad[0][2] + grad[2][0])
        el[5, own, :] = 0.5 * (grad[1][2] + grad[2][1])

    def pack(k, x, part, tiles):
        q = (k % 4) * X + x
        tile = pltpu.roll(part, (2 * q + 1) % Z, 1)
        tiles[k // 4] = jnp.where(pair == q, tile, tiles[k // 4])

    def factors(x, tiles):
        own = pl.ds(x * Y, Y)
        minus_two = -2.0 / tv[own, :]
        factor = (2.0 + 14.0 * bv[own, :].astype(jnp.float32)) * jnp.exp(pv[own, :] * minus_two)
        av[own, :] = factor
        nt[own, :] = minus_two
        for i, at in enumerate((0, X - 1)):
            if x == at:
                xs[i, 6] = factor
                xs[i, 7] = minus_two
        pack(6, x, factor, tiles)
        pack(7, x, minus_two, tiles)

    def elastic(x, tiles):
        own = pl.ds(x * Y, Y)
        for k in range(6):
            part = el[k, own, :] - ev[k, own, :]
            el[k, own, :] = part
            for i, at in enumerate((0, X - 1)):
                if x == at:
                    xs[i, k] = part
            pack(k, x, part, tiles)

    ends = sorted({0, X - 1})
    for x in ends:
        strain(x)
    take(in_sem.at[2], 12 * Y + 2 * N)
    for x in ends:
        elastic(x, tiles)
        factors(x, tiles)
    start(lowers, ("xs", "t", "tx", "ty"))

    inner = [x for x in range(X) if x not in ends]
    for x in inner:
        strain(x)
        factors(x, tiles)
    loads[6].wait()
    for x in inner:
        elastic(x, tiles)
    for k in range(2):
        zs[k] = tiles[k]
    start(lowers, ("zs",))
    for i, line in enumerate((0, Y - 1)):
        for k in range(8):
            src = el.at[k] if k < 6 else (av, nt)[k - 6]
            ys[i, k] = src[pl.ds(line, X, stride=Y), :]
    start(lowers, ("ys",))

    near = [o for o in uppers if sum(o) == 1]
    for o in sorted(near):
        @pl.when(has[o])
        def _(o=o):
            pl.semaphore_wait(ready.at[ready_index(o)], 1)

    for o in mixed:
        low, high = split(o)
        if high in near and minus(low) in near:
            announce(o)
    near.sort()
    start(near, ("zu", "yu", "xu", "t", "zs"))
    others = [o for o in uppers if o not in near]
    far = [o for o in mixed if split(o)[1] not in near or minus(split(o)[0]) not in near]
    close = [o for o in mixed if o not in far]

    diagonal = ("xy", "xz", "yz", "t", "tx", "ty")

    def hear(offsets_in, sem):
        number = sum(has[o].astype(jnp.int32) for o in offsets_in)

        @pl.when(number > 0)
        def _():
            pl.semaphore_wait(sem, number)

        start(offsets_in, diagonal)

    hear(close, told.at[0])
    start(near, ("ys", "xs"))
    hear(others, ready.at[3])
    for o in far:
        announce(o)
    if far:
        hear(far, told.at[1])

    arrive("yu")
    for side, line in enumerate((0, Y - 1)):
        sign = 2.0 * side - 1.0

        @pl.when(has[faces[1][side]])
        def _(side=side, sign=sign, line=line):
            own = pl.ds(line, X, stride=Y)
            for c, (part, factor) in enumerate(TERMS[1]):
                el[part, own, :] = el[part, own, :] + (sign * factor) * ryu[side, c]

    arrive("zu")
    carried = plane
    for d in depths:
        carried = carried + rt[d - 1]
    merged = merge(rzu[0], rzu[1])

    def advance(x):
        own = pl.ds(x * Y, Y)
        e = [el[c, own, :] for c in range(6)]
        for c, (part, factor) in enumerate(TERMS[2]):
            e[part] = e[part] + (2.0 * factor) * edge_term(merged, c * X + x, z_edge)
        load = jnp.broadcast_to(carried[:, 2 * x:2 * x + 1], (Y, Z))
        trace, change = flow(e, av[own, :] * jnp.exp(load * nt[own, :]))
        for c in range(6):
            fv[c, own, :] = ev[c, own, :] + change[c]
            sp[c, pl.ds(Y + x * Y, Y), :] = stress(e, change, trace, c)

    for x in range(X):
        if x not in ends:
            advance(x)
    arrive("xu")
    for side, at in enumerate((0, X - 1)):
        sign = 2.0 * side - 1.0

        @pl.when(has[faces[0][side]])
        def _(side=side, sign=sign, at=at):
            own = pl.ds(at * Y, Y)
            for c, (part, factor) in enumerate(TERMS[0]):
                el[part, own, :] = el[part, own, :] + (sign * factor) * rxu[side, c]

    for x in ends:
        advance(x)

    for x in range(X):
        base = Y + x * Y
        own = pl.ds(x * Y, Y)
        for c in range(3):
            cx, cy, cz = X_SET[c], Y_SET[c], Z_SET[c]
            here = sp[cz, pl.ds(base, Y), :]
            total = (sp[cx, pl.ds(base + Y, Y), :] - sp[cx, pl.ds(base - Y, Y), :]) * 0.5
            total = total + (
                sp[cy, pl.ds(base + 1, Y), :] * not_last - sp[cy, pl.ds(base - 1, Y), :] * not_first
            )
            total = total + (pltpu.roll(here, Z - 1, 1) * z_last - pltpu.roll(here, 1, 1) * z_first)
            if c == 2:
                total = total - 0.5 * rv[own, :]
            mv[c, own, :] = total

    def add(e, axis, factor, values):
        for c, (part, f) in enumerate(TERMS[axis]):
            e[part] = e[part] + (factor * f) * values[c]

    def ends_of(first, last, rows, count):
        return jnp.where(rows == 0, -first, jnp.where(rows == count - 1, last, 0.0))

    def along_gy():
        arrive("ys")
        for side, line in enumerate((0, Y - 1)):
            @pl.when(has[faces[1][side]])
            def _(side=side, line=line):
                e = [rys[side, k] for k in range(6)]
                add(e, 1, 1.0 - 2.0 * side, [uv[c, pl.ds(Y + line, X, stride=Y), :] for c in range(3)])
                add(e, 0, 1.0, [
                    ends_of(rxy[0, side, pl.ds(c, 1), :], rxy[1, side, pl.ds(c, 1), :], row_x, X) for c in range(3)
                ])
                joined = merge(ryz[side, 0, 1, pl.ds(0, X), :], ryz[side, 1, 1, pl.ds(0, X), :])
                add(e, 2, 2.0, [edge_term(joined, 3 * (1 - side) + c, z_edge_x) for c in range(3)])
                load = row_plane
                for d in depths:
                    load = load + rty[side, d - 1]
                trace, change = flow(e, rys[side, 6] * jnp.exp(load * rys[side, 7]))
                own = pl.ds(line, X, stride=Y)
                for c in range(3):
                    mv[c, own, :] = mv[c, own, :] + (side - 0.5) * stress(e, change, trace, Y_SET[c])

    first_row = me[1] == 0

    @pl.when(first_row)
    def _():
        arrive("xy", "yz")
        along_gy()

    @pl.when(jnp.logical_not(first_row))
    def _():
        arrive("yz")

    arrive("zs", "xz")
    block = 2 * X

    def shift(tile, by):
        return pltpu.roll(tile, by % Z, 1) if by % Z else tile

    halo = [jnp.where(even, rzs[0, k], rzs[1, k]) for k in range(2)]
    parts = [shift(halo[k // 4], -(k % 4) * block) for k in range(8)]
    mine = zu[0, pl.ds(0, Y), :]
    from_z = jnp.where(even, shift(mine, -1), -shift(mine, 1))
    from_x = []
    for c in range(3):
        left, right = (jnp.where(lane == Z - 1, rxz[i, 0, c], rxz[i, 1, c]) for i in range(2))
        from_x.append(jnp.where(
            pair == 0, -shift(left, 1), jnp.where(pair == X - 1, shift(right, 2 * X - 1), 0.0)
        ))
    even_row = (lax.broadcasted_iota(jnp.int32, (1, Z), 1) & 1) == 0
    from_y = ends_of(
        jnp.where(even_row, ryz[0, 0, 0, pl.ds(Y - 1, 1), :], ryz[0, 1, 0, pl.ds(Y - 1, 1), :]),
        jnp.where(even_row, ryz[1, 0, 0, pl.ds(0, 1), :], ryz[1, 1, 0, pl.ds(0, 1), :]),
        row, Y,
    )
    e = list(parts[:6])
    add(e, 0, 1.0, from_x)
    for axis, tile in ((1, from_y), (2, from_z)):
        add(e, axis, 1.0, [shift(tile, -c * block) for c in range(3)])
    deeper = plane
    for d in depths:
        if d >= 2:
            deeper = deeper + rt[d - 1]
    load = jnp.where(even, deeper, carried + zt[...])
    trace, change = flow(e, parts[6] * jnp.exp(load * parts[7]))
    known = jnp.where(
        even,
        has[0, 0, -1].astype(jnp.float32),
        has[0, 0, 1].astype(jnp.float32),
    )
    gathered = plane
    for c in range(3):
        tile = shift(stress(e, change, trace, Z_SET[c]) * known, c * block)
        gathered = jnp.where((pair >= c * X) & (pair < (c + 1) * X), tile, gathered)
    jv[...] = jnp.where(even, gathered, shift(gathered, -2))

    @pl.when(jnp.logical_not(first_row))
    def _():
        arrive("xy")

    arrive("xs")
    for side, at in enumerate((0, X - 1)):
        @pl.when(has[faces[0][side]])
        def _(side=side, at=at):
            e = [rxs[side, k] for k in range(6)]
            add(e, 0, 1.0 - 2.0 * side, [uv[c, pl.ds(Y + at * Y, Y), :] for c in range(3)])
            add(e, 1, 1.0, [
                ends_of(rxy[side, 0, pl.ds(c, 1), :], rxy[side, 1, pl.ds(c, 1), :], row, Y) for c in range(3)
            ])
            add(e, 2, 1.0, [
                jnp.where(
                    lane == 0, -pltpu.roll(rxz[side, 0, c], 1, 1),
                    jnp.where(lane == Z - 1, pltpu.roll(rxz[side, 1, c], Z - 1, 1), 0.0),
                )
                for c in range(3)
            ])
            load = plane
            for d in depths:
                load = load + rtx[side, d - 1]
            trace, change = flow(e, rxs[side, 6] * jnp.exp(load * rxs[side, 7]))
            own = pl.ds(at * Y, Y)
            for c in range(3):
                mv[c, own, :] = mv[c, own, :] + (side - 0.5) * stress(e, change, trace, X_SET[c])

    pl.when(jnp.logical_not(first_row))(along_gy)
    for i, departure in enumerate(departures):
        settle(send_sem.at[i], *departure)


def finish(dims, fv, mv, jv, f_hbm, m_hbm, ms, sem):
    X, Y, Z = dims
    copies = [pltpu.make_async_copy(fv, f_hbm, sem.at[0])]
    copies[0].start()
    lane = lax.broadcasted_iota(jnp.int32, (Y, Z), 1)
    z_edge = jnp.where(lane == 0, -0.5, jnp.where(lane == Z - 1, 0.5, 0.0)).astype(jnp.float32)
    joined = jv[...]
    groups = 4
    span = X // groups
    for g in range(groups):
        for x in range(g * span, (g + 1) * span):
            own = pl.ds(x * Y, Y)
            for c in range(3):
                ms[c, own, :] = mv[c, own, :] + edge_term(joined, c * X + x, z_edge)
        rows = pl.ds(g * span * Y, span * Y)
        copies.append(pltpu.make_async_copy(ms.at[:, rows, :], m_hbm.at[:, rows, :], sem.at[1 + g]))
        copies[-1].start()
    for copy in copies:
        copy.wait()


def shards(sizes, u, e, t, r, b):
    X, Y, Z = t.shape
    N = X * Y
    layers = sizes[2]
    assert 8 * X <= Z and Z % 128 == 0 and Y % 8 == 0 and X % 8 == 0
    W = max(X, Y)
    f32 = jnp.float32
    vmem = pltpu.VMEM
    dma = pltpu.SemaphoreType.DMA
    any_space = pl.BlockSpec(memory_space=pl.ANY)
    in_vmem = pl.BlockSpec(memory_space=vmem)
    D = max(layers - 1, 1)
    kept = pl.pallas_call(
        functools.partial(kernel, (X, Y, Z), sizes),
        out_shape=(vmem((6, N, Z), f32), vmem((3, N, Z), f32), vmem((Y, Z), f32)),
        in_specs=[any_space] * 6,
        out_specs=(in_vmem,) * 3,
        scratch_shapes=[
            vmem((3, N + 2 * Y, Z), f32),
            vmem((6, N, Z), f32),
            vmem((N, Z), f32),
            vmem((N, Z), f32),
            vmem((N, Z), jnp.int32),
            vmem((N, Z), f32),
            vmem((N, Z), f32),
            vmem((6, N, Z), f32),
            vmem((N, Z), f32),
            vmem((N, Z), f32),
            vmem((6, N + 2 * Y, Z), f32),
            vmem((2, 8, Y, Z), f32),
            vmem((2, 8, X, Z), f32),
            vmem((3, X, Z), f32),
            vmem((2, W, Z), f32),
            vmem((2, Y, Z), f32),
            vmem((2, 2, 8, Z), f32),
            vmem((Y, Z), f32),
            vmem((2, Y, Z), f32),
            vmem((2, X, Z), f32),
            vmem((2, 3, Y, Z), f32),
            vmem((2, 8, Y, Z), f32),
            vmem((2, 3, X, Z), f32),
            vmem((2, 8, X, Z), f32),
            vmem((2, Y, Z), f32),
            vmem((2, 2, Y, Z), f32),
            vmem((2, 2, 8, Z), f32),
            vmem((2, 2, 3, Y, Z), f32),
            vmem((2, 2, 2, W, Z), f32),
            vmem((D, Y, Z), f32),
            vmem((2, D, Y, Z), f32),
            vmem((2, D, X, Z), f32),
            dma((4,)),
            pltpu.SemaphoreType.REGULAR((4,)),
            pltpu.SemaphoreType.REGULAR((1 if layers == 2 else 2,)),
            dma((6,)),
            dma((9,)),
        ],
        compiler_params=pltpu.CompilerParams(collective_id=0, has_side_effects=True),
        name="strain_step",
    )(u.reshape(3, N, Z), u, e.reshape(6, N, Z), t.reshape(N, Z), r.reshape(N, Z), b.reshape(N, Z))
    f, m = pl.pallas_call(
        functools.partial(finish, (X, Y, Z)),
        out_shape=(jax.ShapeDtypeStruct((6, N, Z), f32), jax.ShapeDtypeStruct((3, N, Z), f32)),
        in_specs=[in_vmem] * 3,
        out_specs=(any_space, any_space),
        scratch_shapes=[vmem((3, N, Z), f32), dma((5,))],
        name="finish",
    )(*(pltpu.with_memory_space_constraint(k, vmem) for k in kept))
    return f.reshape(6, X, Y, Z), m.reshape(3, X, Y, Z)


def solution(mesh):
    sizes = tuple(mesh.shape[a] for a in AXES)
    field = P("gx", "gy", "gz")
    fields = P(None, "gx", "gy", "gz")
    return jax.shard_map(
        functools.partial(shards, sizes),
        mesh=mesh,
        in_specs=(fields, fields, field, field, field),
        out_specs=(fields, fields),
        check_vma=False,
    )
```

```python
import functools

import jax
import jax.numpy as jnp
from jax import lax
from jax.experimental import pallas as pl
from jax.experimental.pallas import tpu as pltpu
from jax.sharding import PartitionSpec as P

MESH = pl.DeviceIdType.MESH
AXES = ("gx", "gy", "gz")
TERMS = (
    ((0, 0.5), (3, 0.25), (4, 0.25)),
    ((3, 0.25), (1, 0.5), (5, 0.25)),
    ((4, 0.25), (5, 0.25), (2, 0.5)),
)
X_SET = (0, 3, 4)
Y_SET = (3, 1, 5)
Z_SET = (4, 5, 2)


def offsets(layers):
    near = [
        (x, y, z)
        for x in (-1, 0, 1)
        for y in (-1, 0, 1)
        for z in (-1, 0, 1)
        if 1 <= abs(x) + abs(y) + abs(z) <= 2
    ]
    far = [
        (x, y, s * d)
        for d in range(2, layers)
        for s in (-1, 1)
        for x, y in ((0, 0), (-1, 0), (1, 0), (0, -1), (0, 1))
    ]
    return near + far


def minus(o):
    return tuple(-v for v in o)


def plus(o, p):
    return tuple(v + w for v, w in zip(o, p))


def split(o):
    return tuple(min(v, 0) for v in o), tuple(max(v, 0) for v in o)


def kinds_of(layers):
    offs = offsets(layers)
    uppers = [o for o in offs if min(o) >= 0]
    lowers = [o for o in offs if max(o) <= 0]
    mixed = [o for o in offs if min(o) < 0 < max(o)]
    return uppers, lowers, mixed


def merge(low, high):
    Z = low.shape[1]
    even = (lax.broadcasted_iota(jnp.int32, low.shape, 1) & 1) == 0
    return jnp.where(even, low, pltpu.roll(high, Z - 2, 1))


def edge_term(tile, q, z_edge):
    Z = tile.shape[1]
    return (pltpu.roll(tile, (Z - 2 * q) % Z, 1) if q else tile) * z_edge


def flow(e, pace):
    trace = e[0] + e[1] + e[2]
    third = trace * (1.0 / 3.0)
    half = [e[0] - third, e[1] - third, e[2] - third, e[3], e[4], e[5]]
    second = half[0] * half[0] + half[1] * half[1] + half[2] * half[2]
    second = second + 2.0 * (half[3] * half[3] + half[4] * half[4] + half[5] * half[5])
    rate = pace * second
    return trace, [rate * h for h in half]


def stress(e, change, trace, part):
    out = 2.0 * (e[part] - change[part])
    return out + trace if part < 3 else out


def kernel(
    dims, sizes,
    u_hbm, u_rows, e_hbm, t_hbm, r_hbm, b_hbm,
    fv, mv, jv,
    uv, ev, tv, rv, bv, pv, tot, el, av, nt, sp,
    xs, ys, yu, zu, zs, xy, zt, xt, yt,
    rxu, rxs, ryu, rys, rzu, rzs, rxy, rxz, ryz, rt, rtx, rty,
    in_sem, ready, told, send_sem, recv_sem,
):
    X, Y, Z = dims
    N = X * Y
    layers = sizes[2]
    depths = range(1, layers)
    me = [lax.axis_index(a) for a in AXES]
    offs = offsets(layers)
    uppers, lowers, mixed = kinds_of(layers)
    W = max(X, Y)

    def ready_index(o):
        return o.index(1) if sum(o) == 1 else 3

    def exists(o):
        ok = None
        for a in range(3):
            if o[a]:
                here = me[a] + o[a]
                test = here < sizes[a] if o[a] > 0 else here >= 0
                ok = test if ok is None else jnp.logical_and(ok, test)
        return ok

    def partner(o):
        return {AXES[a]: me[a] + o[a] for a in range(3) if o[a]}

    has = {o: exists(o) for o in offs}
    faces = {a: [tuple(s if i == a else 0 for i in range(3)) for s in (-1, 1)] for a in range(3)}

    loads = [
        pltpu.make_async_copy(src, dst, in_sem.at[min(i, 2) if i < 6 else 3])
        for i, (src, dst) in enumerate(
            (
                (u_hbm, uv.at[:, pl.ds(Y, N), :]),
                (r_hbm, rv),
                (e_hbm.at[:, pl.ds(0, Y), :], ev.at[:, pl.ds(0, Y), :]),
                (e_hbm.at[:, pl.ds(N - Y, Y), :], ev.at[:, pl.ds(N - Y, Y), :]),
                (t_hbm, tv),
                (b_hbm, bv),
                (e_hbm.at[:, pl.ds(Y, N - 2 * Y), :], ev.at[:, pl.ds(Y, N - 2 * Y), :]),
            )
        )
    ]
    for copy in loads:
        copy.start()

    def take(sem, rows):
        planes = next(k for k in range(1, 7) if rows % (8 * k) == 0 and rows // k <= N + 2 * Y)
        spot = sp.at[pl.ds(0, planes), pl.ds(0, rows // planes)]
        pltpu.make_async_copy(spot, spot, sem).wait()

    barrier = pltpu.get_barrier_semaphore()
    for o in uppers:
        @pl.when(has[o])
        def _(o=o):
            pl.semaphore_signal(barrier, inc=1, device_id=partner(o), device_id_type=MESH)
    expected = jnp.int32(0)
    for o in lowers:
        expected = expected + has[o].astype(jnp.int32)

    plane = jnp.zeros((Y, Z), jnp.float32)
    row_plane = jnp.zeros((X, Z), jnp.float32)
    for c in range(3):
        uv[c, pl.ds(0, Y), :] = plane
        uv[c, pl.ds(Y + N, Y), :] = plane
    for c in range(6):
        sp[c, pl.ds(0, Y), :] = plane
        sp[c, pl.ds(Y + N, Y), :] = plane

    def blank(o, *refs):
        @pl.when(jnp.logical_not(has[o]))
        def _():
            for ref in refs:
                ref[...] = jnp.zeros(ref.shape, jnp.float32)

    for i, sz in enumerate((-1, 1)):
        blank((0, 0, sz), rzu.at[i], rzs.at[i])
        for j, s in enumerate((-1, 1)):
            blank((s, 0, sz), rxz.at[j, i])
            blank((0, s, sz), ryz.at[j, i])
    for i, sx in enumerate((-1, 1)):
        for j, sy in enumerate((-1, 1)):
            blank((sx, sy, 0), rxy.at[i, j])
    for d in depths:
        blank((0, 0, -d), rt.at[d - 1])
        for j, s in enumerate((-1, 1)):
            blank((s, 0, -d), rtx.at[j, d - 1])
            blank((0, s, -d), rty.at[j, d - 1])

    lane = lax.broadcasted_iota(jnp.int32, (Y, Z), 1)
    row = lax.broadcasted_iota(jnp.int32, (Y, Z), 0)
    pair = lane >> 1
    even = (lane & 1) == 0
    not_last = jnp.where(row < Y - 1, 0.5, 0.0).astype(jnp.float32)
    not_first = jnp.where(row > 0, 0.5, 0.0).astype(jnp.float32)
    z_first = jnp.where(lane > 0, 0.5, 0.0).astype(jnp.float32)
    z_last = jnp.where(lane < Z - 1, 0.5, 0.0).astype(jnp.float32)
    z_edge = jnp.where(lane == 0, -0.5, jnp.where(lane == Z - 1, 0.5, 0.0)).astype(jnp.float32)
    if X == Y:
        row_x, z_edge_x = row, z_edge
    else:
        lane_x = lax.broadcasted_iota(jnp.int32, (X, Z), 1)
        row_x = lax.broadcasted_iota(jnp.int32, (X, Z), 0)
        z_edge_x = jnp.where(lane_x == 0, -0.5, jnp.where(lane_x == Z - 1, 0.5, 0.0)).astype(jnp.float32)

    beside = [sum(has[o].astype(jnp.int32) for o in faces[a]) for a in range(3)]
    above, below = me[2], layers - 1 - me[2]

    def products(*ranges):
        values = {1}
        for r in ranges:
            values = {v * w for v in values for w in r}
        return sorted(values - {0})

    some, any_depth = (1, 2), range(layers)
    four = products(some, some)
    arrivals = {
        "xu": (3 * Y, beside[0], some),
        "xs": (Y, beside[0] * (8 + above), products(some, [8 + d for d in any_depth])),
        "yu": (3 * X, beside[1], some),
        "ys": (X, beside[1] * (8 + above), products(some, [8 + d for d in any_depth])),
        "zu": (Y, beside[2] + above, sorted({n + d for n in some for d in any_depth})),
        "zs": (2 * Y, beside[2], some),
        "xy": (8, beside[0] * beside[1], four),
        "xz": (3 * Y, beside[0] * beside[2], four),
        "yz": (2 * W, beside[1] * beside[2], four),
    }
    departures = (
        (Y, beside[0] * (11 + below), products(some, [11 + d for d in any_depth])),
        (X, beside[1] * (11 + below), products(some, [11 + d for d in any_depth])),
        (Y, 3 * beside[2] + below, sorted({3 * n + d for n in some for d in any_depth})),
        arrivals["xy"], arrivals["xz"], arrivals["yz"],
    )
    recv_index = {kind: i for i, kind in enumerate(arrivals)}
    recv_index |= {"tx": recv_index["xs"], "ty": recv_index["ys"], "t": recv_index["zu"]}
    send_index = {
        "xu": 0, "xs": 0, "tx": 0, "yu": 1, "ys": 1, "ty": 1, "zu": 2, "zs": 2, "t": 2, "xy": 3, "xz": 4, "yz": 5,
    }
    sends = {o: [] for o in offs}

    def message(kind, o, src, dst):
        sends[o].append((kind, pltpu.make_async_remote_copy(
            src_ref=src, dst_ref=dst,
            send_sem=send_sem.at[send_index[kind]], recv_sem=recv_sem.at[recv_index[kind]],
            device_id=partner(o), device_id_type=MESH,
        )))

    for i, s in enumerate((-1, 1)):
        k = 1 - i
        at = (Y, Y * X)[i]
        strike = u_hbm.at[:, pl.ds((0, N - Y)[i], Y), :] if s < 0 else uv.at[:, pl.ds(at, Y), :]
        message("xu", (s, 0, 0), strike, rxu.at[k])
        message("xs", (s, 0, 0), xs.at[i], rxs.at[k])
        message("yu", (0, s, 0), u_rows.at[:, :, 0, :] if s < 0 else yu, ryu.at[k])
        message("ys", (0, s, 0), ys.at[i], rys.at[k])
        message("zu", (0, 0, s), zu.at[0, pl.ds(0, Y)], rzu.at[k])
        message("zs", (0, 0, s), zs, rzs.at[k])
        for j, s2 in enumerate((-1, 1)):
            m = 1 - j
            message("xy", (s, s2, 0), xy.at[i, j], rxy.at[k, m])
            strike = u_hbm.at[:, pl.ds(0, Y), :] if s + s2 < 0 else uv.at[:, pl.ds(at, Y), :]
            message("xz", (s, 0, s2), strike, rxz.at[k, m])
            message("yz", (0, s, s2), zu, ryz.at[k, m])
        for d in depths:
            message("tx", (s, 0, d), xt.at[i], rtx.at[k, d - 1])
            message("ty", (0, s, d), yt.at[i], rty.at[k, d - 1])
    for d in depths:
        message("t", (0, 0, d), zt, rt.at[d - 1])

    def settle(sem, rows, count, values):
        for n in values:
            @pl.when(count == n)
            def _(n=n):
                take(sem, n * rows)

    def start(offsets_in, kinds):
        for o in offsets_in:
            chosen = [copy for kind, copy in sends[o] if kind in kinds]
            if chosen:
                @pl.when(has[o])
                def _(chosen=chosen):
                    for copy in chosen:
                        copy.start()

    def arrive(*kinds):
        for kind in kinds:
            settle(recv_sem.at[recv_index[kind]], *arrivals[kind])

    @pl.when(expected > 0)
    def _():
        pl.semaphore_wait(barrier, expected)

    for o in lowers:
        @pl.when(has[o])
        def _(o=o):
            pl.semaphore_signal(
                ready.at[ready_index(minus(o))], inc=1, device_id=partner(o), device_id_type=MESH
            )

    def announce(o):
        low, high = split(o)

        @pl.when(jnp.logical_and(has[minus(low)], has[high]))
        def _():
            kind = 0 if max(high) == 1 and min(low) == -1 else 1
            pl.semaphore_signal(told.at[kind], inc=1, device_id=partner(minus(low)), device_id_type=MESH)

    lowers = sorted(lowers, key=lambda o: (sum(map(abs, o)), o[2], o[1]))
    for kind in ("xz", "yu", "xu"):
        start(lowers, (kind,))

    loads[0].wait()
    tile0 = plane
    for x in range(X):
        for c in range(3):
            q = c * X + x
            tile = pltpu.roll(uv[c, pl.ds(Y + x * Y, Y), :], (2 * q + 1) % Z, 1)
            tile0 = jnp.where(pair == q, tile, tile0)
    zu[0, pl.ds(0, Y), :] = tile0
    start(lowers, ("zu",))
    tile = row_plane
    pair_x = lax.broadcasted_iota(jnp.int32, (X, Z), 1) >> 1
    for i, line in enumerate((0, Y - 1)):
        for c in range(3):
            p = 3 * i + c
            lines = uv[c, pl.ds(Y + line, X, stride=Y), :]
            if i:
                yu[c] = lines
            tile = jnp.where(pair_x == p, pltpu.roll(lines, (2 * p + 1) % Z, 1), tile)
            for j, at in enumerate((0, X - 1)):
                xy[j, i, pl.ds(c, 1), :] = uv[c, pl.ds(Y + at * Y + line, 1), :]
    zu[1, pl.ds(0, X), :] = tile

    start(lowers, ("xy", "yz"))

    loads[1].wait()
    total_depth = Z * layers
    depth = (me[2] * Z + lane).astype(jnp.float32)
    scale = (1.0 + 2.0 * depth / total_depth) / total_depth
    thirds = [[], [], []]
    for x in range(X):
        rest = rv[pl.ds(x * Y, Y), :] * scale
        for k in range(3):
            piece = rest.astype(jnp.bfloat16)
            thirds[k].append(piece)
            rest = rest - piece.astype(jnp.float32)
    weight = jnp.concatenate([jnp.concatenate(k, axis=0) for k in thirds], axis=1)
    above_row = lax.broadcasted_iota(jnp.int32, (Z, 2 * Z), 0)
    column = lax.broadcasted_iota(jnp.int32, (Z, 2 * Z), 1)
    triangle = jnp.where(
        (above_row < column) | (column >= Z),
        1.0,
        jnp.where(above_row == column, 0.5, 0.0),
    ).astype(jnp.bfloat16)
    triangle = jnp.concatenate([triangle] * 3, axis=0)
    sums = jnp.dot(weight, triangle, preferred_element_type=jnp.float32)
    pv[...] = sums[:, :Z] + 1.0
    tot[...] = sums[:, Z:]
    tile = plane
    for x in range(X):
        tile = jnp.where(pair == x, tot[pl.ds(x * Y, Y), :], tile)
    zt[...] = tile
    for i, (at, line) in enumerate(((0, 0), (X - 1, Y - 1))):
        xt[i] = tot[pl.ds(at * Y, Y), :]
        yt[i] = tot[pl.ds(line, X, stride=Y), :]

    tiles = [plane, plane]

    def strain(x):
        base = Y + x * Y
        own = pl.ds(x * Y, Y)
        grad = []
        for c in range(3):
            here = uv[c, pl.ds(base, Y), :]
            grad.append((
                (uv[c, pl.ds(base + Y, Y), :] - uv[c, pl.ds(base - Y, Y), :]) * 0.5,
                uv[c, pl.ds(base + 1, Y), :] * not_last - uv[c, pl.ds(base - 1, Y), :] * not_first,
                pltpu.roll(here, Z - 1, 1) * z_last - pltpu.roll(here, 1, 1) * z_first,
            ))
        el[0, own, :] = grad[0][0]
        el[1, own, :] = grad[1][1]
        el[2, own, :] = grad[2][2]
        el[3, own, :] = 0.5 * (grad[0][1] + grad[1][0])
        el[4, own, :] = 0.5 * (grad[0][2] + grad[2][0])
        el[5, own, :] = 0.5 * (grad[1][2] + grad[2][1])

    def pack(k, x, part, tiles):
        q = (k % 4) * X + x
        tile = pltpu.roll(part, (2 * q + 1) % Z, 1)
        tiles[k // 4] = jnp.where(pair == q, tile, tiles[k // 4])

    def factors(x, tiles):
        own = pl.ds(x * Y, Y)
        minus_two = -2.0 / tv[own, :]
        factor = (2.0 + 14.0 * bv[own, :].astype(jnp.float32)) * jnp.exp(pv[own, :] * minus_two)
        av[own, :] = factor
        nt[own, :] = minus_two
        for i, at in enumerate((0, X - 1)):
            if x == at:
                xs[i, 6] = factor
                xs[i, 7] = minus_two
        pack(6, x, factor, tiles)
        pack(7, x, minus_two, tiles)

    def elastic(x, tiles):
        own = pl.ds(x * Y, Y)
        for k in range(6):
            part = el[k, own, :] - ev[k, own, :]
            el[k, own, :] = part
            for i, at in enumerate((0, X - 1)):
                if x == at:
                    xs[i, k] = part
            pack(k, x, part, tiles)

    ends = sorted({0, X - 1})
    for x in ends:
        strain(x)
    take(in_sem.at[2], 12 * Y + 2 * N)
    for x in ends:
        elastic(x, tiles)
        factors(x, tiles)
    start(lowers, ("xs", "t", "tx", "ty"))

    inner = [x for x in range(X) if x not in ends]
    for x in inner:
        strain(x)
        factors(x, tiles)
    loads[6].wait()
    for x in inner:
        elastic(x, tiles)
    for k in range(2):
        zs[k] = tiles[k]
    start(lowers, ("zs",))
    for i, line in enumerate((0, Y - 1)):
        for k in range(8):
            src = el.at[k] if k < 6 else (av, nt)[k - 6]
            ys[i, k] = src[pl.ds(line, X, stride=Y), :]
    start(lowers, ("ys",))

    near = [o for o in uppers if sum(o) == 1]
    for o in sorted(near):
        @pl.when(has[o])
        def _(o=o):
            pl.semaphore_wait(ready.at[ready_index(o)], 1)

    for o in mixed:
        low, high = split(o)
        if high in near and minus(low) in near:
            announce(o)
    near.sort()
    start(near, ("zu", "yu", "xu", "t", "zs"))
    others = [o for o in uppers if o not in near]
    far = [o for o in mixed if split(o)[1] not in near or minus(split(o)[0]) not in near]
    close = sorted((o for o in mixed if o not in far), key=lambda o: (abs(o[0]), abs(o[2])))

    diagonal = ("xy", "xz", "yz", "t", "tx", "ty")

    def hear(offsets_in, sem):
        number = sum(has[o].astype(jnp.int32) for o in offsets_in)

        @pl.when(number > 0)
        def _():
            pl.semaphore_wait(sem, number)

        start(offsets_in, diagonal)

    hear(close, told.at[0])
    start(near, ("ys", "xs"))
    hear(others, ready.at[3])
    for o in far:
        announce(o)
    if far:
        hear(far, told.at[1])

    arrive("yu")
    for side, line in enumerate((0, Y - 1)):
        sign = 2.0 * side - 1.0

        @pl.when(has[faces[1][side]])
        def _(side=side, sign=sign, line=line):
            own = pl.ds(line, X, stride=Y)
            for c, (part, factor) in enumerate(TERMS[1]):
                el[part, own, :] = el[part, own, :] + (sign * factor) * ryu[side, c]

    arrive("zu")
    carried = plane
    for d in depths:
        carried = carried + rt[d - 1]
    merged = merge(rzu[0], rzu[1])

    def advance(x):
        own = pl.ds(x * Y, Y)
        e = [el[c, own, :] for c in range(6)]
        for c, (part, factor) in enumerate(TERMS[2]):
            e[part] = e[part] + (2.0 * factor) * edge_term(merged, c * X + x, z_edge)
        load = jnp.broadcast_to(carried[:, 2 * x:2 * x + 1], (Y, Z))
        trace, change = flow(e, av[own, :] * jnp.exp(load * nt[own, :]))
        for c in range(6):
            fv[c, own, :] = ev[c, own, :] + change[c]
            sp[c, pl.ds(Y + x * Y, Y), :] = stress(e, change, trace, c)

    for x in range(X):
        if x not in ends:
            advance(x)
    arrive("xu")
    for side, at in enumerate((0, X - 1)):
        sign = 2.0 * side - 1.0

        @pl.when(has[faces[0][side]])
        def _(side=side, sign=sign, at=at):
            own = pl.ds(at * Y, Y)
            for c, (part, factor) in enumerate(TERMS[0]):
                el[part, own, :] = el[part, own, :] + (sign * factor) * rxu[side, c]

    for x in ends:
        advance(x)

    for x in range(X):
        base = Y + x * Y
        own = pl.ds(x * Y, Y)
        for c in range(3):
            cx, cy, cz = X_SET[c], Y_SET[c], Z_SET[c]
            here = sp[cz, pl.ds(base, Y), :]
            total = (sp[cx, pl.ds(base + Y, Y), :] - sp[cx, pl.ds(base - Y, Y), :]) * 0.5
            total = total + (
                sp[cy, pl.ds(base + 1, Y), :] * not_last - sp[cy, pl.ds(base - 1, Y), :] * not_first
            )
            total = total + (pltpu.roll(here, Z - 1, 1) * z_last - pltpu.roll(here, 1, 1) * z_first)
            if c == 2:
                total = total - 0.5 * rv[own, :]
            mv[c, own, :] = total

    def add(e, axis, factor, values):
        for c, (part, f) in enumerate(TERMS[axis]):
            e[part] = e[part] + (factor * f) * values[c]

    def ends_of(first, last, rows, count):
        return jnp.where(rows == 0, -first, jnp.where(rows == count - 1, last, 0.0))

    arrive("xy", "yz", "xz", "ys", "zs", "xs")

    def beyond(axis, side, part):
        got, load, e = part
        trace, change = flow(e, got[6] * jnp.exp(load * got[7]))
        there = has[faces[axis][side]]
        return [
            (side - 0.5) * jnp.where(there, stress(e, change, trace, k), 0.0) for k in (X_SET, Y_SET)[axis]
        ]

    along_y = []
    for side, line in enumerate((0, Y - 1)):
        e = [rys[side, k] for k in range(6)]
        add(e, 1, 1.0 - 2.0 * side, [uv[c, pl.ds(Y + line, X, stride=Y), :] for c in range(3)])
        add(e, 0, 1.0, [
            ends_of(rxy[0, side, pl.ds(c, 1), :], rxy[1, side, pl.ds(c, 1), :], row_x, X) for c in range(3)
        ])
        joined = merge(ryz[side, 0, 1, pl.ds(0, X), :], ryz[side, 1, 1, pl.ds(0, X), :])
        add(e, 2, 2.0, [edge_term(joined, 3 * (1 - side) + c, z_edge_x) for c in range(3)])
        load = row_plane
        for d in depths:
            load = load + rty[side, d - 1]
        along_y.append(beyond(1, side, (rys[side], load, e)))

    along_x = []
    for side, at in enumerate((0, X - 1)):
        e = [rxs[side, k] for k in range(6)]
        add(e, 0, 1.0 - 2.0 * side, [uv[c, pl.ds(Y + at * Y, Y), :] for c in range(3)])
        add(e, 1, 1.0, [
            ends_of(rxy[side, 0, pl.ds(c, 1), :], rxy[side, 1, pl.ds(c, 1), :], row, Y) for c in range(3)
        ])
        add(e, 2, 1.0, [
            jnp.where(
                lane == 0, -pltpu.roll(rxz[side, 0, c], 1, 1),
                jnp.where(lane == Z - 1, pltpu.roll(rxz[side, 1, c], Z - 1, 1), 0.0),
            )
            for c in range(3)
        ])
        load = plane
        for d in depths:
            load = load + rtx[side, d - 1]
        along_x.append(beyond(0, side, (rxs[side], load, e)))

    block = 2 * X

    def shift(tile, by):
        return pltpu.roll(tile, by % Z, 1) if by % Z else tile

    halo = [jnp.where(even, rzs[0, k], rzs[1, k]) for k in range(2)]
    parts = [shift(halo[k // 4], -(k % 4) * block) for k in range(8)]
    mine = zu[0, pl.ds(0, Y), :]
    from_z = jnp.where(even, shift(mine, -1), -shift(mine, 1))
    from_x = []
    for c in range(3):
        left, right = (jnp.where(lane == Z - 1, rxz[i, 0, c], rxz[i, 1, c]) for i in range(2))
        from_x.append(jnp.where(
            pair == 0, -shift(left, 1), jnp.where(pair == X - 1, shift(right, 2 * X - 1), 0.0)
        ))
    even_row = (lax.broadcasted_iota(jnp.int32, (1, Z), 1) & 1) == 0
    from_y = ends_of(
        jnp.where(even_row, ryz[0, 0, 0, pl.ds(Y - 1, 1), :], ryz[0, 1, 0, pl.ds(Y - 1, 1), :]),
        jnp.where(even_row, ryz[1, 0, 0, pl.ds(0, 1), :], ryz[1, 1, 0, pl.ds(0, 1), :]),
        row, Y,
    )
    e = list(parts[:6])
    add(e, 0, 1.0, from_x)
    for axis, tile in ((1, from_y), (2, from_z)):
        add(e, axis, 1.0, [shift(tile, -c * block) for c in range(3)])
    deeper = plane
    for d in depths:
        if d >= 2:
            deeper = deeper + rt[d - 1]
    load = jnp.where(even, deeper, carried + zt[...])
    trace, change = flow(e, parts[6] * jnp.exp(load * parts[7]))
    known = jnp.where(
        even,
        has[0, 0, -1].astype(jnp.float32),
        has[0, 0, 1].astype(jnp.float32),
    )
    gathered = plane
    for c in range(3):
        tile = shift(stress(e, change, trace, Z_SET[c]) * known, c * block)
        gathered = jnp.where((pair >= c * X) & (pair < (c + 1) * X), tile, gathered)
    jv[...] = jnp.where(even, gathered, shift(gathered, -2))

    for c in range(3):
        for side, at in enumerate((0, X - 1)):
            own = pl.ds(at * Y, Y)
            mv[c, own, :] = mv[c, own, :] + along_x[side][c]
        for side, line in enumerate((0, Y - 1)):
            own = pl.ds(line, X, stride=Y)
            mv[c, own, :] = mv[c, own, :] + along_y[side][c]

    for i, departure in enumerate(departures):
        settle(send_sem.at[i], *departure)


def finish(dims, fv, mv, jv, f_hbm, m_hbm, ms, sem):
    X, Y, Z = dims
    copies = [pltpu.make_async_copy(fv, f_hbm, sem.at[0])]
    copies[0].start()
    lane = lax.broadcasted_iota(jnp.int32, (Y, Z), 1)
    z_edge = jnp.where(lane == 0, -0.5, jnp.where(lane == Z - 1, 0.5, 0.0)).astype(jnp.float32)
    joined = jv[...]
    groups = 4
    span = X // groups
    for g in range(groups):
        for x in range(g * span, (g + 1) * span):
            own = pl.ds(x * Y, Y)
            for c in range(3):
                ms[c, own, :] = mv[c, own, :] + edge_term(joined, c * X + x, z_edge)
        rows = pl.ds(g * span * Y, span * Y)
        copies.append(pltpu.make_async_copy(ms.at[:, rows, :], m_hbm.at[:, rows, :], sem.at[1 + g]))
        copies[-1].start()
    for copy in copies:
        copy.wait()


def shards(sizes, u, e, t, r, b):
    X, Y, Z = t.shape
    N = X * Y
    layers = sizes[2]
    assert 8 * X <= Z and Z % 128 == 0 and Y % 8 == 0 and X % 8 == 0
    W = max(X, Y)
    f32 = jnp.float32
    vmem = pltpu.VMEM
    dma = pltpu.SemaphoreType.DMA
    any_space = pl.BlockSpec(memory_space=pl.ANY)
    in_vmem = pl.BlockSpec(memory_space=vmem)
    D = max(layers - 1, 1)
    kept = pl.pallas_call(
        functools.partial(kernel, (X, Y, Z), sizes),
        out_shape=(vmem((6, N, Z), f32), vmem((3, N, Z), f32), vmem((Y, Z), f32)),
        in_specs=[any_space] * 6,
        out_specs=(in_vmem,) * 3,
        scratch_shapes=[
            vmem((3, N + 2 * Y, Z), f32),
            vmem((6, N, Z), f32),
            vmem((N, Z), f32),
            vmem((N, Z), f32),
            vmem((N, Z), jnp.int32),
            vmem((N, Z), f32),
            vmem((N, Z), f32),
            vmem((6, N, Z), f32),
            vmem((N, Z), f32),
            vmem((N, Z), f32),
            vmem((6, N + 2 * Y, Z), f32),
            vmem((2, 8, Y, Z), f32),
            vmem((2, 8, X, Z), f32),
            vmem((3, X, Z), f32),
            vmem((2, W, Z), f32),
            vmem((2, Y, Z), f32),
            vmem((2, 2, 8, Z), f32),
            vmem((Y, Z), f32),
            vmem((2, Y, Z), f32),
            vmem((2, X, Z), f32),
            vmem((2, 3, Y, Z), f32),
            vmem((2, 8, Y, Z), f32),
            vmem((2, 3, X, Z), f32),
            vmem((2, 8, X, Z), f32),
            vmem((2, Y, Z), f32),
            vmem((2, 2, Y, Z), f32),
            vmem((2, 2, 8, Z), f32),
            vmem((2, 2, 3, Y, Z), f32),
            vmem((2, 2, 2, W, Z), f32),
            vmem((D, Y, Z), f32),
            vmem((2, D, Y, Z), f32),
            vmem((2, D, X, Z), f32),
            dma((4,)),
            pltpu.SemaphoreType.REGULAR((4,)),
            pltpu.SemaphoreType.REGULAR((1 if layers == 2 else 2,)),
            dma((6,)),
            dma((9,)),
        ],
        compiler_params=pltpu.CompilerParams(collective_id=0, has_side_effects=True),
        name="strain_step",
    )(u.reshape(3, N, Z), u, e.reshape(6, N, Z), t.reshape(N, Z), r.reshape(N, Z), b.reshape(N, Z))
    f, m = pl.pallas_call(
        functools.partial(finish, (X, Y, Z)),
        out_shape=(jax.ShapeDtypeStruct((6, N, Z), f32), jax.ShapeDtypeStruct((3, N, Z), f32)),
        in_specs=[in_vmem] * 3,
        out_specs=(any_space, any_space),
        scratch_shapes=[vmem((3, N, Z), f32), dma((5,))],
        name="finish",
    )(*(pltpu.with_memory_space_constraint(k, vmem) for k in kept))
    return f.reshape(6, X, Y, Z), m.reshape(3, X, Y, Z)


def solution(mesh):
    sizes = tuple(mesh.shape[a] for a in AXES)
    field = P("gx", "gy", "gz")
    fields = P(None, "gx", "gy", "gz")
    return jax.shard_map(
        functools.partial(shards, sizes),
        mesh=mesh,
        in_specs=(fields, fields, field, field, field),
        out_specs=(fields, fields),
        check_vma=False,
    )
```

```python
import functools

import jax
import jax.numpy as jnp
from jax import lax
from jax.experimental import pallas as pl
from jax.experimental.pallas import tpu as pltpu
from jax.sharding import PartitionSpec as P

MESH = pl.DeviceIdType.MESH
AXES = ("gx", "gy", "gz")
TERMS = (
    ((0, 0.5), (3, 0.25), (4, 0.25)),
    ((3, 0.25), (1, 0.5), (5, 0.25)),
    ((4, 0.25), (5, 0.25), (2, 0.5)),
)
X_SET = (0, 3, 4)
Y_SET = (3, 1, 5)
Z_SET = (4, 5, 2)


def offsets(layers):
    near = [
        (x, y, z)
        for x in (-1, 0, 1)
        for y in (-1, 0, 1)
        for z in (-1, 0, 1)
        if 1 <= abs(x) + abs(y) + abs(z) <= 2
    ]
    far = [
        (x, y, s * d)
        for d in range(2, layers)
        for s in (-1, 1)
        for x, y in ((0, 0), (-1, 0), (1, 0), (0, -1), (0, 1))
    ]
    return near + far


def minus(o):
    return tuple(-v for v in o)


def plus(o, p):
    return tuple(v + w for v, w in zip(o, p))


def split(o):
    return tuple(min(v, 0) for v in o), tuple(max(v, 0) for v in o)


def kinds_of(layers):
    offs = offsets(layers)
    uppers = [o for o in offs if min(o) >= 0]
    lowers = [o for o in offs if max(o) <= 0]
    mixed = [o for o in offs if min(o) < 0 < max(o)]
    return uppers, lowers, mixed


def merge(low, high):
    Z = low.shape[1]
    even = (lax.broadcasted_iota(jnp.int32, low.shape, 1) & 1) == 0
    return jnp.where(even, low, pltpu.roll(high, Z - 2, 1))


def edge_term(tile, q, z_edge):
    Z = tile.shape[1]
    return (pltpu.roll(tile, (Z - 2 * q) % Z, 1) if q else tile) * z_edge


def flow(e, pace):
    trace = e[0] + e[1] + e[2]
    third = trace * (1.0 / 3.0)
    half = [e[0] - third, e[1] - third, e[2] - third, e[3], e[4], e[5]]
    second = half[0] * half[0] + half[1] * half[1] + half[2] * half[2]
    second = second + 2.0 * (half[3] * half[3] + half[4] * half[4] + half[5] * half[5])
    rate = pace * second
    return trace, [rate * h for h in half]


def stress(e, change, trace, part):
    out = 2.0 * (e[part] - change[part])
    return out + trace if part < 3 else out


def kernel(
    dims, sizes,
    u_hbm, u_rows, e_hbm, t_hbm, r_hbm, b_hbm,
    fv, mv, jv,
    uv, tri, ev, tv, rv, bv, pv, tot, el, av, nt, sp,
    xs, ys, yu, zu, zs, xy, zt, xt, yt,
    rxu, rxs, ryu, rys, rzu, rzs, rxy, rxz, ryz, rt, rtx, rty,
    in_sem, ready, told, send_sem, recv_sem,
):
    X, Y, Z = dims
    N = X * Y
    layers = sizes[2]
    depths = range(1, layers)
    me = [lax.axis_index(a) for a in AXES]
    offs = offsets(layers)
    uppers, lowers, mixed = kinds_of(layers)
    W = max(X, Y)

    def ready_index(o):
        return o.index(1) if sum(o) == 1 else 3

    def exists(o):
        ok = None
        for a in range(3):
            if o[a]:
                here = me[a] + o[a]
                test = here < sizes[a] if o[a] > 0 else here >= 0
                ok = test if ok is None else jnp.logical_and(ok, test)
        return ok

    def partner(o):
        return {AXES[a]: me[a] + o[a] for a in range(3) if o[a]}

    has = {o: exists(o) for o in offs}
    faces = {a: [tuple(s if i == a else 0 for i in range(3)) for s in (-1, 1)] for a in range(3)}

    loads = [
        pltpu.make_async_copy(src, dst, in_sem.at[min(i, 2) if i < 6 else 3])
        for i, (src, dst) in enumerate(
            (
                (u_hbm, uv.at[:, pl.ds(Y, N), :]),
                (r_hbm, rv),
                (e_hbm.at[:, pl.ds(0, Y), :], ev.at[:, pl.ds(0, Y), :]),
                (e_hbm.at[:, pl.ds(N - Y, Y), :], ev.at[:, pl.ds(N - Y, Y), :]),
                (t_hbm, tv),
                (b_hbm, bv),
                (e_hbm.at[:, pl.ds(Y, N - 2 * Y), :], ev.at[:, pl.ds(Y, N - 2 * Y), :]),
            )
        )
    ]
    for copy in loads:
        copy.start()

    def take(sem, rows):
        whole = [k for k in range(1, 7) if rows % (8 * k) == 0 and rows // k <= N + 2 * Y]
        planes = whole[0] if whole else rows // 3
        spot = sp.at[pl.ds(0, planes), pl.ds(0, rows // planes)]
        pltpu.make_async_copy(spot, spot, sem).wait()

    barrier = pltpu.get_barrier_semaphore()
    for o in uppers:
        @pl.when(has[o])
        def _(o=o):
            pl.semaphore_signal(barrier, inc=1, device_id=partner(o), device_id_type=MESH)
    expected = jnp.int32(0)
    for o in lowers:
        expected = expected + has[o].astype(jnp.int32)

    plane = jnp.zeros((Y, Z), jnp.float32)
    row_plane = jnp.zeros((X, Z), jnp.float32)
    for c in range(3):
        uv[c, pl.ds(0, Y), :] = plane
        uv[c, pl.ds(Y + N, Y), :] = plane
    for c in range(6):
        sp[c, pl.ds(0, Y), :] = plane
        sp[c, pl.ds(Y + N, Y), :] = plane

    def blank(o, *refs):
        @pl.when(jnp.logical_not(has[o]))
        def _():
            for ref in refs:
                ref[...] = jnp.zeros(ref.shape, jnp.float32)

    for i, sz in enumerate((-1, 1)):
        blank((0, 0, sz), rzu.at[i], rzs.at[i])
        for j, s in enumerate((-1, 1)):
            blank((s, 0, sz), rxz.at[j, i])
            blank((0, s, sz), ryz.at[j, i])
    for i, sx in enumerate((-1, 1)):
        for j, sy in enumerate((-1, 1)):
            blank((sx, sy, 0), rxy.at[i, j])
    for d in depths:
        blank((0, 0, -d), rt.at[d - 1])
        for j, s in enumerate((-1, 1)):
            blank((s, 0, -d), rtx.at[j, d - 1])
            blank((0, s, -d), rty.at[j, d - 1])

    above_row = lax.broadcasted_iota(jnp.int32, (Z, 2 * Z), 0)
    column = lax.broadcasted_iota(jnp.int32, (Z, 2 * Z), 1)
    triangle = jnp.where(
        (above_row < column) | (column >= Z),
        1.0,
        jnp.where(above_row == column, 0.5, 0.0),
    ).astype(jnp.bfloat16)
    tri[...] = triangle

    lane = lax.broadcasted_iota(jnp.int32, (Y, Z), 1)
    row = lax.broadcasted_iota(jnp.int32, (Y, Z), 0)
    pair = lane >> 1
    even = (lane & 1) == 0
    not_last = jnp.where(row < Y - 1, 0.5, 0.0).astype(jnp.float32)
    not_first = jnp.where(row > 0, 0.5, 0.0).astype(jnp.float32)
    z_first = jnp.where(lane > 0, 0.5, 0.0).astype(jnp.float32)
    z_last = jnp.where(lane < Z - 1, 0.5, 0.0).astype(jnp.float32)
    z_edge = jnp.where(lane == 0, -0.5, jnp.where(lane == Z - 1, 0.5, 0.0)).astype(jnp.float32)
    if X == Y:
        row_x, z_edge_x = row, z_edge
    else:
        lane_x = lax.broadcasted_iota(jnp.int32, (X, Z), 1)
        row_x = lax.broadcasted_iota(jnp.int32, (X, Z), 0)
        z_edge_x = jnp.where(lane_x == 0, -0.5, jnp.where(lane_x == Z - 1, 0.5, 0.0)).astype(jnp.float32)

    beside = [sum(has[o].astype(jnp.int32) for o in faces[a]) for a in range(3)]
    above, below = me[2], layers - 1 - me[2]

    def products(*ranges):
        values = {1}
        for r in ranges:
            values = {v * w for v in values for w in r}
        return sorted(values - {0})

    some, any_depth = (1, 2), range(layers)
    four = products(some, some)
    arrivals = {
        "xu": (3 * Y, beside[0], some),
        "xs": (Y, beside[0] * (8 + above), products(some, [8 + d for d in any_depth])),
        "yu": (3 * X, beside[1], some),
        "ys": (X, beside[1] * (8 + above), products(some, [8 + d for d in any_depth])),
        "zu": (Y, beside[2] + above, sorted({n + d for n in some for d in any_depth})),
        "zs": (2 * Y, beside[2], some),
        "xy": (3, beside[0] * beside[1], four),
        "xz": (3 * Y, beside[0] * beside[2], four),
        "yz": (2 * W, beside[1] * beside[2], four),
    }
    departures = (
        (Y, beside[0] * (11 + below), products(some, [11 + d for d in any_depth])),
        (X, beside[1] * (11 + below), products(some, [11 + d for d in any_depth])),
        (Y, 3 * beside[2] + below, sorted({3 * n + d for n in some for d in any_depth})),
        arrivals["xy"], arrivals["xz"], arrivals["yz"],
    )
    recv_index = {kind: i for i, kind in enumerate(arrivals)}
    recv_index |= {"tx": recv_index["xs"], "ty": recv_index["ys"], "t": recv_index["zu"]}
    send_index = {
        "xu": 0, "xs": 0, "tx": 0, "yu": 1, "ys": 1, "ty": 1, "zu": 2, "zs": 2, "t": 2, "xy": 3, "xz": 4, "yz": 5,
    }
    sends = {o: [] for o in offs}

    def message(kind, o, src, dst):
        sends[o].append((kind, pltpu.make_async_remote_copy(
            src_ref=src, dst_ref=dst,
            send_sem=send_sem.at[send_index[kind]], recv_sem=recv_sem.at[recv_index[kind]],
            device_id=partner(o), device_id_type=MESH,
        )))

    for i, s in enumerate((-1, 1)):
        k = 1 - i
        at = (Y, Y * X)[i]
        strike = u_hbm.at[:, pl.ds((0, N - Y)[i], Y), :] if s < 0 else uv.at[:, pl.ds(at, Y), :]
        message("xu", (s, 0, 0), strike, rxu.at[k])
        message("xs", (s, 0, 0), xs.at[i], rxs.at[k])
        message("yu", (0, s, 0), u_rows.at[:, :, 0, :] if s < 0 else yu, ryu.at[k])
        message("ys", (0, s, 0), ys.at[i], rys.at[k])
        message("zu", (0, 0, s), zu.at[0, pl.ds(0, Y)], rzu.at[k])
        message("zs", (0, 0, s), zs, rzs.at[k])
        for j, s2 in enumerate((-1, 1)):
            m = 1 - j
            lines = xy.at[i, j, pl.ds(0, 3), :] if s + s2 >= 0 else u_rows.at[:, 0, 0, :]
            message("xy", (s, s2, 0), lines, rxy.at[k, m, pl.ds(0, 3), :])
            strike = u_hbm.at[:, pl.ds(0, Y), :] if s + s2 < 0 else uv.at[:, pl.ds(at, Y), :]
            message("xz", (s, 0, s2), strike, rxz.at[k, m])
            message("yz", (0, s, s2), zu, ryz.at[k, m])
        for d in depths:
            message("tx", (s, 0, d), xt.at[i], rtx.at[k, d - 1])
            message("ty", (0, s, d), yt.at[i], rty.at[k, d - 1])
    for d in depths:
        message("t", (0, 0, d), zt, rt.at[d - 1])

    def settle(sem, rows, count, values):
        for n in values:
            @pl.when(count == n)
            def _(n=n):
                take(sem, n * rows)

    def start(offsets_in, kinds):
        for o in offsets_in:
            chosen = [copy for kind, copy in sends[o] if kind in kinds]
            if chosen:
                @pl.when(has[o])
                def _(chosen=chosen):
                    for copy in chosen:
                        copy.start()

    def arrive(*kinds):
        for kind in kinds:
            settle(recv_sem.at[recv_index[kind]], *arrivals[kind])

    @pl.when(expected > 0)
    def _():
        pl.semaphore_wait(barrier, expected)

    for o in lowers:
        @pl.when(has[o])
        def _(o=o):
            pl.semaphore_signal(
                ready.at[ready_index(minus(o))], inc=1, device_id=partner(o), device_id_type=MESH
            )

    def announce(o):
        low, high = split(o)

        @pl.when(jnp.logical_and(has[minus(low)], has[high]))
        def _():
            kind = 0 if max(high) == 1 and min(low) == -1 else 1
            pl.semaphore_signal(told.at[kind], inc=1, device_id=partner(minus(low)), device_id_type=MESH)

    lowers = sorted(lowers, key=lambda o: (sum(map(abs, o)), o[2], o[1]))
    for kind in ("xz", "yu", "xy", "xu"):
        start(lowers, (kind,))

    loads[0].wait()
    loads[1].wait()
    total_depth = Z * layers
    depth = (me[2] * Z + lane).astype(jnp.float32)
    scale = (1.0 + 2.0 * depth / total_depth) / total_depth

    def prefix(planes):
        thirds = [[], [], []]
        for x in planes:
            rest = rv[pl.ds(x * Y, Y), :] * scale
            for k in range(3):
                piece = rest.astype(jnp.bfloat16)
                thirds[k].append(piece)
                rest = rest - piece.astype(jnp.float32)
        weight = jnp.concatenate([jnp.concatenate(k, axis=0) for k in thirds], axis=1)
        triangle = jnp.concatenate([tri[...]] * 3, axis=0)
        sums = jnp.dot(weight, triangle, preferred_element_type=jnp.float32)
        for i, x in enumerate(planes):
            pv[pl.ds(x * Y, Y), :] = sums[i * Y:(i + 1) * Y, :Z] + 1.0
            tot[pl.ds(x * Y, Y), :] = sums[i * Y:(i + 1) * Y, Z:]

    tiles = [plane, plane]

    def strain(x):
        base = Y + x * Y
        own = pl.ds(x * Y, Y)
        grad = []
        for c in range(3):
            here = uv[c, pl.ds(base, Y), :]
            grad.append((
                (uv[c, pl.ds(base + Y, Y), :] - uv[c, pl.ds(base - Y, Y), :]) * 0.5,
                uv[c, pl.ds(base + 1, Y), :] * not_last - uv[c, pl.ds(base - 1, Y), :] * not_first,
                pltpu.roll(here, Z - 1, 1) * z_last - pltpu.roll(here, 1, 1) * z_first,
            ))
        el[0, own, :] = grad[0][0]
        el[1, own, :] = grad[1][1]
        el[2, own, :] = grad[2][2]
        el[3, own, :] = 0.5 * (grad[0][1] + grad[1][0])
        el[4, own, :] = 0.5 * (grad[0][2] + grad[2][0])
        el[5, own, :] = 0.5 * (grad[1][2] + grad[2][1])

    def pack(k, x, part, tiles):
        q = (k % 4) * X + x
        tile = pltpu.roll(part, (2 * q + 1) % Z, 1)
        tiles[k // 4] = jnp.where(pair == q, tile, tiles[k // 4])

    def factors(x, tiles):
        own = pl.ds(x * Y, Y)
        minus_two = -2.0 / tv[own, :]
        factor = (2.0 + 14.0 * bv[own, :].astype(jnp.float32)) * jnp.exp(pv[own, :] * minus_two)
        av[own, :] = factor
        nt[own, :] = minus_two
        for i, at in enumerate((0, X - 1)):
            if x == at:
                xs[i, 6] = factor
                xs[i, 7] = minus_two
        pack(6, x, factor, tiles)
        pack(7, x, minus_two, tiles)

    def elastic(x, tiles):
        own = pl.ds(x * Y, Y)
        for k in range(6):
            part = el[k, own, :] - ev[k, own, :]
            el[k, own, :] = part
            for i, at in enumerate((0, X - 1)):
                if x == at:
                    xs[i, k] = part
            pack(k, x, part, tiles)

    ends = sorted({0, X - 1})
    inner = [x for x in range(X) if x not in ends]
    prefix(ends)
    for x in ends:
        strain(x)
    take(in_sem.at[2], 12 * Y + 2 * N)
    for x in ends:
        elastic(x, tiles)
        factors(x, tiles)
    start(lowers, ("xs",))

    tile0 = plane
    for x in range(X):
        for c in range(3):
            q = c * X + x
            tile = pltpu.roll(uv[c, pl.ds(Y + x * Y, Y), :], (2 * q + 1) % Z, 1)
            tile0 = jnp.where(pair == q, tile, tile0)
    zu[0, pl.ds(0, Y), :] = tile0
    start(lowers, ("zu",))
    tile = row_plane
    pair_x = lax.broadcasted_iota(jnp.int32, (X, Z), 1) >> 1
    for i, line in enumerate((0, Y - 1)):
        for c in range(3):
            p = 3 * i + c
            lines = uv[c, pl.ds(Y + line, X, stride=Y), :]
            if i:
                yu[c] = lines
            tile = jnp.where(pair_x == p, pltpu.roll(lines, (2 * p + 1) % Z, 1), tile)
            for j, at in enumerate((0, X - 1)):
                xy[j, i, pl.ds(c, 1), :] = uv[c, pl.ds(Y + at * Y + line, 1), :]
    zu[1, pl.ds(0, X), :] = tile

    start(lowers, ("yz",))

    prefix(inner)
    tile = plane
    for x in range(X):
        tile = jnp.where(pair == x, tot[pl.ds(x * Y, Y), :], tile)
    zt[...] = tile
    for i, (at, line) in enumerate(((0, 0), (X - 1, Y - 1))):
        xt[i] = tot[pl.ds(at * Y, Y), :]
        yt[i] = tot[pl.ds(line, X, stride=Y), :]

    for x in inner:
        strain(x)
    loads[6].wait()
    for x in inner:
        elastic(x, tiles)
        factors(x, tiles)
    for k in range(2):
        zs[k] = tiles[k]
    start(lowers, ("zs", "t", "tx", "ty"))
    for i, line in enumerate((0, Y - 1)):
        for k in range(8):
            src = el.at[k] if k < 6 else (av, nt)[k - 6]
            ys[i, k] = src[pl.ds(line, X, stride=Y), :]
    start(lowers, ("ys",))

    near = [o for o in uppers if sum(o) == 1]
    for o in sorted(near):
        @pl.when(has[o])
        def _(o=o):
            pl.semaphore_wait(ready.at[ready_index(o)], 1)

    for o in mixed:
        low, high = split(o)
        if high in near and minus(low) in near:
            announce(o)
    near.sort()
    start(near, ("zu", "yu", "xu", "t", "zs"))
    others = [o for o in uppers if o not in near]
    far = [o for o in mixed if split(o)[1] not in near or minus(split(o)[0]) not in near]
    close = sorted((o for o in mixed if o not in far), key=lambda o: (abs(o[0]), abs(o[2])))

    diagonal = ("xy", "xz", "yz", "t", "tx", "ty")

    def hear(offsets_in, sem):
        number = sum(has[o].astype(jnp.int32) for o in offsets_in)

        @pl.when(number > 0)
        def _():
            pl.semaphore_wait(sem, number)

        start(offsets_in, diagonal)

    hear(close, told.at[0])
    start(near, ("ys", "xs"))
    hear(others, ready.at[3])
    for o in far:
        announce(o)
    if far:
        hear(far, told.at[1])

    arrive("yu")
    for side, line in enumerate((0, Y - 1)):
        sign = 2.0 * side - 1.0

        @pl.when(has[faces[1][side]])
        def _(side=side, sign=sign, line=line):
            own = pl.ds(line, X, stride=Y)
            for c, (part, factor) in enumerate(TERMS[1]):
                el[part, own, :] = el[part, own, :] + (sign * factor) * ryu[side, c]

    arrive("zu")
    carried = plane
    for d in depths:
        carried = carried + rt[d - 1]
    merged = merge(rzu[0], rzu[1])

    def advance(x):
        own = pl.ds(x * Y, Y)
        e = [el[c, own, :] for c in range(6)]
        for c, (part, factor) in enumerate(TERMS[2]):
            e[part] = e[part] + (2.0 * factor) * edge_term(merged, c * X + x, z_edge)
        load = jnp.broadcast_to(carried[:, 2 * x:2 * x + 1], (Y, Z))
        trace, change = flow(e, av[own, :] * jnp.exp(load * nt[own, :]))
        for c in range(6):
            fv[c, own, :] = ev[c, own, :] + change[c]
            sp[c, pl.ds(Y + x * Y, Y), :] = stress(e, change, trace, c)

    for x in range(X):
        if x not in ends:
            advance(x)
    arrive("xu")
    for side, at in enumerate((0, X - 1)):
        sign = 2.0 * side - 1.0

        @pl.when(has[faces[0][side]])
        def _(side=side, sign=sign, at=at):
            own = pl.ds(at * Y, Y)
            for c, (part, factor) in enumerate(TERMS[0]):
                el[part, own, :] = el[part, own, :] + (sign * factor) * rxu[side, c]

    for x in ends:
        advance(x)

    for x in range(X):
        base = Y + x * Y
        own = pl.ds(x * Y, Y)
        for c in range(3):
            cx, cy, cz = X_SET[c], Y_SET[c], Z_SET[c]
            here = sp[cz, pl.ds(base, Y), :]
            total = (sp[cx, pl.ds(base + Y, Y), :] - sp[cx, pl.ds(base - Y, Y), :]) * 0.5
            total = total + (
                sp[cy, pl.ds(base + 1, Y), :] * not_last - sp[cy, pl.ds(base - 1, Y), :] * not_first
            )
            total = total + (pltpu.roll(here, Z - 1, 1) * z_last - pltpu.roll(here, 1, 1) * z_first)
            if c == 2:
                total = total - 0.5 * rv[own, :]
            mv[c, own, :] = total

    def add(e, axis, factor, values):
        for c, (part, f) in enumerate(TERMS[axis]):
            e[part] = e[part] + (factor * f) * values[c]

    def ends_of(first, last, rows, count):
        return jnp.where(rows == 0, -first, jnp.where(rows == count - 1, last, 0.0))

    arrive("xy", "yz", "xz", "ys", "zs", "xs")

    def beyond(axis, side, part):
        got, load, e = part
        trace, change = flow(e, got[6] * jnp.exp(load * got[7]))
        there = has[faces[axis][side]]
        return [
            (side - 0.5) * jnp.where(there, stress(e, change, trace, k), 0.0) for k in (X_SET, Y_SET)[axis]
        ]

    along_y = []
    for side, line in enumerate((0, Y - 1)):
        e = [rys[side, k] for k in range(6)]
        add(e, 1, 1.0 - 2.0 * side, [uv[c, pl.ds(Y + line, X, stride=Y), :] for c in range(3)])
        add(e, 0, 1.0, [
            ends_of(rxy[0, side, pl.ds(c, 1), :], rxy[1, side, pl.ds(c, 1), :], row_x, X) for c in range(3)
        ])
        joined = merge(ryz[side, 0, 1, pl.ds(0, X), :], ryz[side, 1, 1, pl.ds(0, X), :])
        add(e, 2, 2.0, [edge_term(joined, 3 * (1 - side) + c, z_edge_x) for c in range(3)])
        load = row_plane
        for d in depths:
            load = load + rty[side, d - 1]
        along_y.append(beyond(1, side, (rys[side], load, e)))

    along_x = []
    for side, at in enumerate((0, X - 1)):
        e = [rxs[side, k] for k in range(6)]
        add(e, 0, 1.0 - 2.0 * side, [uv[c, pl.ds(Y + at * Y, Y), :] for c in range(3)])
        add(e, 1, 1.0, [
            ends_of(rxy[side, 0, pl.ds(c, 1), :], rxy[side, 1, pl.ds(c, 1), :], row, Y) for c in range(3)
        ])
        add(e, 2, 1.0, [
            jnp.where(
                lane == 0, -pltpu.roll(rxz[side, 0, c], 1, 1),
                jnp.where(lane == Z - 1, pltpu.roll(rxz[side, 1, c], Z - 1, 1), 0.0),
            )
            for c in range(3)
        ])
        load = plane
        for d in depths:
            load = load + rtx[side, d - 1]
        along_x.append(beyond(0, side, (rxs[side], load, e)))

    block = 2 * X

    def shift(tile, by):
        return pltpu.roll(tile, by % Z, 1) if by % Z else tile

    halo = [jnp.where(even, rzs[0, k], rzs[1, k]) for k in range(2)]
    parts = [shift(halo[k // 4], -(k % 4) * block) for k in range(8)]
    mine = zu[0, pl.ds(0, Y), :]
    from_z = jnp.where(even, shift(mine, -1), -shift(mine, 1))
    from_x = []
    for c in range(3):
        left, right = (jnp.where(lane == Z - 1, rxz[i, 0, c], rxz[i, 1, c]) for i in range(2))
        from_x.append(jnp.where(
            pair == 0, -shift(left, 1), jnp.where(pair == X - 1, shift(right, 2 * X - 1), 0.0)
        ))
    even_row = (lax.broadcasted_iota(jnp.int32, (1, Z), 1) & 1) == 0
    from_y = ends_of(
        jnp.where(even_row, ryz[0, 0, 0, pl.ds(Y - 1, 1), :], ryz[0, 1, 0, pl.ds(Y - 1, 1), :]),
        jnp.where(even_row, ryz[1, 0, 0, pl.ds(0, 1), :], ryz[1, 1, 0, pl.ds(0, 1), :]),
        row, Y,
    )
    e = list(parts[:6])
    add(e, 0, 1.0, from_x)
    for axis, tile in ((1, from_y), (2, from_z)):
        add(e, axis, 1.0, [shift(tile, -c * block) for c in range(3)])
    deeper = plane
    for d in depths:
        if d >= 2:
            deeper = deeper + rt[d - 1]
    load = jnp.where(even, deeper, carried + zt[...])
    trace, change = flow(e, parts[6] * jnp.exp(load * parts[7]))
    known = jnp.where(
        even,
        has[0, 0, -1].astype(jnp.float32),
        has[0, 0, 1].astype(jnp.float32),
    )
    gathered = plane
    for c in range(3):
        tile = shift(stress(e, change, trace, Z_SET[c]) * known, c * block)
        gathered = jnp.where((pair >= c * X) & (pair < (c + 1) * X), tile, gathered)
    jv[...] = jnp.where(even, gathered, shift(gathered, -2))

    for c in range(3):
        for side, at in enumerate((0, X - 1)):
            own = pl.ds(at * Y, Y)
            mv[c, own, :] = mv[c, own, :] + along_x[side][c]
        for side, line in enumerate((0, Y - 1)):
            own = pl.ds(line, X, stride=Y)
            mv[c, own, :] = mv[c, own, :] + along_y[side][c]

    for i, departure in enumerate(departures):
        settle(send_sem.at[i], *departure)


def finish(dims, fv, mv, jv, f_hbm, m_hbm, ms, sem):
    X, Y, Z = dims
    copies = [pltpu.make_async_copy(fv, f_hbm, sem.at[0])]
    copies[0].start()
    lane = lax.broadcasted_iota(jnp.int32, (Y, Z), 1)
    z_edge = jnp.where(lane == 0, -0.5, jnp.where(lane == Z - 1, 0.5, 0.0)).astype(jnp.float32)
    joined = jv[...]
    groups = 4
    span = X // groups
    for g in range(groups):
        for x in range(g * span, (g + 1) * span):
            own = pl.ds(x * Y, Y)
            for c in range(3):
                ms[c, own, :] = mv[c, own, :] + edge_term(joined, c * X + x, z_edge)
        rows = pl.ds(g * span * Y, span * Y)
        copies.append(pltpu.make_async_copy(ms.at[:, rows, :], m_hbm.at[:, rows, :], sem.at[1 + g]))
        copies[-1].start()
    for copy in copies:
        copy.wait()


def shards(sizes, u, e, t, r, b):
    X, Y, Z = t.shape
    N = X * Y
    layers = sizes[2]
    assert 8 * X <= Z and Z % 128 == 0 and Y % 8 == 0 and X % 8 == 0
    W = max(X, Y)
    f32 = jnp.float32
    vmem = pltpu.VMEM
    dma = pltpu.SemaphoreType.DMA
    any_space = pl.BlockSpec(memory_space=pl.ANY)
    in_vmem = pl.BlockSpec(memory_space=vmem)
    D = max(layers - 1, 1)
    kept = pl.pallas_call(
        functools.partial(kernel, (X, Y, Z), sizes),
        out_shape=(vmem((6, N, Z), f32), vmem((3, N, Z), f32), vmem((Y, Z), f32)),
        in_specs=[any_space] * 6,
        out_specs=(in_vmem,) * 3,
        scratch_shapes=[
            vmem((3, N + 2 * Y, Z), f32),
            vmem((Z, 2 * Z), jnp.bfloat16),
            vmem((6, N, Z), f32),
            vmem((N, Z), f32),
            vmem((N, Z), f32),
            vmem((N, Z), jnp.int32),
            vmem((N, Z), f32),
            vmem((N, Z), f32),
            vmem((6, N, Z), f32),
            vmem((N, Z), f32),
            vmem((N, Z), f32),
            vmem((6, N + 2 * Y, Z), f32),
            vmem((2, 8, Y, Z), f32),
            vmem((2, 8, X, Z), f32),
            vmem((3, X, Z), f32),
            vmem((2, W, Z), f32),
            vmem((2, Y, Z), f32),
            vmem((2, 2, 8, Z), f32),
            vmem((Y, Z), f32),
            vmem((2, Y, Z), f32),
            vmem((2, X, Z), f32),
            vmem((2, 3, Y, Z), f32),
            vmem((2, 8, Y, Z), f32),
            vmem((2, 3, X, Z), f32),
            vmem((2, 8, X, Z), f32),
            vmem((2, Y, Z), f32),
            vmem((2, 2, Y, Z), f32),
            vmem((2, 2, 8, Z), f32),
            vmem((2, 2, 3, Y, Z), f32),
            vmem((2, 2, 2, W, Z), f32),
            vmem((D, Y, Z), f32),
            vmem((2, D, Y, Z), f32),
            vmem((2, D, X, Z), f32),
            dma((4,)),
            pltpu.SemaphoreType.REGULAR((4,)),
            pltpu.SemaphoreType.REGULAR((1 if layers == 2 else 2,)),
            dma((6,)),
            dma((9,)),
        ],
        compiler_params=pltpu.CompilerParams(collective_id=0, has_side_effects=True),
        name="strain_step",
    )(u.reshape(3, N, Z), u, e.reshape(6, N, Z), t.reshape(N, Z), r.reshape(N, Z), b.reshape(N, Z))
    f, m = pl.pallas_call(
        functools.partial(finish, (X, Y, Z)),
        out_shape=(jax.ShapeDtypeStruct((6, N, Z), f32), jax.ShapeDtypeStruct((3, N, Z), f32)),
        in_specs=[in_vmem] * 3,
        out_specs=(any_space, any_space),
        scratch_shapes=[vmem((3, N, Z), f32), dma((5,))],
        name="finish",
    )(*(pltpu.with_memory_space_constraint(k, vmem) for k in kept))
    return f.reshape(6, X, Y, Z), m.reshape(3, X, Y, Z)


def solution(mesh):
    sizes = tuple(mesh.shape[a] for a in AXES)
    field = P("gx", "gy", "gz")
    fields = P(None, "gx", "gy", "gz")
    return jax.shard_map(
        functools.partial(shards, sizes),
        mesh=mesh,
        in_specs=(fields, fields, field, field, field),
        out_specs=(fields, fields),
        check_vma=False,
    )
```

```python
import functools

import jax
import jax.numpy as jnp
from jax import lax
from jax.experimental import pallas as pl
from jax.experimental.pallas import tpu as pltpu
from jax.sharding import PartitionSpec as P

MESH = pl.DeviceIdType.MESH
AXES = ("gx", "gy", "gz")
TERMS = (
    ((0, 0.5), (3, 0.25), (4, 0.25)),
    ((3, 0.25), (1, 0.5), (5, 0.25)),
    ((4, 0.25), (5, 0.25), (2, 0.5)),
)
X_SET = (0, 3, 4)
Y_SET = (3, 1, 5)
Z_SET = (4, 5, 2)


def offsets(layers):
    near = [
        (x, y, z)
        for x in (-1, 0, 1)
        for y in (-1, 0, 1)
        for z in (-1, 0, 1)
        if 1 <= abs(x) + abs(y) + abs(z) <= 2
    ]
    far = [
        (x, y, s * d)
        for d in range(2, layers)
        for s in (-1, 1)
        for x, y in ((0, 0), (-1, 0), (1, 0), (0, -1), (0, 1))
    ]
    return near + far


def minus(o):
    return tuple(-v for v in o)


def plus(o, p):
    return tuple(v + w for v, w in zip(o, p))


def split(o):
    return tuple(min(v, 0) for v in o), tuple(max(v, 0) for v in o)


def kinds_of(layers):
    offs = offsets(layers)
    uppers = [o for o in offs if min(o) >= 0]
    lowers = [o for o in offs if max(o) <= 0]
    mixed = [o for o in offs if min(o) < 0 < max(o)]
    return uppers, lowers, mixed


def merge(low, high):
    Z = low.shape[1]
    even = (lax.broadcasted_iota(jnp.int32, low.shape, 1) & 1) == 0
    return jnp.where(even, low, pltpu.roll(high, Z - 2, 1))


def edge_term(tile, q, z_edge):
    Z = tile.shape[1]
    return (pltpu.roll(tile, (Z - 2 * q) % Z, 1) if q else tile) * z_edge


def flow(e, pace):
    trace = e[0] + e[1] + e[2]
    third = trace * (1.0 / 3.0)
    half = [e[0] - third, e[1] - third, e[2] - third, e[3], e[4], e[5]]
    second = half[0] * half[0] + half[1] * half[1] + half[2] * half[2]
    second = second + 2.0 * (half[3] * half[3] + half[4] * half[4] + half[5] * half[5])
    rate = pace * second
    return trace, [rate * h for h in half]


def stress(e, change, trace, part):
    out = 2.0 * (e[part] - change[part])
    return out + trace if part < 3 else out


def kernel(
    dims, sizes,
    u_hbm, u_rows, e_hbm, t_hbm, r_hbm, b_hbm,
    fv, mv, jv,
    uv, tri, ev, tv, rv, bv, pv, tot, el, av, nt, sp,
    xs, ys, yu, zu, zs, xy, zt, xt, yt,
    rxu, rxs, ryu, rys, rzu, rzs, rxy, rxz, ryz, rt, rtx, rty,
    in_sem, ready, told, send_sem, recv_sem,
):
    X, Y, Z = dims
    N = X * Y
    layers = sizes[2]
    depths = range(1, layers)
    me = [lax.axis_index(a) for a in AXES]
    offs = offsets(layers)
    uppers, lowers, mixed = kinds_of(layers)
    W = max(X, Y)

    def ready_index(o):
        return 0 if sum(o) == 1 else 1

    def exists(o):
        ok = None
        for a in range(3):
            if o[a]:
                here = me[a] + o[a]
                test = here < sizes[a] if o[a] > 0 else here >= 0
                ok = test if ok is None else jnp.logical_and(ok, test)
        return ok

    def partner(o):
        return {AXES[a]: me[a] + o[a] for a in range(3) if o[a]}

    has = {o: exists(o) for o in offs}
    faces = {a: [tuple(s if i == a else 0 for i in range(3)) for s in (-1, 1)] for a in range(3)}

    loads = [
        pltpu.make_async_copy(src, dst, in_sem.at[0 if i < 2 else 1 if i < 6 else 2])
        for i, (src, dst) in enumerate(
            (
                (u_hbm, uv.at[:, pl.ds(Y, N), :]),
                (r_hbm, rv),
                (e_hbm.at[:, pl.ds(0, Y), :], ev.at[:, pl.ds(0, Y), :]),
                (e_hbm.at[:, pl.ds(N - Y, Y), :], ev.at[:, pl.ds(N - Y, Y), :]),
                (t_hbm, tv),
                (b_hbm, bv),
                (e_hbm.at[:, pl.ds(Y, N - 2 * Y), :], ev.at[:, pl.ds(Y, N - 2 * Y), :]),
            )
        )
    ]
    for copy in loads:
        copy.start()

    def take(sem, rows):
        whole = [k for k in range(1, 7) if rows % (8 * k) == 0 and rows // k <= N + 2 * Y]
        planes = whole[0] if whole else rows // 3
        spot = sp.at[pl.ds(0, planes), pl.ds(0, rows // planes)]
        pltpu.make_async_copy(spot, spot, sem).wait()

    barrier = pltpu.get_barrier_semaphore()
    for o in uppers:
        @pl.when(has[o])
        def _(o=o):
            pl.semaphore_signal(barrier, inc=1, device_id=partner(o), device_id_type=MESH)
    expected = jnp.int32(0)
    for o in lowers:
        expected = expected + has[o].astype(jnp.int32)

    plane = jnp.zeros((Y, Z), jnp.float32)
    row_plane = jnp.zeros((X, Z), jnp.float32)
    for c in range(3):
        uv[c, pl.ds(0, Y), :] = plane
        uv[c, pl.ds(Y + N, Y), :] = plane
    for c in range(6):
        sp[c, pl.ds(0, Y), :] = plane
        sp[c, pl.ds(Y + N, Y), :] = plane

    def blank(o, *refs):
        @pl.when(jnp.logical_not(has[o]))
        def _():
            for ref in refs:
                ref[...] = jnp.zeros(ref.shape, jnp.float32)

    for i, sz in enumerate((-1, 1)):
        blank((0, 0, sz), rzu.at[i], rzs.at[i])
        for j, s in enumerate((-1, 1)):
            blank((s, 0, sz), rxz.at[j, i])
            blank((0, s, sz), ryz.at[j, i])
    for i, sx in enumerate((-1, 1)):
        for j, sy in enumerate((-1, 1)):
            blank((sx, sy, 0), rxy.at[i, j])
    for d in depths:
        blank((0, 0, -d), rt.at[d - 1])
        for j, s in enumerate((-1, 1)):
            blank((s, 0, -d), rtx.at[j, d - 1])
            blank((0, s, -d), rty.at[j, d - 1])

    above_row = lax.broadcasted_iota(jnp.int32, (Z, 2 * Z), 0)
    column = lax.broadcasted_iota(jnp.int32, (Z, 2 * Z), 1)
    triangle = jnp.where(
        (above_row < column) | (column >= Z),
        1.0,
        jnp.where(above_row == column, 0.5, 0.0),
    ).astype(jnp.bfloat16)
    tri[...] = triangle

    lane = lax.broadcasted_iota(jnp.int32, (Y, Z), 1)
    row = lax.broadcasted_iota(jnp.int32, (Y, Z), 0)
    pair = lane >> 1
    even = (lane & 1) == 0
    not_last = jnp.where(row < Y - 1, 0.5, 0.0).astype(jnp.float32)
    not_first = jnp.where(row > 0, 0.5, 0.0).astype(jnp.float32)
    z_first = jnp.where(lane > 0, 0.5, 0.0).astype(jnp.float32)
    z_last = jnp.where(lane < Z - 1, 0.5, 0.0).astype(jnp.float32)
    z_edge = jnp.where(lane == 0, -0.5, jnp.where(lane == Z - 1, 0.5, 0.0)).astype(jnp.float32)
    if X == Y:
        row_x, z_edge_x = row, z_edge
    else:
        lane_x = lax.broadcasted_iota(jnp.int32, (X, Z), 1)
        row_x = lax.broadcasted_iota(jnp.int32, (X, Z), 0)
        z_edge_x = jnp.where(lane_x == 0, -0.5, jnp.where(lane_x == Z - 1, 0.5, 0.0)).astype(jnp.float32)

    beside = [sum(has[o].astype(jnp.int32) for o in faces[a]) for a in range(3)]
    above, below = me[2], layers - 1 - me[2]

    def products(*ranges):
        values = {1}
        for r in ranges:
            values = {v * w for v in values for w in r}
        return sorted(values - {0})

    some, any_depth = (1, 2), range(layers)
    four = products(some, some)
    arrivals = {
        "xu": (3 * Y, beside[0], some),
        "xs": (Y, beside[0] * (8 + above), products(some, [8 + d for d in any_depth])),
        "yu": (3 * X, beside[1], some),
        "ys": (X, beside[1] * (8 + above), products(some, [8 + d for d in any_depth])),
        "zu": (Y, beside[2] + above, sorted({n + d for n in some for d in any_depth})),
        "zs": (2 * Y, beside[2], some),
        "xy": (3, beside[0] * beside[1], four),
        "xz": (3 * Y, beside[0] * beside[2], four),
        "yz": (2 * W, beside[1] * beside[2], four),
    }
    departures = (
        (Y, beside[0] * (11 + below), products(some, [11 + d for d in any_depth])),
        (X, beside[1] * (11 + below), products(some, [11 + d for d in any_depth])),
        (Y, 3 * beside[2] + below, sorted({3 * n + d for n in some for d in any_depth})),
        arrivals["xy"], arrivals["xz"], arrivals["yz"],
    )
    recv_index = {kind: i for i, kind in enumerate(arrivals)}
    recv_index |= {"tx": recv_index["xs"], "ty": recv_index["ys"], "t": recv_index["zu"]}
    send_index = {
        "xu": 0, "xs": 0, "tx": 0, "yu": 1, "ys": 1, "ty": 1, "zu": 2, "zs": 2, "t": 2, "xy": 3, "xz": 4, "yz": 5,
    }
    sent = [send_sem.at[0], send_sem.at[1], in_sem.at[0], send_sem.at[2], send_sem.at[3], send_sem.at[4]]
    sends = {o: [] for o in offs}

    def message(kind, o, src, dst):
        sends[o].append((kind, pltpu.make_async_remote_copy(
            src_ref=src, dst_ref=dst,
            send_sem=sent[send_index[kind]], recv_sem=recv_sem.at[recv_index[kind]],
            device_id=partner(o), device_id_type=MESH,
        )))

    for i, s in enumerate((-1, 1)):
        k = 1 - i
        at = (Y, Y * X)[i]
        strike = u_hbm.at[:, pl.ds((0, N - Y)[i], Y), :] if s < 0 else uv.at[:, pl.ds(at, Y), :]
        message("xu", (s, 0, 0), strike, rxu.at[k])
        message("xs", (s, 0, 0), xs.at[i], rxs.at[k])
        message("yu", (0, s, 0), u_rows.at[:, :, 0, :] if s < 0 else yu, ryu.at[k])
        message("ys", (0, s, 0), ys.at[i], rys.at[k])
        message("zu", (0, 0, s), zu.at[0, pl.ds(0, Y)], rzu.at[k])
        message("zs", (0, 0, s), zs, rzs.at[k])
        for j, s2 in enumerate((-1, 1)):
            m = 1 - j
            lines = xy.at[i, j, pl.ds(0, 3), :] if s + s2 >= 0 else u_rows.at[:, 0, 0, :]
            message("xy", (s, s2, 0), lines, rxy.at[k, m, pl.ds(0, 3), :])
            strike = u_hbm.at[:, pl.ds(0, Y), :] if s + s2 < 0 else uv.at[:, pl.ds(at, Y), :]
            message("xz", (s, 0, s2), strike, rxz.at[k, m])
            message("yz", (0, s, s2), zu, ryz.at[k, m])
        for d in depths:
            message("tx", (s, 0, d), xt.at[i], rtx.at[k, d - 1])
            message("ty", (0, s, d), yt.at[i], rty.at[k, d - 1])
    for d in depths:
        message("t", (0, 0, d), zt, rt.at[d - 1])

    def settle(sem, rows, count, values):
        for n in values:
            @pl.when(count == n)
            def _(n=n):
                take(sem, n * rows)

    def start(offsets_in, kinds):
        for o in offsets_in:
            chosen = [copy for kind, copy in sends[o] if kind in kinds]
            if chosen:
                @pl.when(has[o])
                def _(chosen=chosen):
                    for copy in chosen:
                        copy.start()

    def arrive(*kinds):
        for kind in kinds:
            settle(recv_sem.at[recv_index[kind]], *arrivals[kind])

    @pl.when(expected > 0)
    def _():
        pl.semaphore_wait(barrier, expected)

    for o in lowers:
        @pl.when(has[o])
        def _(o=o):
            pl.semaphore_signal(
                ready.at[ready_index(minus(o))], inc=1, device_id=partner(o), device_id_type=MESH
            )

    def announce(o):
        low, high = split(o)

        @pl.when(jnp.logical_and(has[minus(low)], has[high]))
        def _():
            kind = 0 if max(high) == 1 and min(low) == -1 else 1
            pl.semaphore_signal(told.at[kind], inc=1, device_id=partner(minus(low)), device_id_type=MESH)

    lowers = sorted(lowers, key=lambda o: (sum(map(abs, o)), o[2], o[1]))
    for kind in ("xz", "yu", "xy", "xu"):
        start(lowers, (kind,))

    take(in_sem.at[0], 4 * N)
    total_depth = Z * layers
    depth = (me[2] * Z + lane).astype(jnp.float32)
    scale = (1.0 + 2.0 * depth / total_depth) / total_depth

    def prefix(planes):
        thirds = [[], [], []]
        for x in planes:
            rest = rv[pl.ds(x * Y, Y), :] * scale
            for k in range(3):
                piece = rest.astype(jnp.bfloat16)
                thirds[k].append(piece)
                rest = rest - piece.astype(jnp.float32)
        weight = jnp.concatenate([jnp.concatenate(k, axis=0) for k in thirds], axis=1)
        triangle = jnp.concatenate([tri[...]] * 3, axis=0)
        sums = jnp.dot(weight, triangle, preferred_element_type=jnp.float32)
        for i, x in enumerate(planes):
            pv[pl.ds(x * Y, Y), :] = sums[i * Y:(i + 1) * Y, :Z] + 1.0
            tot[pl.ds(x * Y, Y), :] = sums[i * Y:(i + 1) * Y, Z:]

    def strain(x):
        base = Y + x * Y
        own = pl.ds(x * Y, Y)
        grad = []
        for c in range(3):
            here = uv[c, pl.ds(base, Y), :]
            grad.append((
                (uv[c, pl.ds(base + Y, Y), :] - uv[c, pl.ds(base - Y, Y), :]) * 0.5,
                uv[c, pl.ds(base + 1, Y), :] * not_last - uv[c, pl.ds(base - 1, Y), :] * not_first,
                pltpu.roll(here, Z - 1, 1) * z_last - pltpu.roll(here, 1, 1) * z_first,
            ))
        el[0, own, :] = grad[0][0]
        el[1, own, :] = grad[1][1]
        el[2, own, :] = grad[2][2]
        el[3, own, :] = 0.5 * (grad[0][1] + grad[1][0])
        el[4, own, :] = 0.5 * (grad[0][2] + grad[2][0])
        el[5, own, :] = 0.5 * (grad[1][2] + grad[2][1])

    def pack(k, x, part, tiles):
        q = (k % 4) * X + x
        tile = pltpu.roll(part, (2 * q + 1) % Z, 1)
        tiles[k // 4] = jnp.where(pair == q, tile, tiles[k // 4])

    def factors(x, tiles):
        own = pl.ds(x * Y, Y)
        minus_two = -2.0 / tv[own, :]
        factor = (2.0 + 14.0 * bv[own, :].astype(jnp.float32)) * jnp.exp(pv[own, :] * minus_two)
        av[own, :] = factor
        nt[own, :] = minus_two
        for i, at in enumerate((0, X - 1)):
            if x == at:
                xs[i, 6] = factor
                xs[i, 7] = minus_two
        if tiles:
            pack(6, x, factor, tiles)
            pack(7, x, minus_two, tiles)

    def elastic(x, tiles):
        own = pl.ds(x * Y, Y)
        for k in range(6):
            part = el[k, own, :] - ev[k, own, :]
            el[k, own, :] = part
            for i, at in enumerate((0, X - 1)):
                if x == at:
                    xs[i, k] = part
            if tiles:
                pack(k, x, part, tiles)

    ends = sorted({0, X - 1})
    inner = [x for x in range(X) if x not in ends]

    def pack_displacement():
        tile0 = plane
        for x in range(X):
            for c in range(3):
                q = c * X + x
                tile = pltpu.roll(uv[c, pl.ds(Y + x * Y, Y), :], (2 * q + 1) % Z, 1)
                tile0 = jnp.where(pair == q, tile, tile0)
        zu[0, pl.ds(0, Y), :] = tile0

    def lines_along_depth():
        tile = row_plane
        pair_x = lax.broadcasted_iota(jnp.int32, (X, Z), 1) >> 1
        for i, line in enumerate((0, Y - 1)):
            for c in range(3):
                p = 3 * i + c
                lines = uv[c, pl.ds(Y + line, X, stride=Y), :]
                if i:
                    yu[c] = lines
                tile = jnp.where(pair_x == p, pltpu.roll(lines, (2 * p + 1) % Z, 1), tile)
                for j, at in enumerate((0, X - 1)):
                    xy[j, i, pl.ds(c, 1), :] = uv[c, pl.ds(Y + at * Y + line, 1), :]
        zu[1, pl.ds(0, X), :] = tile

    def total_tiles():
        tile = plane
        for x in range(X):
            tile = jnp.where(pair == x, tot[pl.ds(x * Y, Y), :], tile)
        zt[...] = tile
        for i, (at, line) in enumerate(((0, 0), (X - 1, Y - 1))):
            xt[i] = tot[pl.ds(at * Y, Y), :]
            yt[i] = tot[pl.ds(line, X, stride=Y), :]

    def along_dip():
        for i, line in enumerate((0, Y - 1)):
            for k in range(8):
                src = el.at[k] if k < 6 else (av, nt)[k - 6]
                ys[i, k] = src[pl.ds(line, X, stride=Y), :]
        start(lowers, ("ys",))

    @pl.when(above == 0)
    def _():
        prefix(ends)
        for x in ends:
            strain(x)
        take(in_sem.at[1], 12 * Y + 2 * N)
        for x in ends:
            elastic(x, None)
            factors(x, None)
        start(lowers, ("xs",))
        prefix(inner)
        for x in inner:
            strain(x)
        loads[6].wait()
        for x in inner:
            elastic(x, None)
            factors(x, None)
        along_dip()
        pack_displacement()
        lines_along_depth()
        total_tiles()
        tiles = [plane, plane]
        for x in range(X):
            for k in range(8):
                src = el.at[k] if k < 6 else (av, nt)[k - 6]
                pack(k, x, src[pl.ds(x * Y, Y), :], tiles)
        for k in range(2):
            zs[k] = tiles[k]

    @pl.when(above > 0)
    def _():
        pack_displacement()
        start(lowers, ("zu",))
        lines_along_depth()
        start(lowers, ("yz",))
        prefix(range(X))
        total_tiles()
        for x in range(X):
            strain(x)
        take(in_sem.at[1], 12 * Y + 2 * N)
        tiles = [plane, plane]
        for x in ends:
            elastic(x, tiles)
            factors(x, tiles)
        start(lowers, ("xs",))
        loads[6].wait()
        for x in inner:
            elastic(x, tiles)
            factors(x, tiles)
        for k in range(2):
            zs[k] = tiles[k]
        start(lowers, ("zs", "t", "tx", "ty"))
        along_dip()

    near = [o for o in uppers if sum(o) == 1]
    number = sum(has[o].astype(jnp.int32) for o in near)

    @pl.when(number > 0)
    def _():
        pl.semaphore_wait(ready.at[0], number)

    for o in mixed:
        low, high = split(o)
        if high in near and minus(low) in near:
            announce(o)
    near.sort()
    start(near, ("zu", "yu", "xu", "t", "zs"))
    others = [o for o in uppers if o not in near]
    far = [o for o in mixed if split(o)[1] not in near or minus(split(o)[0]) not in near]
    close = sorted((o for o in mixed if o not in far), key=lambda o: (abs(o[0]), abs(o[2])))

    diagonal = ("xy", "xz", "yz", "t", "tx", "ty")

    def hear(offsets_in, sem):
        number = sum(has[o].astype(jnp.int32) for o in offsets_in)

        @pl.when(number > 0)
        def _():
            pl.semaphore_wait(sem, number)

        start(offsets_in, diagonal)

    hear(close, told.at[0])
    start(near, ("ys", "xs"))
    hear(others, ready.at[1])
    for o in far:
        announce(o)
    if far:
        hear(far, told.at[1])

    arrive("yu")
    for side, line in enumerate((0, Y - 1)):
        sign = 2.0 * side - 1.0

        @pl.when(has[faces[1][side]])
        def _(side=side, sign=sign, line=line):
            own = pl.ds(line, X, stride=Y)
            for c, (part, factor) in enumerate(TERMS[1]):
                el[part, own, :] = el[part, own, :] + (sign * factor) * ryu[side, c]

    arrive("zu")
    carried = plane
    for d in depths:
        carried = carried + rt[d - 1]
    merged = merge(rzu[0], rzu[1])

    def advance(x):
        own = pl.ds(x * Y, Y)
        e = [el[c, own, :] for c in range(6)]
        for c, (part, factor) in enumerate(TERMS[2]):
            e[part] = e[part] + (2.0 * factor) * edge_term(merged, c * X + x, z_edge)
        load = jnp.broadcast_to(carried[:, 2 * x:2 * x + 1], (Y, Z))
        trace, change = flow(e, av[own, :] * jnp.exp(load * nt[own, :]))
        for c in range(6):
            fv[c, own, :] = ev[c, own, :] + change[c]
            sp[c, pl.ds(Y + x * Y, Y), :] = stress(e, change, trace, c)

    for x in range(X):
        if x not in ends:
            advance(x)
    arrive("xu")
    for side, at in enumerate((0, X - 1)):
        sign = 2.0 * side - 1.0

        @pl.when(has[faces[0][side]])
        def _(side=side, sign=sign, at=at):
            own = pl.ds(at * Y, Y)
            for c, (part, factor) in enumerate(TERMS[0]):
                el[part, own, :] = el[part, own, :] + (sign * factor) * rxu[side, c]

    for x in ends:
        advance(x)

    for x in range(X):
        base = Y + x * Y
        own = pl.ds(x * Y, Y)
        for c in range(3):
            cx, cy, cz = X_SET[c], Y_SET[c], Z_SET[c]
            here = sp[cz, pl.ds(base, Y), :]
            total = (sp[cx, pl.ds(base + Y, Y), :] - sp[cx, pl.ds(base - Y, Y), :]) * 0.5
            total = total + (
                sp[cy, pl.ds(base + 1, Y), :] * not_last - sp[cy, pl.ds(base - 1, Y), :] * not_first
            )
            total = total + (pltpu.roll(here, Z - 1, 1) * z_last - pltpu.roll(here, 1, 1) * z_first)
            if c == 2:
                total = total - 0.5 * rv[own, :]
            mv[c, own, :] = total

    def add(e, axis, factor, values):
        for c, (part, f) in enumerate(TERMS[axis]):
            e[part] = e[part] + (factor * f) * values[c]

    def ends_of(first, last, rows, count):
        return jnp.where(rows == 0, -first, jnp.where(rows == count - 1, last, 0.0))

    arrive("xy", "yz", "xz", "ys", "zs", "xs")

    def beyond(axis, side, part):
        got, load, e = part
        trace, change = flow(e, got[6] * jnp.exp(load * got[7]))
        there = has[faces[axis][side]]
        return [
            (side - 0.5) * jnp.where(there, stress(e, change, trace, k), 0.0) for k in (X_SET, Y_SET)[axis]
        ]

    along_y = []
    for side, line in enumerate((0, Y - 1)):
        e = [rys[side, k] for k in range(6)]
        add(e, 1, 1.0 - 2.0 * side, [uv[c, pl.ds(Y + line, X, stride=Y), :] for c in range(3)])
        add(e, 0, 1.0, [
            ends_of(rxy[0, side, pl.ds(c, 1), :], rxy[1, side, pl.ds(c, 1), :], row_x, X) for c in range(3)
        ])
        joined = merge(ryz[side, 0, 1, pl.ds(0, X), :], ryz[side, 1, 1, pl.ds(0, X), :])
        add(e, 2, 2.0, [edge_term(joined, 3 * (1 - side) + c, z_edge_x) for c in range(3)])
        load = row_plane
        for d in depths:
            load = load + rty[side, d - 1]
        along_y.append(beyond(1, side, (rys[side], load, e)))

    along_x = []
    for side, at in enumerate((0, X - 1)):
        e = [rxs[side, k] for k in range(6)]
        add(e, 0, 1.0 - 2.0 * side, [uv[c, pl.ds(Y + at * Y, Y), :] for c in range(3)])
        add(e, 1, 1.0, [
            ends_of(rxy[side, 0, pl.ds(c, 1), :], rxy[side, 1, pl.ds(c, 1), :], row, Y) for c in range(3)
        ])
        add(e, 2, 1.0, [
            jnp.where(
                lane == 0, -pltpu.roll(rxz[side, 0, c], 1, 1),
                jnp.where(lane == Z - 1, pltpu.roll(rxz[side, 1, c], Z - 1, 1), 0.0),
            )
            for c in range(3)
        ])
        load = plane
        for d in depths:
            load = load + rtx[side, d - 1]
        along_x.append(beyond(0, side, (rxs[side], load, e)))

    block = 2 * X

    def shift(tile, by):
        return pltpu.roll(tile, by % Z, 1) if by % Z else tile

    halo = [jnp.where(even, rzs[0, k], rzs[1, k]) for k in range(2)]
    parts = [shift(halo[k // 4], -(k % 4) * block) for k in range(8)]
    mine = zu[0, pl.ds(0, Y), :]
    from_z = jnp.where(even, shift(mine, -1), -shift(mine, 1))
    from_x = []
    for c in range(3):
        left, right = (jnp.where(lane == Z - 1, rxz[i, 0, c], rxz[i, 1, c]) for i in range(2))
        from_x.append(jnp.where(
            pair == 0, -shift(left, 1), jnp.where(pair == X - 1, shift(right, 2 * X - 1), 0.0)
        ))
    even_row = (lax.broadcasted_iota(jnp.int32, (1, Z), 1) & 1) == 0
    from_y = ends_of(
        jnp.where(even_row, ryz[0, 0, 0, pl.ds(Y - 1, 1), :], ryz[0, 1, 0, pl.ds(Y - 1, 1), :]),
        jnp.where(even_row, ryz[1, 0, 0, pl.ds(0, 1), :], ryz[1, 1, 0, pl.ds(0, 1), :]),
        row, Y,
    )
    e = list(parts[:6])
    add(e, 0, 1.0, from_x)
    for axis, tile in ((1, from_y), (2, from_z)):
        add(e, axis, 1.0, [shift(tile, -c * block) for c in range(3)])
    deeper = plane
    for d in depths:
        if d >= 2:
            deeper = deeper + rt[d - 1]
    load = jnp.where(even, deeper, carried + zt[...])
    trace, change = flow(e, parts[6] * jnp.exp(load * parts[7]))
    known = jnp.where(
        even,
        has[0, 0, -1].astype(jnp.float32),
        has[0, 0, 1].astype(jnp.float32),
    )
    gathered = plane
    for c in range(3):
        tile = shift(stress(e, change, trace, Z_SET[c]) * known, c * block)
        gathered = jnp.where((pair >= c * X) & (pair < (c + 1) * X), tile, gathered)
    jv[...] = jnp.where(even, gathered, shift(gathered, -2))

    for c in range(3):
        for side, at in enumerate((0, X - 1)):
            own = pl.ds(at * Y, Y)
            mv[c, own, :] = mv[c, own, :] + along_x[side][c]
        for side, line in enumerate((0, Y - 1)):
            own = pl.ds(line, X, stride=Y)
            mv[c, own, :] = mv[c, own, :] + along_y[side][c]

    for i, departure in enumerate(departures):
        settle(sent[i], *departure)


def finish(dims, fv, mv, jv, f_hbm, m_hbm, ms, sem):
    X, Y, Z = dims
    copies = [pltpu.make_async_copy(fv, f_hbm, sem.at[0])]
    copies[0].start()
    lane = lax.broadcasted_iota(jnp.int32, (Y, Z), 1)
    z_edge = jnp.where(lane == 0, -0.5, jnp.where(lane == Z - 1, 0.5, 0.0)).astype(jnp.float32)
    joined = jv[...]
    groups = 4
    span = X // groups
    for g in range(groups):
        for x in range(g * span, (g + 1) * span):
            own = pl.ds(x * Y, Y)
            for c in range(3):
                ms[c, own, :] = mv[c, own, :] + edge_term(joined, c * X + x, z_edge)
        rows = pl.ds(g * span * Y, span * Y)
        copies.append(pltpu.make_async_copy(ms.at[:, rows, :], m_hbm.at[:, rows, :], sem.at[1 + g]))
        copies[-1].start()
    for copy in copies:
        copy.wait()


def shards(sizes, u, e, t, r, b):
    X, Y, Z = t.shape
    N = X * Y
    layers = sizes[2]
    assert 8 * X <= Z and Z % 128 == 0 and Y % 8 == 0 and X % 8 == 0
    W = max(X, Y)
    f32 = jnp.float32
    vmem = pltpu.VMEM
    dma = pltpu.SemaphoreType.DMA
    any_space = pl.BlockSpec(memory_space=pl.ANY)
    in_vmem = pl.BlockSpec(memory_space=vmem)
    D = max(layers - 1, 1)
    kept = pl.pallas_call(
        functools.partial(kernel, (X, Y, Z), sizes),
        out_shape=(vmem((6, N, Z), f32), vmem((3, N, Z), f32), vmem((Y, Z), f32)),
        in_specs=[any_space] * 6,
        out_specs=(in_vmem,) * 3,
        scratch_shapes=[
            vmem((3, N + 2 * Y, Z), f32),
            vmem((Z, 2 * Z), jnp.bfloat16),
            vmem((6, N, Z), f32),
            vmem((N, Z), f32),
            vmem((N, Z), f32),
            vmem((N, Z), jnp.int32),
            vmem((N, Z), f32),
            vmem((N, Z), f32),
            vmem((6, N, Z), f32),
            vmem((N, Z), f32),
            vmem((N, Z), f32),
            vmem((6, N + 2 * Y, Z), f32),
            vmem((2, 8, Y, Z), f32),
            vmem((2, 8, X, Z), f32),
            vmem((3, X, Z), f32),
            vmem((2, W, Z), f32),
            vmem((2, Y, Z), f32),
            vmem((2, 2, 8, Z), f32),
            vmem((Y, Z), f32),
            vmem((2, Y, Z), f32),
            vmem((2, X, Z), f32),
            vmem((2, 3, Y, Z), f32),
            vmem((2, 8, Y, Z), f32),
            vmem((2, 3, X, Z), f32),
            vmem((2, 8, X, Z), f32),
            vmem((2, Y, Z), f32),
            vmem((2, 2, Y, Z), f32),
            vmem((2, 2, 8, Z), f32),
            vmem((2, 2, 3, Y, Z), f32),
            vmem((2, 2, 2, W, Z), f32),
            vmem((D, Y, Z), f32),
            vmem((2, D, Y, Z), f32),
            vmem((2, D, X, Z), f32),
            dma((3,)),
            pltpu.SemaphoreType.REGULAR((2,)),
            pltpu.SemaphoreType.REGULAR((1 if layers == 2 else 2,)),
            dma((5,)),
            dma((9,)),
        ],
        compiler_params=pltpu.CompilerParams(collective_id=0, has_side_effects=True),
        name="strain_step",
    )(u.reshape(3, N, Z), u, e.reshape(6, N, Z), t.reshape(N, Z), r.reshape(N, Z), b.reshape(N, Z))
    f, m = pl.pallas_call(
        functools.partial(finish, (X, Y, Z)),
        out_shape=(jax.ShapeDtypeStruct((6, N, Z), f32), jax.ShapeDtypeStruct((3, N, Z), f32)),
        in_specs=[in_vmem] * 3,
        out_specs=(any_space, any_space),
        scratch_shapes=[vmem((3, N, Z), f32), dma((5,))],
        name="finish",
    )(*(pltpu.with_memory_space_constraint(k, vmem) for k in kept))
    return f.reshape(6, X, Y, Z), m.reshape(3, X, Y, Z)


def solution(mesh):
    sizes = tuple(mesh.shape[a] for a in AXES)
    field = P("gx", "gy", "gz")
    fields = P(None, "gx", "gy", "gz")
    return jax.shard_map(
        functools.partial(shards, sizes),
        mesh=mesh,
        in_specs=(fields, fields, field, field, field),
        out_specs=(fields, fields),
        check_vma=False,
    )
```

```python
import functools

import jax
import jax.numpy as jnp
from jax import lax
from jax.experimental import pallas as pl
from jax.experimental.pallas import tpu as pltpu
from jax.sharding import PartitionSpec as P

MESH = pl.DeviceIdType.MESH
AXES = ("gx", "gy", "gz")
TERMS = (
    ((0, 0.5), (3, 0.25), (4, 0.25)),
    ((3, 0.25), (1, 0.5), (5, 0.25)),
    ((4, 0.25), (5, 0.25), (2, 0.5)),
)
X_SET = (0, 3, 4)
Y_SET = (3, 1, 5)
Z_SET = (4, 5, 2)


def offsets(layers):
    near = [
        (x, y, z)
        for x in (-1, 0, 1)
        for y in (-1, 0, 1)
        for z in (-1, 0, 1)
        if 1 <= abs(x) + abs(y) + abs(z) <= 2
    ]
    far = [
        (x, y, s * d)
        for d in range(2, layers)
        for s in (-1, 1)
        for x, y in ((0, 0), (-1, 0), (1, 0), (0, -1), (0, 1))
    ]
    return near + far


def minus(o):
    return tuple(-v for v in o)


def plus(o, p):
    return tuple(v + w for v, w in zip(o, p))


def split(o):
    return tuple(min(v, 0) for v in o), tuple(max(v, 0) for v in o)


def kinds_of(layers):
    offs = offsets(layers)
    uppers = [o for o in offs if min(o) >= 0]
    lowers = [o for o in offs if max(o) <= 0]
    mixed = [o for o in offs if min(o) < 0 < max(o)]
    return uppers, lowers, mixed


def merge(low, high):
    Z = low.shape[1]
    even = (lax.broadcasted_iota(jnp.int32, low.shape, 1) & 1) == 0
    return jnp.where(even, low, pltpu.roll(high, Z - 2, 1))


def edge_term(tile, q, z_edge):
    Z = tile.shape[1]
    return (pltpu.roll(tile, (Z - 2 * q) % Z, 1) if q else tile) * z_edge


def flow(e, pace):
    trace = e[0] + e[1] + e[2]
    third = trace * (1.0 / 3.0)
    half = [e[0] - third, e[1] - third, e[2] - third, e[3], e[4], e[5]]
    second = half[0] * half[0] + half[1] * half[1] + half[2] * half[2]
    second = second + 2.0 * (half[3] * half[3] + half[4] * half[4] + half[5] * half[5])
    rate = pace * second
    return trace, [rate * h for h in half]


def stress(e, change, trace, part):
    out = 2.0 * (e[part] - change[part])
    return out + trace if part < 3 else out


def kernel(
    dims, sizes,
    u_hbm, u_rows, e_hbm, t_hbm, r_hbm, b_hbm,
    fv, mv, jv,
    uv, tri, ev, tv, rv, bv, pv, tot, el, av, nt, sp,
    xs, ys, yu, zu, zs, xy, zt, xt, yt,
    rxu, rxs, ryu, rys, rzu, rzs, rxy, rxz, ryz, rt, rtx, rty,
    in_sem, ready, told, send_sem, recv_sem, spare,
):
    X, Y, Z = dims
    N = X * Y
    layers = sizes[2]
    depths = range(1, layers)
    me = [lax.axis_index(a) for a in AXES]
    offs = offsets(layers)
    uppers, lowers, mixed = kinds_of(layers)
    W = max(X, Y)

    def ready_index(o):
        return 0 if sum(o) == 1 else 1

    def exists(o):
        ok = None
        for a in range(3):
            if o[a]:
                here = me[a] + o[a]
                test = here < sizes[a] if o[a] > 0 else here >= 0
                ok = test if ok is None else jnp.logical_and(ok, test)
        return ok

    def partner(o):
        return {AXES[a]: me[a] + o[a] for a in range(3) if o[a]}

    has = {o: exists(o) for o in offs}
    faces = {a: [tuple(s if i == a else 0 for i in range(3)) for s in (-1, 1)] for a in range(3)}

    loads = [
        pltpu.make_async_copy(src, dst, in_sem.at[0 if i < 2 else 1 if i < 6 else 2])
        for i, (src, dst) in enumerate(
            (
                (u_hbm, uv.at[:, pl.ds(Y, N), :]),
                (r_hbm, rv),
                (e_hbm.at[:, pl.ds(0, Y), :], ev.at[:, pl.ds(0, Y), :]),
                (e_hbm.at[:, pl.ds(N - Y, Y), :], ev.at[:, pl.ds(N - Y, Y), :]),
                (t_hbm, tv),
                (b_hbm, bv),
                (e_hbm.at[:, pl.ds(Y, N - 2 * Y), :], ev.at[:, pl.ds(Y, N - 2 * Y), :]),
            )
        )
    ]
    for copy in loads:
        copy.start()

    def take(sem, rows):
        spot = sp.at[pl.ds(0, rows // 3), pl.ds(0, 3)] if rows % 8 else spare.at[pl.ds(0, rows)]
        pltpu.make_async_copy(spot, spot, sem).wait()

    barrier = pltpu.get_barrier_semaphore()
    for o in uppers:
        @pl.when(has[o])
        def _(o=o):
            pl.semaphore_signal(barrier, inc=1, device_id=partner(o), device_id_type=MESH)
    expected = jnp.int32(0)
    for o in lowers:
        expected = expected + has[o].astype(jnp.int32)

    plane = jnp.zeros((Y, Z), jnp.float32)
    row_plane = jnp.zeros((X, Z), jnp.float32)
    for c in range(3):
        uv[c, pl.ds(0, Y), :] = plane
        uv[c, pl.ds(Y + N, Y), :] = plane
    for c in range(6):
        sp[c, pl.ds(0, Y), :] = plane
        sp[c, pl.ds(Y + N, Y), :] = plane

    def blank(o, *refs):
        @pl.when(jnp.logical_not(has[o]))
        def _():
            for ref in refs:
                ref[...] = jnp.zeros(ref.shape, jnp.float32)

    for i, sz in enumerate((-1, 1)):
        blank((0, 0, sz), rzu.at[i], rzs.at[i])
        for j, s in enumerate((-1, 1)):
            blank((s, 0, sz), rxz.at[j, i])
            blank((0, s, sz), ryz.at[j, i])
    for i, sx in enumerate((-1, 1)):
        for j, sy in enumerate((-1, 1)):
            blank((sx, sy, 0), rxy.at[i, j])
    for d in depths:
        blank((0, 0, -d), rt.at[d - 1])
        for j, s in enumerate((-1, 1)):
            blank((s, 0, -d), rtx.at[j, d - 1])
            blank((0, s, -d), rty.at[j, d - 1])

    above_row = lax.broadcasted_iota(jnp.int32, (Z, 2 * Z), 0)
    column = lax.broadcasted_iota(jnp.int32, (Z, 2 * Z), 1)
    triangle = jnp.where(
        (above_row < column) | (column >= Z),
        1.0,
        jnp.where(above_row == column, 0.5, 0.0),
    ).astype(jnp.bfloat16)
    tri[...] = triangle

    lane = lax.broadcasted_iota(jnp.int32, (Y, Z), 1)
    row = lax.broadcasted_iota(jnp.int32, (Y, Z), 0)
    pair = lane >> 1
    even = (lane & 1) == 0
    not_last = jnp.where(row < Y - 1, 0.5, 0.0).astype(jnp.float32)
    not_first = jnp.where(row > 0, 0.5, 0.0).astype(jnp.float32)
    z_first = jnp.where(lane > 0, 0.5, 0.0).astype(jnp.float32)
    z_last = jnp.where(lane < Z - 1, 0.5, 0.0).astype(jnp.float32)
    z_edge = jnp.where(lane == 0, -0.5, jnp.where(lane == Z - 1, 0.5, 0.0)).astype(jnp.float32)
    if X == Y:
        row_x, z_edge_x = row, z_edge
    else:
        lane_x = lax.broadcasted_iota(jnp.int32, (X, Z), 1)
        row_x = lax.broadcasted_iota(jnp.int32, (X, Z), 0)
        z_edge_x = jnp.where(lane_x == 0, -0.5, jnp.where(lane_x == Z - 1, 0.5, 0.0)).astype(jnp.float32)

    beside = [sum(has[o].astype(jnp.int32) for o in faces[a]) for a in range(3)]
    above, below = me[2], layers - 1 - me[2]

    places = [
        (nx, ny, (d > 0) + (d < layers - 1), d)
        for nx in ((0,), (1,), (1, 2))[min(sizes[0], 3) - 1]
        for ny in ((0,), (1,), (1, 2))[min(sizes[1], 3) - 1]
        for d in range(layers)
    ]
    own_place = (*beside, above)

    def planes(d):
        return 7 + jnp.minimum(d, 1) if isinstance(d, jax.Array) else 7 + min(d, 1)

    def early(nx, ny, nz, d):
        return 3 * X * ny + Y * (nz + d)

    def strike(nx, ny, nz, d):
        return 3 * Y * nx

    def late(nx, ny, nz, d):
        return (planes(d) + d) * (Y * nx + X * ny) + 2 * Y * nz + 3 * Y * nx * nz + 2 * W * ny * nz

    def corner(nx, ny, nz, d):
        return 3 * nx * ny

    def gone(nx, ny, nz, d):
        down = layers - 1 - d
        return (planes(d) + 3 + down) * (Y * nx + X * ny) + Y * (3 * nz + down) + 3 * Y * nx * nz + 2 * W * ny * nz

    groups = (early, strike, late, corner)
    recv_index = {
        "yu": 0, "zu": 0, "t": 0, "xu": 1, "xs": 2, "ys": 2, "zs": 2, "xz": 2, "yz": 2, "tx": 2, "ty": 2, "xy": 3,
    }
    sends = {o: [] for o in offs}

    def message(kind, o, src, dst, few=None):
        sends[o].append((kind if few != 7 else kind + "7", pltpu.make_async_remote_copy(
            src_ref=src, dst_ref=dst,
            send_sem=send_sem.at[int(kind == "xy")], recv_sem=recv_sem.at[recv_index[kind]],
            device_id=partner(o), device_id_type=MESH,
        )))

    for i, s in enumerate((-1, 1)):
        k = 1 - i
        at = (Y, Y * X)[i]
        strike = u_hbm.at[:, pl.ds((0, N - Y)[i], Y), :] if s < 0 else uv.at[:, pl.ds(at, Y), :]
        message("xu", (s, 0, 0), strike, rxu.at[k])
        for few in (7, 8):
            some = pl.ds(0, few)
            message("xs", (s, 0, 0), xs.at[i, some], rxs.at[k, some], few)
            message("ys", (0, s, 0), ys.at[i, some], rys.at[k, some], few)
        message("yu", (0, s, 0), u_rows.at[:, :, 0, :] if s < 0 else yu, ryu.at[k])
        message("zu", (0, 0, s), zu.at[0, pl.ds(0, Y)], rzu.at[k])
        message("zs", (0, 0, s), zs, rzs.at[k])
        for j, s2 in enumerate((-1, 1)):
            m = 1 - j
            lines = xy.at[i, j, pl.ds(0, 3), :] if s + s2 >= 0 else u_rows.at[:, 0, 0, :]
            message("xy", (s, s2, 0), lines, rxy.at[k, m, pl.ds(0, 3), :])
            strike = u_hbm.at[:, pl.ds(0, Y), :] if s + s2 < 0 else uv.at[:, pl.ds(at, Y), :]
            message("xz", (s, 0, s2), strike, rxz.at[k, m])
            message("yz", (0, s, s2), zu, ryz.at[k, m])
        for d in depths:
            message("tx", (s, 0, d), xt.at[i], rtx.at[k, d - 1])
            message("ty", (0, s, d), yt.at[i], rty.at[k, d - 1])
    for d in depths:
        message("t", (0, 0, d), zt, rt.at[d - 1])

    def settle(sem, group):
        rows = group(*own_place)
        for n in sorted({group(*p) for p in places} - {0}):
            @pl.when(rows == n)
            def _(n=n):
                take(sem, n)

    def start(offsets_in, kinds):
        for o in offsets_in:
            chosen = [copy for kind, copy in sends[o] if kind in kinds]
            if chosen:
                @pl.when(has[o])
                def _(chosen=chosen):
                    for copy in chosen:
                        copy.start()

    def arrive(index):
        settle(recv_sem.at[index], groups[index])

    @pl.when(expected > 0)
    def _():
        pl.semaphore_wait(barrier, expected)

    for o in lowers:
        @pl.when(has[o])
        def _(o=o):
            pl.semaphore_signal(
                ready.at[ready_index(minus(o))], inc=1, device_id=partner(o), device_id_type=MESH
            )

    def announce(o):
        low, high = split(o)

        @pl.when(jnp.logical_and(has[minus(low)], has[high]))
        def _():
            kind = 0 if max(high) == 1 and min(low) == -1 else 1
            pl.semaphore_signal(told.at[kind], inc=1, device_id=partner(minus(low)), device_id_type=MESH)

    lowers = sorted(lowers, key=lambda o: (sum(map(abs, o)), o[2], o[1]))
    for kind in ("xz", "yu", "xy", "xu"):
        start(lowers, (kind,))

    take(in_sem.at[0], 4 * N)
    total_depth = Z * layers
    depth = (me[2] * Z + lane).astype(jnp.float32)
    scale = (1.0 + 2.0 * depth / total_depth) / total_depth

    def prefix(planes):
        thirds = [[], [], []]
        for x in planes:
            rest = rv[pl.ds(x * Y, Y), :] * scale
            for k in range(3):
                piece = rest.astype(jnp.bfloat16)
                thirds[k].append(piece)
                rest = rest - piece.astype(jnp.float32)
        weight = jnp.concatenate([jnp.concatenate(k, axis=0) for k in thirds], axis=1)
        triangle = jnp.concatenate([tri[...]] * 3, axis=0)
        sums = jnp.dot(weight, triangle, preferred_element_type=jnp.float32)
        for i, x in enumerate(planes):
            pv[pl.ds(x * Y, Y), :] = sums[i * Y:(i + 1) * Y, :Z] + 1.0
            tot[pl.ds(x * Y, Y), :] = sums[i * Y:(i + 1) * Y, Z:]

    def strain(x):
        base = Y + x * Y
        own = pl.ds(x * Y, Y)
        grad = []
        for c in range(3):
            here = uv[c, pl.ds(base, Y), :]
            grad.append((
                (uv[c, pl.ds(base + Y, Y), :] - uv[c, pl.ds(base - Y, Y), :]) * 0.5,
                uv[c, pl.ds(base + 1, Y), :] * not_last - uv[c, pl.ds(base - 1, Y), :] * not_first,
                pltpu.roll(here, Z - 1, 1) * z_last - pltpu.roll(here, 1, 1) * z_first,
            ))
        el[0, own, :] = grad[0][0]
        el[1, own, :] = grad[1][1]
        el[2, own, :] = grad[2][2]
        el[3, own, :] = 0.5 * (grad[0][1] + grad[1][0])
        el[4, own, :] = 0.5 * (grad[0][2] + grad[2][0])
        el[5, own, :] = 0.5 * (grad[1][2] + grad[2][1])

    def pack(k, x, part, tiles):
        q = (k % 4) * X + x
        tile = pltpu.roll(part, (2 * q + 1) % Z, 1)
        tiles[k // 4] = jnp.where(pair == q, tile, tiles[k // 4])

    def factors(x, tiles):
        own = pl.ds(x * Y, Y)
        minus_two = -2.0 / tv[own, :]
        factor = (2.0 + 14.0 * bv[own, :].astype(jnp.float32)) * jnp.exp(pv[own, :] * minus_two)
        av[own, :] = factor
        nt[own, :] = minus_two
        for i, at in enumerate((0, X - 1)):
            if x == at:
                xs[i, 6] = factor
                xs[i, 7] = minus_two
        if tiles:
            pack(6, x, factor, tiles)
            pack(7, x, minus_two, tiles)

    def elastic(x, tiles):
        own = pl.ds(x * Y, Y)
        for k in range(6):
            part = el[k, own, :] - ev[k, own, :]
            el[k, own, :] = part
            for i, at in enumerate((0, X - 1)):
                if x == at:
                    xs[i, k] = part
            if tiles:
                pack(k, x, part, tiles)

    ends = sorted({0, X - 1})
    inner = [x for x in range(X) if x not in ends]

    def pack_displacement():
        tile0 = plane
        for x in range(X):
            for c in range(3):
                q = c * X + x
                tile = pltpu.roll(uv[c, pl.ds(Y + x * Y, Y), :], (2 * q + 1) % Z, 1)
                tile0 = jnp.where(pair == q, tile, tile0)
        zu[0, pl.ds(0, Y), :] = tile0

    def lines_along_depth():
        tile = row_plane
        pair_x = lax.broadcasted_iota(jnp.int32, (X, Z), 1) >> 1
        for i, line in enumerate((0, Y - 1)):
            for c in range(3):
                p = 3 * i + c
                lines = uv[c, pl.ds(Y + line, X, stride=Y), :]
                if i:
                    yu[c] = lines
                tile = jnp.where(pair_x == p, pltpu.roll(lines, (2 * p + 1) % Z, 1), tile)
                for j, at in enumerate((0, X - 1)):
                    xy[j, i, pl.ds(c, 1), :] = uv[c, pl.ds(Y + at * Y + line, 1), :]
        zu[1, pl.ds(0, X), :] = tile

    def total_tiles():
        tile = plane
        for x in range(X):
            tile = jnp.where(pair == x, tot[pl.ds(x * Y, Y), :], tile)
        zt[...] = tile
        for i, (at, line) in enumerate(((0, 0), (X - 1, Y - 1))):
            xt[i] = tot[pl.ds(at * Y, Y), :]
            yt[i] = tot[pl.ds(line, X, stride=Y), :]

    def along_dip(kind):
        for i, line in enumerate((0, Y - 1)):
            for k in range(8):
                src = el.at[k] if k < 6 else (av, nt)[k - 6]
                ys[i, k] = src[pl.ds(line, X, stride=Y), :]
        start(lowers, (kind,))

    @pl.when(above == 0)
    def _():
        prefix(ends)
        for x in ends:
            strain(x)
        take(in_sem.at[1], 12 * Y + 2 * N)
        for x in ends:
            elastic(x, None)
            factors(x, None)
        start(lowers, ("xs7",))
        prefix(inner)
        for x in inner:
            strain(x)
        loads[6].wait()
        for x in inner:
            elastic(x, None)
            factors(x, None)
        along_dip("ys7")
        pack_displacement()
        lines_along_depth()
        total_tiles()
        tiles = [plane, plane]
        for x in range(X):
            for k in range(8):
                src = el.at[k] if k < 6 else (av, nt)[k - 6]
                pack(k, x, src[pl.ds(x * Y, Y), :], tiles)
        for k in range(2):
            zs[k] = tiles[k]

    @pl.when(above > 0)
    def _():
        pack_displacement()
        start(lowers, ("zu",))
        lines_along_depth()
        start(lowers, ("yz",))
        prefix(range(X))
        total_tiles()
        for x in range(X):
            strain(x)
        take(in_sem.at[1], 12 * Y + 2 * N)
        tiles = [plane, plane]
        for x in ends:
            elastic(x, tiles)
            factors(x, tiles)
        start(lowers, ("xs",))
        loads[6].wait()
        for x in inner:
            elastic(x, tiles)
            factors(x, tiles)
        for k in range(2):
            zs[k] = tiles[k]
        start(lowers, ("zs", "t", "tx", "ty"))
        along_dip("ys")

    near = [o for o in uppers if sum(o) == 1]
    number = sum(has[o].astype(jnp.int32) for o in near)

    @pl.when(number > 0)
    def _():
        pl.semaphore_wait(ready.at[0], number)

    for o in mixed:
        low, high = split(o)
        if high in near and minus(low) in near:
            announce(o)
    near.sort()
    start(near, ("zu", "yu", "xu", "t", "zs"))
    others = [o for o in uppers if o not in near]
    far = [o for o in mixed if split(o)[1] not in near or minus(split(o)[0]) not in near]
    close = sorted((o for o in mixed if o not in far), key=lambda o: (abs(o[0]), abs(o[2])))

    diagonal = ("xy", "xz", "yz", "t", "tx", "ty")

    def hear(offsets_in, sem):
        number = sum(has[o].astype(jnp.int32) for o in offsets_in)

        @pl.when(number > 0)
        def _():
            pl.semaphore_wait(sem, number)

        start(offsets_in, diagonal)

    hear(close, told.at[0])
    for kinds, deeper in ((("ys7", "xs7"), False), (("ys", "xs"), True)):
        @pl.when((above > 0) if deeper else (above == 0))
        def _(kinds=kinds):
            start(near, kinds)

    hear(others, ready.at[1])
    for o in far:
        announce(o)
    if far:
        hear(far, told.at[1])

    arrive(0)
    for side, line in enumerate((0, Y - 1)):
        sign = 2.0 * side - 1.0

        @pl.when(has[faces[1][side]])
        def _(side=side, sign=sign, line=line):
            own = pl.ds(line, X, stride=Y)
            for c, (part, factor) in enumerate(TERMS[1]):
                el[part, own, :] = el[part, own, :] + (sign * factor) * ryu[side, c]

    carried = plane
    for d in depths:
        carried = carried + rt[d - 1]
    merged = merge(rzu[0], rzu[1])

    def advance(x):
        own = pl.ds(x * Y, Y)
        e = [el[c, own, :] for c in range(6)]
        for c, (part, factor) in enumerate(TERMS[2]):
            e[part] = e[part] + (2.0 * factor) * edge_term(merged, c * X + x, z_edge)
        load = jnp.broadcast_to(carried[:, 2 * x:2 * x + 1], (Y, Z))
        trace, change = flow(e, av[own, :] * jnp.exp(load * nt[own, :]))
        for c in range(6):
            fv[c, own, :] = ev[c, own, :] + change[c]
            sp[c, pl.ds(Y + x * Y, Y), :] = stress(e, change, trace, c)

    for x in range(X):
        if x not in ends:
            advance(x)
    arrive(1)
    for side, at in enumerate((0, X - 1)):
        sign = 2.0 * side - 1.0

        @pl.when(has[faces[0][side]])
        def _(side=side, sign=sign, at=at):
            own = pl.ds(at * Y, Y)
            for c, (part, factor) in enumerate(TERMS[0]):
                el[part, own, :] = el[part, own, :] + (sign * factor) * rxu[side, c]

    for x in ends:
        advance(x)

    for x in range(X):
        base = Y + x * Y
        own = pl.ds(x * Y, Y)
        for c in range(3):
            cx, cy, cz = X_SET[c], Y_SET[c], Z_SET[c]
            here = sp[cz, pl.ds(base, Y), :]
            total = (sp[cx, pl.ds(base + Y, Y), :] - sp[cx, pl.ds(base - Y, Y), :]) * 0.5
            total = total + (
                sp[cy, pl.ds(base + 1, Y), :] * not_last - sp[cy, pl.ds(base - 1, Y), :] * not_first
            )
            total = total + (pltpu.roll(here, Z - 1, 1) * z_last - pltpu.roll(here, 1, 1) * z_first)
            if c == 2:
                total = total - 0.5 * rv[own, :]
            mv[c, own, :] = total

    def add(e, axis, factor, values):
        for c, (part, f) in enumerate(TERMS[axis]):
            e[part] = e[part] + (factor * f) * values[c]

    def ends_of(first, last, rows, count):
        return jnp.where(rows == 0, -first, jnp.where(rows == count - 1, last, 0.0))

    arrive(2)
    arrive(3)

    def beyond(axis, side, part):
        got, load, e = part
        trace, change = flow(e, got[6] * jnp.exp(jnp.where(above > 0, load * got[7], 0.0)))
        there = has[faces[axis][side]]
        return [
            (side - 0.5) * jnp.where(there, stress(e, change, trace, k), 0.0) for k in (X_SET, Y_SET)[axis]
        ]

    along_y = []
    for side, line in enumerate((0, Y - 1)):
        e = [rys[side, k] for k in range(6)]
        add(e, 1, 1.0 - 2.0 * side, [uv[c, pl.ds(Y + line, X, stride=Y), :] for c in range(3)])
        add(e, 0, 1.0, [
            ends_of(rxy[0, side, pl.ds(c, 1), :], rxy[1, side, pl.ds(c, 1), :], row_x, X) for c in range(3)
        ])
        joined = merge(ryz[side, 0, 1, pl.ds(0, X), :], ryz[side, 1, 1, pl.ds(0, X), :])
        add(e, 2, 2.0, [edge_term(joined, 3 * (1 - side) + c, z_edge_x) for c in range(3)])
        load = row_plane
        for d in depths:
            load = load + rty[side, d - 1]
        along_y.append(beyond(1, side, (rys[side], load, e)))

    along_x = []
    for side, at in enumerate((0, X - 1)):
        e = [rxs[side, k] for k in range(6)]
        add(e, 0, 1.0 - 2.0 * side, [uv[c, pl.ds(Y + at * Y, Y), :] for c in range(3)])
        add(e, 1, 1.0, [
            ends_of(rxy[side, 0, pl.ds(c, 1), :], rxy[side, 1, pl.ds(c, 1), :], row, Y) for c in range(3)
        ])
        add(e, 2, 1.0, [
            jnp.where(
                lane == 0, -pltpu.roll(rxz[side, 0, c], 1, 1),
                jnp.where(lane == Z - 1, pltpu.roll(rxz[side, 1, c], Z - 1, 1), 0.0),
            )
            for c in range(3)
        ])
        load = plane
        for d in depths:
            load = load + rtx[side, d - 1]
        along_x.append(beyond(0, side, (rxs[side], load, e)))

    block = 2 * X

    def shift(tile, by):
        return pltpu.roll(tile, by % Z, 1) if by % Z else tile

    halo = [jnp.where(even, rzs[0, k], rzs[1, k]) for k in range(2)]
    parts = [shift(halo[k // 4], -(k % 4) * block) for k in range(8)]
    mine = zu[0, pl.ds(0, Y), :]
    from_z = jnp.where(even, shift(mine, -1), -shift(mine, 1))
    from_x = []
    for c in range(3):
        left, right = (jnp.where(lane == Z - 1, rxz[i, 0, c], rxz[i, 1, c]) for i in range(2))
        from_x.append(jnp.where(
            pair == 0, -shift(left, 1), jnp.where(pair == X - 1, shift(right, 2 * X - 1), 0.0)
        ))
    even_row = (lax.broadcasted_iota(jnp.int32, (1, Z), 1) & 1) == 0
    from_y = ends_of(
        jnp.where(even_row, ryz[0, 0, 0, pl.ds(Y - 1, 1), :], ryz[0, 1, 0, pl.ds(Y - 1, 1), :]),
        jnp.where(even_row, ryz[1, 0, 0, pl.ds(0, 1), :], ryz[1, 1, 0, pl.ds(0, 1), :]),
        row, Y,
    )
    e = list(parts[:6])
    add(e, 0, 1.0, from_x)
    for axis, tile in ((1, from_y), (2, from_z)):
        add(e, axis, 1.0, [shift(tile, -c * block) for c in range(3)])
    deeper = plane
    for d in depths:
        if d >= 2:
            deeper = deeper + rt[d - 1]
    load = jnp.where(even, deeper, carried + zt[...])
    trace, change = flow(e, parts[6] * jnp.exp(load * parts[7]))
    known = jnp.where(
        even,
        has[0, 0, -1].astype(jnp.float32),
        has[0, 0, 1].astype(jnp.float32),
    )
    gathered = plane
    for c in range(3):
        tile = shift(stress(e, change, trace, Z_SET[c]) * known, c * block)
        gathered = jnp.where((pair >= c * X) & (pair < (c + 1) * X), tile, gathered)
    jv[...] = jnp.where(even, gathered, shift(gathered, -2))

    for c in range(3):
        for side, at in enumerate((0, X - 1)):
            own = pl.ds(at * Y, Y)
            mv[c, own, :] = mv[c, own, :] + along_x[side][c]
        for side, line in enumerate((0, Y - 1)):
            own = pl.ds(line, X, stride=Y)
            mv[c, own, :] = mv[c, own, :] + along_y[side][c]

    settle(send_sem.at[0], gone)
    settle(send_sem.at[1], corner)


def finish(dims, fv, mv, jv, f_hbm, m_hbm, ms, sem):
    X, Y, Z = dims
    copies = [pltpu.make_async_copy(fv, f_hbm, sem.at[0])]
    copies[0].start()
    lane = lax.broadcasted_iota(jnp.int32, (Y, Z), 1)
    z_edge = jnp.where(lane == 0, -0.5, jnp.where(lane == Z - 1, 0.5, 0.0)).astype(jnp.float32)
    joined = jv[...]
    groups = 4
    span = X // groups
    for g in range(groups):
        for x in range(g * span, (g + 1) * span):
            own = pl.ds(x * Y, Y)
            for c in range(3):
                ms[c, own, :] = mv[c, own, :] + edge_term(joined, c * X + x, z_edge)
        rows = pl.ds(g * span * Y, span * Y)
        copies.append(pltpu.make_async_copy(ms.at[:, rows, :], m_hbm.at[:, rows, :], sem.at[1 + g]))
        copies[-1].start()
    for copy in copies:
        copy.wait()


def shards(sizes, u, e, t, r, b):
    X, Y, Z = t.shape
    N = X * Y
    layers = sizes[2]
    assert 8 * X <= Z and Z % 128 == 0 and Y % 8 == 0 and X % 8 == 0
    W = max(X, Y)
    f32 = jnp.float32
    vmem = pltpu.VMEM
    dma = pltpu.SemaphoreType.DMA
    any_space = pl.BlockSpec(memory_space=pl.ANY)
    in_vmem = pl.BlockSpec(memory_space=vmem)
    D = max(layers - 1, 1)
    kept = pl.pallas_call(
        functools.partial(kernel, (X, Y, Z), sizes),
        out_shape=(vmem((6, N, Z), f32), vmem((3, N, Z), f32), vmem((Y, Z), f32)),
        in_specs=[any_space] * 6,
        out_specs=(in_vmem,) * 3,
        scratch_shapes=[
            vmem((3, N + 2 * Y, Z), f32),
            vmem((Z, 2 * Z), jnp.bfloat16),
            vmem((6, N, Z), f32),
            vmem((N, Z), f32),
            vmem((N, Z), f32),
            vmem((N, Z), jnp.int32),
            vmem((N, Z), f32),
            vmem((N, Z), f32),
            vmem((6, N, Z), f32),
            vmem((N, Z), f32),
            vmem((N, Z), f32),
            vmem((6, N + 2 * Y, Z), f32),
            vmem((2, 8, Y, Z), f32),
            vmem((2, 8, X, Z), f32),
            vmem((3, X, Z), f32),
            vmem((2, W, Z), f32),
            vmem((2, Y, Z), f32),
            vmem((2, 2, 8, Z), f32),
            vmem((Y, Z), f32),
            vmem((2, Y, Z), f32),
            vmem((2, X, Z), f32),
            vmem((2, 3, Y, Z), f32),
            vmem((2, 8, Y, Z), f32),
            vmem((2, 3, X, Z), f32),
            vmem((2, 8, X, Z), f32),
            vmem((2, Y, Z), f32),
            vmem((2, 2, Y, Z), f32),
            vmem((2, 2, 8, Z), f32),
            vmem((2, 2, 3, Y, Z), f32),
            vmem((2, 2, 2, W, Z), f32),
            vmem((D, Y, Z), f32),
            vmem((2, D, Y, Z), f32),
            vmem((2, D, X, Z), f32),
            dma((3,)),
            pltpu.SemaphoreType.REGULAR((2,)),
            pltpu.SemaphoreType.REGULAR((1 if layers == 2 else 2,)),
            dma((2,)),
            dma((4,)),
            vmem(((11 + layers) * 2 * (X + Y) + (18 + layers) * Y + 8 * W, Z), f32),
        ],
        compiler_params=pltpu.CompilerParams(collective_id=0, has_side_effects=True),
        name="strain_step",
    )(u.reshape(3, N, Z), u, e.reshape(6, N, Z), t.reshape(N, Z), r.reshape(N, Z), b.reshape(N, Z))
    f, m = pl.pallas_call(
        functools.partial(finish, (X, Y, Z)),
        out_shape=(jax.ShapeDtypeStruct((6, N, Z), f32), jax.ShapeDtypeStruct((3, N, Z), f32)),
        in_specs=[in_vmem] * 3,
        out_specs=(any_space, any_space),
        scratch_shapes=[vmem((3, N, Z), f32), dma((5,))],
        name="finish",
    )(*(pltpu.with_memory_space_constraint(k, vmem) for k in kept))
    return f.reshape(6, X, Y, Z), m.reshape(3, X, Y, Z)


def solution(mesh):
    sizes = tuple(mesh.shape[a] for a in AXES)
    field = P("gx", "gy", "gz")
    fields = P(None, "gx", "gy", "gz")
    return jax.shard_map(
        functools.partial(shards, sizes),
        mesh=mesh,
        in_specs=(fields, fields, field, field, field),
        out_specs=(fields, fields),
        check_vma=False,
    )
```

```python
import functools

import jax
import jax.numpy as jnp
from jax import lax
from jax.experimental import pallas as pl
from jax.experimental.pallas import tpu as pltpu
from jax.sharding import PartitionSpec as P

MESH = pl.DeviceIdType.MESH
AXES = ("gx", "gy", "gz")
TERMS = (
    ((0, 0.5), (3, 0.25), (4, 0.25)),
    ((3, 0.25), (1, 0.5), (5, 0.25)),
    ((4, 0.25), (5, 0.25), (2, 0.5)),
)
X_SET = (0, 3, 4)
Y_SET = (3, 1, 5)
Z_SET = (4, 5, 2)


def offsets(layers):
    near = [
        (x, y, z)
        for x in (-1, 0, 1)
        for y in (-1, 0, 1)
        for z in (-1, 0, 1)
        if 1 <= abs(x) + abs(y) + abs(z) <= 2
    ]
    far = [
        (x, y, s * d)
        for d in range(2, layers)
        for s in (-1, 1)
        for x, y in ((0, 0), (-1, 0), (1, 0), (0, -1), (0, 1))
    ]
    return near + far


def minus(o):
    return tuple(-v for v in o)


def plus(o, p):
    return tuple(v + w for v, w in zip(o, p))


def split(o):
    return tuple(min(v, 0) for v in o), tuple(max(v, 0) for v in o)


def kinds_of(layers):
    offs = offsets(layers)
    uppers = [o for o in offs if min(o) >= 0]
    lowers = [o for o in offs if max(o) <= 0]
    mixed = [o for o in offs if min(o) < 0 < max(o)]
    return uppers, lowers, mixed


def merge(low, high):
    Z = low.shape[1]
    even = (lax.broadcasted_iota(jnp.int32, low.shape, 1) & 1) == 0
    return jnp.where(even, low, pltpu.roll(high, Z - 2, 1))


def edge_term(tile, q, z_edge):
    Z = tile.shape[1]
    return (pltpu.roll(tile, (Z - 2 * q) % Z, 1) if q else tile) * z_edge


def flow(e, pace):
    trace = e[0] + e[1] + e[2]
    third = trace * (1.0 / 3.0)
    half = [e[0] - third, e[1] - third, e[2] - third, e[3], e[4], e[5]]
    second = half[0] * half[0] + half[1] * half[1] + half[2] * half[2]
    second = second + 2.0 * (half[3] * half[3] + half[4] * half[4] + half[5] * half[5])
    rate = pace * second
    return trace, [rate * h for h in half]


def stress(e, change, trace, part):
    out = 2.0 * (e[part] - change[part])
    return out + trace if part < 3 else out


def kernel(
    dims, sizes,
    u_hbm, u_rows, e_hbm, t_hbm, r_hbm, b_hbm,
    fv, mv, jv, dv,
    uv, tri, zown, ev, tv, rv, bv, pv, tot, el, av, nt, sp,
    xs, ys, yu, zu, zs, xy, zt, xt, yt,
    rxu, rxs, ryu, rys, rzu, rzs, rxy, rxz, ryz, rt, rtx, rty,
    in_sem, ready, told, send_sem, recv_sem, spare,
):
    X, Y, Z = dims
    N = X * Y
    layers = sizes[2]
    depths = range(1, layers)
    me = [lax.axis_index(a) for a in AXES]
    offs = offsets(layers)
    uppers, lowers, mixed = kinds_of(layers)
    W = max(X, Y)

    def ready_index(o):
        return 0 if sum(o) == 1 else 1

    def exists(o):
        ok = None
        for a in range(3):
            if o[a]:
                here = me[a] + o[a]
                test = here < sizes[a] if o[a] > 0 else here >= 0
                ok = test if ok is None else jnp.logical_and(ok, test)
        return ok

    def partner(o):
        return {AXES[a]: me[a] + o[a] for a in range(3) if o[a]}

    has = {o: exists(o) for o in offs}
    faces = {a: [tuple(s if i == a else 0 for i in range(3)) for s in (-1, 1)] for a in range(3)}

    loads = [
        pltpu.make_async_copy(src, dst, in_sem.at[0 if i < 2 else 1 if i < 6 else 2])
        for i, (src, dst) in enumerate(
            (
                (u_hbm, uv.at[:, pl.ds(Y, N), :]),
                (r_hbm, rv),
                (e_hbm.at[:, pl.ds(0, Y), :], ev.at[:, pl.ds(0, Y), :]),
                (e_hbm.at[:, pl.ds(N - Y, Y), :], ev.at[:, pl.ds(N - Y, Y), :]),
                (t_hbm, tv),
                (b_hbm, bv),
                (e_hbm.at[:, pl.ds(Y, N - 2 * Y), :], ev.at[:, pl.ds(Y, N - 2 * Y), :]),
            )
        )
    ]
    for copy in loads:
        copy.start()

    def take(sem, rows):
        spot = sp.at[pl.ds(0, rows // 3), pl.ds(0, 3)] if rows % 8 else spare.at[pl.ds(0, rows)]
        pltpu.make_async_copy(spot, spot, sem).wait()

    barrier = pltpu.get_barrier_semaphore()
    for o in uppers:
        @pl.when(has[o])
        def _(o=o):
            pl.semaphore_signal(barrier, inc=1, device_id=partner(o), device_id_type=MESH)
    expected = jnp.int32(0)
    for o in lowers:
        expected = expected + has[o].astype(jnp.int32)

    plane = jnp.zeros((Y, Z), jnp.float32)
    row_plane = jnp.zeros((X, Z), jnp.float32)
    for c in range(3):
        uv[c, pl.ds(0, Y), :] = plane
        uv[c, pl.ds(Y + N, Y), :] = plane
    for c in range(6):
        sp[c, pl.ds(0, Y), :] = plane
        sp[c, pl.ds(Y + N, Y), :] = plane

    def blank(o, *refs):
        @pl.when(jnp.logical_not(has[o]))
        def _():
            for ref in refs:
                ref[...] = jnp.zeros(ref.shape, jnp.float32)

    for i, sz in enumerate((-1, 1)):
        blank((0, 0, sz), rzu.at[i], rzs.at[i])
        for j, s in enumerate((-1, 1)):
            blank((s, 0, sz), rxz.at[j, i])
            blank((0, s, sz), ryz.at[j, i])
    for i, sx in enumerate((-1, 1)):
        for j, sy in enumerate((-1, 1)):
            blank((sx, sy, 0), rxy.at[i, j])
    for d in depths:
        blank((0, 0, -d), rt.at[d - 1])
        for j, s in enumerate((-1, 1)):
            blank((s, 0, -d), rtx.at[j, d - 1])
            blank((0, s, -d), rty.at[j, d - 1])

    above_row = lax.broadcasted_iota(jnp.int32, (Z, 2 * Z), 0)
    column = lax.broadcasted_iota(jnp.int32, (Z, 2 * Z), 1)
    triangle = jnp.where(
        (above_row < column) | (column >= Z),
        1.0,
        jnp.where(above_row == column, 0.5, 0.0),
    ).astype(jnp.bfloat16)
    tri[...] = triangle

    lane = lax.broadcasted_iota(jnp.int32, (Y, Z), 1)
    row = lax.broadcasted_iota(jnp.int32, (Y, Z), 0)
    pair = lane >> 1
    even = (lane & 1) == 0
    not_last = jnp.where(row < Y - 1, 0.5, 0.0).astype(jnp.float32)
    not_first = jnp.where(row > 0, 0.5, 0.0).astype(jnp.float32)
    z_first = jnp.where(lane > 0, 0.5, 0.0).astype(jnp.float32)
    z_last = jnp.where(lane < Z - 1, 0.5, 0.0).astype(jnp.float32)
    z_edge = jnp.where(lane == 0, -0.5, jnp.where(lane == Z - 1, 0.5, 0.0)).astype(jnp.float32)
    if X == Y:
        row_x, z_edge_x = row, z_edge
    else:
        lane_x = lax.broadcasted_iota(jnp.int32, (X, Z), 1)
        row_x = lax.broadcasted_iota(jnp.int32, (X, Z), 0)
        z_edge_x = jnp.where(lane_x == 0, -0.5, jnp.where(lane_x == Z - 1, 0.5, 0.0)).astype(jnp.float32)

    beside = [sum(has[o].astype(jnp.int32) for o in faces[a]) for a in range(3)]
    above, below = me[2], layers - 1 - me[2]

    places = [
        (nx, ny, (d > 0) + (d < layers - 1), d)
        for nx in ((0,), (1,), (1, 2))[min(sizes[0], 3) - 1]
        for ny in ((0,), (1,), (1, 2))[min(sizes[1], 3) - 1]
        for d in range(layers)
    ]
    own_place = (*beside, above)

    def planes(d):
        return 7 + jnp.minimum(d, 1) if isinstance(d, jax.Array) else 7 + min(d, 1)

    def early(nx, ny, nz, d):
        return 3 * X * ny + Y * (nz + d)

    def strike(nx, ny, nz, d):
        return 3 * Y * nx

    def late(nx, ny, nz, d):
        return (planes(d) + d) * (Y * nx + X * ny) + 2 * Y * nz + 3 * Y * nx * nz + 2 * W * ny * nz

    def corner(nx, ny, nz, d):
        return 3 * nx * ny

    def gone(nx, ny, nz, d):
        down = layers - 1 - d
        return (planes(d) + 3 + down) * (Y * nx + X * ny) + Y * (3 * nz + down) + 3 * Y * nx * nz + 2 * W * ny * nz

    groups = (early, strike, late, corner)
    recv_index = {
        "yu": 0, "zu": 0, "t": 0, "xu": 1, "xs": 2, "ys": 2, "zs": 2, "xz": 2, "yz": 2, "tx": 2, "ty": 2, "xy": 3,
    }
    sends = {o: [] for o in offs}

    def message(kind, o, src, dst, few=None):
        sends[o].append((kind if few != 7 else kind + "7", pltpu.make_async_remote_copy(
            src_ref=src, dst_ref=dst,
            send_sem=send_sem.at[int(kind == "xy")], recv_sem=recv_sem.at[recv_index[kind]],
            device_id=partner(o), device_id_type=MESH,
        )))

    for i, s in enumerate((-1, 1)):
        k = 1 - i
        at = (Y, Y * X)[i]
        strike = u_hbm.at[:, pl.ds((0, N - Y)[i], Y), :] if s < 0 else uv.at[:, pl.ds(at, Y), :]
        message("xu", (s, 0, 0), strike, rxu.at[k])
        for few in (7, 8):
            some = pl.ds(0, few)
            message("xs", (s, 0, 0), xs.at[i, some], rxs.at[k, some], few)
            message("ys", (0, s, 0), ys.at[i, some], rys.at[k, some], few)
        message("yu", (0, s, 0), u_rows.at[:, :, 0, :] if s < 0 else yu.at[1], ryu.at[k])
        message("zu", (0, 0, s), zu.at[0, pl.ds(0, Y)], rzu.at[k])
        message("zs", (0, 0, s), zs, rzs.at[k])
        for j, s2 in enumerate((-1, 1)):
            m = 1 - j
            lines = xy.at[i, j, pl.ds(0, 3), :] if s + s2 >= 0 else u_rows.at[:, 0, 0, :]
            message("xy", (s, s2, 0), lines, rxy.at[k, m, pl.ds(0, 3), :])
            strike = u_hbm.at[:, pl.ds(0, Y), :] if s + s2 < 0 else uv.at[:, pl.ds(at, Y), :]
            message("xz", (s, 0, s2), strike, rxz.at[k, m])
            message("yz", (0, s, s2), zu, ryz.at[k, m])
        for d in depths:
            message("tx", (s, 0, d), xt.at[i], rtx.at[k, d - 1])
            message("ty", (0, s, d), yt.at[i], rty.at[k, d - 1])
    for d in depths:
        message("t", (0, 0, d), zt, rt.at[d - 1])

    def settle(sem, group):
        rows = group(*own_place)
        for n in sorted({group(*p) for p in places} - {0}):
            @pl.when(rows == n)
            def _(n=n):
                take(sem, n)

    def start(offsets_in, kinds):
        for o in offsets_in:
            chosen = [copy for kind, copy in sends[o] if kind in kinds]
            if chosen:
                @pl.when(has[o])
                def _(chosen=chosen):
                    for copy in chosen:
                        copy.start()

    def arrive(index):
        settle(recv_sem.at[index], groups[index])

    @pl.when(expected > 0)
    def _():
        pl.semaphore_wait(barrier, expected)

    for o in lowers:
        @pl.when(has[o])
        def _(o=o):
            pl.semaphore_signal(
                ready.at[ready_index(minus(o))], inc=1, device_id=partner(o), device_id_type=MESH
            )

    def announce(o):
        low, high = split(o)

        @pl.when(jnp.logical_and(has[minus(low)], has[high]))
        def _():
            kind = 0 if max(high) == 1 and min(low) == -1 else 1
            pl.semaphore_signal(told.at[kind], inc=1, device_id=partner(minus(low)), device_id_type=MESH)

    lowers = sorted(lowers, key=lambda o: (sum(map(abs, o)), o[2], o[1]))
    for kind in ("xz", "yu", "xy", "xu"):
        start(lowers, (kind,))

    take(in_sem.at[0], 4 * N)
    total_depth = Z * layers
    depth = (me[2] * Z + lane).astype(jnp.float32)
    scale = (1.0 + 2.0 * depth / total_depth) / total_depth

    def prefix(planes):
        thirds = [[], [], []]
        for x in planes:
            rest = rv[pl.ds(x * Y, Y), :] * scale
            for k in range(3):
                piece = rest.astype(jnp.bfloat16)
                thirds[k].append(piece)
                rest = rest - piece.astype(jnp.float32)
        weight = jnp.concatenate([jnp.concatenate(k, axis=0) for k in thirds], axis=1)
        triangle = jnp.concatenate([tri[...]] * 3, axis=0)
        sums = jnp.dot(weight, triangle, preferred_element_type=jnp.float32)
        for i, x in enumerate(planes):
            pv[pl.ds(x * Y, Y), :] = sums[i * Y:(i + 1) * Y, :Z] + 1.0
            tot[pl.ds(x * Y, Y), :] = sums[i * Y:(i + 1) * Y, Z:]

    def strain(x):
        base = Y + x * Y
        own = pl.ds(x * Y, Y)
        grad = []
        for c in range(3):
            here = uv[c, pl.ds(base, Y), :]
            grad.append((
                (uv[c, pl.ds(base + Y, Y), :] - uv[c, pl.ds(base - Y, Y), :]) * 0.5,
                uv[c, pl.ds(base + 1, Y), :] * not_last - uv[c, pl.ds(base - 1, Y), :] * not_first,
                pltpu.roll(here, Z - 1, 1) * z_last - pltpu.roll(here, 1, 1) * z_first,
            ))
        el[0, own, :] = grad[0][0]
        el[1, own, :] = grad[1][1]
        el[2, own, :] = grad[2][2]
        el[3, own, :] = 0.5 * (grad[0][1] + grad[1][0])
        el[4, own, :] = 0.5 * (grad[0][2] + grad[2][0])
        el[5, own, :] = 0.5 * (grad[1][2] + grad[2][1])

    def pack(k, x, part, tiles):
        q = (k % 4) * X + x
        tile = pltpu.roll(part, (2 * q + 1) % Z, 1)
        tiles[k // 4] = jnp.where(pair == q, tile, tiles[k // 4])

    def factors(x, tiles):
        own = pl.ds(x * Y, Y)
        minus_two = -2.0 / tv[own, :]
        factor = (2.0 + 14.0 * bv[own, :].astype(jnp.float32)) * jnp.exp(pv[own, :] * minus_two)
        av[own, :] = factor
        nt[own, :] = minus_two
        for i, at in enumerate((0, X - 1)):
            if x == at:
                xs[i, 6] = factor
                xs[i, 7] = minus_two
        if tiles:
            pack(6, x, factor, tiles)
            pack(7, x, minus_two, tiles)

    def elastic(x, tiles):
        own = pl.ds(x * Y, Y)
        for k in range(6):
            part = el[k, own, :] - ev[k, own, :]
            el[k, own, :] = part
            for i, at in enumerate((0, X - 1)):
                if x == at:
                    xs[i, k] = part
            if tiles:
                pack(k, x, part, tiles)

    ends = sorted({0, X - 1})
    inner = [x for x in range(X) if x not in ends]

    def pack_displacement():
        tile0 = plane
        for x in range(X):
            for c in range(3):
                q = c * X + x
                tile = pltpu.roll(uv[c, pl.ds(Y + x * Y, Y), :], (2 * q + 1) % Z, 1)
                tile0 = jnp.where(pair == q, tile, tile0)
        zu[0, pl.ds(0, Y), :] = tile0

    def lines_along_depth():
        tile = row_plane
        pair_x = lax.broadcasted_iota(jnp.int32, (X, Z), 1) >> 1
        for i, line in enumerate((0, Y - 1)):
            for c in range(3):
                p = 3 * i + c
                lines = uv[c, pl.ds(Y + line, X, stride=Y), :]
                yu[i, c] = lines
                tile = jnp.where(pair_x == p, pltpu.roll(lines, (2 * p + 1) % Z, 1), tile)
                for j, at in enumerate((0, X - 1)):
                    xy[j, i, pl.ds(c, 1), :] = uv[c, pl.ds(Y + at * Y + line, 1), :]
        zu[1, pl.ds(0, X), :] = tile

    def total_tiles():
        tile = plane
        for x in range(X):
            tile = jnp.where(pair == x, tot[pl.ds(x * Y, Y), :], tile)
        zt[...] = tile
        for i, (at, line) in enumerate(((0, 0), (X - 1, Y - 1))):
            xt[i] = tot[pl.ds(at * Y, Y), :]
            yt[i] = tot[pl.ds(line, X, stride=Y), :]

    def along_dip(kind):
        for i, line in enumerate((0, Y - 1)):
            for k in range(8):
                src = el.at[k] if k < 6 else (av, nt)[k - 6]
                ys[i, k] = src[pl.ds(line, X, stride=Y), :]
        start(lowers, (kind,))

    @pl.when(above == 0)
    def _():
        prefix(ends)
        for x in ends:
            strain(x)
        take(in_sem.at[1], 12 * Y + 2 * N)
        for x in ends:
            elastic(x, None)
            factors(x, None)
        start(lowers, ("xs7",))
        prefix(inner)
        for x in inner:
            strain(x)
        loads[6].wait()
        for x in inner:
            elastic(x, None)
            factors(x, None)
        along_dip("ys7")
        pack_displacement()
        lines_along_depth()
        total_tiles()
        tiles = [plane, plane]
        for x in range(X):
            for k in range(8):
                src = el.at[k] if k < 6 else (av, nt)[k - 6]
                pack(k, x, src[pl.ds(x * Y, Y), :], tiles)
        for k in range(2):
            zs[k] = tiles[k]

    @pl.when(above > 0)
    def _():
        pack_displacement()
        start(lowers, ("zu",))
        lines_along_depth()
        start(lowers, ("yz",))
        prefix(range(X))
        total_tiles()
        for x in range(X):
            strain(x)
        take(in_sem.at[1], 12 * Y + 2 * N)
        tiles = [plane, plane]
        for x in ends:
            elastic(x, tiles)
            factors(x, tiles)
        start(lowers, ("xs",))
        loads[6].wait()
        for x in inner:
            elastic(x, tiles)
            factors(x, tiles)
        for k in range(2):
            zs[k] = tiles[k]
        start(lowers, ("zs", "t", "tx", "ty"))
        along_dip("ys")

    near = [o for o in uppers if sum(o) == 1]
    number = sum(has[o].astype(jnp.int32) for o in near)

    @pl.when(number > 0)
    def _():
        pl.semaphore_wait(ready.at[0], number)

    for o in mixed:
        low, high = split(o)
        if high in near and minus(low) in near:
            announce(o)
    near.sort()
    start(near, ("zu", "yu", "xu", "t", "zs"))
    others = [o for o in uppers if o not in near]
    far = [o for o in mixed if split(o)[1] not in near or minus(split(o)[0]) not in near]
    close = sorted((o for o in mixed if o not in far), key=lambda o: (abs(o[0]), abs(o[2])))

    diagonal = ("xy", "xz", "yz", "t", "tx", "ty")

    def hear(offsets_in, sem):
        number = sum(has[o].astype(jnp.int32) for o in offsets_in)

        @pl.when(number > 0)
        def _():
            pl.semaphore_wait(sem, number)

        start(offsets_in, diagonal)

    hear(close, told.at[0])
    for kinds, deeper in ((("ys7", "xs7"), False), (("ys", "xs"), True)):
        @pl.when((above > 0) if deeper else (above == 0))
        def _(kinds=kinds):
            start(near, kinds)

    hear(others, ready.at[1])
    for o in far:
        announce(o)
    if far:
        hear(far, told.at[1])

    block = 2 * X

    def shift(tile, by):
        return pltpu.roll(tile, by % Z, 1) if by % Z else tile

    mine = zu[0, pl.ds(0, Y), :]
    from_z = jnp.where(even, shift(mine, -1), -shift(mine, 1))
    for c in range(3):
        zown[c] = shift(from_z, -c * block)

    arrive(0)
    for side, line in enumerate((0, Y - 1)):
        sign = 2.0 * side - 1.0

        @pl.when(has[faces[1][side]])
        def _(side=side, sign=sign, line=line):
            own = pl.ds(line, X, stride=Y)
            for c, (part, factor) in enumerate(TERMS[1]):
                el[part, own, :] = el[part, own, :] + (sign * factor) * ryu[side, c]

    carried = plane
    for d in depths:
        carried = carried + rt[d - 1]
    merged = merge(rzu[0], rzu[1])

    def advance(x):
        own = pl.ds(x * Y, Y)
        e = [el[c, own, :] for c in range(6)]
        for c, (part, factor) in enumerate(TERMS[2]):
            e[part] = e[part] + (2.0 * factor) * edge_term(merged, c * X + x, z_edge)
        load = jnp.broadcast_to(carried[:, 2 * x:2 * x + 1], (Y, Z))
        trace, change = flow(e, av[own, :] * jnp.exp(load * nt[own, :]))
        for c in range(6):
            fv[c, own, :] = ev[c, own, :] + change[c]
            sp[c, pl.ds(Y + x * Y, Y), :] = stress(e, change, trace, c)

    for x in range(X):
        if x not in ends:
            advance(x)
    arrive(1)
    for side, at in enumerate((0, X - 1)):
        sign = 2.0 * side - 1.0

        @pl.when(has[faces[0][side]])
        def _(side=side, sign=sign, at=at):
            own = pl.ds(at * Y, Y)
            for c, (part, factor) in enumerate(TERMS[0]):
                el[part, own, :] = el[part, own, :] + (sign * factor) * rxu[side, c]

    for x in ends:
        advance(x)

    for x in range(X):
        base = Y + x * Y
        own = pl.ds(x * Y, Y)
        for c in range(3):
            cx, cy, cz = X_SET[c], Y_SET[c], Z_SET[c]
            here = sp[cz, pl.ds(base, Y), :]
            total = (sp[cx, pl.ds(base + Y, Y), :] - sp[cx, pl.ds(base - Y, Y), :]) * 0.5
            total = total + (
                sp[cy, pl.ds(base + 1, Y), :] * not_last - sp[cy, pl.ds(base - 1, Y), :] * not_first
            )
            total = total + (pltpu.roll(here, Z - 1, 1) * z_last - pltpu.roll(here, 1, 1) * z_first)
            if c == 2:
                total = total - 0.5 * rv[own, :]
            mv[c, own, :] = total

    def add(e, axis, factor, values):
        for c, (part, f) in enumerate(TERMS[axis]):
            e[part] = e[part] + (factor * f) * values[c]

    def ends_of(first, last, rows, count):
        return jnp.where(rows == 0, -first, jnp.where(rows == count - 1, last, 0.0))

    arrive(2)
    arrive(3)

    def beyond(axis, side, part):
        got, load, e = part
        trace, change = flow(e, got[6] * jnp.exp(jnp.where(above > 0, load * got[7], 0.0)))
        there = has[faces[axis][side]]
        return [
            (side - 0.5) * jnp.where(there, stress(e, change, trace, k), 0.0) for k in (X_SET, Y_SET)[axis]
        ]

    for side in range(2):
        e = [rys[side, k] for k in range(6)]
        add(e, 1, 1.0 - 2.0 * side, [yu[side, c] for c in range(3)])
        add(e, 0, 1.0, [
            ends_of(rxy[0, side, pl.ds(c, 1), :], rxy[1, side, pl.ds(c, 1), :], row_x, X) for c in range(3)
        ])
        joined = merge(ryz[side, 0, 1, pl.ds(0, X), :], ryz[side, 1, 1, pl.ds(0, X), :])
        add(e, 2, 2.0, [edge_term(joined, 3 * (1 - side) + c, z_edge_x) for c in range(3)])
        load = row_plane
        for d in depths:
            load = load + rty[side, d - 1]
        for c, tile in enumerate(beyond(1, side, (rys[side], load, e))):
            dv[side, c] = tile

    along_x = []
    for side, at in enumerate((0, X - 1)):
        e = [rxs[side, k] for k in range(6)]
        add(e, 0, 1.0 - 2.0 * side, [uv[c, pl.ds(Y + at * Y, Y), :] for c in range(3)])
        add(e, 1, 1.0, [
            ends_of(rxy[side, 0, pl.ds(c, 1), :], rxy[side, 1, pl.ds(c, 1), :], row, Y) for c in range(3)
        ])
        add(e, 2, 1.0, [
            jnp.where(
                lane == 0, -pltpu.roll(rxz[side, 0, c], 1, 1),
                jnp.where(lane == Z - 1, pltpu.roll(rxz[side, 1, c], Z - 1, 1), 0.0),
            )
            for c in range(3)
        ])
        load = plane
        for d in depths:
            load = load + rtx[side, d - 1]
        along_x.append(beyond(0, side, (rxs[side], load, e)))

    halo = [jnp.where(even, rzs[0, k], rzs[1, k]) for k in range(2)]
    parts = [shift(halo[k // 4], -(k % 4) * block) for k in range(8)]
    from_x = []
    for c in range(3):
        left, right = (jnp.where(lane == Z - 1, rxz[i, 0, c], rxz[i, 1, c]) for i in range(2))
        from_x.append(jnp.where(
            pair == 0, -shift(left, 1), jnp.where(pair == X - 1, shift(right, 2 * X - 1), 0.0)
        ))
    even_row = (lax.broadcasted_iota(jnp.int32, (1, Z), 1) & 1) == 0
    from_y = ends_of(
        jnp.where(even_row, ryz[0, 0, 0, pl.ds(Y - 1, 1), :], ryz[0, 1, 0, pl.ds(Y - 1, 1), :]),
        jnp.where(even_row, ryz[1, 0, 0, pl.ds(0, 1), :], ryz[1, 1, 0, pl.ds(0, 1), :]),
        row, Y,
    )
    e = list(parts[:6])
    add(e, 0, 1.0, from_x)
    add(e, 1, 1.0, [shift(from_y, -c * block) for c in range(3)])
    add(e, 2, 1.0, [zown[c] for c in range(3)])
    deeper = plane
    for d in depths:
        if d >= 2:
            deeper = deeper + rt[d - 1]
    load = jnp.where(even, deeper, carried + zt[...])
    trace, change = flow(e, parts[6] * jnp.exp(load * parts[7]))
    known = jnp.where(
        even,
        has[0, 0, -1].astype(jnp.float32),
        has[0, 0, 1].astype(jnp.float32),
    )
    for c in range(3):
        jv[c] = jnp.where(pair < X, stress(e, change, trace, Z_SET[c]) * known, 0.0)

    for c in range(3):
        for side, at in enumerate((0, X - 1)):
            own = pl.ds(at * Y, Y)
            mv[c, own, :] = mv[c, own, :] + along_x[side][c]

    settle(send_sem.at[0], gone)
    settle(send_sem.at[1], corner)


def finish(dims, fv, mv, jv, dv, f_hbm, m_hbm, ms, sem):
    X, Y, Z = dims
    copies = [pltpu.make_async_copy(fv, f_hbm, sem.at[0])]
    copies[0].start()
    lane = lax.broadcasted_iota(jnp.int32, (Y, Z), 1)
    z_edge = jnp.where(lane == 0, -0.5, jnp.where(lane == Z - 1, 0.5, 0.0)).astype(jnp.float32)
    row = lax.broadcasted_iota(jnp.int32, (Y, Z), 0)
    joined = [merge(jv[c], jv[c]) for c in range(3)]
    groups = 4
    span = X // groups
    for g in range(groups):
        for x in range(g * span, (g + 1) * span):
            own = pl.ds(x * Y, Y)
            for c in range(3):
                first, last = (dv[side, c, pl.ds(x, 1), :] for side in range(2))
                edge = jnp.where(row == 0, first, jnp.where(row == Y - 1, last, 0.0))
                ms[c, own, :] = mv[c, own, :] + edge + edge_term(joined[c], x, z_edge)
        rows = pl.ds(g * span * Y, span * Y)
        copies.append(pltpu.make_async_copy(ms.at[:, rows, :], m_hbm.at[:, rows, :], sem.at[1 + g]))
        copies[-1].start()
    for copy in copies:
        copy.wait()


def shards(sizes, u, e, t, r, b):
    X, Y, Z = t.shape
    N = X * Y
    layers = sizes[2]
    assert 8 * X <= Z and Z % 128 == 0 and Y % 8 == 0 and X % 8 == 0
    W = max(X, Y)
    f32 = jnp.float32
    vmem = pltpu.VMEM
    dma = pltpu.SemaphoreType.DMA
    any_space = pl.BlockSpec(memory_space=pl.ANY)
    in_vmem = pl.BlockSpec(memory_space=vmem)
    D = max(layers - 1, 1)
    kept = pl.pallas_call(
        functools.partial(kernel, (X, Y, Z), sizes),
        out_shape=(vmem((6, N, Z), f32), vmem((3, N, Z), f32), vmem((3, Y, Z), f32), vmem((2, 3, X, Z), f32)),
        in_specs=[any_space] * 6,
        out_specs=(in_vmem,) * 4,
        scratch_shapes=[
            vmem((3, N + 2 * Y, Z), f32),
            vmem((Z, 2 * Z), jnp.bfloat16),
            vmem((3, Y, Z), f32),
            vmem((6, N, Z), f32),
            vmem((N, Z), f32),
            vmem((N, Z), f32),
            vmem((N, Z), jnp.int32),
            vmem((N, Z), f32),
            vmem((N, Z), f32),
            vmem((6, N, Z), f32),
            vmem((N, Z), f32),
            vmem((N, Z), f32),
            vmem((6, N + 2 * Y, Z), f32),
            vmem((2, 8, Y, Z), f32),
            vmem((2, 8, X, Z), f32),
            vmem((2, 3, X, Z), f32),
            vmem((2, W, Z), f32),
            vmem((2, Y, Z), f32),
            vmem((2, 2, 8, Z), f32),
            vmem((Y, Z), f32),
            vmem((2, Y, Z), f32),
            vmem((2, X, Z), f32),
            vmem((2, 3, Y, Z), f32),
            vmem((2, 8, Y, Z), f32),
            vmem((2, 3, X, Z), f32),
            vmem((2, 8, X, Z), f32),
            vmem((2, Y, Z), f32),
            vmem((2, 2, Y, Z), f32),
            vmem((2, 2, 8, Z), f32),
            vmem((2, 2, 3, Y, Z), f32),
            vmem((2, 2, 2, W, Z), f32),
            vmem((D, Y, Z), f32),
            vmem((2, D, Y, Z), f32),
            vmem((2, D, X, Z), f32),
            dma((3,)),
            pltpu.SemaphoreType.REGULAR((2,)),
            pltpu.SemaphoreType.REGULAR((1 if layers == 2 else 2,)),
            dma((2,)),
            dma((4,)),
            vmem(((11 + layers) * 2 * (X + Y) + (18 + layers) * Y + 8 * W, Z), f32),
        ],
        compiler_params=pltpu.CompilerParams(collective_id=0, has_side_effects=True),
        name="strain_step",
    )(u.reshape(3, N, Z), u, e.reshape(6, N, Z), t.reshape(N, Z), r.reshape(N, Z), b.reshape(N, Z))
    f, m = pl.pallas_call(
        functools.partial(finish, (X, Y, Z)),
        out_shape=(jax.ShapeDtypeStruct((6, N, Z), f32), jax.ShapeDtypeStruct((3, N, Z), f32)),
        in_specs=[in_vmem] * 4,
        out_specs=(any_space, any_space),
        scratch_shapes=[vmem((3, N, Z), f32), dma((5,))],
        name="finish",
    )(*(pltpu.with_memory_space_constraint(k, vmem) for k in kept))
    return f.reshape(6, X, Y, Z), m.reshape(3, X, Y, Z)


def solution(mesh):
    sizes = tuple(mesh.shape[a] for a in AXES)
    field = P("gx", "gy", "gz")
    fields = P(None, "gx", "gy", "gz")
    return jax.shard_map(
        functools.partial(shards, sizes),
        mesh=mesh,
        in_specs=(fields, fields, field, field, field),
        out_specs=(fields, fields),
        check_vma=False,
    )
```

```python
import functools

import jax
import jax.numpy as jnp
from jax import lax
from jax.experimental import pallas as pl
from jax.experimental.pallas import tpu as pltpu
from jax.sharding import PartitionSpec as P

MESH = pl.DeviceIdType.MESH
AXES = ("gx", "gy", "gz")
TERMS = (
    ((0, 0.5), (3, 0.25), (4, 0.25)),
    ((3, 0.25), (1, 0.5), (5, 0.25)),
    ((4, 0.25), (5, 0.25), (2, 0.5)),
)
X_SET = (0, 3, 4)
Y_SET = (3, 1, 5)
Z_SET = (4, 5, 2)


def offsets(layers):
    near = [
        (x, y, z)
        for x in (-1, 0, 1)
        for y in (-1, 0, 1)
        for z in (-1, 0, 1)
        if 1 <= abs(x) + abs(y) + abs(z) <= 2
    ]
    far = [
        (x, y, s * d)
        for d in range(2, layers)
        for s in (-1, 1)
        for x, y in ((0, 0), (-1, 0), (1, 0), (0, -1), (0, 1))
    ]
    return near + far


def minus(o):
    return tuple(-v for v in o)


def plus(o, p):
    return tuple(v + w for v, w in zip(o, p))


def split(o):
    return tuple(min(v, 0) for v in o), tuple(max(v, 0) for v in o)


def kinds_of(layers):
    offs = offsets(layers)
    uppers = [o for o in offs if min(o) >= 0]
    lowers = [o for o in offs if max(o) <= 0]
    mixed = [o for o in offs if min(o) < 0 < max(o)]
    return uppers, lowers, mixed


def merge(low, high):
    Z = low.shape[1]
    even = (lax.broadcasted_iota(jnp.int32, low.shape, 1) & 1) == 0
    return jnp.where(even, low, pltpu.roll(high, Z - 2, 1))


def edge_term(tile, q, z_edge):
    Z = tile.shape[1]
    return (pltpu.roll(tile, (Z - 2 * q) % Z, 1) if q else tile) * z_edge


def flow(e, pace):
    trace = e[0] + e[1] + e[2]
    third = trace * (1.0 / 3.0)
    half = [e[0] - third, e[1] - third, e[2] - third, e[3], e[4], e[5]]
    second = half[0] * half[0] + half[1] * half[1] + half[2] * half[2]
    second = second + 2.0 * (half[3] * half[3] + half[4] * half[4] + half[5] * half[5])
    rate = pace * second
    return trace, [rate * h for h in half]


def stress(e, change, trace, part):
    out = 2.0 * (e[part] - change[part])
    return out + trace if part < 3 else out


def kernel(
    dims, sizes,
    u_hbm, u_rows, e_hbm, t_hbm, r_hbm, b_hbm,
    fv, mv, jv, dv,
    uv, tri, zown, ev, tv, rv, bv, pv, tot, el, av, nt, sp,
    xs, ys, yu, zu, zs, xy, zt, xt, yt,
    rxu, rxs, ryu, rys, rzu, rzs, rxy, rxz, ryz, rt, rtx, rty,
    in_sem, ready, told, send_sem, recv_sem, spare,
):
    X, Y, Z = dims
    N = X * Y
    layers = sizes[2]
    depths = range(1, layers)
    me = [lax.axis_index(a) for a in AXES]
    offs = offsets(layers)
    uppers, lowers, mixed = kinds_of(layers)
    W = max(X, Y)

    def ready_index(o):
        return 0 if sum(o) == 1 else 1

    def exists(o):
        ok = None
        for a in range(3):
            if o[a]:
                here = me[a] + o[a]
                test = here < sizes[a] if o[a] > 0 else here >= 0
                ok = test if ok is None else jnp.logical_and(ok, test)
        return ok

    def partner(o):
        return {AXES[a]: me[a] + o[a] for a in range(3) if o[a]}

    has = {o: exists(o) for o in offs}
    faces = {a: [tuple(s if i == a else 0 for i in range(3)) for s in (-1, 1)] for a in range(3)}

    loads = [
        pltpu.make_async_copy(src, dst, in_sem.at[0 if i < 2 else 1 if i < 6 else 2])
        for i, (src, dst) in enumerate(
            (
                (u_hbm, uv.at[:, pl.ds(Y, N), :]),
                (r_hbm, rv),
                (e_hbm.at[:, pl.ds(0, Y), :], ev.at[:, pl.ds(0, Y), :]),
                (e_hbm.at[:, pl.ds(N - Y, Y), :], ev.at[:, pl.ds(N - Y, Y), :]),
                (t_hbm, tv),
                (b_hbm, bv),
                (e_hbm.at[:, pl.ds(Y, N - 2 * Y), :], ev.at[:, pl.ds(Y, N - 2 * Y), :]),
            )
        )
    ]
    for copy in loads:
        copy.start()

    def take(sem, rows):
        spot = sp.at[pl.ds(0, rows // 3), pl.ds(0, 3)] if rows % 8 else spare.at[pl.ds(0, rows)]
        pltpu.make_async_copy(spot, spot, sem).wait()

    barrier = pltpu.get_barrier_semaphore()
    for o in uppers:
        @pl.when(has[o])
        def _(o=o):
            pl.semaphore_signal(barrier, inc=1, device_id=partner(o), device_id_type=MESH)
    expected = jnp.int32(0)
    for o in lowers:
        expected = expected + has[o].astype(jnp.int32)

    plane = jnp.zeros((Y, Z), jnp.float32)
    row_plane = jnp.zeros((X, Z), jnp.float32)
    for c in range(3):
        uv[c, pl.ds(0, Y), :] = plane
        uv[c, pl.ds(Y + N, Y), :] = plane
    for c in range(6):
        sp[c, pl.ds(0, Y), :] = plane
        sp[c, pl.ds(Y + N, Y), :] = plane

    def blank(o, *refs):
        @pl.when(jnp.logical_not(has[o]))
        def _():
            for ref in refs:
                ref[...] = jnp.zeros(ref.shape, jnp.float32)

    for i, sz in enumerate((-1, 1)):
        blank((0, 0, sz), rzu.at[i], rzs.at[i])
        for j, s in enumerate((-1, 1)):
            blank((s, 0, sz), rxz.at[j, i])
            blank((0, s, sz), ryz.at[j, i])
    for i, sx in enumerate((-1, 1)):
        for j, sy in enumerate((-1, 1)):
            blank((sx, sy, 0), rxy.at[i, j])
    for d in depths:
        blank((0, 0, -d), rt.at[d - 1])
        for j, s in enumerate((-1, 1)):
            blank((s, 0, -d), rtx.at[j, d - 1])
            blank((0, s, -d), rty.at[j, d - 1])

    above_row = lax.broadcasted_iota(jnp.int32, (Z, 2 * Z), 0)
    column = lax.broadcasted_iota(jnp.int32, (Z, 2 * Z), 1)
    triangle = jnp.where(
        (above_row < column) | (column >= Z),
        1.0,
        jnp.where(above_row == column, 0.5, 0.0),
    ).astype(jnp.bfloat16)
    tri[...] = triangle

    lane = lax.broadcasted_iota(jnp.int32, (Y, Z), 1)
    row = lax.broadcasted_iota(jnp.int32, (Y, Z), 0)
    pair = lane >> 1
    even = (lane & 1) == 0
    not_last = jnp.where(row < Y - 1, 0.5, 0.0).astype(jnp.float32)
    not_first = jnp.where(row > 0, 0.5, 0.0).astype(jnp.float32)
    z_first = jnp.where(lane > 0, 0.5, 0.0).astype(jnp.float32)
    z_last = jnp.where(lane < Z - 1, 0.5, 0.0).astype(jnp.float32)
    z_edge = jnp.where(lane == 0, -0.5, jnp.where(lane == Z - 1, 0.5, 0.0)).astype(jnp.float32)
    if X == Y:
        row_x, z_edge_x = row, z_edge
    else:
        lane_x = lax.broadcasted_iota(jnp.int32, (X, Z), 1)
        row_x = lax.broadcasted_iota(jnp.int32, (X, Z), 0)
        z_edge_x = jnp.where(lane_x == 0, -0.5, jnp.where(lane_x == Z - 1, 0.5, 0.0)).astype(jnp.float32)

    beside = [sum(has[o].astype(jnp.int32) for o in faces[a]) for a in range(3)]
    above, below = me[2], layers - 1 - me[2]

    places = [
        (nx, ny, (d > 0) + (d < layers - 1), d)
        for nx in ((0,), (1,), (1, 2))[min(sizes[0], 3) - 1]
        for ny in ((0,), (1,), (1, 2))[min(sizes[1], 3) - 1]
        for d in range(layers)
    ]
    own_place = (*beside, above)

    def planes(d):
        return 7 + jnp.minimum(d, 1) if isinstance(d, jax.Array) else 7 + min(d, 1)

    def sides(nx, ny, nz, d):
        return 3 * X * ny + 3 * Y * nx

    def depths_of(nx, ny, nz, d):
        return Y * (nz + d)

    def late(nx, ny, nz, d):
        return (planes(d) + d) * (Y * nx + X * ny) + 2 * Y * nz + 3 * Y * nx * nz + 2 * W * ny * nz

    def corner(nx, ny, nz, d):
        return 3 * nx * ny

    def gone(nx, ny, nz, d):
        down = layers - 1 - d
        return (planes(d) + 3 + down) * (Y * nx + X * ny) + Y * (3 * nz + down) + 3 * Y * nx * nz + 2 * W * ny * nz

    groups = (sides, depths_of, late, corner)
    recv_index = {
        "yu": 0, "xu": 0, "zu": 1, "t": 1, "xs": 2, "ys": 2, "zs": 2, "xz": 2, "yz": 2, "tx": 2, "ty": 2, "xy": 3,
    }
    sends = {o: [] for o in offs}

    def message(kind, o, src, dst, few=None):
        sends[o].append((kind if few != 7 else kind + "7", pltpu.make_async_remote_copy(
            src_ref=src, dst_ref=dst,
            send_sem=send_sem.at[int(kind == "xy")], recv_sem=recv_sem.at[recv_index[kind]],
            device_id=partner(o), device_id_type=MESH,
        )))

    for i, s in enumerate((-1, 1)):
        k = 1 - i
        at = (Y, Y * X)[i]
        strike = u_hbm.at[:, pl.ds((0, N - Y)[i], Y), :] if s < 0 else uv.at[:, pl.ds(at, Y), :]
        message("xu", (s, 0, 0), strike, rxu.at[k])
        for few in (7, 8):
            some = pl.ds(0, few)
            message("xs", (s, 0, 0), xs.at[i, some], rxs.at[k, some], few)
            message("ys", (0, s, 0), ys.at[i, some], rys.at[k, some], few)
        message("yu", (0, s, 0), u_rows.at[:, :, 0, :] if s < 0 else yu.at[1], ryu.at[k])
        message("zu", (0, 0, s), zu.at[0, pl.ds(0, Y)], rzu.at[k])
        message("zs", (0, 0, s), zs, rzs.at[k])
        for j, s2 in enumerate((-1, 1)):
            m = 1 - j
            lines = xy.at[i, j, pl.ds(0, 3), :] if s + s2 >= 0 else u_rows.at[:, 0, 0, :]
            message("xy", (s, s2, 0), lines, rxy.at[k, m, pl.ds(0, 3), :])
            strike = u_hbm.at[:, pl.ds(0, Y), :] if s + s2 < 0 else uv.at[:, pl.ds(at, Y), :]
            message("xz", (s, 0, s2), strike, rxz.at[k, m])
            message("yz", (0, s, s2), zu, ryz.at[k, m])
        for d in depths:
            message("tx", (s, 0, d), xt.at[i], rtx.at[k, d - 1])
            message("ty", (0, s, d), yt.at[i], rty.at[k, d - 1])
    for d in depths:
        message("t", (0, 0, d), zt, rt.at[d - 1])

    def settle(sem, group):
        rows = group(*own_place)
        for n in sorted({group(*p) for p in places} - {0}):
            @pl.when(rows == n)
            def _(n=n):
                take(sem, n)

    def start(offsets_in, kinds):
        for o in offsets_in:
            chosen = [copy for kind, copy in sends[o] if kind in kinds]
            if chosen:
                @pl.when(has[o])
                def _(chosen=chosen):
                    for copy in chosen:
                        copy.start()

    def arrive(index):
        settle(recv_sem.at[index], groups[index])

    @pl.when(expected > 0)
    def _():
        pl.semaphore_wait(barrier, expected)

    for o in lowers:
        @pl.when(has[o])
        def _(o=o):
            pl.semaphore_signal(
                ready.at[ready_index(minus(o))], inc=1, device_id=partner(o), device_id_type=MESH
            )

    def announce(o):
        low, high = split(o)

        @pl.when(jnp.logical_and(has[minus(low)], has[high]))
        def _():
            kind = 0 if max(high) == 1 and min(low) == -1 else 1
            pl.semaphore_signal(told.at[kind], inc=1, device_id=partner(minus(low)), device_id_type=MESH)

    lowers = sorted(lowers, key=lambda o: (sum(map(abs, o)), o[2], o[1]))
    for kind in ("xz", "yu", "xy", "xu"):
        start(lowers, (kind,))

    take(in_sem.at[0], 4 * N)
    total_depth = Z * layers
    depth = (me[2] * Z + lane).astype(jnp.float32)
    scale = (1.0 + 2.0 * depth / total_depth) / total_depth

    def prefix(planes):
        thirds = [[], [], []]
        for x in planes:
            rest = rv[pl.ds(x * Y, Y), :] * scale
            for k in range(3):
                piece = rest.astype(jnp.bfloat16)
                thirds[k].append(piece)
                rest = rest - piece.astype(jnp.float32)
        weight = jnp.concatenate([jnp.concatenate(k, axis=0) for k in thirds], axis=1)
        triangle = jnp.concatenate([tri[...]] * 3, axis=0)
        sums = jnp.dot(weight, triangle, preferred_element_type=jnp.float32)
        for i, x in enumerate(planes):
            pv[pl.ds(x * Y, Y), :] = sums[i * Y:(i + 1) * Y, :Z] + 1.0
            tot[pl.ds(x * Y, Y), :] = sums[i * Y:(i + 1) * Y, Z:]

    def strain(x):
        base = Y + x * Y
        own = pl.ds(x * Y, Y)
        grad = []
        for c in range(3):
            here = uv[c, pl.ds(base, Y), :]
            grad.append((
                (uv[c, pl.ds(base + Y, Y), :] - uv[c, pl.ds(base - Y, Y), :]) * 0.5,
                uv[c, pl.ds(base + 1, Y), :] * not_last - uv[c, pl.ds(base - 1, Y), :] * not_first,
                pltpu.roll(here, Z - 1, 1) * z_last - pltpu.roll(here, 1, 1) * z_first,
            ))
        el[0, own, :] = grad[0][0]
        el[1, own, :] = grad[1][1]
        el[2, own, :] = grad[2][2]
        el[3, own, :] = 0.5 * (grad[0][1] + grad[1][0])
        el[4, own, :] = 0.5 * (grad[0][2] + grad[2][0])
        el[5, own, :] = 0.5 * (grad[1][2] + grad[2][1])

    def pack(k, x, part, tiles):
        q = (k % 4) * X + x
        tile = pltpu.roll(part, (2 * q + 1) % Z, 1)
        tiles[k // 4] = jnp.where(pair == q, tile, tiles[k // 4])

    def factors(x, tiles):
        own = pl.ds(x * Y, Y)
        minus_two = -2.0 / tv[own, :]
        factor = (2.0 + 14.0 * bv[own, :].astype(jnp.float32)) * jnp.exp(pv[own, :] * minus_two)
        av[own, :] = factor
        nt[own, :] = minus_two
        for i, at in enumerate((0, X - 1)):
            if x == at:
                xs[i, 6] = factor
                xs[i, 7] = minus_two
        if tiles:
            pack(6, x, factor, tiles)
            pack(7, x, minus_two, tiles)

    def elastic(x, tiles):
        own = pl.ds(x * Y, Y)
        for k in range(6):
            part = el[k, own, :] - ev[k, own, :]
            el[k, own, :] = part
            for i, at in enumerate((0, X - 1)):
                if x == at:
                    xs[i, k] = part
            if tiles:
                pack(k, x, part, tiles)

    ends = sorted({0, X - 1})
    inner = [x for x in range(X) if x not in ends]

    def pack_displacement():
        tile0 = plane
        for x in range(X):
            for c in range(3):
                q = c * X + x
                tile = pltpu.roll(uv[c, pl.ds(Y + x * Y, Y), :], (2 * q + 1) % Z, 1)
                tile0 = jnp.where(pair == q, tile, tile0)
        zu[0, pl.ds(0, Y), :] = tile0

    def lines_along_depth():
        tile = row_plane
        pair_x = lax.broadcasted_iota(jnp.int32, (X, Z), 1) >> 1
        for i, line in enumerate((0, Y - 1)):
            for c in range(3):
                p = 3 * i + c
                lines = uv[c, pl.ds(Y + line, X, stride=Y), :]
                yu[i, c] = lines
                tile = jnp.where(pair_x == p, pltpu.roll(lines, (2 * p + 1) % Z, 1), tile)
                for j, at in enumerate((0, X - 1)):
                    xy[j, i, pl.ds(c, 1), :] = uv[c, pl.ds(Y + at * Y + line, 1), :]
        zu[1, pl.ds(0, X), :] = tile

    def total_tiles():
        tile = plane
        for x in range(X):
            tile = jnp.where(pair == x, tot[pl.ds(x * Y, Y), :], tile)
        zt[...] = tile
        for i, (at, line) in enumerate(((0, 0), (X - 1, Y - 1))):
            xt[i] = tot[pl.ds(at * Y, Y), :]
            yt[i] = tot[pl.ds(line, X, stride=Y), :]

    def along_dip(kind):
        for i, line in enumerate((0, Y - 1)):
            for k in range(8):
                src = el.at[k] if k < 6 else (av, nt)[k - 6]
                ys[i, k] = src[pl.ds(line, X, stride=Y), :]
        start(lowers, (kind,))

    @pl.when(above == 0)
    def _():
        prefix(ends)
        for x in ends:
            strain(x)
        take(in_sem.at[1], 12 * Y + 2 * N)
        for x in ends:
            elastic(x, None)
            factors(x, None)
        start(lowers, ("xs7",))
        prefix(inner)
        for x in inner:
            strain(x)
        loads[6].wait()
        for x in inner:
            elastic(x, None)
            factors(x, None)
        along_dip("ys7")
        pack_displacement()
        lines_along_depth()
        total_tiles()
        tiles = [plane, plane]
        for x in range(X):
            for k in range(8):
                src = el.at[k] if k < 6 else (av, nt)[k - 6]
                pack(k, x, src[pl.ds(x * Y, Y), :], tiles)
        for k in range(2):
            zs[k] = tiles[k]

    @pl.when(above > 0)
    def _():
        pack_displacement()
        start(lowers, ("zu",))
        lines_along_depth()
        start(lowers, ("yz",))
        prefix(range(X))
        for x in range(X):
            strain(x)
        take(in_sem.at[1], 12 * Y + 2 * N)
        tiles = [plane, plane]
        for x in ends:
            elastic(x, tiles)
            factors(x, tiles)
        start(lowers, ("xs",))
        loads[6].wait()
        for x in inner:
            elastic(x, tiles)
            factors(x, tiles)
        for k in range(2):
            zs[k] = tiles[k]
        start(lowers, ("zs",))
        along_dip("ys")
        total_tiles()
        start(lowers, ("t", "tx", "ty"))

    near = [o for o in uppers if sum(o) == 1]
    number = sum(has[o].astype(jnp.int32) for o in near)

    @pl.when(number > 0)
    def _():
        pl.semaphore_wait(ready.at[0], number)

    for o in mixed:
        low, high = split(o)
        if high in near and minus(low) in near:
            announce(o)
    near.sort()
    start(near, ("zu", "yu", "xu", "t", "zs"))
    others = [o for o in uppers if o not in near]
    far = [o for o in mixed if split(o)[1] not in near or minus(split(o)[0]) not in near]
    close = sorted((o for o in mixed if o not in far), key=lambda o: (abs(o[0]), abs(o[2])))

    diagonal = ("xy", "xz", "yz", "t", "tx", "ty")

    def hear(offsets_in, sem):
        number = sum(has[o].astype(jnp.int32) for o in offsets_in)

        @pl.when(number > 0)
        def _():
            pl.semaphore_wait(sem, number)

        start(offsets_in, diagonal)

    hear(close, told.at[0])
    for kinds, deeper in ((("ys7", "xs7"), False), (("ys", "xs"), True)):
        @pl.when((above > 0) if deeper else (above == 0))
        def _(kinds=kinds):
            start(near, kinds)

    hear(others, ready.at[1])
    for o in far:
        announce(o)
    if far:
        hear(far, told.at[1])

    block = 2 * X

    def shift(tile, by):
        return pltpu.roll(tile, by % Z, 1) if by % Z else tile

    mine = zu[0, pl.ds(0, Y), :]
    from_z = jnp.where(even, shift(mine, -1), -shift(mine, 1))
    for c in range(3):
        zown[c] = shift(from_z, -c * block)

    arrive(0)
    for side, line in enumerate((0, Y - 1)):
        sign = 2.0 * side - 1.0

        @pl.when(has[faces[1][side]])
        def _(side=side, sign=sign, line=line):
            own = pl.ds(line, X, stride=Y)
            for c, (part, factor) in enumerate(TERMS[1]):
                el[part, own, :] = el[part, own, :] + (sign * factor) * ryu[side, c]

    for side, at in enumerate((0, X - 1)):
        sign = 2.0 * side - 1.0

        @pl.when(has[faces[0][side]])
        def _(side=side, sign=sign, at=at):
            own = pl.ds(at * Y, Y)
            for c, (part, factor) in enumerate(TERMS[0]):
                el[part, own, :] = el[part, own, :] + (sign * factor) * rxu[side, c]

    arrive(1)
    carried = plane
    for d in depths:
        carried = carried + rt[d - 1]
    merged = merge(rzu[0], rzu[1])

    def advance(x):
        own = pl.ds(x * Y, Y)
        e = [el[c, own, :] for c in range(6)]
        for c, (part, factor) in enumerate(TERMS[2]):
            e[part] = e[part] + (2.0 * factor) * edge_term(merged, c * X + x, z_edge)
        load = jnp.broadcast_to(carried[:, 2 * x:2 * x + 1], (Y, Z))
        trace, change = flow(e, av[own, :] * jnp.exp(load * nt[own, :]))
        for c in range(6):
            fv[c, own, :] = ev[c, own, :] + change[c]
            sp[c, pl.ds(Y + x * Y, Y), :] = stress(e, change, trace, c)

    for x in range(X):
        advance(x)

    for x in range(X):
        base = Y + x * Y
        own = pl.ds(x * Y, Y)
        for c in range(3):
            cx, cy, cz = X_SET[c], Y_SET[c], Z_SET[c]
            here = sp[cz, pl.ds(base, Y), :]
            total = (sp[cx, pl.ds(base + Y, Y), :] - sp[cx, pl.ds(base - Y, Y), :]) * 0.5
            total = total + (
                sp[cy, pl.ds(base + 1, Y), :] * not_last - sp[cy, pl.ds(base - 1, Y), :] * not_first
            )
            total = total + (pltpu.roll(here, Z - 1, 1) * z_last - pltpu.roll(here, 1, 1) * z_first)
            if c == 2:
                total = total - 0.5 * rv[own, :]
            mv[c, own, :] = total

    def add(e, axis, factor, values):
        for c, (part, f) in enumerate(TERMS[axis]):
            e[part] = e[part] + (factor * f) * values[c]

    def ends_of(first, last, rows, count):
        return jnp.where(rows == 0, -first, jnp.where(rows == count - 1, last, 0.0))

    arrive(2)
    arrive(3)

    def beyond(axis, side, part):
        got, load, e = part
        trace, change = flow(e, got[6] * jnp.exp(jnp.where(above > 0, load * got[7], 0.0)))
        there = has[faces[axis][side]]
        return [
            (side - 0.5) * jnp.where(there, stress(e, change, trace, k), 0.0) for k in (X_SET, Y_SET)[axis]
        ]

    for side in range(2):
        e = [rys[side, k] for k in range(6)]
        add(e, 1, 1.0 - 2.0 * side, [yu[side, c] for c in range(3)])
        add(e, 0, 1.0, [
            ends_of(rxy[0, side, pl.ds(c, 1), :], rxy[1, side, pl.ds(c, 1), :], row_x, X) for c in range(3)
        ])
        joined = merge(ryz[side, 0, 1, pl.ds(0, X), :], ryz[side, 1, 1, pl.ds(0, X), :])
        add(e, 2, 2.0, [edge_term(joined, 3 * (1 - side) + c, z_edge_x) for c in range(3)])
        load = row_plane
        for d in depths:
            load = load + rty[side, d - 1]
        for c, tile in enumerate(beyond(1, side, (rys[side], load, e))):
            dv[side, c] = tile

    along_x = []
    for side, at in enumerate((0, X - 1)):
        e = [rxs[side, k] for k in range(6)]
        add(e, 0, 1.0 - 2.0 * side, [uv[c, pl.ds(Y + at * Y, Y), :] for c in range(3)])
        add(e, 1, 1.0, [
            ends_of(rxy[side, 0, pl.ds(c, 1), :], rxy[side, 1, pl.ds(c, 1), :], row, Y) for c in range(3)
        ])
        add(e, 2, 1.0, [
            jnp.where(
                lane == 0, -pltpu.roll(rxz[side, 0, c], 1, 1),
                jnp.where(lane == Z - 1, pltpu.roll(rxz[side, 1, c], Z - 1, 1), 0.0),
            )
            for c in range(3)
        ])
        load = plane
        for d in depths:
            load = load + rtx[side, d - 1]
        along_x.append(beyond(0, side, (rxs[side], load, e)))

    halo = [jnp.where(even, rzs[0, k], rzs[1, k]) for k in range(2)]
    parts = [shift(halo[k // 4], -(k % 4) * block) for k in range(8)]
    from_x = []
    for c in range(3):
        left, right = (jnp.where(lane == Z - 1, rxz[i, 0, c], rxz[i, 1, c]) for i in range(2))
        from_x.append(jnp.where(
            pair == 0, -shift(left, 1), jnp.where(pair == X - 1, shift(right, 2 * X - 1), 0.0)
        ))
    even_row = (lax.broadcasted_iota(jnp.int32, (1, Z), 1) & 1) == 0
    from_y = ends_of(
        jnp.where(even_row, ryz[0, 0, 0, pl.ds(Y - 1, 1), :], ryz[0, 1, 0, pl.ds(Y - 1, 1), :]),
        jnp.where(even_row, ryz[1, 0, 0, pl.ds(0, 1), :], ryz[1, 1, 0, pl.ds(0, 1), :]),
        row, Y,
    )
    e = list(parts[:6])
    add(e, 0, 1.0, from_x)
    add(e, 1, 1.0, [shift(from_y, -c * block) for c in range(3)])
    add(e, 2, 1.0, [zown[c] for c in range(3)])
    deeper = plane
    for d in depths:
        if d >= 2:
            deeper = deeper + rt[d - 1]
    load = jnp.where(even, deeper, carried + zt[...])
    trace, change = flow(e, parts[6] * jnp.exp(load * parts[7]))
    known = jnp.where(
        even,
        has[0, 0, -1].astype(jnp.float32),
        has[0, 0, 1].astype(jnp.float32),
    )
    for c in range(3):
        jv[c] = jnp.where(pair < X, stress(e, change, trace, Z_SET[c]) * known, 0.0)

    for c in range(3):
        for side, at in enumerate((0, X - 1)):
            own = pl.ds(at * Y, Y)
            mv[c, own, :] = mv[c, own, :] + along_x[side][c]

    settle(send_sem.at[0], gone)
    settle(send_sem.at[1], corner)


def finish(dims, fv, mv, jv, dv, f_hbm, m_hbm, ms, sem):
    X, Y, Z = dims
    copies = [pltpu.make_async_copy(fv, f_hbm, sem.at[0])]
    copies[0].start()
    lane = lax.broadcasted_iota(jnp.int32, (Y, Z), 1)
    z_edge = jnp.where(lane == 0, -0.5, jnp.where(lane == Z - 1, 0.5, 0.0)).astype(jnp.float32)
    row = lax.broadcasted_iota(jnp.int32, (Y, Z), 0)
    joined = [merge(jv[c], jv[c]) for c in range(3)]
    groups = 4
    span = X // groups
    for g in range(groups):
        for x in range(g * span, (g + 1) * span):
            own = pl.ds(x * Y, Y)
            for c in range(3):
                first, last = (dv[side, c, pl.ds(x, 1), :] for side in range(2))
                edge = jnp.where(row == 0, first, jnp.where(row == Y - 1, last, 0.0))
                ms[c, own, :] = mv[c, own, :] + edge + edge_term(joined[c], x, z_edge)
        rows = pl.ds(g * span * Y, span * Y)
        copies.append(pltpu.make_async_copy(ms.at[:, rows, :], m_hbm.at[:, rows, :], sem.at[1 + g]))
        copies[-1].start()
    for copy in copies:
        copy.wait()


def shards(sizes, u, e, t, r, b):
    X, Y, Z = t.shape
    N = X * Y
    layers = sizes[2]
    assert 8 * X <= Z and Z % 128 == 0 and Y % 8 == 0 and X % 8 == 0
    W = max(X, Y)
    f32 = jnp.float32
    vmem = pltpu.VMEM
    dma = pltpu.SemaphoreType.DMA
    any_space = pl.BlockSpec(memory_space=pl.ANY)
    in_vmem = pl.BlockSpec(memory_space=vmem)
    D = max(layers - 1, 1)
    kept = pl.pallas_call(
        functools.partial(kernel, (X, Y, Z), sizes),
        out_shape=(vmem((6, N, Z), f32), vmem((3, N, Z), f32), vmem((3, Y, Z), f32), vmem((2, 3, X, Z), f32)),
        in_specs=[any_space] * 6,
        out_specs=(in_vmem,) * 4,
        scratch_shapes=[
            vmem((3, N + 2 * Y, Z), f32),
            vmem((Z, 2 * Z), jnp.bfloat16),
            vmem((3, Y, Z), f32),
            vmem((6, N, Z), f32),
            vmem((N, Z), f32),
            vmem((N, Z), f32),
            vmem((N, Z), jnp.int32),
            vmem((N, Z), f32),
            vmem((N, Z), f32),
            vmem((6, N, Z), f32),
            vmem((N, Z), f32),
            vmem((N, Z), f32),
            vmem((6, N + 2 * Y, Z), f32),
            vmem((2, 8, Y, Z), f32),
            vmem((2, 8, X, Z), f32),
            vmem((2, 3, X, Z), f32),
            vmem((2, W, Z), f32),
            vmem((2, Y, Z), f32),
            vmem((2, 2, 8, Z), f32),
            vmem((Y, Z), f32),
            vmem((2, Y, Z), f32),
            vmem((2, X, Z), f32),
            vmem((2, 3, Y, Z), f32),
            vmem((2, 8, Y, Z), f32),
            vmem((2, 3, X, Z), f32),
            vmem((2, 8, X, Z), f32),
            vmem((2, Y, Z), f32),
            vmem((2, 2, Y, Z), f32),
            vmem((2, 2, 8, Z), f32),
            vmem((2, 2, 3, Y, Z), f32),
            vmem((2, 2, 2, W, Z), f32),
            vmem((D, Y, Z), f32),
            vmem((2, D, Y, Z), f32),
            vmem((2, D, X, Z), f32),
            dma((3,)),
            pltpu.SemaphoreType.REGULAR((2,)),
            pltpu.SemaphoreType.REGULAR((1 if layers == 2 else 2,)),
            dma((2,)),
            dma((4,)),
            vmem(((11 + layers) * 2 * (X + Y) + (18 + layers) * Y + 8 * W, Z), f32),
        ],
        compiler_params=pltpu.CompilerParams(collective_id=0, has_side_effects=True),
        name="strain_step",
    )(u.reshape(3, N, Z), u, e.reshape(6, N, Z), t.reshape(N, Z), r.reshape(N, Z), b.reshape(N, Z))
    f, m = pl.pallas_call(
        functools.partial(finish, (X, Y, Z)),
        out_shape=(jax.ShapeDtypeStruct((6, N, Z), f32), jax.ShapeDtypeStruct((3, N, Z), f32)),
        in_specs=[in_vmem] * 4,
        out_specs=(any_space, any_space),
        scratch_shapes=[vmem((3, N, Z), f32), dma((5,))],
        name="finish",
    )(*(pltpu.with_memory_space_constraint(k, vmem) for k in kept))
    return f.reshape(6, X, Y, Z), m.reshape(3, X, Y, Z)


def solution(mesh):
    sizes = tuple(mesh.shape[a] for a in AXES)
    field = P("gx", "gy", "gz")
    fields = P(None, "gx", "gy", "gz")
    return jax.shard_map(
        functools.partial(shards, sizes),
        mesh=mesh,
        in_specs=(fields, fields, field, field, field),
        out_specs=(fields, fields),
        check_vma=False,
    )
```

```python
import functools

import jax
import jax.numpy as jnp
from jax import lax
from jax.experimental import pallas as pl
from jax.experimental.pallas import tpu as pltpu
from jax.sharding import PartitionSpec as P

MESH = pl.DeviceIdType.MESH
AXES = ("gx", "gy", "gz")
TERMS = (
    ((0, 0.5), (3, 0.25), (4, 0.25)),
    ((3, 0.25), (1, 0.5), (5, 0.25)),
    ((4, 0.25), (5, 0.25), (2, 0.5)),
)
X_SET = (0, 3, 4)
Y_SET = (3, 1, 5)
Z_SET = (4, 5, 2)


def offsets(layers):
    near = [
        (x, y, z)
        for x in (-1, 0, 1)
        for y in (-1, 0, 1)
        for z in (-1, 0, 1)
        if 1 <= abs(x) + abs(y) + abs(z) <= 2
    ]
    far = [
        (x, y, s * d)
        for d in range(2, layers)
        for s in (-1, 1)
        for x, y in ((0, 0), (-1, 0), (1, 0), (0, -1), (0, 1))
    ]
    return near + far


def minus(o):
    return tuple(-v for v in o)


def plus(o, p):
    return tuple(v + w for v, w in zip(o, p))


def split(o):
    return tuple(min(v, 0) for v in o), tuple(max(v, 0) for v in o)


def kinds_of(layers):
    offs = offsets(layers)
    uppers = [o for o in offs if min(o) >= 0]
    lowers = [o for o in offs if max(o) <= 0]
    mixed = [o for o in offs if min(o) < 0 < max(o)]
    return uppers, lowers, mixed


def merge(low, high):
    Z = low.shape[1]
    even = (lax.broadcasted_iota(jnp.int32, low.shape, 1) & 1) == 0
    return jnp.where(even, low, pltpu.roll(high, Z - 2, 1))


def edge_term(tile, q, z_edge):
    Z = tile.shape[1]
    return (pltpu.roll(tile, (Z - 2 * q) % Z, 1) if q else tile) * z_edge


def flow(e, pace):
    trace = e[0] + e[1] + e[2]
    third = trace * (1.0 / 3.0)
    half = [e[0] - third, e[1] - third, e[2] - third, e[3], e[4], e[5]]
    second = half[0] * half[0] + half[1] * half[1] + half[2] * half[2]
    second = second + 2.0 * (half[3] * half[3] + half[4] * half[4] + half[5] * half[5])
    rate = pace * second
    return trace, [rate * h for h in half]


def stress(e, change, trace, part):
    out = 2.0 * (e[part] - change[part])
    return out + trace if part < 3 else out


def kernel(
    dims, sizes,
    u_hbm, u_rows, e_hbm, t_hbm, r_hbm, b_hbm,
    fv, mv, jv, dv,
    uv, tri, zown, ev, tv, rv, bv, pv, tot, el, av, nt, sp,
    xs, ys, yu, zu, zs, xy, zt, xt, yt,
    rxu, rxs, ryu, rys, rzu, rzs, rxy, rxz, ryz, rt, rtx, rty,
    in_sem, ready, told, send_sem, recv_sem, spare,
):
    X, Y, Z = dims
    N = X * Y
    layers = sizes[2]
    depths = range(1, layers)
    me = [lax.axis_index(a) for a in AXES]
    offs = offsets(layers)
    uppers, lowers, mixed = kinds_of(layers)
    W = max(X, Y)

    def ready_index(o):
        return 0 if sum(o) == 1 else 1

    def exists(o):
        ok = None
        for a in range(3):
            if o[a]:
                here = me[a] + o[a]
                test = here < sizes[a] if o[a] > 0 else here >= 0
                ok = test if ok is None else jnp.logical_and(ok, test)
        return ok

    def partner(o):
        return {AXES[a]: me[a] + o[a] for a in range(3) if o[a]}

    has = {o: exists(o) for o in offs}
    faces = {a: [tuple(s if i == a else 0 for i in range(3)) for s in (-1, 1)] for a in range(3)}

    loads = [
        pltpu.make_async_copy(src, dst, in_sem.at[0 if i < 2 else 1 if i < 6 else 2])
        for i, (src, dst) in enumerate(
            (
                (u_hbm, uv.at[:, pl.ds(Y, N), :]),
                (r_hbm, rv),
                (e_hbm.at[:, pl.ds(0, Y), :], ev.at[:, pl.ds(0, Y), :]),
                (e_hbm.at[:, pl.ds(N - Y, Y), :], ev.at[:, pl.ds(N - Y, Y), :]),
                (t_hbm, tv),
                (b_hbm, bv),
                (e_hbm.at[:, pl.ds(Y, N - 2 * Y), :], ev.at[:, pl.ds(Y, N - 2 * Y), :]),
            )
        )
    ]
    for copy in loads:
        copy.start()

    def take(sem, rows):
        spot = spare.at[pl.ds(0, rows)]
        pltpu.make_async_copy(spot, spot, sem).wait()

    barrier = pltpu.get_barrier_semaphore()
    for o in uppers:
        @pl.when(has[o])
        def _(o=o):
            pl.semaphore_signal(barrier, inc=1, device_id=partner(o), device_id_type=MESH)
    expected = jnp.int32(0)
    for o in lowers:
        expected = expected + has[o].astype(jnp.int32)

    plane = jnp.zeros((Y, Z), jnp.float32)
    row_plane = jnp.zeros((X, Z), jnp.float32)
    for c in range(3):
        uv[c, pl.ds(0, Y), :] = plane
        uv[c, pl.ds(Y + N, Y), :] = plane
    for c in range(6):
        sp[c, pl.ds(0, Y), :] = plane
        sp[c, pl.ds(Y + N, Y), :] = plane

    def blank(o, *refs):
        @pl.when(jnp.logical_not(has[o]))
        def _():
            for ref in refs:
                ref[...] = jnp.zeros(ref.shape, jnp.float32)

    for i, sz in enumerate((-1, 1)):
        blank((0, 0, sz), rzu.at[i], rzs.at[i])
        for j, s in enumerate((-1, 1)):
            blank((s, 0, sz), rxz.at[j, i])
            blank((0, s, sz), ryz.at[j, i])
    for i, sx in enumerate((-1, 1)):
        for j, sy in enumerate((-1, 1)):
            blank((sx, sy, 0), rxy.at[i, j])
    for d in depths:
        blank((0, 0, -d), rt.at[d - 1])
        for j, s in enumerate((-1, 1)):
            blank((s, 0, -d), rtx.at[j, d - 1])
            blank((0, s, -d), rty.at[j, d - 1])

    above_row = lax.broadcasted_iota(jnp.int32, (Z, 2 * Z), 0)
    column = lax.broadcasted_iota(jnp.int32, (Z, 2 * Z), 1)
    triangle = jnp.where(
        (above_row < column) | (column >= Z),
        1.0,
        jnp.where(above_row == column, 0.5, 0.0),
    ).astype(jnp.bfloat16)
    tri[...] = triangle

    lane = lax.broadcasted_iota(jnp.int32, (Y, Z), 1)
    row = lax.broadcasted_iota(jnp.int32, (Y, Z), 0)
    pair = lane >> 1
    even = (lane & 1) == 0
    not_last = jnp.where(row < Y - 1, 0.5, 0.0).astype(jnp.float32)
    not_first = jnp.where(row > 0, 0.5, 0.0).astype(jnp.float32)
    z_first = jnp.where(lane > 0, 0.5, 0.0).astype(jnp.float32)
    z_last = jnp.where(lane < Z - 1, 0.5, 0.0).astype(jnp.float32)
    z_edge = jnp.where(lane == 0, -0.5, jnp.where(lane == Z - 1, 0.5, 0.0)).astype(jnp.float32)
    if X == Y:
        row_x, z_edge_x = row, z_edge
    else:
        lane_x = lax.broadcasted_iota(jnp.int32, (X, Z), 1)
        row_x = lax.broadcasted_iota(jnp.int32, (X, Z), 0)
        z_edge_x = jnp.where(lane_x == 0, -0.5, jnp.where(lane_x == Z - 1, 0.5, 0.0)).astype(jnp.float32)

    beside = [sum(has[o].astype(jnp.int32) for o in faces[a]) for a in range(3)]
    above, below = me[2], layers - 1 - me[2]

    places = [
        (nx, ny, (d > 0) + (d < layers - 1), d)
        for nx in ((0,), (1,), (1, 2))[min(sizes[0], 3) - 1]
        for ny in ((0,), (1,), (1, 2))[min(sizes[1], 3) - 1]
        for d in range(layers)
    ]
    own_place = (*beside, above)

    def planes(d):
        return 7 + jnp.minimum(d, 1) if isinstance(d, jax.Array) else 7 + min(d, 1)

    def sides(nx, ny, nz, d):
        return 3 * X * ny + 3 * Y * nx

    def depths_of(nx, ny, nz, d):
        return Y * (nz + d)

    def corners(nx, ny, nz):
        return 3 * nx * ny + 3 * Y * nx * nz + 2 * W * ny * nz

    def late(nx, ny, nz, d):
        return (planes(d) + d) * (Y * nx + X * ny) + 2 * Y * nz + corners(nx, ny, nz)

    def gone(nx, ny, nz, d):
        down = layers - 1 - d
        return (planes(d) + 3 + down) * (Y * nx + X * ny) + Y * (3 * nz + down) + corners(nx, ny, nz)

    groups = (sides, depths_of, late)
    recv_index = {
        "yu": 0, "xu": 0, "zu": 1, "t": 1, "xs": 2, "ys": 2, "zs": 2, "xz": 2, "yz": 2, "tx": 2, "ty": 2, "xy": 2,
    }
    sends = {o: [] for o in offs}

    def message(kind, o, src, dst, few=None):
        sends[o].append((kind if few != 7 else kind + "7", pltpu.make_async_remote_copy(
            src_ref=src, dst_ref=dst,
            send_sem=send_sem.at[0], recv_sem=recv_sem.at[recv_index[kind]],
            device_id=partner(o), device_id_type=MESH,
        )))

    for i, s in enumerate((-1, 1)):
        k = 1 - i
        at = (Y, Y * X)[i]
        strike = u_hbm.at[:, pl.ds((0, N - Y)[i], Y), :] if s < 0 else uv.at[:, pl.ds(at, Y), :]
        message("xu", (s, 0, 0), strike, rxu.at[k])
        for few in (7, 8):
            some = pl.ds(0, few)
            message("xs", (s, 0, 0), xs.at[i, some], rxs.at[k, some], few)
            message("ys", (0, s, 0), ys.at[i, some], rys.at[k, some], few)
        message("yu", (0, s, 0), u_rows.at[:, :, 0, :] if s < 0 else yu.at[1], ryu.at[k])
        message("zu", (0, 0, s), zu.at[0, pl.ds(0, Y)], rzu.at[k])
        message("zs", (0, 0, s), zs, rzs.at[k])
        for j, s2 in enumerate((-1, 1)):
            m = 1 - j
            lines = xy.at[i, j, pl.ds(0, 3), :] if s + s2 >= 0 else u_rows.at[:, 0, 0, :]
            message("xy", (s, s2, 0), lines, rxy.at[k, m, pl.ds(0, 3), :])
            strike = u_hbm.at[:, pl.ds(0, Y), :] if s + s2 < 0 else uv.at[:, pl.ds(at, Y), :]
            message("xz", (s, 0, s2), strike, rxz.at[k, m])
            message("yz", (0, s, s2), zu, ryz.at[k, m])
        for d in depths:
            message("tx", (s, 0, d), xt.at[i], rtx.at[k, d - 1])
            message("ty", (0, s, d), yt.at[i], rty.at[k, d - 1])
    for d in depths:
        message("t", (0, 0, d), zt, rt.at[d - 1])

    def settle(sem, group):
        rows = group(*own_place)
        for n in sorted({group(*p) for p in places} - {0}):
            @pl.when(rows == n)
            def _(n=n):
                take(sem, n)

    def start(offsets_in, kinds):
        for o in offsets_in:
            chosen = [copy for kind, copy in sends[o] if kind in kinds]
            if chosen:
                @pl.when(has[o])
                def _(chosen=chosen):
                    for copy in chosen:
                        copy.start()

    def arrive(index):
        settle(recv_sem.at[index], groups[index])

    @pl.when(expected > 0)
    def _():
        pl.semaphore_wait(barrier, expected)

    for o in lowers:
        @pl.when(has[o])
        def _(o=o):
            pl.semaphore_signal(
                ready.at[ready_index(minus(o))], inc=1, device_id=partner(o), device_id_type=MESH
            )

    def announce(o):
        low, high = split(o)

        @pl.when(jnp.logical_and(has[minus(low)], has[high]))
        def _():
            kind = 0 if max(high) == 1 and min(low) == -1 else 1
            pl.semaphore_signal(told.at[kind], inc=1, device_id=partner(minus(low)), device_id_type=MESH)

    lowers = sorted(lowers, key=lambda o: (sum(map(abs, o)), o[2], o[1]))
    for kind in ("xz", "yu", "xy", "xu"):
        start(lowers, (kind,))

    take(in_sem.at[0], 4 * N)
    total_depth = Z * layers
    depth = (me[2] * Z + lane).astype(jnp.float32)
    scale = (1.0 + 2.0 * depth / total_depth) / total_depth

    def prefix(planes):
        thirds = [[], [], []]
        for x in planes:
            rest = rv[pl.ds(x * Y, Y), :] * scale
            for k in range(3):
                piece = rest.astype(jnp.bfloat16)
                thirds[k].append(piece)
                rest = rest - piece.astype(jnp.float32)
        weight = jnp.concatenate([jnp.concatenate(k, axis=0) for k in thirds], axis=1)
        triangle = jnp.concatenate([tri[...]] * 3, axis=0)
        sums = jnp.dot(weight, triangle, preferred_element_type=jnp.float32)
        for i, x in enumerate(planes):
            pv[pl.ds(x * Y, Y), :] = sums[i * Y:(i + 1) * Y, :Z] + 1.0
            tot[pl.ds(x * Y, Y), :] = sums[i * Y:(i + 1) * Y, Z:]

    def strain(x):
        base = Y + x * Y
        own = pl.ds(x * Y, Y)
        grad = []
        for c in range(3):
            here = uv[c, pl.ds(base, Y), :]
            grad.append((
                (uv[c, pl.ds(base + Y, Y), :] - uv[c, pl.ds(base - Y, Y), :]) * 0.5,
                uv[c, pl.ds(base + 1, Y), :] * not_last - uv[c, pl.ds(base - 1, Y), :] * not_first,
                pltpu.roll(here, Z - 1, 1) * z_last - pltpu.roll(here, 1, 1) * z_first,
            ))
        el[0, own, :] = grad[0][0]
        el[1, own, :] = grad[1][1]
        el[2, own, :] = grad[2][2]
        el[3, own, :] = 0.5 * (grad[0][1] + grad[1][0])
        el[4, own, :] = 0.5 * (grad[0][2] + grad[2][0])
        el[5, own, :] = 0.5 * (grad[1][2] + grad[2][1])

    def pack(k, x, part, tiles):
        q = (k % 4) * X + x
        tile = pltpu.roll(part, (2 * q + 1) % Z, 1)
        tiles[k // 4] = jnp.where(pair == q, tile, tiles[k // 4])

    def factors(x, tiles):
        own = pl.ds(x * Y, Y)
        minus_two = -2.0 / tv[own, :]
        factor = (2.0 + 14.0 * bv[own, :].astype(jnp.float32)) * jnp.exp(pv[own, :] * minus_two)
        av[own, :] = factor
        nt[own, :] = minus_two
        for i, at in enumerate((0, X - 1)):
            if x == at:
                xs[i, 6] = factor
                xs[i, 7] = minus_two
        if tiles:
            pack(6, x, factor, tiles)
            pack(7, x, minus_two, tiles)

    def elastic(x, tiles):
        own = pl.ds(x * Y, Y)
        for k in range(6):
            part = el[k, own, :] - ev[k, own, :]
            el[k, own, :] = part
            for i, at in enumerate((0, X - 1)):
                if x == at:
                    xs[i, k] = part
            if tiles:
                pack(k, x, part, tiles)

    ends = sorted({0, X - 1})
    inner = [x for x in range(X) if x not in ends]

    def pack_displacement():
        tile0 = plane
        for x in range(X):
            for c in range(3):
                q = c * X + x
                tile = pltpu.roll(uv[c, pl.ds(Y + x * Y, Y), :], (2 * q + 1) % Z, 1)
                tile0 = jnp.where(pair == q, tile, tile0)
        zu[0, pl.ds(0, Y), :] = tile0

    def lines_along_depth():
        tile = row_plane
        pair_x = lax.broadcasted_iota(jnp.int32, (X, Z), 1) >> 1
        for i, line in enumerate((0, Y - 1)):
            for c in range(3):
                p = 3 * i + c
                lines = uv[c, pl.ds(Y + line, X, stride=Y), :]
                yu[i, c] = lines
                tile = jnp.where(pair_x == p, pltpu.roll(lines, (2 * p + 1) % Z, 1), tile)
                for j, at in enumerate((0, X - 1)):
                    xy[j, i, pl.ds(c, 1), :] = uv[c, pl.ds(Y + at * Y + line, 1), :]
        zu[1, pl.ds(0, X), :] = tile

    def total_tiles():
        tile = plane
        for x in range(X):
            tile = jnp.where(pair == x, tot[pl.ds(x * Y, Y), :], tile)
        zt[...] = tile
        for i, (at, line) in enumerate(((0, 0), (X - 1, Y - 1))):
            xt[i] = tot[pl.ds(at * Y, Y), :]
            yt[i] = tot[pl.ds(line, X, stride=Y), :]

    def along_dip(kind):
        for i, line in enumerate((0, Y - 1)):
            for k in range(8):
                src = el.at[k] if k < 6 else (av, nt)[k - 6]
                ys[i, k] = src[pl.ds(line, X, stride=Y), :]
        start(lowers, (kind,))

    @pl.when(above == 0)
    def _():
        prefix(ends)
        for x in ends:
            strain(x)
        take(in_sem.at[1], 12 * Y + 2 * N)
        for x in ends:
            elastic(x, None)
            factors(x, None)
        start(lowers, ("xs7",))
        prefix(inner)
        for x in inner:
            strain(x)
        loads[6].wait()
        for x in inner:
            elastic(x, None)
            factors(x, None)
        along_dip("ys7")
        pack_displacement()
        lines_along_depth()
        total_tiles()
        tiles = [plane, plane]
        for x in range(X):
            for k in range(8):
                src = el.at[k] if k < 6 else (av, nt)[k - 6]
                pack(k, x, src[pl.ds(x * Y, Y), :], tiles)
        for k in range(2):
            zs[k] = tiles[k]

    @pl.when(above > 0)
    def _():
        pack_displacement()
        start(lowers, ("zu",))
        lines_along_depth()
        start(lowers, ("yz",))
        prefix(range(X))
        for x in range(X):
            strain(x)
        take(in_sem.at[1], 12 * Y + 2 * N)
        tiles = [plane, plane]
        for x in ends:
            elastic(x, tiles)
            factors(x, tiles)
        start(lowers, ("xs",))
        loads[6].wait()
        for x in inner:
            elastic(x, tiles)
            factors(x, tiles)
        for k in range(2):
            zs[k] = tiles[k]
        start(lowers, ("zs",))
        along_dip("ys")
        total_tiles()
        start(lowers, ("t", "tx", "ty"))

    near = [o for o in uppers if sum(o) == 1]
    number = sum(has[o].astype(jnp.int32) for o in near)

    @pl.when(number > 0)
    def _():
        pl.semaphore_wait(ready.at[0], number)

    for o in mixed:
        low, high = split(o)
        if high in near and minus(low) in near:
            announce(o)
    near.sort()
    start(near, ("zu", "yu", "xu", "t", "zs"))
    others = [o for o in uppers if o not in near]
    far = [o for o in mixed if split(o)[1] not in near or minus(split(o)[0]) not in near]
    close = sorted((o for o in mixed if o not in far), key=lambda o: (abs(o[0]), abs(o[2])))

    diagonal = ("xy", "xz", "yz", "t", "tx", "ty")

    def hear(offsets_in, sem):
        number = sum(has[o].astype(jnp.int32) for o in offsets_in)

        @pl.when(number > 0)
        def _():
            pl.semaphore_wait(sem, number)

        start(offsets_in, diagonal)

    hear(close, told.at[0])
    for kinds, deeper in ((("ys7", "xs7"), False), (("ys", "xs"), True)):
        @pl.when((above > 0) if deeper else (above == 0))
        def _(kinds=kinds):
            start(near, kinds)

    hear(others, ready.at[1])
    for o in far:
        announce(o)
    if far:
        hear(far, told.at[1])

    block = 2 * X

    def shift(tile, by):
        return pltpu.roll(tile, by % Z, 1) if by % Z else tile

    mine = zu[0, pl.ds(0, Y), :]
    from_z = jnp.where(even, shift(mine, -1), -shift(mine, 1))
    for c in range(3):
        zown[c] = shift(from_z, -c * block)

    arrive(0)
    for side, line in enumerate((0, Y - 1)):
        sign = 2.0 * side - 1.0

        @pl.when(has[faces[1][side]])
        def _(side=side, sign=sign, line=line):
            own = pl.ds(line, X, stride=Y)
            for c, (part, factor) in enumerate(TERMS[1]):
                el[part, own, :] = el[part, own, :] + (sign * factor) * ryu[side, c]

    for side, at in enumerate((0, X - 1)):
        sign = 2.0 * side - 1.0

        @pl.when(has[faces[0][side]])
        def _(side=side, sign=sign, at=at):
            own = pl.ds(at * Y, Y)
            for c, (part, factor) in enumerate(TERMS[0]):
                el[part, own, :] = el[part, own, :] + (sign * factor) * rxu[side, c]

    arrive(1)
    carried = plane
    for d in depths:
        carried = carried + rt[d - 1]
    merged = merge(rzu[0], rzu[1])

    def advance(x):
        own = pl.ds(x * Y, Y)
        e = [el[c, own, :] for c in range(6)]
        for c, (part, factor) in enumerate(TERMS[2]):
            e[part] = e[part] + (2.0 * factor) * edge_term(merged, c * X + x, z_edge)
        load = jnp.broadcast_to(carried[:, 2 * x:2 * x + 1], (Y, Z))
        trace, change = flow(e, av[own, :] * jnp.exp(load * nt[own, :]))
        for c in range(6):
            fv[c, own, :] = ev[c, own, :] + change[c]
            sp[c, pl.ds(Y + x * Y, Y), :] = stress(e, change, trace, c)

    for x in range(X):
        advance(x)

    for x in range(X):
        base = Y + x * Y
        own = pl.ds(x * Y, Y)
        for c in range(3):
            cx, cy, cz = X_SET[c], Y_SET[c], Z_SET[c]
            here = sp[cz, pl.ds(base, Y), :]
            total = (sp[cx, pl.ds(base + Y, Y), :] - sp[cx, pl.ds(base - Y, Y), :]) * 0.5
            total = total + (
                sp[cy, pl.ds(base + 1, Y), :] * not_last - sp[cy, pl.ds(base - 1, Y), :] * not_first
            )
            total = total + (pltpu.roll(here, Z - 1, 1) * z_last - pltpu.roll(here, 1, 1) * z_first)
            if c == 2:
                total = total - 0.5 * rv[own, :]
            mv[c, own, :] = total

    def add(e, axis, factor, values):
        for c, (part, f) in enumerate(TERMS[axis]):
            e[part] = e[part] + (factor * f) * values[c]

    def ends_of(first, last, rows, count):
        return jnp.where(rows == 0, -first, jnp.where(rows == count - 1, last, 0.0))

    arrive(2)

    def beyond(axis, side, part):
        got, load, e = part
        trace, change = flow(e, got[6] * jnp.exp(jnp.where(above > 0, load * got[7], 0.0)))
        there = has[faces[axis][side]]
        return [
            (side - 0.5) * jnp.where(there, stress(e, change, trace, k), 0.0) for k in (X_SET, Y_SET)[axis]
        ]

    for side in range(2):
        e = [rys[side, k] for k in range(6)]
        add(e, 1, 1.0 - 2.0 * side, [yu[side, c] for c in range(3)])
        add(e, 0, 1.0, [
            ends_of(rxy[0, side, pl.ds(c, 1), :], rxy[1, side, pl.ds(c, 1), :], row_x, X) for c in range(3)
        ])
        joined = merge(ryz[side, 0, 1, pl.ds(0, X), :], ryz[side, 1, 1, pl.ds(0, X), :])
        add(e, 2, 2.0, [edge_term(joined, 3 * (1 - side) + c, z_edge_x) for c in range(3)])
        load = row_plane
        for d in depths:
            load = load + rty[side, d - 1]
        for c, tile in enumerate(beyond(1, side, (rys[side], load, e))):
            dv[side, c] = tile

    along_x = []
    for side, at in enumerate((0, X - 1)):
        e = [rxs[side, k] for k in range(6)]
        add(e, 0, 1.0 - 2.0 * side, [uv[c, pl.ds(Y + at * Y, Y), :] for c in range(3)])
        add(e, 1, 1.0, [
            ends_of(rxy[side, 0, pl.ds(c, 1), :], rxy[side, 1, pl.ds(c, 1), :], row, Y) for c in range(3)
        ])
        add(e, 2, 1.0, [
            jnp.where(
                lane == 0, -pltpu.roll(rxz[side, 0, c], 1, 1),
                jnp.where(lane == Z - 1, pltpu.roll(rxz[side, 1, c], Z - 1, 1), 0.0),
            )
            for c in range(3)
        ])
        load = plane
        for d in depths:
            load = load + rtx[side, d - 1]
        along_x.append(beyond(0, side, (rxs[side], load, e)))

    halo = [jnp.where(even, rzs[0, k], rzs[1, k]) for k in range(2)]
    parts = [shift(halo[k // 4], -(k % 4) * block) for k in range(8)]
    from_x = []
    for c in range(3):
        left, right = (jnp.where(lane == Z - 1, rxz[i, 0, c], rxz[i, 1, c]) for i in range(2))
        from_x.append(jnp.where(
            pair == 0, -shift(left, 1), jnp.where(pair == X - 1, shift(right, 2 * X - 1), 0.0)
        ))
    even_row = (lax.broadcasted_iota(jnp.int32, (1, Z), 1) & 1) == 0
    from_y = ends_of(
        jnp.where(even_row, ryz[0, 0, 0, pl.ds(Y - 1, 1), :], ryz[0, 1, 0, pl.ds(Y - 1, 1), :]),
        jnp.where(even_row, ryz[1, 0, 0, pl.ds(0, 1), :], ryz[1, 1, 0, pl.ds(0, 1), :]),
        row, Y,
    )
    e = list(parts[:6])
    add(e, 0, 1.0, from_x)
    add(e, 1, 1.0, [shift(from_y, -c * block) for c in range(3)])
    add(e, 2, 1.0, [zown[c] for c in range(3)])
    deeper = plane
    for d in depths:
        if d >= 2:
            deeper = deeper + rt[d - 1]
    load = jnp.where(even, deeper, carried + zt[...])
    trace, change = flow(e, parts[6] * jnp.exp(load * parts[7]))
    known = jnp.where(
        even,
        has[0, 0, -1].astype(jnp.float32),
        has[0, 0, 1].astype(jnp.float32),
    )
    for c in range(3):
        jv[c] = jnp.where(pair < X, stress(e, change, trace, Z_SET[c]) * known, 0.0)

    for c in range(3):
        for side, at in enumerate((0, X - 1)):
            own = pl.ds(at * Y, Y)
            mv[c, own, :] = mv[c, own, :] + along_x[side][c]

    settle(send_sem.at[0], gone)


def finish(dims, fv, mv, jv, dv, f_hbm, m_hbm, ms, sem):
    X, Y, Z = dims
    copies = [pltpu.make_async_copy(fv, f_hbm, sem.at[0])]
    copies[0].start()
    lane = lax.broadcasted_iota(jnp.int32, (Y, Z), 1)
    z_edge = jnp.where(lane == 0, -0.5, jnp.where(lane == Z - 1, 0.5, 0.0)).astype(jnp.float32)
    row = lax.broadcasted_iota(jnp.int32, (Y, Z), 0)
    joined = [merge(jv[c], jv[c]) for c in range(3)]
    groups = 4
    span = X // groups
    for g in range(groups):
        for x in range(g * span, (g + 1) * span):
            own = pl.ds(x * Y, Y)
            for c in range(3):
                first, last = (dv[side, c, pl.ds(x, 1), :] for side in range(2))
                edge = jnp.where(row == 0, first, jnp.where(row == Y - 1, last, 0.0))
                ms[c, own, :] = mv[c, own, :] + edge + edge_term(joined[c], x, z_edge)
        rows = pl.ds(g * span * Y, span * Y)
        copies.append(pltpu.make_async_copy(ms.at[:, rows, :], m_hbm.at[:, rows, :], sem.at[1 + g]))
        copies[-1].start()
    for copy in copies:
        copy.wait()


def shards(sizes, u, e, t, r, b):
    X, Y, Z = t.shape
    N = X * Y
    layers = sizes[2]
    assert 8 * X <= Z and Z % 128 == 0 and Y % 8 == 0 and X % 8 == 0
    W = max(X, Y)
    f32 = jnp.float32
    vmem = pltpu.VMEM
    dma = pltpu.SemaphoreType.DMA
    any_space = pl.BlockSpec(memory_space=pl.ANY)
    in_vmem = pl.BlockSpec(memory_space=vmem)
    D = max(layers - 1, 1)
    kept = pl.pallas_call(
        functools.partial(kernel, (X, Y, Z), sizes),
        out_shape=(vmem((6, N, Z), f32), vmem((3, N, Z), f32), vmem((3, Y, Z), f32), vmem((2, 3, X, Z), f32)),
        in_specs=[any_space] * 6,
        out_specs=(in_vmem,) * 4,
        scratch_shapes=[
            vmem((3, N + 2 * Y, Z), f32),
            vmem((Z, 2 * Z), jnp.bfloat16),
            vmem((3, Y, Z), f32),
            vmem((6, N, Z), f32),
            vmem((N, Z), f32),
            vmem((N, Z), f32),
            vmem((N, Z), jnp.int32),
            vmem((N, Z), f32),
            vmem((N, Z), f32),
            vmem((6, N, Z), f32),
            vmem((N, Z), f32),
            vmem((N, Z), f32),
            vmem((6, N + 2 * Y, Z), f32),
            vmem((2, 8, Y, Z), f32),
            vmem((2, 8, X, Z), f32),
            vmem((2, 3, X, Z), f32),
            vmem((2, W, Z), f32),
            vmem((2, Y, Z), f32),
            vmem((2, 2, 8, Z), f32),
            vmem((Y, Z), f32),
            vmem((2, Y, Z), f32),
            vmem((2, X, Z), f32),
            vmem((2, 3, Y, Z), f32),
            vmem((2, 8, Y, Z), f32),
            vmem((2, 3, X, Z), f32),
            vmem((2, 8, X, Z), f32),
            vmem((2, Y, Z), f32),
            vmem((2, 2, Y, Z), f32),
            vmem((2, 2, 8, Z), f32),
            vmem((2, 2, 3, Y, Z), f32),
            vmem((2, 2, 2, W, Z), f32),
            vmem((D, Y, Z), f32),
            vmem((2, D, Y, Z), f32),
            vmem((2, D, X, Z), f32),
            dma((3,)),
            pltpu.SemaphoreType.REGULAR((2,)),
            pltpu.SemaphoreType.REGULAR((1 if layers == 2 else 2,)),
            dma((1,)),
            dma((3,)),
            vmem(((11 + layers) * 2 * (X + Y) + (18 + layers) * Y + 8 * W, Z), f32),
        ],
        compiler_params=pltpu.CompilerParams(collective_id=0, has_side_effects=True),
        name="strain_step",
    )(u.reshape(3, N, Z), u, e.reshape(6, N, Z), t.reshape(N, Z), r.reshape(N, Z), b.reshape(N, Z))
    f, m = pl.pallas_call(
        functools.partial(finish, (X, Y, Z)),
        out_shape=(jax.ShapeDtypeStruct((6, N, Z), f32), jax.ShapeDtypeStruct((3, N, Z), f32)),
        in_specs=[in_vmem] * 4,
        out_specs=(any_space, any_space),
        scratch_shapes=[vmem((3, N, Z), f32), dma((5,))],
        name="finish",
    )(*(pltpu.with_memory_space_constraint(k, vmem) for k in kept))
    return f.reshape(6, X, Y, Z), m.reshape(3, X, Y, Z)


def solution(mesh):
    sizes = tuple(mesh.shape[a] for a in AXES)
    field = P("gx", "gy", "gz")
    fields = P(None, "gx", "gy", "gz")
    return jax.shard_map(
        functools.partial(shards, sizes),
        mesh=mesh,
        in_specs=(fields, fields, field, field, field),
        out_specs=(fields, fields),
        check_vma=False,
    )
```
